32 devices in a mesh: dp: 8 (over z, x), th: 2 (over core), tw: 2 (over y).
Axes of the slice: x: 2, y: 2, z: 4, core: 2. Of those that a mesh axis runs over, the one named last changes fastest.
Arguments:
- tokens: bfloat16 [16, 1536, 768], P('dp', ('th', 'tw')), may hold values from -6 to 6
- segment_ids: int32 [16, 1536], P('dp'), may hold values from 0 to 7, never falling along the last dimension, each value on 1 to 768 neighbouring positions
- norm1_gain: float32 [768], replicated, may hold values from 0.5 to 1.5
- norm1_shift: float32 [768], replicated, may hold values from -3 to 3
- w_qkv: bfloat16 [3, 768, 768], P(None, None, ('th', 'tw')), may hold values from -0.21875 to 0.21875
- b_qv: float32 [2, 768], P(None, ('th', 'tw')), may hold values from -3 to 3
- w_out: bfloat16 [768, 768], P(('th', 'tw')), may hold values from -0.875 to 0.875
- b_out: float32 [768], replicated, may hold values from -3 to 3
- norm2_gain: float32 [768], replicated, may hold values from 0.5 to 1.5
- norm2_shift: float32 [768], replicated, may hold values from -3 to 3
- w_up: bfloat16 [768, 3072], replicated, may hold values from -0.21875 to 0.21875
- b_up: float32 [3072], replicated, may hold values from -3 to 3
- w_down: bfloat16 [3072, 768], replicated, may hold values from -0.109375 to 0.109375
- b_down: float32 [768], replicated, may hold values from -3 to 3
- cotangent: bfloat16 [16, 1536, 768], P('dp', ('th', 'tw')), may hold values from -6 to 6
Outputs:
- block_out: bfloat16 [16, 1536, 768], P('dp', ('th', 'tw'))
- grad_tokens: bfloat16 [16, 1536, 768], P('dp', ('th', 'tw'))
- grad_norm1_gain: float32 [768], replicated
- grad_norm1_shift: float32 [768], replicated
- grad_w_qkv: float32 [3, 768, 768], P(None, None, ('th', 'tw'))
- grad_b_qv: float32 [2, 768], P(None, ('th', 'tw'))
- grad_w_out: float32 [768, 768], P(('th', 'tw'))
- grad_b_out: float32 [768], replicated
- grad_norm2_gain: float32 [768], replicated
- grad_norm2_shift: float32 [768], replicated
- grad_w_up: float32 [768, 3072], replicated
- grad_b_up: float32 [3072], replicated
- grad_w_down: float32 [3072, 768], replicated
- grad_b_down: float32 [768], replicated
The draws below stay inside these ranges and needn't reach their ends.
Inputs may be any that keep to these rules, and one draw needn't show every extreme that they name: `segment_ids`: within each row the ids never fall, and one image holds 1 to 768 tokens.
All inputs are finite; a program needn't handle non-finite values.
Results may differ from the reference program's by a relative error of at most 0.015.
Values may be sent and summed in bfloat16 or wider, within the bound.
A program may use at most 192 MiB of HBM per device.

```python
import math
from functools import partial
import jax
import jax.numpy as jnp
import numpy as np
from jax import lax

D = 768
HD = 64
FF = 3072
ROW_LEN = 1536
ROWS_DEV = 2
SEGS = 8
ROWS = 16


def block_levels(own_key, dims, shards, low, high):
    def one(position, parts):
        steps = jax.random.uniform(jax.random.fold_in(jax.random.fold_in(own_key, 6), position), (parts,), jnp.float32, low / len(shards), high / len(shards))
        return jnp.repeat(jnp.exp(steps), dims[position] // parts).reshape((-1,) + (1,) * (len(dims) - position - 1))

    level = one(*shards[0])
    for cut in shards[1:]:
        level = level * one(*cut)
    return level


def length_profile(count, total, reach, slope):
    weights = [(1 << 20) // math.isqrt(rank ** slope) + 1 for rank in range(2, count + 1)]
    surplus, given = total - reach - (count - 1), [1] * (count - 1)
    while surplus > 0:
        movable = [i for i in range(count - 1) if given[i] < reach]
        mass, left = sum([weights[i] for i in movable]), surplus
        for i in movable:
            more = min(reach - given[i], max(1, left * weights[i] // mass), surplus)
            given[i] = given[i] + more
            surplus = surplus - more
    return np.array([reach] + given)


def ragged(rng, number_of, total, reach, lean):
    if number_of == 2:
        one = jax.random.randint(rng, (), max(1, total - reach), min(reach, total - 1) + 1)
        return jnp.stack([one, total - one])
    sizes = jnp.asarray(length_profile(number_of, total, reach, lean), jnp.int32)
    pairs = (number_of - 1) // 2
    donor, taker = sizes[1:1 + 2 * pairs:2], sizes[2:2 + 2 * pairs:2]
    margin = jnp.minimum(donor - 1, reach - taker)
    moved = jax.random.randint(jax.random.fold_in(rng, 1), (pairs,), 0, 1 << 20) % (margin + 1)
    sizes = sizes.at[1:1 + 2 * pairs:2].set(donor - moved).at[2:2 + 2 * pairs:2].set(taker + moved)
    return sizes[jax.random.permutation(jax.random.fold_in(rng, 2), number_of)]


def scatter_about(stream_key, extent, deviation, limit, pieces=(), dtype=jnp.bfloat16):
    drawn = deviation * jax.random.normal(stream_key, extent, jnp.float32)
    if pieces:
        drawn = drawn * block_levels(stream_key, extent, pieces, -0.22, 0.18)
    return jnp.clip(drawn, -limit, limit).astype(dtype)


def setup_inputs(seed: int = 0) -> dict:
    streams_of = jax.random.split(jax.random.key(seed), 16)
    tokens = scatter_about(streams_of[0], (ROWS, ROW_LEN, D), 1.0, 6.0, ((0, 8), (1, 4)))
    segment_ids = jax.vmap(lambda own: jnp.searchsorted(jnp.cumsum(ragged(own, SEGS, ROW_LEN, ROW_LEN // 2, 1)), jnp.arange(ROW_LEN), side="right"))(jax.random.split(streams_of[1], ROWS)).reshape((ROWS, ROW_LEN)).astype(jnp.int32)
    norm1_gain = jnp.clip(1.0 + 0.1 * jax.random.normal(streams_of[2], (D,), jnp.float32), 0.5, 1.5)
    norm1_shift = scatter_about(streams_of[3], (D,), 0.5, 3.0, (), jnp.float32)
    w_qkv = scatter_about(streams_of[4], (3, D, D), D ** -0.5, 0.21875, ((2, 4),))
    b_qv = scatter_about(streams_of[5], (2, D), 0.5, 3.0, ((1, 4),), jnp.float32)
    w_out = scatter_about(streams_of[6], (D, D), (D // 16) ** -0.5, 0.875, ((0, 4),))
    b_out = scatter_about(streams_of[7], (D,), 0.5, 3.0, (), jnp.float32)
    norm2_gain = jnp.clip(1.0 + 0.1 * jax.random.normal(streams_of[8], (D,), jnp.float32), 0.5, 1.5)
    norm2_shift = scatter_about(streams_of[9], (D,), 0.5, 3.0, (), jnp.float32)
    w_up = scatter_about(streams_of[10], (D, FF), D ** -0.5, 0.21875)
    b_up = scatter_about(streams_of[11], (FF,), 0.5, 3.0, (), jnp.float32)
    w_down = scatter_about(streams_of[12], (FF, D), FF ** -0.5, 0.109375)
    b_down = scatter_about(streams_of[13], (D,), 0.5, 3.0, (), jnp.float32)
    cotangent = scatter_about(streams_of[14], (ROWS, ROW_LEN, D), 1.0, 6.0, ((0, 8), (1, 4)))
    return dict(tokens=tokens, segment_ids=segment_ids, norm1_gain=norm1_gain, norm1_shift=norm1_shift, w_qkv=w_qkv, b_qv=b_qv, w_out=w_out, b_out=b_out, norm2_gain=norm2_gain, norm2_shift=norm2_shift, w_up=w_up, b_up=b_up, w_down=w_down, b_down=b_down, cotangent=cotangent)


@jax.custom_vjp
def low(v):
    return lax.optimization_barrier(v.astype(jnp.bfloat16)).astype(jnp.float32)

@jax.custom_vjp
def low_back(v):
    return v

def low_keep(v):
    return (low(v), None)

def low_pass(kept, grad):
    return (grad,)

def back_keep(v):
    return (v, None)

def back_low(kept, grad):
    return (low(grad),)
low.defvjp(low_keep, low_pass)
low_back.defvjp(back_keep, back_low)
EPSILON = 1e-06
PRECISE = lax.Precision.HIGHEST

def layer_norm(field, norm_gain, norm_shift):
    average = lax.optimization_barrier(jnp.mean(field, axis=-1, keepdims=True))
    centred = field - average
    spread = lax.optimization_barrier(jnp.mean(centred * centred, axis=-1, keepdims=True))
    return centred * lax.rsqrt(spread + EPSILON) * norm_gain + norm_shift

def group_forward(parameters, row_items):
    norm1_gain, norm1_shift, w_qkv, b_qv, w_out, b_out, norm2_gain, norm2_shift, w_up, b_up, w_down, b_down = parameters
    inputs, segments = row_items
    group_rows, length = (inputs.shape[0], inputs.shape[1])
    head_count = w_qkv.shape[2] // HD
    normed_one = low(layer_norm(inputs, norm1_gain, norm1_shift))
    projected = jnp.einsum('gld,cde->gcle', normed_one, w_qkv, precision=PRECISE)
    bias_rows = jnp.stack([b_qv[0], jnp.zeros_like(b_qv[0]), b_qv[1]])
    projected = low(low_back(projected + bias_rows[None, :, None, :]))
    query_all = projected[:, 0].reshape(group_rows, length, head_count, HD)
    key_all = projected[:, 1].reshape(group_rows, length, head_count, HD)
    value_all = projected[:, 2].reshape(group_rows, length, head_count, HD)
    scores = jnp.einsum('gqhe,gkhe->ghqk', query_all, key_all, precision=PRECISE) * HD ** (-0.5)
    scores = low_back(scores)
    same_image = segments[:, :, None] == segments[:, None, :]
    scores = jnp.where(same_image[:, None], scores, -1000000000.0)
    probability = low(jax.nn.softmax(scores, axis=-1))
    attended = jnp.einsum('ghqk,gkhe->gqhe', probability, value_all, precision=PRECISE)
    attended = low(low_back(attended.reshape(group_rows, length, head_count * HD)))
    branch = low_back(jnp.einsum('gle,ed->gld', attended, w_out, precision=PRECISE) + b_out)
    middle = inputs + branch
    normed_two = low(layer_norm(middle, norm2_gain, norm2_shift))
    hidden_pre = low_back(jnp.einsum('gld,df->glf', normed_two, w_up, precision=PRECISE) + b_up)
    activated = low(jax.nn.gelu(hidden_pre, approximate=False))
    projected_down = low_back(jnp.einsum('glf,fd->gld', activated, w_down, precision=PRECISE) + b_down)
    return middle + projected_down

def reference(tokens, segment_ids, norm1_gain, norm1_shift, w_qkv, b_qv, w_out, b_out, norm2_gain, norm2_shift, w_up, b_up, w_down, b_down, cotangent):

    def forward(inputs, *parameters):
        grouped = inputs.reshape(ROWS // ROWS_DEV, ROWS_DEV, ROW_LEN, D)
        segments = segment_ids.reshape(ROWS // ROWS_DEV, ROWS_DEV, ROW_LEN)
        group_step = jax.checkpoint(partial(group_forward, parameters))
        return lax.map(group_step, (grouped, segments)).reshape(ROWS, ROW_LEN, D)
    weights = [norm1_gain, norm1_shift, w_qkv, b_qv, w_out, b_out, norm2_gain, norm2_shift, w_up, b_up, w_down, b_down]
    floats = [weight.astype(jnp.float32) for weight in weights]
    result, pullback = jax.vjp(forward, tokens.astype(jnp.float32), *floats)
    gradients = pullback(cotangent.astype(jnp.float32))
    return (result.astype(jnp.bfloat16), gradients[0].astype(jnp.bfloat16), gradients[1], gradients[2], gradients[3], gradients[4], gradients[5], gradients[6], gradients[7], gradients[8], gradients[9], gradients[10], gradients[11], gradients[12])
```

```python
import jax
import jax.numpy as jnp
from jax import lax
from jax.experimental import pallas as pl
from jax.experimental.pallas import tpu as pltpu
from jax.sharding import PartitionSpec as P

NT=(((1,),(1,)),((),())); NN=(((1,),(0,)),((),())); TN=(((0,),(0,)),((),()))
F32=jnp.float32; BF=jnp.bfloat16
BQ=256; BK=256; HD=64
def dot(a,b,d): return lax.dot_general(a,b,d,preferred_element_type=F32)

def fwd_kernel(lo_ref, hi_ref, q_ref, k_ref, v_ref, mq_ref, mk_ref, o_ref, lse_ref, m_ref, l_ref, acc_ref):
    i=pl.program_id(0)
    pairs=q_ref.shape[1]//128
    lane=lax.broadcasted_iota(jnp.int32,(1,128),1)
    halves=(lane<HD, lane>=HD)
    m_ref[...]=jnp.full(m_ref.shape,-1e30,F32)
    l_ref[...]=jnp.zeros_like(l_ref)
    acc_ref[...]=jnp.zeros_like(acc_ref)
    def body(j,_):
        ks=pl.ds(pl.multiple_of(j*BK,BK),BK)
        mk=mk_ref[ks,:]
        for p in range(pairs):
            cols=slice(p*128,(p+1)*128)
            qx=jnp.concatenate([q_ref[:,cols],mq_ref[...]],1)
            k2=k_ref[ks,cols]; v2=v_ref[ks,cols]
            ps=[]
            for e in range(2):
                h=2*p+e
                kx=jnp.concatenate([jnp.where(halves[e],k2,jnp.zeros_like(k2)),mk],1)
                s=dot(kx,qx,NT)
                m_old=m_ref[h:h+1,:]
                m_new=jnp.maximum(m_old,jnp.max(s,axis=0,keepdims=True))
                alpha=jnp.exp(m_old-m_new)
                pe=jnp.exp(s-m_new)
                l_ref[h:h+1,:]=l_ref[h:h+1,:]*alpha+jnp.sum(pe,axis=0,keepdims=True)
                m_ref[h:h+1,:]=m_new
                acc_ref[h*HD:(h+1)*HD,:]=acc_ref[h*HD:(h+1)*HD,:]*alpha
                ps.append(pe.astype(BF))
            vcat=jnp.concatenate([jnp.where(halves[0],v2,jnp.zeros_like(v2)),jnp.where(halves[1],v2,jnp.zeros_like(v2))],0)
            acc_ref[cols,:]+=dot(vcat,jnp.concatenate(ps,0),TN)
        return 0
    lax.fori_loop(lo_ref[i],hi_ref[i],body,0)
    for p in range(pairs):
        parts=[]
        for e in range(2):
            h=2*p+e
            parts.append(acc_ref[h*HD:(h+1)*HD,:]*(1.0/l_ref[h:h+1,:]))
        o_ref[:,p*128:(p+1)*128]=jnp.concatenate(parts,0).T.astype(BF)
    lse_ref[...]=m_ref[...]+jnp.log(jnp.maximum(l_ref[...],1e-37))

def attn_fwd(q,k,v,mq,mk,lo,hi):
    L,C=q.shape
    return pl.pallas_call(fwd_kernel,
        grid_spec=pltpu.PrefetchScalarGridSpec(num_scalar_prefetch=2,grid=(L//BQ,),
          in_specs=[pl.BlockSpec((BQ,C),lambda i,*_:(i,0)),pl.BlockSpec((L,C),lambda i,*_:(0,0)),pl.BlockSpec((L,C),lambda i,*_:(0,0)),
                    pl.BlockSpec((BQ,128),lambda i,*_:(i,0)),pl.BlockSpec((L,128),lambda i,*_:(0,0))],
          out_specs=[pl.BlockSpec((BQ,C),lambda i,*_:(i,0)),pl.BlockSpec((8,BQ),lambda i,*_:(0,i))],
          scratch_shapes=[pltpu.VMEM((8,BQ),F32),pltpu.VMEM((8,BQ),F32),pltpu.VMEM((C,BQ),F32)]),
        out_shape=[jax.ShapeDtypeStruct((L,C),BF),jax.ShapeDtypeStruct((8,L),F32)],
        name="attention_forward",
    )(lo,hi,q,k,v,mq,mk)

def bwd_kernel(lo_ref, hi_ref, q_ref, k_ref, v_ref, do_ref, o_ref, lse_ref, mq_ref, mk_ref, dq_ref, dk_ref, dv_ref, dk_acc, dv_acc, dq_acc, qcat, docat):
    i=pl.program_id(0); n=pl.num_programs(0)
    C=q_ref.shape[1]; pairs=C//128
    lane=lax.broadcasted_iota(jnp.int32,(1,128),1)
    halves=(lane<HD, lane>=HD)
    @pl.when(i==0)
    def _():
        dk_acc[...]=jnp.zeros_like(dk_acc); dv_acc[...]=jnp.zeros_like(dv_acc)
    dq_acc[...]=jnp.zeros_like(dq_acc)
    sel=(lax.broadcasted_iota(jnp.int32,(8,C),1)//HD==lax.broadcasted_iota(jnp.int32,(8,C),0)).astype(F32)
    delta=lax.dot_general(sel,do_ref[...].astype(F32)*o_ref[...].astype(F32),NT,precision=lax.Precision.HIGHEST,preferred_element_type=F32)
    for p in range(pairs):
        cols=slice(p*128,(p+1)*128)
        for e in range(2):
            q2=q_ref[:,cols]; d2=do_ref[:,cols]
            qcat[p,e*BQ:(e+1)*BQ,:]=jnp.where(halves[e],q2,jnp.zeros_like(q2))
            docat[p,e*BQ:(e+1)*BQ,:]=jnp.where(halves[e],d2,jnp.zeros_like(d2))
    lse=lse_ref[...]
    def body(j,_):
        ks=pl.ds(pl.multiple_of(j*BK,BK),BK)
        mk=mk_ref[ks,:]
        for p in range(pairs):
            cols=slice(p*128,(p+1)*128)
            qx=jnp.concatenate([q_ref[:,cols],mq_ref[...]],1)
            k2=k_ref[ks,cols]; v2=v_ref[ks,cols]; d2=do_ref[:,cols]
            ps=[]; dss=[]; kms=[]
            for e in range(2):
                h=2*p+e
                km=jnp.where(halves[e],k2,jnp.zeros_like(k2)); vm=jnp.where(halves[e],v2,jnp.zeros_like(v2))
                s=dot(jnp.concatenate([km,mk],1),qx,NT)
                pr=jnp.exp(s-lse[h:h+1,:])
                dp=dot(vm,d2,NT)
                ds=pr*(dp-delta[h:h+1,:])
                ps.append(pr.astype(BF)); dss.append(ds.astype(BF)); kms.append(km)
            dv_acc[ks,cols]+=dot(jnp.concatenate(ps,1),docat[p],NN)
            dk_acc[ks,cols]+=dot(jnp.concatenate(dss,1),qcat[p],NN)
            dq_acc[cols,:]+=dot(jnp.concatenate(kms,0),jnp.concatenate(dss,0),TN)
        return 0
    lax.fori_loop(lo_ref[i],hi_ref[i],body,0)
    dq_ref[...]=(dq_acc[...]*0.125).T.astype(BF)
    @pl.when(i==n-1)
    def _():
        dk_ref[...]=dk_acc[...].astype(BF); dv_ref[...]=dv_acc[...].astype(BF)

def attn_bwd(q,k,v,do,o,lse,mq,mk,lo,hi):
    L,C=q.shape
    blk=pl.BlockSpec((BQ,C),lambda i,*_:(i,0)); full=pl.BlockSpec((L,C),lambda i,*_:(0,0))
    return pl.pallas_call(bwd_kernel,
        grid_spec=pltpu.PrefetchScalarGridSpec(num_scalar_prefetch=2,grid=(L//BQ,),
          in_specs=[blk,full,full,blk,blk,pl.BlockSpec((8,BQ),lambda i,*_:(0,i)),pl.BlockSpec((BQ,128),lambda i,*_:(i,0)),pl.BlockSpec((L,128),lambda i,*_:(0,0))],
          out_specs=[blk,full,full],
          scratch_shapes=[pltpu.VMEM((L,C),F32),pltpu.VMEM((L,C),F32),pltpu.VMEM((C,BQ),F32),pltpu.VMEM((C//128,2*BQ,128),BF),pltpu.VMEM((C//128,2*BQ,128),BF)]),
        out_shape=[jax.ShapeDtypeStruct((L,C),BF)]*3,
        name="attention_backward",
    )(lo,hi,q,k,v,do,o,lse,mq,mk)

def seg_tables(seg):
    L=seg.shape[0]
    lane=jnp.arange(128,dtype=jnp.int32)[None,:]
    same=seg[:,None]==lane
    mk=same.astype(BF)
    mq=jnp.where(same|(lane>=8),0.0,-float(2**40)).astype(BF)
    first=seg[::BQ]; last=seg[BQ-1::BQ]
    lo=jnp.sum(seg[None,:]<first[:,None],axis=1,dtype=jnp.int32)//BK
    hi=(jnp.sum(seg[None,:]<=last[:,None],axis=1,dtype=jnp.int32)+BK-1)//BK
    return mq,mk,lo,hi

EPSILON = 1e-06


def layer_norm(field, norm_gain, norm_shift):
    average = jnp.mean(field, axis=-1, keepdims=True)
    centred = field - average
    spread = jnp.mean(centred * centred, axis=-1, keepdims=True)
    return centred * lax.rsqrt(spread + EPSILON) * norm_gain + norm_shift


def gelu_exact(field):
    return jax.nn.gelu(field, approximate=False)


SWAP = [(0, 1), (1, 0)]


def swap(value, axis):
    return lax.ppermute(value, axis, SWAP)


def in_order(mine, other, index, axis):
    return jnp.where(
        index == 0, jnp.concatenate([mine, other], axis), jnp.concatenate([other, mine], axis)
    )


def own_row(rows, tw):
    mine = lax.dynamic_index_in_dim(rows, tw, 0, keepdims=False)
    other = lax.dynamic_index_in_dim(rows, 1 - tw, 0, keepdims=False)
    return in_order(mine, swap(other, "tw"), tw, 0)


def back_rows(half, tw):
    quarter = half.shape[0] // 2
    mine = lax.dynamic_slice_in_dim(half, tw * quarter, quarter, 0)
    other = lax.dynamic_slice_in_dim(half, (1 - tw) * quarter, quarter, 0)
    got = swap(other, "tw")
    return jnp.where(tw == 0, jnp.stack([mine, got]), jnp.stack([got, mine]))


def whole_row(half, th):
    return in_order(half, swap(half, "th"), th, 0)


def sum_halves(partial, th):
    half = partial.shape[0] // 2
    mine = lax.dynamic_slice_in_dim(partial, th * half, half, 0)
    other = lax.dynamic_slice_in_dim(partial, (1 - th) * half, half, 0)
    return mine + swap(other.astype(BF), "th").astype(F32)


def mm(spec, a, b):
    return jnp.einsum(spec, a, b, preferred_element_type=F32)


def body(
    tokens,
    segment_ids,
    norm1_gain,
    norm1_shift,
    w_qkv,
    b_qv,
    w_out,
    b_out,
    norm2_gain,
    norm2_shift,
    w_up,
    b_up,
    w_down,
    b_down,
    cotangent,
):
    th, tw = lax.axis_index("th"), lax.axis_index("tw")
    d = tokens.shape[-1]
    mine = w_qkv.shape[2]
    inputs = own_row(tokens, tw).astype(F32)
    w_qkv_other = swap(w_qkv, "tw")
    w_heads = jnp.concatenate([w_qkv, w_qkv_other], 2)
    b_heads = jnp.concatenate([b_qv, swap(b_qv, "tw")], 1)
    w_out_heads = jnp.concatenate([w_out, swap(w_out, "tw")], 0)
    cot = own_row(cotangent, tw)
    seg = lax.dynamic_index_in_dim(segment_ids, tw, 0, keepdims=False)
    tables = seg_tables(seg)

    normed_one, norm_one_back = jax.vjp(layer_norm, inputs, norm1_gain, norm1_shift)
    normed_row = whole_row(normed_one.astype(BF), th)
    query = (mm("ld,de->le", normed_row, w_heads[0]) + b_heads[0]).astype(BF) * BF(0.125)
    key = mm("ld,de->le", normed_row, w_heads[1]).astype(BF)
    value = (mm("ld,de->le", normed_row, w_heads[2]) + b_heads[1]).astype(BF)
    attended, totals = attn_fwd(query, key, value, *tables)
    middle = inputs + sum_halves(mm("le,ed->ld", attended, w_out_heads), th) + b_out
    normed_two, norm_two_back = jax.vjp(layer_norm, middle, norm2_gain, norm2_shift)
    second_low = normed_two.astype(BF)
    hidden_pre = mm("ld,df->lf", second_low, w_up) + b_up
    activated, gelu_back = jax.vjp(gelu_exact, hidden_pre)
    active_low = activated.astype(BF)
    grad_w_down = mm("lf,ld->fd", active_low, cot)
    grad_active = mm("ld,fd->lf", cot, w_down)
    grad_hidden = gelu_back(grad_active)[0].astype(BF)
    grad_w_up = mm("ld,lf->df", second_low, grad_hidden)
    big = lax.psum((grad_w_up.astype(BF), grad_w_down.astype(BF)), ("dp", "th", "tw"))
    block_out = middle + (mm("lf,fd->ld", active_low, w_down) + b_down)
    block_out = back_rows(block_out.astype(BF), tw)
    upstream = cot.astype(F32)
    grad_b_down = jnp.sum(upstream, axis=0)
    grad_b_up = jnp.sum(grad_hidden.astype(F32), axis=0)
    grad_normed_two = mm("lf,df->ld", grad_hidden, w_up)
    grad_mid_norm, grad_gain_two, grad_shift_two = norm_two_back(grad_normed_two)
    grad_middle = upstream + grad_mid_norm
    grad_branch = grad_middle.astype(BF)
    grad_b_out = jnp.sum(grad_branch.astype(F32), axis=0)
    grad_whole = whole_row(grad_branch, th)
    grad_heads = mm("ld,ed->le", grad_whole, w_out_heads).astype(BF)
    grad_w_out = mm("le,ld->ed", attended, grad_whole)
    dq, dk, dv = attn_bwd(query, key, value, grad_heads, attended, totals, *tables)
    grad_w_qkv = jnp.stack([mm("ld,le->de", normed_row, g) for g in (dq, dk, dv)])
    grad_normed = (
        mm("le,de->ld", dq, w_heads[0]) + mm("le,de->ld", dk, w_heads[1]) + mm("le,de->ld", dv, w_heads[2])
    )
    grad_tile = sum_halves(grad_normed, th)
    grad_inputs, grad_gain_one, grad_shift_one = norm_one_back(grad_tile)
    grad_tokens = back_rows((grad_middle + grad_inputs).astype(BF), tw)

    def reduce_heads(grad, axis):
        own = lax.slice_in_dim(grad, 0, mine, axis=axis)
        other = lax.slice_in_dim(grad, mine, 2 * mine, axis=axis)
        return (own + swap(other.astype(BF), "tw").astype(F32)).astype(BF)

    heads = lax.psum((reduce_heads(grad_w_qkv, 2), reduce_heads(grad_w_out, 0)), "dp")
    grad_b = jnp.stack([jnp.sum(dq.astype(F32), 0), jnp.sum(dv.astype(F32), 0)])
    place = jnp.zeros((2, d), F32)
    place = lax.dynamic_update_slice(place, grad_b[:, :mine], (0, (2 * th + tw) * mine))
    place = lax.dynamic_update_slice(place, grad_b[:, mine:], (0, (2 * th + 1 - tw) * mine))
    vectors = (grad_gain_one, grad_shift_one, grad_b_out, grad_gain_two, grad_shift_two, grad_b_down, grad_b_up, place.reshape(-1))
    small = lax.psum(jnp.concatenate(vectors), ("dp", "th", "tw"))
    small_b_qv = lax.dynamic_slice_in_dim(small[-2 * d :].reshape(2, d), (2 * th + tw) * mine, mine, 1)
    return (
        block_out,
        grad_tokens,
        small[:d],
        small[d : 2 * d],
        heads[0].astype(F32),
        small_b_qv,
        heads[1].astype(F32),
        small[2 * d : 3 * d],
        small[3 * d : 4 * d],
        small[4 * d : 5 * d],
        big[0].astype(F32),
        small[6 * d : -2 * d],
        big[1].astype(F32),
        small[5 * d : 6 * d],
    )


def solution(mesh):
    return jax.shard_map(
        body,
        mesh=mesh,
        in_specs=(
            P("dp", ("th", "tw"), None),
            P("dp", None),
            P(),
            P(),
            P(None, None, ("th", "tw")),
            P(None, ("th", "tw")),
            P(("th", "tw"), None),
            P(),
            P(),
            P(),
            P(),
            P(),
            P(),
            P(),
            P("dp", ("th", "tw"), None),
        ),
        out_specs=(
            P("dp", ("th", "tw"), None),
            P("dp", ("th", "tw"), None),
            P(),
            P(),
            P(None, None, ("th", "tw")),
            P(None, ("th", "tw")),
            P(("th", "tw"), None),
            P(),
            P(),
            P(),
            P(),
            P(),
            P(),
            P(),
        ),
        check_vma=False,
    )
```

```python
import functools

import jax
import jax.numpy as jnp
from jax import lax
from jax.experimental import pallas as pl
from jax.experimental.pallas import tpu as pltpu
from jax.sharding import PartitionSpec as P

NT=(((1,),(1,)),((),())); NN=(((1,),(0,)),((),())); TN=(((0,),(0,)),((),()))
F32=jnp.float32; BF=jnp.bfloat16
BQ=256; BK=256; HD=64
def dot(a,b,d): return lax.dot_general(a,b,d,preferred_element_type=F32)

def fwd_kernel(lo_ref, hi_ref, q_ref, k_ref, v_ref, mq_ref, mk_ref, o_ref, lse_ref, m_ref, l_ref, acc_ref):
    i=pl.program_id(0)
    pairs=q_ref.shape[1]//128
    lane=lax.broadcasted_iota(jnp.int32,(1,128),1)
    halves=(lane<HD, lane>=HD)
    m_ref[...]=jnp.full(m_ref.shape,-1e30,F32)
    l_ref[...]=jnp.zeros_like(l_ref)
    acc_ref[...]=jnp.zeros_like(acc_ref)
    def body(j,_):
        ks=pl.ds(pl.multiple_of(j*BK,BK),BK)
        mk=mk_ref[ks,:]
        for p in range(pairs):
            cols=slice(p*128,(p+1)*128)
            qx=jnp.concatenate([q_ref[:,cols],mq_ref[...]],1)
            k2=k_ref[ks,cols]; v2=v_ref[ks,cols]
            ps=[]
            for e in range(2):
                h=2*p+e
                kx=jnp.concatenate([jnp.where(halves[e],k2,jnp.zeros_like(k2)),mk],1)
                s=dot(kx,qx,NT)
                m_old=m_ref[h:h+1,:]
                m_new=jnp.maximum(m_old,jnp.max(s,axis=0,keepdims=True))
                alpha=jnp.exp(m_old-m_new)
                pe=jnp.exp(s-m_new)
                l_ref[h:h+1,:]=l_ref[h:h+1,:]*alpha+jnp.sum(pe,axis=0,keepdims=True)
                m_ref[h:h+1,:]=m_new
                acc_ref[h*HD:(h+1)*HD,:]=acc_ref[h*HD:(h+1)*HD,:]*alpha
                ps.append(pe.astype(BF))
            vcat=jnp.concatenate([jnp.where(halves[0],v2,jnp.zeros_like(v2)),jnp.where(halves[1],v2,jnp.zeros_like(v2))],0)
            acc_ref[cols,:]+=dot(vcat,jnp.concatenate(ps,0),TN)
        return 0
    lax.fori_loop(lo_ref[i],hi_ref[i],body,0)
    for p in range(pairs):
        parts=[]
        for e in range(2):
            h=2*p+e
            parts.append(acc_ref[h*HD:(h+1)*HD,:]*(1.0/l_ref[h:h+1,:]))
        o_ref[:,p*128:(p+1)*128]=jnp.concatenate(parts,0).T.astype(BF)
    lse_ref[...]=m_ref[...]+jnp.log(jnp.maximum(l_ref[...],1e-37))

def attn_fwd(q,k,v,mq,mk,lo,hi):
    L,C=q.shape
    return pl.pallas_call(fwd_kernel,
        grid_spec=pltpu.PrefetchScalarGridSpec(num_scalar_prefetch=2,grid=(L//BQ,),
          in_specs=[pl.BlockSpec((BQ,C),lambda i,*_:(i,0)),pl.BlockSpec((L,C),lambda i,*_:(0,0)),pl.BlockSpec((L,C),lambda i,*_:(0,0)),
                    pl.BlockSpec((BQ,128),lambda i,*_:(i,0)),pl.BlockSpec((L,128),lambda i,*_:(0,0))],
          out_specs=[pl.BlockSpec((BQ,C),lambda i,*_:(i,0)),pl.BlockSpec((8,BQ),lambda i,*_:(0,i))],
          scratch_shapes=[pltpu.VMEM((8,BQ),F32),pltpu.VMEM((8,BQ),F32),pltpu.VMEM((C,BQ),F32)]),
        out_shape=[jax.ShapeDtypeStruct((L,C),BF),jax.ShapeDtypeStruct((8,L),F32)],
        name="attention_forward",
    )(lo,hi,q,k,v,mq,mk)

def bwd_kernel(lo_ref, hi_ref, q_ref, k_ref, v_ref, do_ref, o_ref, lse_ref, mq_ref, mk_ref, dq_ref, dk_ref, dv_ref, dk_acc, dv_acc, dq_acc, qcat, docat):
    i=pl.program_id(0); n=pl.num_programs(0)
    C=q_ref.shape[1]; pairs=C//128
    lane=lax.broadcasted_iota(jnp.int32,(1,128),1)
    halves=(lane<HD, lane>=HD)
    @pl.when(i==0)
    def _():
        dk_acc[...]=jnp.zeros_like(dk_acc); dv_acc[...]=jnp.zeros_like(dv_acc)
    dq_acc[...]=jnp.zeros_like(dq_acc)
    sel=(lax.broadcasted_iota(jnp.int32,(8,C),1)//HD==lax.broadcasted_iota(jnp.int32,(8,C),0)).astype(F32)
    delta=lax.dot_general(sel,do_ref[...].astype(F32)*o_ref[...].astype(F32),NT,precision=lax.Precision.HIGHEST,preferred_element_type=F32)
    for p in range(pairs):
        cols=slice(p*128,(p+1)*128)
        for e in range(2):
            q2=q_ref[:,cols]; d2=do_ref[:,cols]
            qcat[p,e*BQ:(e+1)*BQ,:]=jnp.where(halves[e],q2,jnp.zeros_like(q2))
            docat[p,e*BQ:(e+1)*BQ,:]=jnp.where(halves[e],d2,jnp.zeros_like(d2))
    lse=lse_ref[...]
    def body(j,_):
        ks=pl.ds(pl.multiple_of(j*BK,BK),BK)
        mk=mk_ref[ks,:]
        for p in range(pairs):
            cols=slice(p*128,(p+1)*128)
            qx=jnp.concatenate([q_ref[:,cols],mq_ref[...]],1)
            k2=k_ref[ks,cols]; v2=v_ref[ks,cols]; d2=do_ref[:,cols]
            ps=[]; dss=[]; kms=[]
            for e in range(2):
                h=2*p+e
                km=jnp.where(halves[e],k2,jnp.zeros_like(k2)); vm=jnp.where(halves[e],v2,jnp.zeros_like(v2))
                s=dot(jnp.concatenate([km,mk],1),qx,NT)
                pr=jnp.exp(s-lse[h:h+1,:])
                dp=dot(vm,d2,NT)
                ds=pr*(dp-delta[h:h+1,:])
                ps.append(pr.astype(BF)); dss.append(ds.astype(BF)); kms.append(km)
            dv_acc[ks,cols]+=dot(jnp.concatenate(ps,1),docat[p],NN)
            dk_acc[ks,cols]+=dot(jnp.concatenate(dss,1),qcat[p],NN)
            dq_acc[cols,:]+=dot(jnp.concatenate(kms,0),jnp.concatenate(dss,0),TN)
        return 0
    lax.fori_loop(lo_ref[i],hi_ref[i],body,0)
    dq_ref[...]=(dq_acc[...]*0.125).T.astype(BF)
    @pl.when(i==n-1)
    def _():
        dk_ref[...]=dk_acc[...].astype(BF); dv_ref[...]=dv_acc[...].astype(BF)

def attn_bwd(q,k,v,do,o,lse,mq,mk,lo,hi):
    L,C=q.shape
    blk=pl.BlockSpec((BQ,C),lambda i,*_:(i,0)); full=pl.BlockSpec((L,C),lambda i,*_:(0,0))
    return pl.pallas_call(bwd_kernel,
        grid_spec=pltpu.PrefetchScalarGridSpec(num_scalar_prefetch=2,grid=(L//BQ,),
          in_specs=[blk,full,full,blk,blk,pl.BlockSpec((8,BQ),lambda i,*_:(0,i)),pl.BlockSpec((BQ,128),lambda i,*_:(i,0)),pl.BlockSpec((L,128),lambda i,*_:(0,0))],
          out_specs=[blk,full,full],
          scratch_shapes=[pltpu.VMEM((L,C),F32),pltpu.VMEM((L,C),F32),pltpu.VMEM((C,BQ),F32),pltpu.VMEM((C//128,2*BQ,128),BF),pltpu.VMEM((C//128,2*BQ,128),BF)]),
        out_shape=[jax.ShapeDtypeStruct((L,C),BF)]*3,
        name="attention_backward",
    )(lo,hi,q,k,v,do,o,lse,mq,mk)

def seg_tables(seg):
    L=seg.shape[0]
    lane=jnp.arange(128,dtype=jnp.int32)[None,:]
    same=seg[:,None]==lane
    mk=same.astype(BF)
    mq=jnp.where(same|(lane>=8),0.0,-float(2**40)).astype(BF)
    first=seg[::BQ]; last=seg[BQ-1::BQ]
    lo=jnp.sum(seg[None,:]<first[:,None],axis=1,dtype=jnp.int32)//BK
    hi=(jnp.sum(seg[None,:]<=last[:,None],axis=1,dtype=jnp.int32)+BK-1)//BK
    return mq,mk,lo,hi


TT=256; FC=512
LAG=2; GLAG=2; HLAG=2; HC=3; HSP=2

def bits_of(dp): return dp.bit_length()-1

def big_plan(dp,rows):
    n=bits_of(dp)
    orders=(["tw"]+list(range(n)),[0,"tw"]+list(range(1,n)),[1,2,0,"tw"]+list(range(3,n)))
    unit=16<<(n+1)
    units=rows//unit
    third=max(1,units//4)
    shares=[units-units//3-third,units//3,third]
    return streams(orders,shares,unit)

def head_plan(dp,rows):
    n=bits_of(dp)
    orders=(["tw"]+list(range(n)),[1,2,0,"tw"]+list(range(3,n)))
    unit=16<<n
    units=rows//unit
    low=max(1,units//6)
    return streams(orders,[units-low,low],unit)

def streams(orders,shares,unit):
    out=[]; start=0
    for order,share in zip(orders,shares):
        out.append((order,start,share*unit)); start+=share*unit
    return out

class Peers:
    def __init__(self):
        self.dp=lax.axis_index("dp"); self.th=lax.axis_index("th"); self.tw=lax.axis_index("tw")
    def bit(self,axis):
        return self.tw if axis=="tw" else (self.dp//(1<<axis))%2
    def peer(self,axis):
        if axis=="tw": return {"tw":1-self.tw}
        if axis=="th": return {"th":1-self.th}
        return {"dp":self.dp+(1-2*self.bit(axis))*(1<<axis)}

def send(src,dst,ssem,rsem,peer):
    return pltpu.make_async_remote_copy(src,dst,ssem,rsem,device_id=peer,device_id_type=pl.DeviceIdType.MESH)

def barrier(p,axes):
    sem=pltpu.get_barrier_semaphore()
    for a in axes:
        pl.semaphore_signal(sem,inc=1,device_id=p.peer(a),device_id_type=pl.DeviceIdType.MESH)
    pl.semaphore_wait(sem,len(axes))

def halves(p,order,row,rows,keep_tw=False):
    out=[]
    for axis in order:
        if keep_tw and axis=="tw": out.append((row,row,rows)); continue
        rows//=2; bit=p.bit(axis)
        out.append((row+(1-bit)*rows,row+bit*rows,rows)); row=row+bit*rows
    return out
def al(x): return x if isinstance(x,int) else pl.multiple_of(x,16)
def rows_at(row,n): return pl.ds(al(row),n)

def ffn_kernel(dp,n2,n2T,cot,cotT,wu,wd,bu,bo,gn,gb,red,act,gh,dw,chip_recv,*rest):
    CH=dw.shape[0]; D=n2.shape[1]; T=n2.shape[0]
    plan=big_plan(dp,dw.shape[2]); n=len(plan[0][0]); K=len(plan)
    recv=[rest[k*n:(k+1)*n] for k in range(K)]
    send_sem,recv_sem,chip_send,chip_got=rest[K*n:]
    p=Peers(); g=pl.program_id(0)
    regs=[halves(p,*s) for s in plan]
    def copy(k,s,c):
        out,_,nr=regs[k][s]
        return send(dw.at[c,p.th,rows_at(out,nr),:],recv[k][s].at[c],send_sem.at[k,s,c],recv_sem.at[k,s,c],p.peer(plan[k][0][s]))
    def chip_copy(c):
        return send(dw.at[c,1-p.th],chip_recv.at[c],chip_send.at[c],chip_got.at[c],p.peer("th"))
    @pl.when(g==0)
    def _():
        barrier(p,["th"]+plan[0][0])
        bo[...]=jnp.zeros_like(bo); gn[...]=jnp.zeros_like(gn)
    for s in reversed(range(n)):
        c=g-1-LAG*(s+1)
        @pl.when((c>=0)&(c<CH))
        def _():
            out=0
            for k in range(K):
                copy(k,s,c).wait_recv()
                _,kr,nr=regs[k][s]
                at=(c,p.th,rows_at(kr,nr),slice(None))
                new=dw[at].astype(F32)+recv[k][s][c].astype(F32)
                if s<n-1: dw[at]=new.astype(BF)
                else:
                    red[c,out:out+nr,:]=new.astype(BF); out+=nr
    for s in reversed(range(n)):
        c=g-1-LAG*s
        @pl.when((c>=0)&(c<CH))
        def _():
            for k in range(K): copy(k,s,c).start()
    @pl.when(g<CH)
    def _():
        gsum=jnp.zeros((1,FC),F32)
        for t in range(T//TT):
            r=slice(t*TT,(t+1)*TT)
            h=dot(n2[r,:],wu[...],NN)+bu[...]
            ga=dot(cot[r,:],wd[...],NT)
            cdf=0.5*(1.0+lax.erf(h*(0.5**0.5)))
            a=(h*cdf).astype(BF)
            gr=(ga*(cdf+h*(jnp.exp(h*h*-0.5)*0.3989422804014327))).astype(BF)
            act[r,:]=a; gh[r,:]=gr
            gsum+=jnp.sum(gr.astype(F32),0,keepdims=True)
        gb[...]=gsum
        for t in range(D//TT):
            r=slice(t*TT,(t+1)*TT)
            for m,(lhs,rhs) in enumerate(((n2T,gh),(cotT,act))):
                x=dot(lhs[r,:],rhs[...],NN).astype(BF)
                for q in range(FC//128): dw[g,m,q*D+t*TT:q*D+(t+1)*TT,:]=x[:,q*128:(q+1)*128]
        chip_copy(g).start()
        for t in range(T//TT):
            r=slice(t*TT,(t+1)*TT)
            bo[r,:]+=dot(act[r,:],wd[...],NN)
            gn[r,:]+=dot(gh[r,:],wu[...],NT)
        chip_copy(g).wait_recv()
        def add(q,_):
            r=rows_at(q*TT,TT)
            dw[g,p.th,r,:]=(dw[g,p.th,r,:].astype(F32)+chip_recv[g,r,:].astype(F32)).astype(BF)
            return 0
        lax.fori_loop(0,dw.shape[2]//TT,add,0)
    @pl.when(g==CH+LAG*n)
    def _():
        def drain(c,_):
            chip_copy(c).wait_send()
            for k in range(K):
                for s in range(n): copy(k,s,c).wait_send()
            return 0
        lax.fori_loop(0,CH,drain,0)

def ffn(dp,n2,n2T,cot,cotT,wu,wd,bu):
    T,D=n2.shape; FF=wu.shape[1]; CH=FF//FC; R=FC//128*D
    plan=big_plan(dp,R); n=len(plan[0][0])
    full=pl.BlockSpec((T,D),lambda c:(0,0))
    m=lambda c: jnp.minimum(c,CH-1)
    fin=R>>n
    recv=[pltpu.VMEM((CH,rows>>(s+1),128),BF) for _,_,rows in plan for s in range(n)]
    return pl.pallas_call(functools.partial(ffn_kernel,dp),grid=(CH+LAG*n+1,),
      in_specs=[full]*4+[pl.BlockSpec((D,FC),lambda c:(0,m(c))),pl.BlockSpec((FC,D),lambda c:(m(c),0)),pl.BlockSpec((1,FC),lambda c:(0,m(c)))],
      out_specs=[full,full,pl.BlockSpec((1,FC),lambda c:(0,m(c))),pl.BlockSpec((CH,fin,128),lambda c:(0,0,0))],
      out_shape=[jax.ShapeDtypeStruct((T,D),F32)]*2+[jax.ShapeDtypeStruct((1,FF),F32),jax.ShapeDtypeStruct((CH,fin,128),BF)],
      scratch_shapes=[pltpu.VMEM((T,FC),BF)]*2+[pltpu.VMEM((CH,2,R,128),BF),pltpu.VMEM((CH,R,128),BF)]+recv
        +[pltpu.SemaphoreType.DMA((len(plan),n,CH))]*2+[pltpu.SemaphoreType.DMA((CH,))]*2,
      compiler_params=pltpu.CompilerParams(vmem_limit_bytes=60*2**20,collective_id=0,has_side_effects=True),name="feed_forward")(n2,n2T,cot,cotT,wu,wd,bu)

def finish_kernel(dp,red,heads,vec,up,down,heads_out,vec_out,full,hp,hg,vbuf,vrecv,*rest):
    CH=full.shape[0]; R=full.shape[2]; D=up.shape[0]
    plan=big_plan(dp,R); n=len(plan[0][0]); K=len(plan)
    HR=hp.shape[2]; hplan=head_plan(dp,HR); HK=len(hplan)
    hrecv=[rest[k*n:(k+1)*n] for k in range(HK)]
    send_sem,recv_sem,chip_send,chip_got,hs_sem,hr_sem,ha_send,ha_recv,vs_sem,vr_sem=rest[HK*n:]
    p=Peers(); g=pl.program_id(0); last=pl.num_programs(0)-1
    regs=[halves(p,*s) for s in plan]
    hregs=[halves(p,*s,keep_tw=True) for s in hplan]
    def gat(k,s,c,landed):
        other,mine,nr=regs[k][s]
        ref=full.at[c,p.th,rows_at(other if landed else mine,nr),:]
        return send(ref,ref,send_sem.at[k,s,c],recv_sem.at[k,s,c],p.peer(plan[k][0][s]))
    def chip(c,landed):
        ref=full.at[c,1-p.th if landed else p.th]
        return send(ref,ref,chip_send.at[c],chip_got.at[c],p.peer("th"))
    def hsum(k,s,c):
        order=hplan[k][0]; other,_,nr=hregs[k][s]
        if order[s]=="tw": src=hp.at[c,pl.ds(1,1),rows_at(other,nr),:]
        elif order.index("tw")>s: src=hp.at[c,:,rows_at(other,nr),:]
        else: src=hp.at[c,pl.ds(0,1),rows_at(other,nr),:]
        return send(src,hrecv[k][s].at[c],hs_sem.at[k,s,c],hr_sem.at[k,s,c],p.peer(order[s]))
    def hgat(k,s,c,landed):
        order=hplan[k][0]; other,mine,nr=hregs[k][s]
        ref=hg.at[c,rows_at(other if landed else mine,nr),:]
        return send(ref,ref,ha_send.at[k,s,c],ha_recv.at[k,s,c],p.peer(order[s]))
    backs=[[s for s in reversed(range(n)) if o[s]!="tw"] for o,_,_ in hplan]
    vaxes=["th","tw"]+list(range(n-1))
    def vcopy(i): return send(vbuf.at[i],vrecv.at[i],vs_sem.at[i],vr_sem.at[i],p.peer(vaxes[i]))
    @pl.when(g==0)
    def _():
        out=0
        for k in range(K):
            _,kr,nr=regs[k][n-1]
            for c in range(CH): full[c,p.th,rows_at(kr,nr),:]=red[c,out:out+nr,:]
            out+=nr
        for c in range(hp.shape[0]):
            hp[c]=heads[:,c*HR:(c+1)*HR,:]
        vbuf[0]=vec[...]
        barrier(p,["th"]+plan[0][0])
    steps=n+n-1
    for j in range(steps+1):
        for c in range(hp.shape[0]):
            @pl.when(g==HSP*c+HLAG*j)
            def _():
                for k in range(HK):
                    order=hplan[k][0]
                    if 0<j<=n:
                        s=j-1
                        hsum(k,s,c).wait_recv()
                        _,kr,nr=hregs[k][s]
                        q=slice(0,2) if order.index("tw")>s else slice(0,1)
                        at=(c,q,rows_at(kr,nr),slice(None))
                        new=(hp[at].astype(F32)+hrecv[k][s][c].astype(F32)).astype(BF)
                        if j<n: hp[at]=new
                        else: hg[c,rows_at(kr,nr),:]=new[0]
                    elif j>n: hgat(k,backs[k][j-n-1],c,True).wait_recv()
                for k in range(HK):
                    if j<n: hsum(k,j,c).start()
                    elif j<steps: hgat(k,backs[k][j-n],c,False).start()
                if j==steps: heads_out[c*HR:(c+1)*HR,:]=hg[c]
    for i in range(len(vaxes)+1):
        @pl.when(g==HLAG*i)
        def _():
            if i>0:
                vcopy(i-1).wait_recv()
                x=vbuf[i-1]+vrecv[i-1]
                if i<len(vaxes): vbuf[i]=x
                else: vec_out[...]=x
            if i<len(vaxes): vcopy(i).start()
    for j in reversed(range(n+1)):
        c=g-GLAG*j
        @pl.when((c>=0)&(c<CH))
        def _():
            if j>0:
                for k in range(K): gat(k,n-j,c,True).wait_recv()
            if j<n:
                for k in range(K): gat(k,n-1-j,c,False).start()
            else: chip(c,False).start()
    c=g-GLAG*(n+1)
    @pl.when((c>=0)&(c<CH))
    def _():
        chip(c,True).wait_recv()
        for q in range(FC//128):
            cols=slice(q*128,(q+1)*128)
            up[:,cols]=full[c,0,q*D:(q+1)*D,:]
            down[:,cols]=full[c,1,q*D:(q+1)*D,:]
    @pl.when(g==last)
    def _():
        def drain(c,_):
            chip(c,False).wait_send()
            for k in range(K):
                for s in range(n): gat(k,s,c,False).wait_send()
            return 0
        lax.fori_loop(0,CH,drain,0)
        for c in range(hp.shape[0]):
            for k in range(HK):
                for s in range(n): hsum(k,s,c).wait_send()
                for s in backs[k]: hgat(k,s,c,False).wait_send()
        for i in range(len(vaxes)): vcopy(i).wait_send()

def finish(dp,red,heads,vec,D):
    CH,fin,_=red.shape; R=FC//128*D
    plan=big_plan(dp,R); n=len(plan[0][0])
    HRA=heads.shape[1]; HR=HRA//HC; hplan=head_plan(dp,HR)
    m=lambda g: jnp.clip(g-GLAG*(n+1),0,CH-1)
    hrecv=[]
    for order,_,rows in hplan:
        q=2
        for axis in order:
            if axis=="tw": q=1
            else: rows//=2
            hrecv.append(pltpu.VMEM((HC,q,rows,128),BF))
    V=vec.shape[0]; nv=n+1
    whole=lambda x: pl.BlockSpec(x.shape,lambda g:(0,)*x.ndim)
    grid=max(CH+GLAG*(n+1),HSP*(HC-1)+HLAG*(2*n-1)+1,HLAG*nv+1)
    return pl.pallas_call(functools.partial(finish_kernel,dp),grid=(grid,),
      in_specs=[whole(red),whole(heads),whole(vec)],
      out_specs=[pl.BlockSpec((D,FC),lambda g:(0,m(g)))]*2+[pl.BlockSpec((HRA,128),lambda g:(0,0)),whole(vec)],
      out_shape=[jax.ShapeDtypeStruct((D,CH*FC),BF)]*2+[jax.ShapeDtypeStruct((HRA,128),BF),jax.ShapeDtypeStruct(vec.shape,F32)],
      scratch_shapes=[pltpu.VMEM((CH,2,R,128),BF),pltpu.VMEM((HC,2,HR,128),BF),pltpu.VMEM((HC,HR,128),BF),pltpu.VMEM((nv,V,128),F32),pltpu.VMEM((nv,V,128),F32)]+hrecv
        +[pltpu.SemaphoreType.DMA((len(plan),n,CH))]*2+[pltpu.SemaphoreType.DMA((CH,))]*2+[pltpu.SemaphoreType.DMA((len(hplan),n,HC))]*4+[pltpu.SemaphoreType.DMA((nv,))]*2,
      compiler_params=pltpu.CompilerParams(vmem_limit_bytes=60*2**20,collective_id=1,has_side_effects=True),name="finish_gradients")(red,heads,vec)


EPSILON = 1e-06


def layer_norm(field, norm_gain, norm_shift):
    average = jnp.mean(field, axis=-1, keepdims=True)
    centred = field - average
    spread = jnp.mean(centred * centred, axis=-1, keepdims=True)
    return centred * lax.rsqrt(spread + EPSILON) * norm_gain + norm_shift


def gelu_exact(field):
    return jax.nn.gelu(field, approximate=False)


SWAP = [(0, 1), (1, 0)]


def swap(value, axis):
    return lax.ppermute(value, axis, SWAP)


def in_order(mine, other, index, axis):
    return jnp.where(
        index == 0, jnp.concatenate([mine, other], axis), jnp.concatenate([other, mine], axis)
    )


def own_row(rows, tw):
    mine = lax.dynamic_index_in_dim(rows, tw, 0, keepdims=False)
    other = lax.dynamic_index_in_dim(rows, 1 - tw, 0, keepdims=False)
    return in_order(mine, swap(other, "tw"), tw, 0)


def back_rows(half, tw):
    quarter = half.shape[0] // 2
    mine = lax.dynamic_slice_in_dim(half, tw * quarter, quarter, 0)
    other = lax.dynamic_slice_in_dim(half, (1 - tw) * quarter, quarter, 0)
    got = swap(other, "tw")
    return jnp.where(tw == 0, jnp.stack([mine, got]), jnp.stack([got, mine]))


def whole_row(half, th):
    return in_order(half, swap(half, "th"), th, 0)


def sum_halves(partial, th):
    half = partial.shape[0] // 2
    mine = lax.dynamic_slice_in_dim(partial, th * half, half, 0)
    other = lax.dynamic_slice_in_dim(partial, (1 - th) * half, half, 0)
    return mine + swap(other.astype(BF), "th").astype(F32)


def mm(spec, a, b):
    return jnp.einsum(spec, a, b, preferred_element_type=F32)


def body(
    dp_size,
    tokens,
    segment_ids,
    norm1_gain,
    norm1_shift,
    w_qkv,
    b_qv,
    w_out,
    b_out,
    norm2_gain,
    norm2_shift,
    w_up,
    b_up,
    w_down,
    b_down,
    cotangent,
):
    th, tw = lax.axis_index("th"), lax.axis_index("tw")
    d = tokens.shape[-1]
    mine = w_qkv.shape[2]
    inputs = own_row(tokens, tw).astype(F32)
    w_qkv_other = swap(w_qkv, "tw")
    w_heads = jnp.concatenate([w_qkv, w_qkv_other], 2)
    b_heads = jnp.concatenate([b_qv, swap(b_qv, "tw")], 1)
    w_out_heads = jnp.concatenate([w_out, swap(w_out, "tw")], 0)
    cot = own_row(cotangent, tw)
    seg = lax.dynamic_index_in_dim(segment_ids, tw, 0, keepdims=False)
    tables = seg_tables(seg)

    normed_one, norm_one_back = jax.vjp(layer_norm, inputs, norm1_gain, norm1_shift)
    normed_row = whole_row(normed_one.astype(BF), th)
    query = (mm("ld,de->le", normed_row, w_heads[0]) + b_heads[0]).astype(BF) * BF(0.125)
    key = mm("ld,de->le", normed_row, w_heads[1]).astype(BF)
    value = (mm("ld,de->le", normed_row, w_heads[2]) + b_heads[1]).astype(BF)
    attended, totals = attn_fwd(query, key, value, *tables)
    middle = inputs + sum_halves(mm("le,ed->ld", attended, w_out_heads), th) + b_out
    normed_two, norm_two_back = jax.vjp(layer_norm, middle, norm2_gain, norm2_shift)
    second_low = normed_two.astype(BF)
    ffn_out, grad_normed_two, grad_b_up, red = ffn(
        dp_size, second_low, second_low.T, cot, cot.T, w_up, w_down, b_up[None]
    )
    block_out = middle + (ffn_out + b_down)
    block_out = back_rows(block_out.astype(BF), tw)
    upstream = cot.astype(F32)
    grad_b_down = jnp.sum(upstream, axis=0)
    grad_mid_norm, grad_gain_two, grad_shift_two = norm_two_back(grad_normed_two)
    grad_middle = upstream + grad_mid_norm
    grad_branch = grad_middle.astype(BF)
    grad_b_out = jnp.sum(grad_branch.astype(F32), axis=0)
    grad_whole = whole_row(grad_branch, th)
    grad_heads = mm("ld,ed->le", grad_whole, w_out_heads).astype(BF)
    grad_w_out = mm("ld,le->de", grad_whole, attended).astype(BF)
    dq, dk, dv = attn_bwd(query, key, value, grad_heads, attended, totals, *tables)
    grad_normed = (
        mm("le,de->ld", dq, w_heads[0]) + mm("le,de->ld", dk, w_heads[1]) + mm("le,de->ld", dv, w_heads[2])
    )
    grad_tile = sum_halves(grad_normed, th)
    grad_inputs, grad_gain_one, grad_shift_one = norm_one_back(grad_tile)
    grad_tokens = back_rows((grad_middle + grad_inputs).astype(BF), tw)

    grad_w = [mm("ld,le->de", normed_row, g).astype(BF) for g in (dq, dk, dv)] + [grad_w_out]
    heads = jnp.stack(
        [jnp.concatenate([g[:, q * mine : (q + 1) * mine] for g in grad_w], 1) for q in range(2)]
    )
    heads = heads.reshape(2, d, -1, 128).transpose(0, 2, 1, 3).reshape(2, -1, 128)
    grad_b = jnp.stack([jnp.sum(dq.astype(F32), 0), jnp.sum(dv.astype(F32), 0)])
    place = jnp.zeros((2, d), F32)
    place = lax.dynamic_update_slice(place, grad_b[:, :mine], (0, (2 * th + tw) * mine))
    place = lax.dynamic_update_slice(place, grad_b[:, mine:], (0, (2 * th + 1 - tw) * mine))
    vectors = (grad_gain_one, grad_shift_one, grad_b_out, grad_gain_two, grad_shift_two, grad_b_down, grad_b_up, place.reshape(-1))
    small = jnp.concatenate([v.reshape(-1) for v in vectors]).reshape(-1, 128)
    up, down, heads, small = finish(dp_size, red, heads, small, d)
    small = small.reshape(-1)
    heads = heads.reshape(-1, d, 128).transpose(1, 0, 2).reshape(d, 4, mine).astype(F32)
    small_b_qv = lax.dynamic_slice_in_dim(small[-2 * d :].reshape(2, d), (2 * th + tw) * mine, mine, 1)
    return (
        block_out,
        grad_tokens,
        small[:d],
        small[d : 2 * d],
        heads[:, :3].transpose(1, 0, 2),
        small_b_qv,
        heads[:, 3].T,
        small[2 * d : 3 * d],
        small[3 * d : 4 * d],
        small[4 * d : 5 * d],
        up.astype(F32),
        small[6 * d : -2 * d],
        down.astype(F32).T,
        small[5 * d : 6 * d],
    )


def solution(mesh):
    return jax.shard_map(
        functools.partial(body, mesh.shape["dp"]),
        mesh=mesh,
        in_specs=(
            P("dp", ("th", "tw"), None),
            P("dp", None),
            P(),
            P(),
            P(None, None, ("th", "tw")),
            P(None, ("th", "tw")),
            P(("th", "tw"), None),
            P(),
            P(),
            P(),
            P(),
            P(),
            P(),
            P(),
            P("dp", ("th", "tw"), None),
        ),
        out_specs=(
            P("dp", ("th", "tw"), None),
            P("dp", ("th", "tw"), None),
            P(),
            P(),
            P(None, None, ("th", "tw")),
            P(None, ("th", "tw")),
            P(("th", "tw"), None),
            P(),
            P(),
            P(),
            P(),
            P(),
            P(),
            P(),
        ),
        check_vma=False,
    )
```

```python
import functools

import jax
import jax.numpy as jnp
from jax import lax
from jax.experimental import pallas as pl
from jax.experimental.pallas import tpu as pltpu
from jax.sharding import PartitionSpec as P

NT=(((1,),(1,)),((),())); NN=(((1,),(0,)),((),())); TN=(((0,),(0,)),((),()))
F32=jnp.float32; BF=jnp.bfloat16
BQ=256; BK=256; HD=64
def dot(a,b,d): return lax.dot_general(a,b,d,preferred_element_type=F32)

def fwd_kernel(lo_ref, hi_ref, q_ref, k_ref, v_ref, mq_ref, mk_ref, o_ref, lse_ref, m_ref, l_ref, acc_ref):
    i=pl.program_id(0)
    pairs=q_ref.shape[1]//128
    lane=lax.broadcasted_iota(jnp.int32,(1,128),1)
    halves=(lane<HD, lane>=HD)
    m_ref[...]=jnp.full(m_ref.shape,-1e30,F32)
    l_ref[...]=jnp.zeros_like(l_ref)
    acc_ref[...]=jnp.zeros_like(acc_ref)
    def body(j,_):
        ks=pl.ds(pl.multiple_of(j*BK,BK),BK)
        mk=mk_ref[ks,:]
        for p in range(pairs):
            cols=slice(p*128,(p+1)*128)
            qx=jnp.concatenate([q_ref[:,cols],mq_ref[...]],1)
            k2=k_ref[ks,cols]; v2=v_ref[ks,cols]
            ps=[]
            for e in range(2):
                h=2*p+e
                kx=jnp.concatenate([jnp.where(halves[e],k2,jnp.zeros_like(k2)),mk],1)
                s=dot(kx,qx,NT)
                m_old=m_ref[h:h+1,:]
                m_new=jnp.maximum(m_old,jnp.max(s,axis=0,keepdims=True))
                alpha=jnp.exp(m_old-m_new)
                pe=jnp.exp(s-m_new)
                l_ref[h:h+1,:]=l_ref[h:h+1,:]*alpha+jnp.sum(pe,axis=0,keepdims=True)
                m_ref[h:h+1,:]=m_new
                acc_ref[h*HD:(h+1)*HD,:]=acc_ref[h*HD:(h+1)*HD,:]*alpha
                ps.append(pe.astype(BF))
            vcat=jnp.concatenate([jnp.where(halves[0],v2,jnp.zeros_like(v2)),jnp.where(halves[1],v2,jnp.zeros_like(v2))],0)
            acc_ref[cols,:]+=dot(vcat,jnp.concatenate(ps,0),TN)
        return 0
    lax.fori_loop(lo_ref[i],hi_ref[i],body,0)
    for p in range(pairs):
        parts=[]
        for e in range(2):
            h=2*p+e
            parts.append(acc_ref[h*HD:(h+1)*HD,:]*(1.0/l_ref[h:h+1,:]))
        o_ref[:,p*128:(p+1)*128]=jnp.concatenate(parts,0).T.astype(BF)
    lse_ref[...]=m_ref[...]+jnp.log(jnp.maximum(l_ref[...],1e-37))

def attn_fwd(q,k,v,mq,mk,lo,hi):
    L,C=q.shape
    return pl.pallas_call(fwd_kernel,
        grid_spec=pltpu.PrefetchScalarGridSpec(num_scalar_prefetch=2,grid=(L//BQ,),
          in_specs=[pl.BlockSpec((BQ,C),lambda i,*_:(i,0)),pl.BlockSpec((L,C),lambda i,*_:(0,0)),pl.BlockSpec((L,C),lambda i,*_:(0,0)),
                    pl.BlockSpec((BQ,128),lambda i,*_:(i,0)),pl.BlockSpec((L,128),lambda i,*_:(0,0))],
          out_specs=[pl.BlockSpec((BQ,C),lambda i,*_:(i,0)),pl.BlockSpec((8,BQ),lambda i,*_:(0,i))],
          scratch_shapes=[pltpu.VMEM((8,BQ),F32),pltpu.VMEM((8,BQ),F32),pltpu.VMEM((C,BQ),F32)]),
        out_shape=[jax.ShapeDtypeStruct((L,C),BF),jax.ShapeDtypeStruct((8,L),F32)],
        name="attention_forward",
    )(lo,hi,q,k,v,mq,mk)

def bwd_kernel(lo_ref, hi_ref, q_ref, k_ref, v_ref, do_ref, o_ref, lse_ref, mq_ref, mk_ref, dq_ref, dk_ref, dv_ref, dk_acc, dv_acc, dq_acc, qcat, docat):
    i=pl.program_id(0); n=pl.num_programs(0)
    C=q_ref.shape[1]; pairs=C//128
    lane=lax.broadcasted_iota(jnp.int32,(1,128),1)
    halves=(lane<HD, lane>=HD)
    @pl.when(i==0)
    def _():
        dk_acc[...]=jnp.zeros_like(dk_acc); dv_acc[...]=jnp.zeros_like(dv_acc)
    dq_acc[...]=jnp.zeros_like(dq_acc)
    sel=(lax.broadcasted_iota(jnp.int32,(8,C),1)//HD==lax.broadcasted_iota(jnp.int32,(8,C),0)).astype(F32)
    delta=lax.dot_general(sel,do_ref[...].astype(F32)*o_ref[...].astype(F32),NT,precision=lax.Precision.HIGHEST,preferred_element_type=F32)
    for p in range(pairs):
        cols=slice(p*128,(p+1)*128)
        for e in range(2):
            q2=q_ref[:,cols]; d2=do_ref[:,cols]
            qcat[p,e*BQ:(e+1)*BQ,:]=jnp.where(halves[e],q2,jnp.zeros_like(q2))
            docat[p,e*BQ:(e+1)*BQ,:]=jnp.where(halves[e],d2,jnp.zeros_like(d2))
    lse=lse_ref[...]
    def body(j,_):
        ks=pl.ds(pl.multiple_of(j*BK,BK),BK)
        mk=mk_ref[ks,:]
        for p in range(pairs):
            cols=slice(p*128,(p+1)*128)
            qx=jnp.concatenate([q_ref[:,cols],mq_ref[...]],1)
            k2=k_ref[ks,cols]; v2=v_ref[ks,cols]; d2=do_ref[:,cols]
            ps=[]; dss=[]; kms=[]
            for e in range(2):
                h=2*p+e
                km=jnp.where(halves[e],k2,jnp.zeros_like(k2)); vm=jnp.where(halves[e],v2,jnp.zeros_like(v2))
                s=dot(jnp.concatenate([km,mk],1),qx,NT)
                pr=jnp.exp(s-lse[h:h+1,:])
                dp=dot(vm,d2,NT)
                ds=pr*(dp-delta[h:h+1,:])
                ps.append(pr.astype(BF)); dss.append(ds.astype(BF)); kms.append(km)
            dv_acc[ks,cols]+=dot(jnp.concatenate(ps,1),docat[p],NN)
            dk_acc[ks,cols]+=dot(jnp.concatenate(dss,1),qcat[p],NN)
            dq_acc[cols,:]+=dot(jnp.concatenate(kms,0),jnp.concatenate(dss,0),TN)
        return 0
    lax.fori_loop(lo_ref[i],hi_ref[i],body,0)
    dq_ref[...]=(dq_acc[...]*0.125).T.astype(BF)
    @pl.when(i==n-1)
    def _():
        dk_ref[...]=dk_acc[...].astype(BF); dv_ref[...]=dv_acc[...].astype(BF)

def attn_bwd(q,k,v,do,o,lse,mq,mk,lo,hi):
    L,C=q.shape
    blk=pl.BlockSpec((BQ,C),lambda i,*_:(i,0)); full=pl.BlockSpec((L,C),lambda i,*_:(0,0))
    return pl.pallas_call(bwd_kernel,
        grid_spec=pltpu.PrefetchScalarGridSpec(num_scalar_prefetch=2,grid=(L//BQ,),
          in_specs=[blk,full,full,blk,blk,pl.BlockSpec((8,BQ),lambda i,*_:(0,i)),pl.BlockSpec((BQ,128),lambda i,*_:(i,0)),pl.BlockSpec((L,128),lambda i,*_:(0,0))],
          out_specs=[blk,full,full],
          scratch_shapes=[pltpu.VMEM((L,C),F32),pltpu.VMEM((L,C),F32),pltpu.VMEM((C,BQ),F32),pltpu.VMEM((C//128,2*BQ,128),BF),pltpu.VMEM((C//128,2*BQ,128),BF)]),
        out_shape=[jax.ShapeDtypeStruct((L,C),BF)]*3,
        name="attention_backward",
    )(lo,hi,q,k,v,do,o,lse,mq,mk)

def seg_tables(seg):
    L=seg.shape[0]
    lane=jnp.arange(128,dtype=jnp.int32)[None,:]
    same=seg[:,None]==lane
    mk=same.astype(BF)
    mq=jnp.where(same|(lane>=8),0.0,-float(2**40)).astype(BF)
    first=seg[::BQ]; last=seg[BQ-1::BQ]
    lo=jnp.sum(seg[None,:]<first[:,None],axis=1,dtype=jnp.int32)//BK
    hi=(jnp.sum(seg[None,:]<=last[:,None],axis=1,dtype=jnp.int32)+BK-1)//BK
    return mq,mk,lo,hi


TT=256; FC=512
LAG=2; GLAG=2; HLAG=2; HC=3; HSP=2

def bits_of(dp): return dp.bit_length()-1

def big_plan(dp,rows):
    n=bits_of(dp)
    orders=(["tw"]+list(range(n)),[0,"tw"]+list(range(1,n)),[1,2,0,"tw"]+list(range(3,n)))
    unit=16<<(n+1)
    units=rows//unit
    third=max(1,units//4)
    shares=[units-units//3-third,units//3,third]
    return streams(orders,shares,unit)

def head_plan(dp,rows):
    n=bits_of(dp)
    orders=(["tw"]+list(range(n)),[1,2,0,"tw"]+list(range(3,n)))
    unit=16<<n
    units=rows//unit
    low=max(1,units//6)
    return streams(orders,[units-low,low],unit)

def streams(orders,shares,unit):
    out=[]; start=0
    for order,share in zip(orders,shares):
        out.append((order,start,share*unit)); start+=share*unit
    return out

class Peers:
    def __init__(self):
        self.dp=lax.axis_index("dp"); self.th=lax.axis_index("th"); self.tw=lax.axis_index("tw")
    def bit(self,axis):
        return self.tw if axis=="tw" else (self.dp//(1<<axis))%2
    def peer(self,axis):
        if axis=="tw": return {"tw":1-self.tw}
        if axis=="th": return {"th":1-self.th}
        return {"dp":self.dp+(1-2*self.bit(axis))*(1<<axis)}

def send(src,dst,ssem,rsem,peer):
    return pltpu.make_async_remote_copy(src,dst,ssem,rsem,device_id=peer,device_id_type=pl.DeviceIdType.MESH)

def barrier(p,axes):
    sem=pltpu.get_barrier_semaphore()
    for a in axes:
        pl.semaphore_signal(sem,inc=1,device_id=p.peer(a),device_id_type=pl.DeviceIdType.MESH)
    pl.semaphore_wait(sem,len(axes))

def halves(p,order,row,rows,keep_tw=False):
    out=[]
    for axis in order:
        if keep_tw and axis=="tw": out.append((row,row,rows)); continue
        rows//=2; bit=p.bit(axis)
        out.append((row+(1-bit)*rows,row+bit*rows,rows)); row=row+bit*rows
    return out
def al(x): return x if isinstance(x,int) else pl.multiple_of(x,16)
def rows_at(row,n): return pl.ds(al(row),n)

EPS=1e-06
def norm_parts(x):
    mean=jnp.mean(x,axis=-1,keepdims=True)
    cen=x-mean
    r=lax.rsqrt(jnp.mean(cen*cen,axis=-1,keepdims=True)+EPS)
    return cen*r,r
def norm_back(e,n,r,gain):
    t=e*gain
    return r*(t-jnp.mean(t,axis=-1,keepdims=True)-n*jnp.mean(t*n,axis=-1,keepdims=True))
def colsum(x): return jnp.sum(x,axis=0,keepdims=True)

def ffn_kernel(dp,att,wo,x,vin,cot,cotT,wu,wd,bu,mine,other,gm,gb,vec,red,gheads,gwo,
               mid,n2,n2T,bo,gn,obuf,orecv,grow,act,gh,dw,chip_recv,osem,gsem,*rest):
    CH=dw.shape[0]; T,D=x.shape
    plan=big_plan(dp,dw.shape[2]); n=len(plan[0][0]); K=len(plan)
    recv=[rest[k*n:(k+1)*n] for k in range(K)]
    send_sem,recv_sem,chip_send,chip_got=rest[K*n:]
    p=Peers(); g=pl.program_id(0); last=pl.num_programs(0)-1
    tiles=[slice(t*TT,(t+1)*TT) for t in range(T//TT)]
    regs=[halves(p,*s) for s in plan]
    def copy(k,s,c):
        out,_,nr=regs[k][s]
        return send(dw.at[c,p.th,rows_at(out,nr),:],recv[k][s].at[c],send_sem.at[k,s,c],recv_sem.at[k,s,c],p.peer(plan[k][0][s]))
    def chip_copy(c):
        return send(dw.at[c,1-p.th],chip_recv.at[c],chip_send.at[c],chip_got.at[c],p.peer("th"))
    def ocopy(): return send(obuf,orecv,osem.at[0],osem.at[1],p.peer("th"))
    def gcopy(landed):
        ref=grow.at[rows_at((1-p.th if landed else p.th)*T,T),:]
        return send(ref,ref,gsem.at[0],gsem.at[1],p.peer("th"))
    @pl.when(g==0)
    def _():
        barrier(p,["th"]+plan[0][0])
        for r in tiles:
            obuf[r,:]=dot(att[rows_at((1-p.th)*T+r.start,TT),:],wo[...],NN).astype(BF)
        for t,r in enumerate(tiles):
            mid[r,:]=x[r,:].astype(F32)+dot(att[rows_at(p.th*T+r.start,TT),:],wo[...],NN)+vin[0:1,:]
            if t==0: ocopy().start()
        ocopy().wait_recv()
        for r in tiles:
            m=mid[r,:]+orecv[r,:].astype(F32)
            mid[r,:]=m
            nn,_=norm_parts(m)
            y=(nn*vin[1:2,:]+vin[2:3,:]).astype(BF)
            n2[r,:]=y; n2T[:,r]=y.T
        bo[...]=jnp.zeros_like(bo); gn[...]=jnp.zeros_like(gn)
    for s in reversed(range(n)):
        c=g-1-LAG*(s+1)
        @pl.when((c>=0)&(c<CH))
        def _():
            out=0
            for k in range(K):
                copy(k,s,c).wait_recv()
                _,kr,nr=regs[k][s]
                at=(c,p.th,rows_at(kr,nr),slice(None))
                new=dw[at].astype(F32)+recv[k][s][c].astype(F32)
                if s<n-1: dw[at]=new.astype(BF)
                else:
                    red[c,out:out+nr,:]=new.astype(BF); out+=nr
    for s in reversed(range(n)):
        c=g-1-LAG*s
        @pl.when((c>=0)&(c<CH))
        def _():
            for k in range(K): copy(k,s,c).start()
    @pl.when(g<CH)
    def _():
        gsum=jnp.zeros((1,FC),F32)
        for r in tiles:
            h=dot(n2[r,:],wu[...],NN)+bu[...]
            ga=dot(cot[r,:],wd[...],NT)
            cdf=0.5*(1.0+lax.erf(h*(0.5**0.5)))
            a=(h*cdf).astype(BF)
            gr=(ga*(cdf+h*(jnp.exp(h*h*-0.5)*0.3989422804014327))).astype(BF)
            act[r,:]=a; gh[r,:]=gr
            gsum+=colsum(gr.astype(F32))
        gb[...]=gsum
        for t in range(D//TT):
            r=slice(t*TT,(t+1)*TT)
            for m,(lhs,rhs) in enumerate(((n2T,gh),(cotT,act))):
                y=dot(lhs[r,:],rhs[...],NN).astype(BF)
                for q in range(FC//128): dw[g,m,q*D+t*TT:q*D+(t+1)*TT,:]=y[:,q*128:(q+1)*128]
        for t,r in enumerate(tiles):
            bo[r,:]+=dot(act[r,:],wd[...],NN)
            if t==0: chip_copy(g).start()
            gn[r,:]+=dot(gh[r,:],wu[...],NT)
        chip_copy(g).wait_recv()
        def add(q,_):
            r=rows_at(q*TT,TT)
            dw[g,p.th,r,:]=(dw[g,p.th,r,:].astype(F32)+chip_recv[g,r,:].astype(F32)).astype(BF)
            return 0
        lax.fori_loop(0,dw.shape[2]//TT,add,0)
    @pl.when(g==CH)
    def _():
        vec[...]=jnp.zeros_like(vec)
        for r in tiles:
            m=mid[r,:]
            nn,rs=norm_parts(m)
            e=gn[r,:]; ct=cot[r,:].astype(F32)
            gmid=ct+norm_back(e,nn,rs,vin[1:2,:])
            gm[r,:]=gmid
            gbr=gmid.astype(BF)
            grow[rows_at(p.th*T+r.start,TT),:]=gbr
            vec[0:1,:]+=colsum(gbr.astype(F32)); vec[1:2,:]+=colsum(e*nn); vec[2:3,:]+=colsum(e); vec[3:4,:]+=colsum(ct)
            n2[r,:]=(m+bo[r,:]+vin[3:4,:]).astype(BF)
        gcopy(False).start()
        mine[...]=n2[rows_at(p.tw*(T//2),T//2),:]
        other[...]=n2[rows_at((1-p.tw)*(T//2),T//2),:]
    @pl.when(g==CH+1)
    def _():
        gcopy(True).wait_recv()
        for t in range(2*T//TT):
            r=slice(t*TT,(t+1)*TT)
            gheads[r,:]=dot(grow[r,:],wo[...],NT).astype(BF)
        for t in range(D//TT):
            r=slice(t*TT,(t+1)*TT)
            gwo[r,:]=dot(grow[:,r],att[...],TN).astype(BF)
    @pl.when(g==last)
    def _():
        ocopy().wait_send(); gcopy(False).wait_send()
        def drain(c,_):
            chip_copy(c).wait_send()
            for k in range(K):
                for s in range(n): copy(k,s,c).wait_send()
            return 0
        lax.fori_loop(0,CH,drain,0)

def whole(shape):
    return pl.BlockSpec(shape,lambda g:(0,)*len(shape),pipeline_mode=pl.Buffered(1))

def ffn(dp,att,wo,x,vin,cot,cotT,wu,wd,bu):
    T,D=x.shape; FF=wu.shape[1]; CH=FF//FC; R=FC//128*D; C=att.shape[1]
    plan=big_plan(dp,R); n=len(plan[0][0])
    m=lambda c: jnp.minimum(c,CH-1)
    fin=R>>n
    recv=[pltpu.VMEM((CH,rows>>(s+1),128),BF) for _,_,rows in plan for s in range(n)]
    outs=[((T//2,D),BF),((T//2,D),BF),((T,D),F32),((1,FF),F32),((8,D),F32),((CH,fin,128),BF),((2*T,C),BF),((D,C),BF)]
    specs=[whole(o[0]) for o in outs]
    specs[3]=pl.BlockSpec((1,FC),lambda c:(0,m(c)))
    return pl.pallas_call(functools.partial(ffn_kernel,dp),grid=(CH+LAG*n+1,),
      in_specs=[whole(v.shape) for v in (att,wo,x,vin,cot,cotT)]+[pl.BlockSpec((D,FC),lambda c:(0,m(c))),pl.BlockSpec((FC,D),lambda c:(m(c),0)),pl.BlockSpec((1,FC),lambda c:(0,m(c)))],
      out_specs=specs,out_shape=[jax.ShapeDtypeStruct(*o) for o in outs],
      scratch_shapes=[pltpu.VMEM((T,D),F32),pltpu.VMEM((T,D),BF),pltpu.VMEM((D,T),BF),pltpu.VMEM((T,D),F32),pltpu.VMEM((T,D),F32),
          pltpu.VMEM((T,D),BF),pltpu.VMEM((T,D),BF),pltpu.VMEM((2*T,D),BF)]
        +[pltpu.VMEM((T,FC),BF)]*2+[pltpu.VMEM((CH,2,R,128),BF),pltpu.VMEM((CH,R,128),BF),pltpu.SemaphoreType.DMA((2,)),pltpu.SemaphoreType.DMA((2,))]+recv
        +[pltpu.SemaphoreType.DMA((len(plan),n,CH))]*2+[pltpu.SemaphoreType.DMA((CH,))]*2,
      compiler_params=pltpu.CompilerParams(vmem_limit_bytes=60*2**20,collective_id=0,has_side_effects=True),name="feed_forward")(att,wo,x,vin,cot,cotT,wu,wd,bu)

def finish_kernel(dp,red,dq,dk,dv,normT,wh,gwo,x,gain,gm,vec,gbu,up,down,heads_out,vec_out,tok,full,hp,hg,vbuf,vrecv,own,obuf,orecv,tbuf,trecv,osem,tsem,*rest):
    CH=full.shape[0]; R=full.shape[2]; D=up.shape[0]; T=x.shape[0]; C=dq.shape[1]
    tiles=[slice(t*TT,(t+1)*TT) for t in range(T//TT)]
    plan=big_plan(dp,R); n=len(plan[0][0]); K=len(plan)
    HR=hp.shape[2]; hplan=head_plan(dp,HR); HK=len(hplan)
    hrecv=[rest[k*n:(k+1)*n] for k in range(HK)]
    send_sem,recv_sem,chip_send,chip_got,hs_sem,hr_sem,ha_send,ha_recv,vs_sem,vr_sem=rest[HK*n:]
    p=Peers(); g=pl.program_id(0); last=pl.num_programs(0)-1
    regs=[halves(p,*s) for s in plan]
    hregs=[halves(p,*s,keep_tw=True) for s in hplan]
    def gat(k,s,c,landed):
        other,mine,nr=regs[k][s]
        ref=full.at[c,p.th,rows_at(other if landed else mine,nr),:]
        return send(ref,ref,send_sem.at[k,s,c],recv_sem.at[k,s,c],p.peer(plan[k][0][s]))
    def chip(c,landed):
        ref=full.at[c,1-p.th if landed else p.th]
        return send(ref,ref,chip_send.at[c],chip_got.at[c],p.peer("th"))
    def hsum(k,s,c):
        order=hplan[k][0]; other,_,nr=hregs[k][s]
        if order[s]=="tw": src=hp.at[c,pl.ds(1,1),rows_at(other,nr),:]
        elif order.index("tw")>s: src=hp.at[c,:,rows_at(other,nr),:]
        else: src=hp.at[c,pl.ds(0,1),rows_at(other,nr),:]
        return send(src,hrecv[k][s].at[c],hs_sem.at[k,s,c],hr_sem.at[k,s,c],p.peer(order[s]))
    def hgat(k,s,c,landed):
        order=hplan[k][0]; other,mine,nr=hregs[k][s]
        ref=hg.at[c,rows_at(other if landed else mine,nr),:]
        return send(ref,ref,ha_send.at[k,s,c],ha_recv.at[k,s,c],p.peer(order[s]))
    backs=[[s for s in reversed(range(n)) if o[s]!="tw"] for o,_,_ in hplan]
    vaxes=["th","tw"]+list(range(n-1))
    def vcopy(i): return send(vbuf.at[i],vrecv.at[i],vs_sem.at[i],vr_sem.at[i],p.peer(vaxes[i]))
    @pl.when(g==0)
    def _():
        out=0
        for k in range(K):
            _,kr,nr=regs[k][n-1]
            for c in range(CH): full[c,p.th,rows_at(kr,nr),:]=red[c,out:out+nr,:]
            out+=nr
        barrier(p,["th"]+plan[0][0])
    def ocopy(): return send(obuf,orecv,osem.at[0],osem.at[1],p.peer("th"))
    def tcopy(): return send(tbuf.at[rows_at((1-p.tw)*(T//2),T//2),:],trecv,tsem.at[0],tsem.at[1],p.peer("tw"))
    for j in reversed(range(n+1)):
        c=g-GLAG*j
        @pl.when((c>=0)&(c<CH))
        def _():
            if j>0:
                for k in range(K): gat(k,n-j,c,True).wait_recv()
            if j<n:
                for k in range(K): gat(k,n-1-j,c,False).start()
            else: chip(c,False).start()
    @pl.when(g==0)
    def _():
        for r in tiles:
            parts=[dot(normT[r,:],d[...],NN).astype(BF) for d in (dq,dk,dv)]+[gwo[r,:]]
            for q in range(2):
                y=jnp.concatenate([z[:,q*(C//2):(q+1)*(C//2)] for z in parts],1)
                for i in range(y.shape[1]//128):
                    row=i*D+r.start
                    hp[row//HR,q,row%HR:row%HR+TT,:]=y[:,i*128:(i+1)*128]
    @pl.when(g==1)
    def _():
        for half in (1-p.th,p.th):
            for t,r in enumerate(tiles):
                rr=rows_at(half*T+r.start,TT)
                y=dot(dq[rr,:],wh[0],NT)+dot(dk[rr,:],wh[1],NT)+dot(dv[rr,:],wh[2],NT)
                if half is p.th:
                    own[r,:]=y
                    if t==0: ocopy().start()
                else: obuf[r,:]=y.astype(BF)
    @pl.when(g==2)
    def _():
        ocopy().wait_recv()
        vbuf[0]=jnp.zeros(vbuf.shape[1:],F32)
        gsum=jnp.zeros((1,D),F32); ssum=gsum
        for r in tiles:
            e=own[r,:]+orecv[r,:].astype(F32)
            nn,rs=norm_parts(x[r,:].astype(F32))
            tbuf[r,:]=(gm[r,:]+norm_back(e,nn,rs,gain[...])).astype(BF)
            gsum+=colsum(e*nn); ssum+=colsum(e)
        rows=[gsum,ssum]+[vec[i:i+1,:] for i in range(4)]+[gbu[...]]
        at=0
        for v in rows:
            for i in range(v.shape[1]//128):
                vbuf[0,at:at+1,:]=v[:,i*128:(i+1)*128]; at+=1
        for i,d in enumerate((dq,dv)):
            bs=colsum(d[...].astype(F32))
            for q in range(2):
                quarter=2*p.th+(p.tw if q==0 else 1-p.tw)
                y=jnp.concatenate([bs[:,q*(C//2):(q+1)*(C//2)],jnp.zeros((1,256-C//2),F32)],1)
                for z in range(2):
                    vbuf[0,pl.ds(at+quarter*4+i*2+z,1),:]=y[:,z*128:(z+1)*128]
    @pl.when(g==3)
    def _():
        tcopy().start()
        tok[p.tw]=tbuf[rows_at(p.tw*(T//2),T//2),:]
    steps=n+n-1
    for j in range(steps+1):
        for c in range(hp.shape[0]):
            @pl.when(g==1+HSP*c+HLAG*j)
            def _():
                for k in range(HK):
                    order=hplan[k][0]
                    if 0<j<=n:
                        s=j-1
                        hsum(k,s,c).wait_recv()
                        _,kr,nr=hregs[k][s]
                        q=slice(0,2) if order.index("tw")>s else slice(0,1)
                        at=(c,q,rows_at(kr,nr),slice(None))
                        new=(hp[at].astype(F32)+hrecv[k][s][c].astype(F32)).astype(BF)
                        if j<n: hp[at]=new
                        else: hg[c,rows_at(kr,nr),:]=new[0]
                    elif j>n: hgat(k,backs[k][j-n-1],c,True).wait_recv()
                for k in range(HK):
                    if j<n: hsum(k,j,c).start()
                    elif j<steps: hgat(k,backs[k][j-n],c,False).start()
                if j==steps: heads_out[c*HR:(c+1)*HR,:]=hg[c]
    for i in range(len(vaxes)+1):
        @pl.when(g==3+HLAG*i)
        def _():
            if i>0:
                vcopy(i-1).wait_recv()
                x=vbuf[i-1]+vrecv[i-1]
                if i<len(vaxes): vbuf[i]=x
                else: vec_out[...]=x
            if i<len(vaxes): vcopy(i).start()
    c=g-GLAG*(n+1)
    @pl.when((c>=0)&(c<CH))
    def _():
        chip(c,True).wait_recv()
        for q in range(FC//128):
            cols=slice(q*128,(q+1)*128)
            up[:,cols]=full[c,0,q*D:(q+1)*D,:]
            down[:,cols]=full[c,1,q*D:(q+1)*D,:]
    @pl.when(g==last)
    def _():
        def drain(c,_):
            chip(c,False).wait_send()
            for k in range(K):
                for s in range(n): gat(k,s,c,False).wait_send()
            return 0
        lax.fori_loop(0,CH,drain,0)
        for c in range(hp.shape[0]):
            for k in range(HK):
                for s in range(n): hsum(k,s,c).wait_send()
                for s in backs[k]: hgat(k,s,c,False).wait_send()
        for i in range(len(vaxes)): vcopy(i).wait_send()
        ocopy().wait_send(); tcopy().wait()
        tok[1-p.tw]=trecv[...]

def finish(dp,red,dq,dk,dv,normT,wh,gwo,x,gain,gm,vec,gbu):
    T,D=x.shape; CH,fin,_=red.shape; R=FC//128*D
    plan=big_plan(dp,R); n=len(plan[0][0])
    HRA=2*dq.shape[1]//128*D; HR=HRA//HC; hplan=head_plan(dp,HR)
    m=lambda g: jnp.clip(g-GLAG*(n+1),0,CH-1)
    hrecv=[]
    for order,_,rows in hplan:
        q=2
        for axis in order:
            if axis=="tw": q=1
            else: rows//=2
            hrecv.append(pltpu.VMEM((HC,q,rows,128),BF))
    V=(6*D+gbu.shape[1])//128+16; nv=n+1; args=(red,dq,dk,dv,normT,wh,gwo,x,gain,gm,vec,gbu)
    grid=max(CH+GLAG*(n+1),1+HSP*(HC-1)+HLAG*(2*n-1)+1,3+HLAG*nv+1)
    return pl.pallas_call(functools.partial(finish_kernel,dp),grid=(grid,),
      in_specs=[whole(a.shape) for a in args],
      out_specs=[pl.BlockSpec((D,FC),lambda g:(0,m(g)))]*2+[whole((HRA,128)),whole((V,128)),whole((2,T//2,D))],
      out_shape=[jax.ShapeDtypeStruct((D,CH*FC),BF)]*2+[jax.ShapeDtypeStruct((HRA,128),BF),jax.ShapeDtypeStruct((V,128),F32),jax.ShapeDtypeStruct((2,T//2,D),BF)],
      scratch_shapes=[pltpu.VMEM((CH,2,R,128),BF),pltpu.VMEM((HC,2,HR,128),BF),pltpu.VMEM((HC,HR,128),BF),pltpu.VMEM((nv,V,128),F32),pltpu.VMEM((nv,V,128),F32),pltpu.VMEM((T,D),F32)]+[pltpu.VMEM((T,D),BF)]*3+[pltpu.VMEM((T//2,D),BF)]+[pltpu.SemaphoreType.DMA((2,))]*2+hrecv
        +[pltpu.SemaphoreType.DMA((len(plan),n,CH))]*2+[pltpu.SemaphoreType.DMA((CH,))]*2+[pltpu.SemaphoreType.DMA((len(hplan),n,HC))]*4+[pltpu.SemaphoreType.DMA((nv,))]*2,
      compiler_params=pltpu.CompilerParams(vmem_limit_bytes=60*2**20,collective_id=1,has_side_effects=True),name="finish_gradients")(*args)

def widen_kernel(where,up,down,heads,mine,got,wup,wdown,wqkv,wout,blk):
    D=heads.shape[1]; q=wout.shape[0]; g=pl.program_id(0)
    wup[...]=up[...].astype(F32)
    wdown[...]=down[...].astype(F32).T
    @pl.when(g==0)
    def _():
        for r in range(D//TT):
            rr=slice(r*TT,(r+1)*TT)
            y=jnp.concatenate([heads[i,rr,:] for i in range(heads.shape[0])],1).astype(F32)
            for c in range(3): wqkv[c,rr,:]=y[:,c*q:(c+1)*q]
            wout[:,rr]=y[:,3*q:].T
        blk[where[0]]=mine[...]; blk[1-where[0]]=got[...]

def widen(tw,up,down,heads,mine,got):
    D,FF=up.shape; heads=heads.reshape(-1,D,128); q=heads.shape[0]*128//4; T2=mine.shape[0]
    outs=[(D,FF),(FF,D),(3,D,q),(q,D)]
    return pl.pallas_call(widen_kernel,grid=(FF//FC,),
      in_specs=[pl.BlockSpec(memory_space=pltpu.SMEM)]+[pl.BlockSpec((D,FC),lambda g:(0,g))]*2+[whole(a.shape) for a in (heads,mine,got)],
      out_specs=[pl.BlockSpec((D,FC),lambda g:(0,g)),pl.BlockSpec((FC,D),lambda g:(g,0)),whole(outs[2]),whole(outs[3]),whole((2,T2,D))],
      out_shape=[jax.ShapeDtypeStruct(o,F32) for o in outs]+[jax.ShapeDtypeStruct((2,T2,D),BF)],
      compiler_params=pltpu.CompilerParams(vmem_limit_bytes=50*2**20),name="widen")(tw.reshape(1),up,down,heads,mine,got)


def layer_norm(field, norm_gain, norm_shift):
    return norm_parts(field)[0] * norm_gain + norm_shift


SWAP = [(0, 1), (1, 0)]


def swap(value, axis):
    return lax.ppermute(value, axis, SWAP)


def in_order(mine, other, index, axis):
    return jnp.where(
        index == 0, jnp.concatenate([mine, other], axis), jnp.concatenate([other, mine], axis)
    )


def own_row(rows, tw):
    mine = lax.dynamic_index_in_dim(rows, tw, 0, keepdims=False)
    other = lax.dynamic_index_in_dim(rows, 1 - tw, 0, keepdims=False)
    return in_order(mine, swap(other, "tw"), tw, 0)


def whole_row(half, th):
    return in_order(half, swap(half, "th"), th, 0)


def mm(spec, a, b):
    return jnp.einsum(spec, a, b, preferred_element_type=F32)


def body(
    dp_size,
    tokens,
    segment_ids,
    norm1_gain,
    norm1_shift,
    w_qkv,
    b_qv,
    w_out,
    b_out,
    norm2_gain,
    norm2_shift,
    w_up,
    b_up,
    w_down,
    b_down,
    cotangent,
):
    th, tw = lax.axis_index("th"), lax.axis_index("tw")
    d = tokens.shape[-1]
    mine = w_qkv.shape[2]
    x = own_row(tokens, tw)
    w_heads = jnp.concatenate([w_qkv, swap(w_qkv, "tw")], 2)
    b_heads = jnp.concatenate([b_qv, swap(b_qv, "tw")], 1)
    w_out_heads = jnp.concatenate([w_out, swap(w_out, "tw")], 0)
    cot = own_row(cotangent, tw)
    seg = lax.dynamic_index_in_dim(segment_ids, tw, 0, keepdims=False)
    tables = seg_tables(seg)
    normed = layer_norm(x.astype(F32), norm1_gain, norm1_shift).astype(BF)
    normed_row = whole_row(normed, th)
    query = (mm("ld,de->le", normed_row, w_heads[0]) + b_heads[0]).astype(BF) * BF(0.125)
    key = mm("ld,de->le", normed_row, w_heads[1]).astype(BF)
    value = (mm("ld,de->le", normed_row, w_heads[2]) + b_heads[1]).astype(BF)
    attended, totals = attn_fwd(query, key, value, *tables)
    vectors = jnp.stack([b_out, norm2_gain, norm2_shift, b_down] + [jnp.zeros_like(b_out)] * 4)
    out_mine, out_other, grad_middle, grad_b_up, sums, red, grad_heads, grad_w_out = ffn(
        dp_size, attended, w_out_heads, x, vectors, cot, cot.T, w_up, w_down, b_up[None]
    )
    out_got = swap(out_other, "tw")
    dq, dk, dv = attn_bwd(query, key, value, grad_heads, attended, totals, *tables)
    up, down, heads, small, grad_tokens = finish(
        dp_size, red, dq, dk, dv, normed_row.T, w_heads, grad_w_out, x, norm1_gain[None], grad_middle, sums, grad_b_up
    )
    up, down, w_qkv_grad, w_out_grad, block_out = widen(tw, up, down, heads, out_mine, out_got)
    parts = small.reshape(-1)
    b_qv_grad = lax.dynamic_slice_in_dim(small[-16:].reshape(4, 2, 256), 2 * th + tw, 1, 0)[0, :, :mine]
    return (
        block_out,
        grad_tokens,
        parts[:d],
        parts[d : 2 * d],
        w_qkv_grad,
        b_qv_grad,
        w_out_grad,
        parts[2 * d : 3 * d],
        parts[3 * d : 4 * d],
        parts[4 * d : 5 * d],
        up,
        parts[6 * d : -16 * 128],
        down,
        parts[5 * d : 6 * d],
    )


def solution(mesh):
    return jax.shard_map(
        functools.partial(body, mesh.shape["dp"]),
        mesh=mesh,
        in_specs=(
            P("dp", ("th", "tw"), None),
            P("dp", None),
            P(),
            P(),
            P(None, None, ("th", "tw")),
            P(None, ("th", "tw")),
            P(("th", "tw"), None),
            P(),
            P(),
            P(),
            P(),
            P(),
            P(),
            P(),
            P("dp", ("th", "tw"), None),
        ),
        out_specs=(
            P("dp", ("th", "tw"), None),
            P("dp", ("th", "tw"), None),
            P(),
            P(),
            P(None, None, ("th", "tw")),
            P(None, ("th", "tw")),
            P(("th", "tw"), None),
            P(),
            P(),
            P(),
            P(),
            P(),
            P(),
            P(),
        ),
        check_vma=False,
    )
```

```python
import functools

import jax
import jax.numpy as jnp
from jax import lax
from jax.experimental import pallas as pl
from jax.experimental.pallas import tpu as pltpu
from jax.sharding import PartitionSpec as P

NT=(((1,),(1,)),((),())); NN=(((1,),(0,)),((),())); TN=(((0,),(0,)),((),()))
F32=jnp.float32; BF=jnp.bfloat16
BQ=256; BK=256; HD=64
def dot(a,b,d): return lax.dot_general(a,b,d,preferred_element_type=F32)

def fwd_kernel(lo_ref, hi_ref, q_ref, k_ref, v_ref, mq_ref, mk_ref, o_ref, lse_ref, m_ref, l_ref, acc_ref):
    i=pl.program_id(0)
    pairs=q_ref.shape[1]//128
    lane=lax.broadcasted_iota(jnp.int32,(1,128),1)
    halves=(lane<HD, lane>=HD)
    m_ref[...]=jnp.full(m_ref.shape,-1e30,F32)
    l_ref[...]=jnp.zeros_like(l_ref)
    acc_ref[...]=jnp.zeros_like(acc_ref)
    def body(j,_):
        ks=pl.ds(pl.multiple_of(j*BK,BK),BK)
        mk=mk_ref[ks,:]
        for p in range(pairs):
            cols=slice(p*128,(p+1)*128)
            qx=jnp.concatenate([q_ref[:,cols],mq_ref[...]],1)
            k2=k_ref[ks,cols]; v2=v_ref[ks,cols]
            ps=[]
            for e in range(2):
                h=2*p+e
                kx=jnp.concatenate([jnp.where(halves[e],k2,jnp.zeros_like(k2)),mk],1)
                s=dot(kx,qx,NT)
                m_old=m_ref[h:h+1,:]
                m_new=jnp.maximum(m_old,jnp.max(s,axis=0,keepdims=True))
                alpha=jnp.exp(m_old-m_new)
                pe=jnp.exp(s-m_new)
                l_ref[h:h+1,:]=l_ref[h:h+1,:]*alpha+jnp.sum(pe,axis=0,keepdims=True)
                m_ref[h:h+1,:]=m_new
                acc_ref[h*HD:(h+1)*HD,:]=acc_ref[h*HD:(h+1)*HD,:]*alpha
                ps.append(pe.astype(BF))
            vcat=jnp.concatenate([jnp.where(halves[0],v2,jnp.zeros_like(v2)),jnp.where(halves[1],v2,jnp.zeros_like(v2))],0)
            acc_ref[cols,:]+=dot(vcat,jnp.concatenate(ps,0),TN)
        return 0
    lax.fori_loop(lo_ref[i],hi_ref[i],body,0)
    for p in range(pairs):
        parts=[]
        for e in range(2):
            h=2*p+e
            parts.append(acc_ref[h*HD:(h+1)*HD,:]*(1.0/l_ref[h:h+1,:]))
        o_ref[:,p*128:(p+1)*128]=jnp.concatenate(parts,0).T.astype(BF)
    lse_ref[...]=m_ref[...]+jnp.log(jnp.maximum(l_ref[...],1e-37))

def attn_fwd(q,k,v,mq,mk,lo,hi):
    L,C=q.shape
    return pl.pallas_call(fwd_kernel,
        grid_spec=pltpu.PrefetchScalarGridSpec(num_scalar_prefetch=2,grid=(L//BQ,),
          in_specs=[pl.BlockSpec((BQ,C),lambda i,*_:(i,0)),pl.BlockSpec((L,C),lambda i,*_:(0,0)),pl.BlockSpec((L,C),lambda i,*_:(0,0)),
                    pl.BlockSpec((BQ,128),lambda i,*_:(i,0)),pl.BlockSpec((L,128),lambda i,*_:(0,0))],
          out_specs=[pl.BlockSpec((BQ,C),lambda i,*_:(i,0)),pl.BlockSpec((8,BQ),lambda i,*_:(0,i))],
          scratch_shapes=[pltpu.VMEM((8,BQ),F32),pltpu.VMEM((8,BQ),F32),pltpu.VMEM((C,BQ),F32)]),
        out_shape=[jax.ShapeDtypeStruct((L,C),BF),jax.ShapeDtypeStruct((8,L),F32)],
        name="attention_forward",
    )(lo,hi,q,k,v,mq,mk)

def bwd_kernel(lo_ref, hi_ref, q_ref, k_ref, v_ref, do_ref, o_ref, lse_ref, mq_ref, mk_ref, dq_ref, dk_ref, dv_ref, dk_acc, dv_acc, dq_acc, qcat, docat):
    i=pl.program_id(0); n=pl.num_programs(0)
    C=q_ref.shape[1]; pairs=C//128
    lane=lax.broadcasted_iota(jnp.int32,(1,128),1)
    halves=(lane<HD, lane>=HD)
    @pl.when(i==0)
    def _():
        dk_acc[...]=jnp.zeros_like(dk_acc); dv_acc[...]=jnp.zeros_like(dv_acc)
    dq_acc[...]=jnp.zeros_like(dq_acc)
    sel=(lax.broadcasted_iota(jnp.int32,(8,C),1)//HD==lax.broadcasted_iota(jnp.int32,(8,C),0)).astype(F32)
    delta=lax.dot_general(sel,do_ref[...].astype(F32)*o_ref[...].astype(F32),NT,precision=lax.Precision.HIGHEST,preferred_element_type=F32)
    for p in range(pairs):
        cols=slice(p*128,(p+1)*128)
        for e in range(2):
            q2=q_ref[:,cols]; d2=do_ref[:,cols]
            qcat[p,e*BQ:(e+1)*BQ,:]=jnp.where(halves[e],q2,jnp.zeros_like(q2))
            docat[p,e*BQ:(e+1)*BQ,:]=jnp.where(halves[e],d2,jnp.zeros_like(d2))
    lse=lse_ref[...]
    def body(j,_):
        ks=pl.ds(pl.multiple_of(j*BK,BK),BK)
        mk=mk_ref[ks,:]
        for p in range(pairs):
            cols=slice(p*128,(p+1)*128)
            qx=jnp.concatenate([q_ref[:,cols],mq_ref[...]],1)
            k2=k_ref[ks,cols]; v2=v_ref[ks,cols]; d2=do_ref[:,cols]
            ps=[]; dss=[]; kms=[]
            for e in range(2):
                h=2*p+e
                km=jnp.where(halves[e],k2,jnp.zeros_like(k2)); vm=jnp.where(halves[e],v2,jnp.zeros_like(v2))
                s=dot(jnp.concatenate([km,mk],1),qx,NT)
                pr=jnp.exp(s-lse[h:h+1,:])
                dp=dot(vm,d2,NT)
                ds=pr*(dp-delta[h:h+1,:])
                ps.append(pr.astype(BF)); dss.append(ds.astype(BF)); kms.append(km)
            dv_acc[ks,cols]+=dot(jnp.concatenate(ps,1),docat[p],NN)
            dk_acc[ks,cols]+=dot(jnp.concatenate(dss,1),qcat[p],NN)
            dq_acc[cols,:]+=dot(jnp.concatenate(kms,0),jnp.concatenate(dss,0),TN)
        return 0
    lax.fori_loop(lo_ref[i],hi_ref[i],body,0)
    dq_ref[...]=(dq_acc[...]*0.125).T.astype(BF)
    @pl.when(i==n-1)
    def _():
        dk_ref[...]=dk_acc[...].astype(BF); dv_ref[...]=dv_acc[...].astype(BF)

def attn_bwd(q,k,v,do,o,lse,mq,mk,lo,hi):
    L,C=q.shape
    blk=pl.BlockSpec((BQ,C),lambda i,*_:(i,0)); full=pl.BlockSpec((L,C),lambda i,*_:(0,0))
    return pl.pallas_call(bwd_kernel,
        grid_spec=pltpu.PrefetchScalarGridSpec(num_scalar_prefetch=2,grid=(L//BQ,),
          in_specs=[blk,full,full,blk,blk,pl.BlockSpec((8,BQ),lambda i,*_:(0,i)),pl.BlockSpec((BQ,128),lambda i,*_:(i,0)),pl.BlockSpec((L,128),lambda i,*_:(0,0))],
          out_specs=[blk,full,full],
          scratch_shapes=[pltpu.VMEM((L,C),F32),pltpu.VMEM((L,C),F32),pltpu.VMEM((C,BQ),F32),pltpu.VMEM((C//128,2*BQ,128),BF),pltpu.VMEM((C//128,2*BQ,128),BF)]),
        out_shape=[jax.ShapeDtypeStruct((L,C),BF)]*3,
        name="attention_backward",
    )(lo,hi,q,k,v,do,o,lse,mq,mk)

def block_ranges(seg):
    first=seg[::BQ]; last=seg[BQ-1::BQ]
    lo=jnp.sum(seg[None,:]<first[:,None],axis=1,dtype=jnp.int32)//BK
    hi=(jnp.sum(seg[None,:]<=last[:,None],axis=1,dtype=jnp.int32)+BK-1)//BK
    return lo,hi


TT=256; FC=512
LAG=2; GLAG=2; HLAG=2; HC=3; HSP=2

def bits_of(dp): return dp.bit_length()-1

def big_plan(dp,rows):
    n=bits_of(dp)
    orders=(["tw"]+list(range(n)),[0,"tw"]+list(range(1,n)),[1,2,0,"tw"]+list(range(3,n)))
    unit=16<<(n+1)
    units=rows//unit
    third=max(1,units//4)
    shares=[units-units//3-third,units//3,third]
    return streams(orders,shares,unit)

def head_plan(dp,rows):
    n=bits_of(dp)
    orders=(["tw"]+list(range(n)),[1,2,0,"tw"]+list(range(3,n)))
    unit=16<<n
    units=rows//unit
    low=max(1,units//6)
    return streams(orders,[units-low,low],unit)

def streams(orders,shares,unit):
    out=[]; start=0
    for order,share in zip(orders,shares):
        out.append((order,start,share*unit)); start+=share*unit
    return out

class Peers:
    def __init__(self):
        self.dp=lax.axis_index("dp"); self.th=lax.axis_index("th"); self.tw=lax.axis_index("tw")
    def bit(self,axis):
        return self.tw if axis=="tw" else (self.dp//(1<<axis))%2
    def peer(self,axis):
        if axis=="tw": return {"tw":1-self.tw}
        if axis=="th": return {"th":1-self.th}
        return {"dp":self.dp+(1-2*self.bit(axis))*(1<<axis)}

def send(src,dst,ssem,rsem,peer):
    return pltpu.make_async_remote_copy(src,dst,ssem,rsem,device_id=peer,device_id_type=pl.DeviceIdType.MESH)

def barrier(p,axes):
    sem=pltpu.get_barrier_semaphore()
    for a in axes:
        pl.semaphore_signal(sem,inc=1,device_id=p.peer(a),device_id_type=pl.DeviceIdType.MESH)
    pl.semaphore_wait(sem,len(axes))

def halves(p,order,row,rows,keep_tw=False):
    out=[]
    for axis in order:
        if keep_tw and axis=="tw": out.append((row,row,rows)); continue
        rows//=2; bit=p.bit(axis)
        out.append((row+(1-bit)*rows,row+bit*rows,rows)); row=row+bit*rows
    return out
def al(x): return x if isinstance(x,int) else pl.multiple_of(x,16)
def rows_at(row,n): return pl.ds(al(row),n)

EPS=1e-06
def norm_parts(x):
    mean=jnp.mean(x,axis=-1,keepdims=True)
    cen=x-mean
    r=lax.rsqrt(jnp.mean(cen*cen,axis=-1,keepdims=True)+EPS)
    return cen*r,r
def norm_back(e,n,r,gain):
    t=e*gain
    return r*(t-jnp.mean(t,axis=-1,keepdims=True)-n*jnp.mean(t*n,axis=-1,keepdims=True))
def colsum(x): return jnp.sum(x,axis=0,keepdims=True)

def ffn_kernel(dp,att,wo,x,vin,cot,wu,wd,bu,mine,other,gm,gb,vec,red,gheads,gwo,
               cotT,mid,n2,n2T,bo,gn,obuf,orecv,grow,act,gh,dw,chip_recv,osem,gsem,*rest):
    CH=dw.shape[0]; T,D=x.shape
    plan=big_plan(dp,dw.shape[2]); n=len(plan[0][0]); K=len(plan)
    recv=[rest[k*n:(k+1)*n] for k in range(K)]
    send_sem,recv_sem,chip_send,chip_got=rest[K*n:]
    p=Peers(); g=pl.program_id(0); last=pl.num_programs(0)-1
    tiles=[slice(t*TT,(t+1)*TT) for t in range(T//TT)]
    regs=[halves(p,*s) for s in plan]
    def copy(k,s,c):
        out,_,nr=regs[k][s]
        return send(dw.at[c,p.th,rows_at(out,nr),:],recv[k][s].at[c],send_sem.at[k,s,c],recv_sem.at[k,s,c],p.peer(plan[k][0][s]))
    def chip_copy(c):
        return send(dw.at[c,1-p.th],chip_recv.at[c],chip_send.at[c],chip_got.at[c],p.peer("th"))
    def ocopy(): return send(obuf,orecv,osem.at[0],osem.at[1],p.peer("th"))
    def gcopy(landed):
        ref=grow.at[rows_at((1-p.th if landed else p.th)*T,T),:]
        return send(ref,ref,gsem.at[0],gsem.at[1],p.peer("th"))
    @pl.when(g==0)
    def _():
        barrier(p,["th"]+plan[0][0])
        for r in tiles:
            obuf[r,:]=dot(att[rows_at((1-p.th)*T+r.start,TT),:],wo[...],NN).astype(BF)
        for t,r in enumerate(tiles):
            mid[r,:]=x[r,:].astype(F32)+dot(att[rows_at(p.th*T+r.start,TT),:],wo[...],NN)+vin[0:1,:]
            if t==0: ocopy().start()
            cotT[:,r]=cot[r,:].T
        ocopy().wait_recv()
        for r in tiles:
            m=mid[r,:]+orecv[r,:].astype(F32)
            mid[r,:]=m
            nn,_=norm_parts(m)
            y=(nn*vin[1:2,:]+vin[2:3,:]).astype(BF)
            n2[r,:]=y; n2T[:,r]=y.T
        bo[...]=jnp.zeros_like(bo); gn[...]=jnp.zeros_like(gn)
    for s in reversed(range(n)):
        c=g-1-LAG*(s+1)
        @pl.when((c>=0)&(c<CH))
        def _():
            out=0
            for k in range(K):
                copy(k,s,c).wait_recv()
                _,kr,nr=regs[k][s]
                at=(c,p.th,rows_at(kr,nr),slice(None))
                new=dw[at].astype(F32)+recv[k][s][c].astype(F32)
                if s<n-1: dw[at]=new.astype(BF)
                else:
                    red[c,out:out+nr,:]=new.astype(BF); out+=nr
    for s in reversed(range(n)):
        c=g-1-LAG*s
        @pl.when((c>=0)&(c<CH))
        def _():
            for k in range(K): copy(k,s,c).start()
    @pl.when(g<CH)
    def _():
        gsum=jnp.zeros((1,FC),F32)
        for r in tiles:
            h=dot(n2[r,:],wu[...],NN)+bu[...]
            ga=dot(cot[r,:],wd[...],NT)
            cdf=0.5*(1.0+lax.erf(h*(0.5**0.5)))
            a=(h*cdf).astype(BF)
            gr=(ga*(cdf+h*(jnp.exp(h*h*-0.5)*0.3989422804014327))).astype(BF)
            act[r,:]=a; gh[r,:]=gr
            gsum+=colsum(gr.astype(F32))
        gb[...]=gsum
        for t in range(D//TT):
            r=slice(t*TT,(t+1)*TT)
            for m,(lhs,rhs) in enumerate(((n2T,gh),(cotT,act))):
                y=dot(lhs[r,:],rhs[...],NN).astype(BF)
                for q in range(FC//128): dw[g,m,q*D+t*TT:q*D+(t+1)*TT,:]=y[:,q*128:(q+1)*128]
        for t,r in enumerate(tiles):
            bo[r,:]+=dot(act[r,:],wd[...],NN)
            if t==0: chip_copy(g).start()
            gn[r,:]+=dot(gh[r,:],wu[...],NT)
        chip_copy(g).wait_recv()
        def add(q,_):
            r=rows_at(q*TT,TT)
            dw[g,p.th,r,:]=(dw[g,p.th,r,:].astype(F32)+chip_recv[g,r,:].astype(F32)).astype(BF)
            return 0
        lax.fori_loop(0,dw.shape[2]//TT,add,0)
    @pl.when(g==CH)
    def _():
        vec[...]=jnp.zeros_like(vec)
        for r in tiles:
            m=mid[r,:]
            nn,rs=norm_parts(m)
            e=gn[r,:]; ct=cot[r,:].astype(F32)
            gmid=ct+norm_back(e,nn,rs,vin[1:2,:])
            gm[r,:]=gmid
            gbr=gmid.astype(BF)
            grow[rows_at(p.th*T+r.start,TT),:]=gbr
            vec[0:1,:]+=colsum(gbr.astype(F32)); vec[1:2,:]+=colsum(e*nn); vec[2:3,:]+=colsum(e); vec[3:4,:]+=colsum(ct)
            n2[r,:]=(m+bo[r,:]+vin[3:4,:]).astype(BF)
        gcopy(False).start()
        mine[...]=n2[rows_at(p.tw*(T//2),T//2),:]
        other[...]=n2[rows_at((1-p.tw)*(T//2),T//2),:]
    @pl.when(g==CH+1)
    def _():
        gcopy(True).wait_recv()
        for t in range(2*T//TT):
            r=slice(t*TT,(t+1)*TT)
            gheads[r,:]=dot(grow[r,:],wo[...],NT).astype(BF)
        for t in range(D//TT):
            r=slice(t*TT,(t+1)*TT)
            gwo[r,:]=dot(grow[:,r],att[...],TN).astype(BF)
    @pl.when(g==last)
    def _():
        ocopy().wait_send(); gcopy(False).wait_send()
        def drain(c,_):
            chip_copy(c).wait_send()
            for k in range(K):
                for s in range(n): copy(k,s,c).wait_send()
            return 0
        lax.fori_loop(0,CH,drain,0)

def whole(shape):
    return pl.BlockSpec(shape,lambda g:(0,)*len(shape),pipeline_mode=pl.Buffered(1))

def ffn(dp,att,wo,x,vin,cot,wu,wd,bu):
    T,D=x.shape; FF=wu.shape[1]; CH=FF//FC; R=FC//128*D; C=att.shape[1]
    plan=big_plan(dp,R); n=len(plan[0][0])
    m=lambda c: jnp.minimum(c,CH-1)
    fin=R>>n
    recv=[pltpu.VMEM((CH,rows>>(s+1),128),BF) for _,_,rows in plan for s in range(n)]
    outs=[((T//2,D),BF),((T//2,D),BF),((T,D),F32),((1,FF),F32),((8,D),F32),((CH,fin,128),BF),((2*T,C),BF),((D,C),BF)]
    specs=[whole(o[0]) for o in outs]
    specs[3]=pl.BlockSpec((1,FC),lambda c:(0,m(c)))
    return pl.pallas_call(functools.partial(ffn_kernel,dp),grid=(CH+LAG*n+1,),
      in_specs=[whole(v.shape) for v in (att,wo,x,vin,cot)]+[pl.BlockSpec((D,FC),lambda c:(0,m(c))),pl.BlockSpec((FC,D),lambda c:(m(c),0)),pl.BlockSpec((1,FC),lambda c:(0,m(c)))],
      out_specs=specs,out_shape=[jax.ShapeDtypeStruct(*o) for o in outs],
      scratch_shapes=[pltpu.VMEM((D,T),BF),pltpu.VMEM((T,D),F32),pltpu.VMEM((T,D),BF),pltpu.VMEM((D,T),BF),pltpu.VMEM((T,D),F32),pltpu.VMEM((T,D),F32),
          pltpu.VMEM((T,D),BF),pltpu.VMEM((T,D),BF),pltpu.VMEM((2*T,D),BF)]
        +[pltpu.VMEM((T,FC),BF)]*2+[pltpu.VMEM((CH,2,R,128),BF),pltpu.VMEM((CH,R,128),BF),pltpu.SemaphoreType.DMA((2,)),pltpu.SemaphoreType.DMA((2,))]+recv
        +[pltpu.SemaphoreType.DMA((len(plan),n,CH))]*2+[pltpu.SemaphoreType.DMA((CH,))]*2,
      compiler_params=pltpu.CompilerParams(vmem_limit_bytes=60*2**20,collective_id=0,has_side_effects=True),name="feed_forward")(att,wo,x,vin,cot,wu,wd,bu)

def finish_kernel(dp,red,dq,dk,dv,normT,wh,gwo,x,gain,gm,vec,gbu,up,down,heads_out,vec_out,tok,full,hp,hg,vbuf,vrecv,own,obuf,orecv,tbuf,trecv,osem,tsem,*rest):
    CH=full.shape[0]; R=full.shape[2]; D=up.shape[0]; T=x.shape[0]; C=dq.shape[1]
    tiles=[slice(t*TT,(t+1)*TT) for t in range(T//TT)]
    plan=big_plan(dp,R); n=len(plan[0][0]); K=len(plan)
    HR=hp.shape[2]; hplan=head_plan(dp,HR); HK=len(hplan)
    hrecv=[rest[k*n:(k+1)*n] for k in range(HK)]
    send_sem,recv_sem,chip_send,chip_got,hs_sem,hr_sem,ha_send,ha_recv,vs_sem,vr_sem=rest[HK*n:]
    p=Peers(); g=pl.program_id(0); last=pl.num_programs(0)-1
    regs=[halves(p,*s) for s in plan]
    hregs=[halves(p,*s,keep_tw=True) for s in hplan]
    def gat(k,s,c,landed):
        other,mine,nr=regs[k][s]
        ref=full.at[c,p.th,rows_at(other if landed else mine,nr),:]
        return send(ref,ref,send_sem.at[k,s,c],recv_sem.at[k,s,c],p.peer(plan[k][0][s]))
    def chip(c,landed):
        ref=full.at[c,1-p.th if landed else p.th]
        return send(ref,ref,chip_send.at[c],chip_got.at[c],p.peer("th"))
    def hsum(k,s,c):
        order=hplan[k][0]; other,_,nr=hregs[k][s]
        if order[s]=="tw": src=hp.at[c,pl.ds(1,1),rows_at(other,nr),:]
        elif order.index("tw")>s: src=hp.at[c,:,rows_at(other,nr),:]
        else: src=hp.at[c,pl.ds(0,1),rows_at(other,nr),:]
        return send(src,hrecv[k][s].at[c],hs_sem.at[k,s,c],hr_sem.at[k,s,c],p.peer(order[s]))
    def hgat(k,s,c,landed):
        order=hplan[k][0]; other,mine,nr=hregs[k][s]
        ref=hg.at[c,rows_at(other if landed else mine,nr),:]
        return send(ref,ref,ha_send.at[k,s,c],ha_recv.at[k,s,c],p.peer(order[s]))
    backs=[[s for s in reversed(range(n)) if o[s]!="tw"] for o,_,_ in hplan]
    vaxes=["th","tw"]+list(range(n-1))
    def vcopy(i): return send(vbuf.at[i],vrecv.at[i],vs_sem.at[i],vr_sem.at[i],p.peer(vaxes[i]))
    @pl.when(g==0)
    def _():
        out=0
        for k in range(K):
            _,kr,nr=regs[k][n-1]
            for c in range(CH): full[c,p.th,rows_at(kr,nr),:]=red[c,out:out+nr,:]
            out+=nr
        barrier(p,["th"]+plan[0][0])
    def ocopy(): return send(obuf,orecv,osem.at[0],osem.at[1],p.peer("th"))
    def tcopy(): return send(tbuf.at[rows_at((1-p.tw)*(T//2),T//2),:],trecv,tsem.at[0],tsem.at[1],p.peer("tw"))
    for j in reversed(range(n+1)):
        c=g-GLAG*j
        @pl.when((c>=0)&(c<CH))
        def _():
            if j>0:
                for k in range(K): gat(k,n-j,c,True).wait_recv()
            if j<n:
                for k in range(K): gat(k,n-1-j,c,False).start()
            else: chip(c,False).start()
    @pl.when(g==0)
    def _():
        for r in tiles:
            parts=[dot(normT[r,:],d[...],NN).astype(BF) for d in (dq,dk,dv)]+[gwo[r,:]]
            for q in range(2):
                y=jnp.concatenate([z[:,q*(C//2):(q+1)*(C//2)] for z in parts],1)
                for i in range(y.shape[1]//128):
                    row=i*D+r.start
                    hp[row//HR,q,row%HR:row%HR+TT,:]=y[:,i*128:(i+1)*128]
    @pl.when(g==1)
    def _():
        for half in (1-p.th,p.th):
            for t,r in enumerate(tiles):
                rr=rows_at(half*T+r.start,TT)
                y=dot(dq[rr,:],wh[0],NT)+dot(dk[rr,:],wh[1],NT)+dot(dv[rr,:],wh[2],NT)
                if half is p.th:
                    own[r,:]=y
                    if t==0: ocopy().start()
                else: obuf[r,:]=y.astype(BF)
    @pl.when(g==2)
    def _():
        ocopy().wait_recv()
        vbuf[0]=jnp.zeros(vbuf.shape[1:],F32)
        gsum=jnp.zeros((1,D),F32); ssum=gsum
        for r in tiles:
            e=own[r,:]+orecv[r,:].astype(F32)
            nn,rs=norm_parts(x[r,:].astype(F32))
            tbuf[r,:]=(gm[r,:]+norm_back(e,nn,rs,gain[...])).astype(BF)
            gsum+=colsum(e*nn); ssum+=colsum(e)
        rows=[gsum,ssum]+[vec[i:i+1,:] for i in range(4)]+[gbu[...]]
        at=0
        for v in rows:
            for i in range(v.shape[1]//128):
                vbuf[0,at:at+1,:]=v[:,i*128:(i+1)*128]; at+=1
        for i,d in enumerate((dq,dv)):
            bs=colsum(d[...].astype(F32))
            for q in range(2):
                quarter=2*p.th+(p.tw if q==0 else 1-p.tw)
                y=jnp.concatenate([bs[:,q*(C//2):(q+1)*(C//2)],jnp.zeros((1,256-C//2),F32)],1)
                for z in range(2):
                    vbuf[0,pl.ds(at+quarter*4+i*2+z,1),:]=y[:,z*128:(z+1)*128]
    @pl.when(g==3)
    def _():
        tcopy().start()
        tok[p.tw]=tbuf[rows_at(p.tw*(T//2),T//2),:]
    steps=n+n-1
    for j in range(steps+1):
        for c in range(hp.shape[0]):
            @pl.when(g==1+HSP*c+HLAG*j)
            def _():
                for k in range(HK):
                    order=hplan[k][0]
                    if 0<j<=n:
                        s=j-1
                        hsum(k,s,c).wait_recv()
                        _,kr,nr=hregs[k][s]
                        q=slice(0,2) if order.index("tw")>s else slice(0,1)
                        at=(c,q,rows_at(kr,nr),slice(None))
                        new=(hp[at].astype(F32)+hrecv[k][s][c].astype(F32)).astype(BF)
                        if j<n: hp[at]=new
                        else: hg[c,rows_at(kr,nr),:]=new[0]
                    elif j>n: hgat(k,backs[k][j-n-1],c,True).wait_recv()
                for k in range(HK):
                    if j<n: hsum(k,j,c).start()
                    elif j<steps: hgat(k,backs[k][j-n],c,False).start()
                if j==steps: heads_out[c*HR:(c+1)*HR,:]=hg[c]
    for i in range(len(vaxes)+1):
        @pl.when(g==3+HLAG*i)
        def _():
            if i>0:
                vcopy(i-1).wait_recv()
                x=vbuf[i-1]+vrecv[i-1]
                if i<len(vaxes): vbuf[i]=x
                else: vec_out[...]=x
            if i<len(vaxes): vcopy(i).start()
    c=g-GLAG*(n+1)
    @pl.when((c>=0)&(c<CH))
    def _():
        chip(c,True).wait_recv()
        for q in range(FC//128):
            cols=slice(q*128,(q+1)*128)
            up[:,cols]=full[c,0,q*D:(q+1)*D,:]
            down[:,cols]=full[c,1,q*D:(q+1)*D,:]
    @pl.when(g==last)
    def _():
        def drain(c,_):
            chip(c,False).wait_send()
            for k in range(K):
                for s in range(n): gat(k,s,c,False).wait_send()
            return 0
        lax.fori_loop(0,CH,drain,0)
        for c in range(hp.shape[0]):
            for k in range(HK):
                for s in range(n): hsum(k,s,c).wait_send()
                for s in backs[k]: hgat(k,s,c,False).wait_send()
        for i in range(len(vaxes)): vcopy(i).wait_send()
        ocopy().wait_send(); tcopy().wait()
        tok[1-p.tw]=trecv[...]

def finish(dp,red,dq,dk,dv,normT,wh,gwo,x,gain,gm,vec,gbu):
    T,D=x.shape; CH,fin,_=red.shape; R=FC//128*D
    plan=big_plan(dp,R); n=len(plan[0][0])
    HRA=2*dq.shape[1]//128*D; HR=HRA//HC; hplan=head_plan(dp,HR)
    m=lambda g: jnp.clip(g-GLAG*(n+1),0,CH-1)
    hrecv=[]
    for order,_,rows in hplan:
        q=2
        for axis in order:
            if axis=="tw": q=1
            else: rows//=2
            hrecv.append(pltpu.VMEM((HC,q,rows,128),BF))
    V=(6*D+gbu.shape[1])//128+16; nv=n+1; args=(red,dq,dk,dv,normT,wh,gwo,x,gain,gm,vec,gbu)
    grid=max(CH+GLAG*(n+1),1+HSP*(HC-1)+HLAG*(2*n-1)+1,3+HLAG*nv+1)
    return pl.pallas_call(functools.partial(finish_kernel,dp),grid=(grid,),
      in_specs=[whole(a.shape) for a in args],
      out_specs=[pl.BlockSpec((D,FC),lambda g:(0,m(g)))]*2+[whole((HRA,128)),whole((V,128)),whole((2,T//2,D))],
      out_shape=[jax.ShapeDtypeStruct((D,CH*FC),BF)]*2+[jax.ShapeDtypeStruct((HRA,128),BF),jax.ShapeDtypeStruct((V,128),F32),jax.ShapeDtypeStruct((2,T//2,D),BF)],
      scratch_shapes=[pltpu.VMEM((CH,2,R,128),BF),pltpu.VMEM((HC,2,HR,128),BF),pltpu.VMEM((HC,HR,128),BF),pltpu.VMEM((nv,V,128),F32),pltpu.VMEM((nv,V,128),F32),pltpu.VMEM((T,D),F32)]+[pltpu.VMEM((T,D),BF)]*3+[pltpu.VMEM((T//2,D),BF)]+[pltpu.SemaphoreType.DMA((2,))]*2+hrecv
        +[pltpu.SemaphoreType.DMA((len(plan),n,CH))]*2+[pltpu.SemaphoreType.DMA((CH,))]*2+[pltpu.SemaphoreType.DMA((len(hplan),n,HC))]*4+[pltpu.SemaphoreType.DMA((nv,))]*2,
      compiler_params=pltpu.CompilerParams(vmem_limit_bytes=60*2**20,collective_id=1,has_side_effects=True),name="finish_gradients")(*args)

def widen_kernel(where,up,down,heads,mine,got,wup,wdown,wqkv,wout,blk):
    D=heads.shape[1]; q=wout.shape[0]; g=pl.program_id(0)
    wup[...]=up[...].astype(F32)
    wdown[...]=down[...].astype(F32).T
    @pl.when(g==0)
    def _():
        for r in range(D//TT):
            rr=slice(r*TT,(r+1)*TT)
            y=jnp.concatenate([heads[i,rr,:] for i in range(heads.shape[0])],1).astype(F32)
            for c in range(3): wqkv[c,rr,:]=y[:,c*q:(c+1)*q]
            wout[:,rr]=y[:,3*q:].T
        blk[where[0]]=mine[...]; blk[1-where[0]]=got[...]

def widen(tw,up,down,heads,mine,got):
    D,FF=up.shape; heads=heads.reshape(-1,D,128); q=heads.shape[0]*128//4; T2=mine.shape[0]
    outs=[(D,FF),(FF,D),(3,D,q),(q,D)]
    return pl.pallas_call(widen_kernel,grid=(FF//FC,),
      in_specs=[pl.BlockSpec(memory_space=pltpu.SMEM)]+[pl.BlockSpec((D,FC),lambda g:(0,g))]*2+[whole(a.shape) for a in (heads,mine,got)],
      out_specs=[pl.BlockSpec((D,FC),lambda g:(0,g)),pl.BlockSpec((FC,D),lambda g:(g,0)),whole(outs[2]),whole(outs[3]),whole((2,T2,D))],
      out_shape=[jax.ShapeDtypeStruct(o,F32) for o in outs]+[jax.ShapeDtypeStruct((2,T2,D),BF)],
      compiler_params=pltpu.CompilerParams(vmem_limit_bytes=50*2**20),name="widen")(tw.reshape(1),up,down,heads,mine,got)

def front_kernel(tok,w,b,gain,shift,seg,x_o,normT_o,q_o,k_o,v_o,wh_o,mq_o,mk_o,x,norm,normT,qkv,wh,wgot,bgot,mq,mk,tsem,bsem,csem,ysem,xsem,osem):
    p=Peers(); Q,D=tok.shape[1:]; T=2*Q; L=2*T; E=w.shape[2]; HALF=D//2
    barrier(p,["th","tw",0])
    def tcopy(): return send(tok.at[1-p.tw],x.at[rows_at(p.tw*Q,Q),:],tsem.at[0],tsem.at[1],p.peer("tw"))
    def bcopy(): return send(b,bgot,bsem.at[0],bsem.at[1],p.peer("tw"))
    def ycopy(c):
        r=rows_at(p.bit(0)*HALF,HALF)
        return send(w.at[c,r,:],wgot.at[c,r,:],ysem.at[0,c],ysem.at[1,c],p.peer("tw"))
    def xcopy(c,landed):
        ref=wgot.at[c,rows_at((1-p.bit(0) if landed else p.bit(0))*HALF,HALF),:]
        return send(ref,ref,xsem.at[0,c],xsem.at[1,c],p.peer(0))
    def ccopy(i,landed):
        core=1-p.th if landed else p.th
        quarter=p.tw if i==0 else 1-p.tw
        ref=norm.at[rows_at(core*T+quarter*Q,Q),:]
        return send(ref,ref,csem.at[0,i],csem.at[1,i],p.peer("th"))
    tcopy().start(); bcopy().start()
    for c in range(3): ycopy(c).start()
    def normalize(src,row):
        for t in range(Q//128):
            v=src(t)
            y=(norm_parts(v.astype(F32))[0]*gain[...]+shift[...]).astype(BF)
            norm[rows_at(row+t*128,128),:]=y
    def put(src,dst,i): return pltpu.make_async_copy(src,dst,osem.at[i])
    x[rows_at(p.tw*Q,Q),:]=tok[p.tw]
    normalize(lambda t: tok[p.tw,t*128:(t+1)*128,:],p.th*T+p.tw*Q)
    onehot=lax.broadcasted_iota(jnp.int32,(128,L),0)
    same=onehot==seg[...]
    mk[...]=jnp.where(same,1.0,0.0).T.astype(BF)
    ccopy(0,False).start()
    mq[...]=jnp.where(same|(onehot>=8),0.0,-float(2**40)).T.astype(BF)
    put(mk,mk_o,0).start(); put(mq,mq_o,1).start()
    tcopy().wait_recv()
    normalize(lambda t: x[rows_at((1-p.tw)*Q+t*128,128),:],p.th*T+(1-p.tw)*Q)
    put(x,x_o,2).start()
    bcopy().wait_recv()
    tiles=[slice(t*TT,(t+1)*TT) for t in range(L//TT)]
    def bias(c,ref): return ref[c//2:c//2+1,:] if c!=1 else None
    def project(c,wt,bs,r):
        y=dot(norm[r,:],wt,NN)
        if bs is not None: y=y+bs
        y=y.astype(BF)
        return y*BF(0.125) if c==0 else y
    ccopy(1,False).start()
    ccopy(0,True).wait_recv()
    ccopy(1,True).wait_recv()
    for c in range(3):
        for r in tiles: qkv[c,r,0:E]=project(c,w[c],bias(c,b),r)
    for r in tiles: normT[:,r]=norm[r,:].T
    put(normT,normT_o,3).start()
    for c in range(3):
        ycopy(c).wait_recv()
        xcopy(c,False).start()
    for c in range(3):
        xcopy(c,True).wait_recv()
        for r in tiles: qkv[c,r,E:2*E]=project(c,wgot[c],bias(c,bgot),r)
        put(qkv.at[c],(q_o,k_o,v_o)[c],4+c).start()
        wh[c,:,0:E]=w[c]; wh[c,:,E:2*E]=wgot[c]
    put(wh,wh_o,7).start()
    for src,dst,i in ((mk,mk_o,0),(mq,mq_o,1),(x,x_o,2),(normT,normT_o,3),(wh,wh_o,7)): put(src,dst,i).wait()
    for c in range(3):
        put(qkv.at[c],(q_o,k_o,v_o)[c],4+c).wait()
        ycopy(c).wait_send(); xcopy(c,False).wait_send()
    tcopy().wait_send(); bcopy().wait_send()
    for i in range(2): ccopy(i,False).wait_send()

def front(tok,w,b,gain,shift,seg):
    _,Q,D=tok.shape; T=2*Q; L=2*T; E=w.shape[2]
    outs=[((T,D),BF),((D,L),BF)]+[((L,2*E),BF)]*3+[((3,D,2*E),BF)]+[((L,128),BF)]*2
    sem=pltpu.SemaphoreType.DMA
    return pl.pallas_call(front_kernel,
      in_specs=[pl.BlockSpec(memory_space=pltpu.VMEM)]*6,out_specs=[pl.BlockSpec(memory_space=pl.ANY)]*len(outs),
      out_shape=[jax.ShapeDtypeStruct(*o) for o in outs],
      scratch_shapes=[pltpu.VMEM((T,D),BF),pltpu.VMEM((L,D),BF),pltpu.VMEM((D,L),BF),pltpu.VMEM((3,L,2*E),BF),pltpu.VMEM((3,D,2*E),BF),pltpu.VMEM((3,D,E),BF),
        pltpu.VMEM(b.shape,F32),pltpu.VMEM((L,128),BF),pltpu.VMEM((L,128),BF),sem((2,)),sem((2,)),sem((2,2)),sem((2,3)),sem((2,3)),sem((8,))],
      compiler_params=pltpu.CompilerParams(vmem_limit_bytes=60*2**20,collective_id=2,has_side_effects=True),name="front")(tok,w,b,gain,shift,seg)


SWAP = [(0, 1), (1, 0)]


def swap(value, axis):
    return lax.ppermute(value, axis, SWAP)


def in_order(mine, other, index, axis):
    return jnp.where(
        index == 0, jnp.concatenate([mine, other], axis), jnp.concatenate([other, mine], axis)
    )


def own_row(rows, tw):
    mine = lax.dynamic_index_in_dim(rows, tw, 0, keepdims=False)
    other = lax.dynamic_index_in_dim(rows, 1 - tw, 0, keepdims=False)
    return in_order(mine, swap(other, "tw"), tw, 0)


def body(
    dp_size,
    tokens,
    segment_ids,
    norm1_gain,
    norm1_shift,
    w_qkv,
    b_qv,
    w_out,
    b_out,
    norm2_gain,
    norm2_shift,
    w_up,
    b_up,
    w_down,
    b_down,
    cotangent,
):
    th, tw = lax.axis_index("th"), lax.axis_index("tw")
    d = tokens.shape[-1]
    mine = w_qkv.shape[2]
    seg = lax.dynamic_index_in_dim(segment_ids, tw, 0)
    x, normed_t, query, key, value, w_heads, mq, mk = front(tokens, w_qkv, b_qv, norm1_gain[None], norm1_shift[None], seg)
    tables = (mq, mk, *block_ranges(seg[0]))
    later = lax.optimization_barrier((cotangent, w_out, query))
    cot = own_row(later[0], tw)
    w_out_heads = jnp.concatenate([w_out, swap(later[1], "tw")], 0)
    attended, totals = attn_fwd(query, key, value, *tables)
    vectors = jnp.stack([b_out, norm2_gain, norm2_shift, b_down] + [jnp.zeros_like(b_out)] * 4)
    out_mine, out_other, grad_middle, grad_b_up, sums, red, grad_heads, grad_w_out = ffn(
        dp_size, attended, w_out_heads, x, vectors, cot, w_up, w_down, b_up[None]
    )
    out_got = swap(out_other, "tw")
    dq, dk, dv = attn_bwd(query, key, value, grad_heads, attended, totals, *tables)
    up, down, heads, small, grad_tokens = finish(
        dp_size, red, dq, dk, dv, normed_t, w_heads, grad_w_out, x, norm1_gain[None], grad_middle, sums, grad_b_up
    )
    up, down, w_qkv_grad, w_out_grad, block_out = widen(tw, up, down, heads, out_mine, out_got)
    parts = small.reshape(-1)
    b_qv_grad = lax.dynamic_slice_in_dim(small[-16:].reshape(4, 2, 256), 2 * th + tw, 1, 0)[0, :, :mine]
    return (
        block_out,
        grad_tokens,
        parts[:d],
        parts[d : 2 * d],
        w_qkv_grad,
        b_qv_grad,
        w_out_grad,
        parts[2 * d : 3 * d],
        parts[3 * d : 4 * d],
        parts[4 * d : 5 * d],
        up,
        parts[6 * d : -16 * 128],
        down,
        parts[5 * d : 6 * d],
    )


def solution(mesh):
    return jax.shard_map(
        functools.partial(body, mesh.shape["dp"]),
        mesh=mesh,
        in_specs=(
            P("dp", ("th", "tw"), None),
            P("dp", None),
            P(),
            P(),
            P(None, None, ("th", "tw")),
            P(None, ("th", "tw")),
            P(("th", "tw"), None),
            P(),
            P(),
            P(),
            P(),
            P(),
            P(),
            P(),
            P("dp", ("th", "tw"), None),
        ),
        out_specs=(
            P("dp", ("th", "tw"), None),
            P("dp", ("th", "tw"), None),
            P(),
            P(),
            P(None, None, ("th", "tw")),
            P(None, ("th", "tw")),
            P(("th", "tw"), None),
            P(),
            P(),
            P(),
            P(),
            P(),
            P(),
            P(),
        ),
        check_vma=False,
    )
```

```python
import functools

import jax
import jax.numpy as jnp
from jax import lax
from jax.experimental import pallas as pl
from jax.experimental.pallas import tpu as pltpu
from jax.sharding import PartitionSpec as P

NT=(((1,),(1,)),((),())); NN=(((1,),(0,)),((),())); TN=(((0,),(0,)),((),()))
F32=jnp.float32; BF=jnp.bfloat16
BQ=256; BK=256; HD=64
def dot(a,b,d): return lax.dot_general(a,b,d,preferred_element_type=F32)

def fwd_kernel(lo_ref, hi_ref, q_ref, k_ref, v_ref, mq_ref, mk_ref, o_ref, lse_ref, m_ref, l_ref, acc_ref):
    i=pl.program_id(0)
    pairs=q_ref.shape[1]//128
    lane=lax.broadcasted_iota(jnp.int32,(1,128),1)
    halves=(lane<HD, lane>=HD)
    m_ref[...]=jnp.full(m_ref.shape,-1e30,F32)
    l_ref[...]=jnp.zeros_like(l_ref)
    acc_ref[...]=jnp.zeros_like(acc_ref)
    def body(j,_):
        ks=pl.ds(pl.multiple_of(j*BK,BK),BK)
        mk=mk_ref[ks,:]
        for p in range(pairs):
            cols=slice(p*128,(p+1)*128)
            qx=jnp.concatenate([q_ref[:,cols],mq_ref[...]],1)
            k2=k_ref[ks,cols]; v2=v_ref[ks,cols]
            ps=[]
            for e in range(2):
                h=2*p+e
                kx=jnp.concatenate([jnp.where(halves[e],k2,jnp.zeros_like(k2)),mk],1)
                s=dot(kx,qx,NT)
                m_old=m_ref[h:h+1,:]
                m_new=jnp.maximum(m_old,jnp.max(s,axis=0,keepdims=True))
                alpha=jnp.exp(m_old-m_new)
                pe=jnp.exp(s-m_new)
                l_ref[h:h+1,:]=l_ref[h:h+1,:]*alpha+jnp.sum(pe,axis=0,keepdims=True)
                m_ref[h:h+1,:]=m_new
                acc_ref[h*HD:(h+1)*HD,:]=acc_ref[h*HD:(h+1)*HD,:]*alpha
                ps.append(pe.astype(BF))
            vcat=jnp.concatenate([jnp.where(halves[0],v2,jnp.zeros_like(v2)),jnp.where(halves[1],v2,jnp.zeros_like(v2))],0)
            acc_ref[cols,:]+=dot(vcat,jnp.concatenate(ps,0),TN)
        return 0
    lax.fori_loop(lo_ref[i],hi_ref[i],body,0)
    for p in range(pairs):
        parts=[]
        for e in range(2):
            h=2*p+e
            parts.append(acc_ref[h*HD:(h+1)*HD,:]*(1.0/l_ref[h:h+1,:]))
        o_ref[:,p*128:(p+1)*128]=jnp.concatenate(parts,0).T.astype(BF)
    lse_ref[...]=m_ref[...]+jnp.log(jnp.maximum(l_ref[...],1e-37))

def attn_fwd(q,k,v,mq,mk,lo,hi):
    L,C=q.shape
    return pl.pallas_call(fwd_kernel,
        grid_spec=pltpu.PrefetchScalarGridSpec(num_scalar_prefetch=2,grid=(L//BQ,),
          in_specs=[pl.BlockSpec((BQ,C),lambda i,*_:(i,0)),pl.BlockSpec((L,C),lambda i,*_:(0,0)),pl.BlockSpec((L,C),lambda i,*_:(0,0)),
                    pl.BlockSpec((BQ,128),lambda i,*_:(i,0)),pl.BlockSpec((L,128),lambda i,*_:(0,0))],
          out_specs=[pl.BlockSpec((BQ,C),lambda i,*_:(i,0)),pl.BlockSpec((8,BQ),lambda i,*_:(0,i))],
          scratch_shapes=[pltpu.VMEM((8,BQ),F32),pltpu.VMEM((8,BQ),F32),pltpu.VMEM((C,BQ),F32)]),
        out_shape=[jax.ShapeDtypeStruct((L,C),BF),jax.ShapeDtypeStruct((8,L),F32)],
        name="attention_forward",
    )(lo,hi,q,k,v,mq,mk)

def bwd_kernel(lo_ref, hi_ref, q_ref, k_ref, v_ref, do_ref, o_ref, lse_ref, mq_ref, mk_ref, dq_ref, dk_ref, dv_ref, dk_acc, dv_acc, dq_acc, qcat, docat):
    i=pl.program_id(0); n=pl.num_programs(0)
    C=q_ref.shape[1]; pairs=C//128
    lane=lax.broadcasted_iota(jnp.int32,(1,128),1)
    halves=(lane<HD, lane>=HD)
    @pl.when(i==0)
    def _():
        dk_acc[...]=jnp.zeros_like(dk_acc); dv_acc[...]=jnp.zeros_like(dv_acc)
    dq_acc[...]=jnp.zeros_like(dq_acc)
    sel=(lax.broadcasted_iota(jnp.int32,(8,C),1)//HD==lax.broadcasted_iota(jnp.int32,(8,C),0)).astype(F32)
    delta=lax.dot_general(sel,do_ref[...].astype(F32)*o_ref[...].astype(F32),NT,precision=lax.Precision.HIGHEST,preferred_element_type=F32)
    for p in range(pairs):
        cols=slice(p*128,(p+1)*128)
        for e in range(2):
            q2=q_ref[:,cols]; d2=do_ref[:,cols]
            qcat[p,e*BQ:(e+1)*BQ,:]=jnp.where(halves[e],q2,jnp.zeros_like(q2))
            docat[p,e*BQ:(e+1)*BQ,:]=jnp.where(halves[e],d2,jnp.zeros_like(d2))
    lse=lse_ref[...]
    def body(j,_):
        ks=pl.ds(pl.multiple_of(j*BK,BK),BK)
        mk=mk_ref[ks,:]
        for p in range(pairs):
            cols=slice(p*128,(p+1)*128)
            qx=jnp.concatenate([q_ref[:,cols],mq_ref[...]],1)
            k2=k_ref[ks,cols]; v2=v_ref[ks,cols]; d2=do_ref[:,cols]
            ps=[]; dss=[]; kms=[]
            for e in range(2):
                h=2*p+e
                km=jnp.where(halves[e],k2,jnp.zeros_like(k2)); vm=jnp.where(halves[e],v2,jnp.zeros_like(v2))
                s=dot(jnp.concatenate([km,mk],1),qx,NT)
                pr=jnp.exp(s-lse[h:h+1,:])
                dp=dot(vm,d2,NT)
                ds=pr*(dp-delta[h:h+1,:])
                ps.append(pr.astype(BF)); dss.append(ds.astype(BF)); kms.append(km)
            dv_acc[ks,cols]+=dot(jnp.concatenate(ps,1),docat[p],NN)
            dk_acc[ks,cols]+=dot(jnp.concatenate(dss,1),qcat[p],NN)
            dq_acc[cols,:]+=dot(jnp.concatenate(kms,0),jnp.concatenate(dss,0),TN)
        return 0
    lax.fori_loop(lo_ref[i],hi_ref[i],body,0)
    dq_ref[...]=(dq_acc[...]*0.125).T.astype(BF)
    @pl.when(i==n-1)
    def _():
        dk_ref[...]=dk_acc[...].astype(BF); dv_ref[...]=dv_acc[...].astype(BF)

def attn_bwd(q,k,v,do,o,lse,mq,mk,lo,hi):
    L,C=q.shape
    blk=pl.BlockSpec((BQ,C),lambda i,*_:(i,0)); full=pl.BlockSpec((L,C),lambda i,*_:(0,0))
    return pl.pallas_call(bwd_kernel,
        grid_spec=pltpu.PrefetchScalarGridSpec(num_scalar_prefetch=2,grid=(L//BQ,),
          in_specs=[blk,full,full,blk,blk,pl.BlockSpec((8,BQ),lambda i,*_:(0,i)),pl.BlockSpec((BQ,128),lambda i,*_:(i,0)),pl.BlockSpec((L,128),lambda i,*_:(0,0))],
          out_specs=[blk,full,full],
          scratch_shapes=[pltpu.VMEM((L,C),F32),pltpu.VMEM((L,C),F32),pltpu.VMEM((C,BQ),F32),pltpu.VMEM((C//128,2*BQ,128),BF),pltpu.VMEM((C//128,2*BQ,128),BF)]),
        out_shape=[jax.ShapeDtypeStruct((L,C),BF)]*3,
        name="attention_backward",
    )(lo,hi,q,k,v,do,o,lse,mq,mk)

def block_ranges(seg):
    first=seg[::BQ]; last=seg[BQ-1::BQ]
    lo=jnp.sum(seg[None,:]<first[:,None],axis=1,dtype=jnp.int32)//BK
    hi=(jnp.sum(seg[None,:]<=last[:,None],axis=1,dtype=jnp.int32)+BK-1)//BK
    return lo,hi


TT=256; FC=512
LAG=2; GLAG=3; HLAG=3; HSP=2; GSP=4; VLAG=2; FL=3

def bits_of(dp): return dp.bit_length()-1

def big_plan(dp,rows):
    n=bits_of(dp)
    orders=(["tw"]+list(range(n)),[0,"tw"]+list(range(1,n)),[1,2,0,"tw"]+list(range(3,n)))
    unit=16<<(n+1)
    units=rows//unit
    third=max(1,units//4)
    shares=[units-units//3-third,units//3,third]
    return streams(orders,shares,unit)

def head_plan(dp,rows):
    n=bits_of(dp)
    orders=(["tw"]+list(range(n)),[0,"tw"]+list(range(1,n)),[1,2,0,"tw"]+list(range(3,n)))
    unit=16<<n
    units=rows//unit
    low=max(1,units//6)
    mid=max(1,units//3)
    return streams(orders,[units-mid-low,mid,low],unit)

def streams(orders,shares,unit):
    out=[]; start=0
    for order,share in zip(orders,shares):
        out.append((order,start,share*unit)); start+=share*unit
    return out

class Peers:
    def __init__(self):
        self.dp=lax.axis_index("dp"); self.th=lax.axis_index("th"); self.tw=lax.axis_index("tw")
    def bit(self,axis):
        return self.tw if axis=="tw" else (self.dp//(1<<axis))%2
    def peer(self,axis):
        if axis=="tw": return {"tw":1-self.tw}
        if axis=="th": return {"th":1-self.th}
        return {"dp":self.dp+(1-2*self.bit(axis))*(1<<axis)}

def send(src,dst,ssem,rsem,peer):
    return pltpu.make_async_remote_copy(src,dst,ssem,rsem,device_id=peer,device_id_type=pl.DeviceIdType.MESH)

def barrier(p,axes):
    sem=pltpu.get_barrier_semaphore()
    for a in axes:
        pl.semaphore_signal(sem,inc=1,device_id=p.peer(a),device_id_type=pl.DeviceIdType.MESH)
    pl.semaphore_wait(sem,len(axes))

def halves(p,order,row,rows,keep_tw=False):
    out=[]
    for axis in order:
        if keep_tw and axis=="tw": out.append((row,row,rows)); continue
        rows//=2; bit=p.bit(axis)
        out.append((row+(1-bit)*rows,row+bit*rows,rows)); row=row+bit*rows
    return out
def run_steps(steps):
    total=max(f+sp*(cnt-1) for f,sp,cnt,_ in steps)+1
    def body(i,_):
        for r in range(2):
            g=2*i+r
            for f,sp,cnt,what in steps:
                if sp==2:
                    if f%2!=r: continue
                    c=i-f//2
                else: c=g-f
                if cnt==1:
                    pl.when(c==0)(functools.partial(what,0))
                else: pl.when((c>=0)&(c<cnt))(functools.partial(what,c))
        return 0
    lax.fori_loop(0,(total+1)//2,body,0)
def al(x): return x if isinstance(x,int) else pl.multiple_of(x,16)
def rows_at(row,n): return pl.ds(al(row),n)

EPS=1e-06
def norm_parts(x):
    mean=jnp.mean(x,axis=-1,keepdims=True)
    cen=x-mean
    r=lax.rsqrt(jnp.mean(cen*cen,axis=-1,keepdims=True)+EPS)
    return cen*r,r
def norm_back(e,n,r,gain):
    t=e*gain
    return r*(t-jnp.mean(t,axis=-1,keepdims=True)-n*jnp.mean(t*n,axis=-1,keepdims=True))
def colsum(x): return jnp.sum(x,axis=0,keepdims=True)

def ffn_kernel(dp,att,wo,x,vin,cot,wu_h,wd_h,bu,mine,other,gm,gb,vec,red,gheads,gwo,
               wu,wd,cotT,mid,n2,n2T,obuf,orecv,grow,act,gh,dw,chip_recv,wsem,osem,gsem,*rest):
    CH=dw.shape[0]; T,D=x.shape; SLOTS=chip_recv.shape[0]
    plan=big_plan(dp,dw.shape[2]); n=len(plan[0][0]); K=len(plan)
    recv=[rest[k*n:(k+1)*n] for k in range(K)]
    send_sem,recv_sem,chip_send,chip_got=rest[K*n:]
    p=Peers()
    tiles=[slice(t*TT,(t+1)*TT) for t in range(T//TT)]; NT_=len(tiles)
    regs=[halves(p,*s) for s in plan]
    def copy(k,s,c):
        out,_,nr=regs[k][s]
        return send(dw.at[c,p.th,rows_at(out,nr),:],recv[k][s].at[c],send_sem.at[k,s,c],recv_sem.at[k,s,c],p.peer(plan[k][0][s]))
    def chip_copy(c):
        return send(dw.at[c,1-p.th],chip_recv.at[c%SLOTS],chip_send.at[c],chip_got.at[c],p.peer("th"))
    def ocopy(): return send(obuf,orecv,osem.at[0],osem.at[1],p.peer("th"))
    def gcopy(landed):
        ref=grow.at[rows_at((1-p.th if landed else p.th)*T,T),:]
        return send(ref,ref,gsem.at[0],gsem.at[1],p.peer("th"))
    def wload(c):
        return (pltpu.make_async_copy(wu_h.at[:,pl.ds(pl.multiple_of(c*FC,FC),FC)],wu.at[c],wsem.at[0,c]),
                pltpu.make_async_copy(wd_h.at[pl.ds(pl.multiple_of(c*FC,FC),FC),:],wd.at[c],wsem.at[1,c]))
    def load(c,_):
        for w in wload(c): w.start()
        return 0
    lax.fori_loop(0,CH,load,0)
    barrier(p,["th"]+plan[0][0])
    for r in tiles:
        obuf[r,:]=dot(att[rows_at((1-p.th)*T+r.start,TT),:],wo[...],NN).astype(BF)
    for t,r in enumerate(tiles):
        mid[r,:]=x[r,:].astype(F32)+dot(att[rows_at(p.th*T+r.start,TT),:],wo[...],NN)+vin[0:1,:]
        if t==0: ocopy().start()
        cotT[:,r]=cot[r,:].T
    ocopy().wait_recv()
    for r in tiles:
        m=mid[r,:]+orecv[r,:].astype(F32)
        mid[r,:]=m
        nn,_=norm_parts(m)
        y=(nn*vin[1:2,:]+vin[2:3,:]).astype(BF)
        n2[r,:]=y; n2T[:,r]=y.T
    vec[...]=jnp.zeros_like(vec)
    def sum_step(s,c):
        news=[]
        for k in range(K):
            copy(k,s,c).wait_recv()
            _,kr,nr=regs[k][s]
            at=(c,p.th,rows_at(kr,nr),slice(None))
            new=(dw[at].astype(F32)+recv[k][s][c].astype(F32)).astype(BF)
            if s<n-1: dw[at]=new
            else: news.append((kr,nr,new))
        if s<n-1:
            for k in range(K): copy(k,s+1,c).start()
        else:
            out=0
            for kr,nr,new in news:
                red[c,out:out+nr,:]=new; out+=nr
    def chip_sum(c):
        chip_copy(c).wait_recv()
        def add(q,_):
            r=rows_at(q*TT,TT)
            dw[c,p.th,r,:]=(dw[c,p.th,r,:].astype(F32)+chip_recv[c%SLOTS,r,:].astype(F32)).astype(BF)
            return 0
        lax.fori_loop(0,dw.shape[2]//TT,add,0)
        for k in range(K): copy(k,0,c).start()
    def hidden(c):
        for w in wload(c): w.wait()
        cols=pl.ds(pl.multiple_of(c*FC,FC),FC)
        gsum=jnp.zeros((1,FC),F32)
        for r in tiles:
            h=dot(n2[r,:],wu[c],NN)+bu[:,cols]
            ga=dot(cot[r,:],wd[c],NT)
            cdf=0.5*(1.0+lax.erf(h*(0.5**0.5)))
            a=(h*cdf).astype(BF)
            gr=(ga*(cdf+h*(jnp.exp(h*h*-0.5)*0.3989422804014327))).astype(BF)
            act[c,r,:]=a; gh[c,r,:]=gr
            gsum+=colsum(gr.astype(F32))
        gb[:,cols]=gsum
    def weight_grads(c):
        for t in range(D//TT):
            r=slice(t*TT,(t+1)*TT)
            for m,(lhs,rhs) in enumerate(((n2T,gh),(cotT,act))):
                y=dot(lhs[r,:],rhs[c],NN).astype(BF)
                for q in range(FC//128): dw[c,m,q*D+t*TT:q*D+(t+1)*TT,:]=y[:,q*128:(q+1)*128]
    def norm_two_back(t):
        r=rows_at(t*TT,TT)
        e=dot(gh[0,r,:],wu[0],NT)
        for c in range(1,CH): e+=dot(gh[c,r,:],wu[c],NT)
        nn,rs=norm_parts(mid[r,:])
        ct=cot[r,:].astype(F32)
        gmid=ct+norm_back(e,nn,rs,vin[1:2,:])
        gm[r,:]=gmid
        gbr=gmid.astype(BF)
        grow[rows_at(p.th*T+t*TT,TT),:]=gbr
        vec[0:1,:]+=colsum(gbr.astype(F32)); vec[1:2,:]+=colsum(e*nn); vec[2:3,:]+=colsum(e); vec[3:4,:]+=colsum(ct)
    def block_out(t):
        r=rows_at(t*TT,TT)
        y=mid[r,:]+vin[3:4,:]
        for c in range(CH): y+=dot(act[c,r,:],wd[c],NN)
        n2[r,:]=y.astype(BF)
    def split_out(_):
        gcopy(True).wait_recv()
        mine[...]=n2[rows_at(p.tw*(T//2),T//2),:]
        other[...]=n2[rows_at((1-p.tw)*(T//2),T//2),:]
    def grad_heads(u):
        for t in range(NT_):
            r=rows_at(u*T+t*TT,TT)
            gheads[r,:]=dot(grow[r,:],wo[...],NT).astype(BF)
    def grad_wo(_):
        for t in range(D//TT):
            r=slice(t*TT,(t+1)*TT)
            gwo[r,:]=dot(grow[:,r],att[...],TN).astype(BF)
    P2=2*CH; P3=P2+NT_; P4=P3+NT_
    part=functools.partial
    steps=[(3+FL*(s+1),2,CH,part(sum_step,s)) for s in reversed(range(n))]
    steps+=[(3,2,CH,chip_sum),(2,2,CH,lambda c: chip_copy(c).start())]
    steps+=[(0,2,CH,hidden),(1,2,CH,weight_grads),(P2,1,NT_,norm_two_back),(P3,1,1,lambda _: gcopy(False).start()),(P3,1,NT_,block_out),
            (P4,1,1,split_out),(P4,1,2,grad_heads),(P4+2,1,1,grad_wo)]
    run_steps(steps)
    ocopy().wait_send(); gcopy(False).wait_send()
    def drain(c,_):
        chip_copy(c).wait_send()
        for k in range(K):
            for s in range(n): copy(k,s,c).wait_send()
        return 0
    lax.fori_loop(0,CH,drain,0)

def whole(shape):
    return pl.BlockSpec(memory_space=pltpu.VMEM)

def ffn(dp,att,wo,x,vin,cot,wu,wd,bu):
    T,D=x.shape; FF=wu.shape[1]; CH=FF//FC; R=FC//128*D; C=att.shape[1]
    plan=big_plan(dp,R); n=len(plan[0][0])
    fin=R>>n
    recv=[pltpu.VMEM((CH,rows>>(s+1),128),BF) for _,_,rows in plan for s in range(n)]
    outs=[((T//2,D),BF),((T//2,D),BF),((T,D),F32),((1,FF),F32),((8,D),F32),((CH,fin,128),BF),((2*T,C),BF),((D,C),BF)]
    specs=[whole(o[0]) for o in outs]
    hbm=pl.BlockSpec(memory_space=pl.ANY)
    V=pltpu.VMEM; sem=pltpu.SemaphoreType.DMA
    return pl.pallas_call(functools.partial(ffn_kernel,dp),
      in_specs=[whole(v.shape) for v in (att,wo,x,vin,cot)]+[hbm,hbm,whole(bu.shape)],
      out_specs=specs,out_shape=[jax.ShapeDtypeStruct(*o) for o in outs],
      scratch_shapes=[V((CH,D,FC),BF),V((CH,FC,D),BF),V((D,T),BF),V((T,D),F32),V((T,D),BF),V((D,T),BF),V((T,D),BF),V((T,D),BF),V((2*T,D),BF),
          V((CH,T,FC),BF),V((CH,T,FC),BF),V((CH,2,R,128),BF),V((3,R,128),BF),sem((2,CH)),sem((2,)),sem((2,))]+recv
        +[sem((len(plan),n,CH))]*2+[sem((CH,))]*2,
      compiler_params=pltpu.CompilerParams(vmem_limit_bytes=63*2**20+2**19,collective_id=0,has_side_effects=True),name="feed_forward")(att,wo,x,vin,cot,wu,wd,bu)

def finish_kernel(dp,red,dq_h,dk_h,dv_h,normT_h,wh_h,gwo_h,x_h,gm_h,vin,vec,gbu,gathered,heads_out,vec_out,tok,full,fsem,dq,dk,dv,normT,wh,gwo,x,gm,isem,hp,hg,vbuf,vrecv,own,obuf,orecv,tbuf,trecv,vrow,osem,tsem,*rest):
    CH=full.shape[0]; R=full.shape[2]; T,D=x.shape; C=dq.shape[1]; Q=T//2
    plan=big_plan(dp,R); n=len(plan[0][0]); K=len(plan)
    HR=hp.shape[2]; hplan=head_plan(dp,HR); HK=len(hplan); HC=hp.shape[0]
    hrecv=[rest[k*n:(k+1)*n] for k in range(HK)]
    send_sem,recv_sem,chip_send,chip_got,hs_sem,hr_sem,ha_send,ha_recv,vs_sem,vr_sem=rest[HK*n:]
    p=Peers()
    regs=[halves(p,*s) for s in plan]
    hregs=[halves(p,*s,keep_tw=True) for s in hplan]
    def gat(k,s,c,landed):
        other,mine,nr=regs[k][s]
        ref=full.at[c,p.th,rows_at(other if landed else mine,nr),:]
        return send(ref,ref,send_sem.at[k,s,c],recv_sem.at[k,s,c],p.peer(plan[k][0][s]))
    def chip(c,landed):
        ref=full.at[c,1-p.th if landed else p.th]
        return send(ref,ref,chip_send.at[c],chip_got.at[c],p.peer("th"))
    def fput(c): return pltpu.make_async_copy(full.at[c],gathered.at[c],fsem.at[c])
    def hsum(k,s,c):
        order=hplan[k][0]; other,_,nr=hregs[k][s]
        if order[s]=="tw": src=hp.at[c,pl.ds(1,1),rows_at(other,nr),:]
        elif order.index("tw")>s: src=hp.at[c,:,rows_at(other,nr),:]
        else: src=hp.at[c,pl.ds(0,1),rows_at(other,nr),:]
        return send(src,hrecv[k][s].at[c],hs_sem.at[k,s,c],hr_sem.at[k,s,c],p.peer(order[s]))
    def hgat(k,s,c,landed):
        order=hplan[k][0]; other,mine,nr=hregs[k][s]
        ref=hg.at[c,rows_at(other if landed else mine,nr),:]
        return send(ref,ref,ha_send.at[k,s,c],ha_recv.at[k,s,c],p.peer(order[s]))
    backs=[[s for s in reversed(range(n)) if o[s]!="tw"] for o,_,_ in hplan]
    vaxes=["th","tw"]+list(range(n-1))
    def vcopy(i): return send(vbuf.at[i],vrecv.at[i],vs_sem.at[i],vr_sem.at[i],p.peer(vaxes[i]))
    def ocopy(): return send(obuf,orecv,osem.at[0],osem.at[1],p.peer("th"))
    def tcopy(): return send(tbuf.at[rows_at((1-p.tw)*Q,Q),:],trecv,tsem.at[0],tsem.at[1],p.peer("tw"))
    loads=[pltpu.make_async_copy(a,b,isem.at[i]) for i,(a,b) in enumerate(((normT_h,normT),(dq_h,dq),(dk_h,dk),(dv_h,dv),(gwo_h,gwo),(wh_h,wh),(x_h,x),(gm_h,gm)))]
    for l in loads: l.start()
    def arrived(a,b):
        for l in loads[a:b]: l.wait()
    out=0
    for k in range(K):
        _,kr,nr=regs[k][n-1]
        for c in range(CH): full[c,p.th,rows_at(kr,nr),:]=red[c,out:out+nr,:]
        out+=nr
    vbuf[0]=jnp.zeros(vbuf.shape[1:],F32)
    vrow[...]=jnp.zeros(vrow.shape,F32)
    barrier(p,["th"]+plan[0][0])
    last=n+n-1
    def head_step(j,c):
        for k in range(HK):
            order=hplan[k][0]
            if 0<j<=n:
                s=j-1
                hsum(k,s,c).wait_recv()
                _,kr,nr=hregs[k][s]
                q=slice(0,2) if order.index("tw")>s else slice(0,1)
                at=(c,q,rows_at(kr,nr),slice(None))
                new=(hp[at].astype(F32)+hrecv[k][s][c].astype(F32)).astype(BF)
                if j<n: hp[at]=new
                else: hg[c,rows_at(kr,nr),:]=new[0]
            elif j>n: hgat(k,backs[k][j-n-1],c,True).wait_recv()
        for k in range(HK):
            if j<n: hsum(k,j,c).start()
            elif j<last: hgat(k,backs[k][j-n],c,False).start()
        if j==last: heads_out[c]=hg[c]
    def gather_step(j,c):
        if 0<j<=n:
            for k in range(K): gat(k,n-j,c,True).wait_recv()
        if j<n:
            for k in range(K): gat(k,n-1-j,c,False).start()
        elif j==n: chip(c,False).start()
        else:
            chip(c,True).wait_recv()
            fput(c).start()
    HT=D//HC
    def weight_grads(t):
        r=rows_at(t*HT,HT)
        parts=[dot(normT[r,:],d[...],NN).astype(BF) for d in (dq,dk,dv)]+[gwo[r,:]]
        for q in range(2):
            y=jnp.concatenate([z[:,q*(C//2):(q+1)*(C//2)] for z in parts],1)
            for i in range(y.shape[1]//128): hp[t,q,i*HT:(i+1)*HT,:]=y[:,i*128:(i+1)*128]
    def norm_grad(core,t):
        rr=rows_at(core*T+t*TT,TT)
        return dot(dq[rr,:],wh[0],NN)+dot(dk[rr,:],wh[1],NN)+dot(dv[rr,:],wh[2],NN)
    def other_half(t): obuf[rows_at(t*TT,TT),:]=norm_grad(1-p.th,t).astype(BF)
    def own_half(t): own[rows_at(t*TT,TT),:]=norm_grad(p.th,t)
    def norm_one_back(i):
        quarter=(1-i)*(1-p.tw)+i*p.tw
        for t in range(Q//128):
            r=rows_at(quarter*Q+t*128,128)
            e=own[r,:]+orecv[r,:].astype(F32)
            nn,rs=norm_parts(x[r,:].astype(F32))
            tbuf[r,:]=(gm[r,:]+norm_back(e,nn,rs,vin[4:5,:])).astype(BF)
            vrow[0:1,:]+=colsum(e*nn); vrow[1:2,:]+=colsum(e)
    def vectors(_):
        tok[p.tw]=tbuf[rows_at(p.tw*Q,Q),:]
        rows=[vrow[0:1,:],vrow[1:2,:]]+[vec[i:i+1,:] for i in range(4)]+[gbu[...]]
        at=0
        for v in rows:
            for i in range(v.shape[1]//128):
                vbuf[0,at:at+1,:]=v[:,i*128:(i+1)*128]; at+=1
        for i,d in enumerate((dq,dv)):
            bs=colsum(d[...].astype(F32))
            for q in range(2):
                quarter=2*p.th+(p.tw if q==0 else 1-p.tw)
                y=jnp.concatenate([bs[:,q*(C//2):(q+1)*(C//2)],jnp.zeros((1,256-C//2),F32)],1)
                for z in range(2):
                    vbuf[0,pl.ds(at+quarter*4+i*2+z,1),:]=y[:,z*128:(z+1)*128]
    def vector_step(i,_):
        if i>0:
            vcopy(i-1).wait_recv()
            y=vbuf[i-1]+vrecv[i-1]
            if i<len(vaxes): vbuf[i]=y
            else: vec_out[...]=y
        if i<len(vaxes): vcopy(i).start()
    part=functools.partial
    NT_=T//TT; G1=HC; G2=G1+2*NT_
    steps=[(1+HLAG*j,HSP,HC,part(head_step,j)) for j in reversed(range(last+1))]
    steps+=[(GLAG*j,2,CH,part(gather_step,j)) for j in reversed(range(n+2))]
    steps+=[(G2+3+VLAG*i,1,1,part(vector_step,i)) for i in range(len(vaxes)+1)]
    steps+=[(0,1,1,lambda _: arrived(0,5)),(0,1,HC,weight_grads),(G1,1,1,lambda _: arrived(5,6)),(G2,1,1,lambda _: arrived(6,8)),(G1,1,NT_,other_half),(G1+NT_,1,1,lambda _: ocopy().start()),(G1+NT_,1,NT_,own_half),
            (G2,1,1,lambda _: ocopy().wait_recv()),(G2+1,1,1,lambda _: tcopy().start()),(G2,1,2,norm_one_back),(G2+2,1,1,vectors)]
    run_steps(steps)
    def drain(c,_):
        chip(c,False).wait_send(); fput(c).wait()
        for k in range(K):
            for s in range(n): gat(k,s,c,False).wait_send()
        return 0
    lax.fori_loop(0,CH,drain,0)
    def hdrain(c,_):
        for k in range(HK):
            for s in range(n): hsum(k,s,c).wait_send()
            for s in backs[k]: hgat(k,s,c,False).wait_send()
        return 0
    lax.fori_loop(0,HC,hdrain,0)
    for i in range(len(vaxes)): vcopy(i).wait_send()
    ocopy().wait_send(); tcopy().wait()
    tok[1-p.tw]=trecv[...]

def finish(dp,red,dq,dk,dv,normT,wh,gwo,x,gm,vin,vec,gbu):
    T,D=x.shape; CH,fin,_=red.shape; R=FC//128*D
    plan=big_plan(dp,R); n=len(plan[0][0])
    HC=D//TT; HR=2*dq.shape[1]//128*TT; hplan=head_plan(dp,HR)
    hrecv=[]
    for order,_,rows in hplan:
        q=2
        for axis in order:
            if axis=="tw": q=1
            else: rows//=2
            hrecv.append(pltpu.VMEM((HC,q,rows,128),BF))
    V=(6*D+gbu.shape[1])//128+16; nv=n+1; args=(red,dq,dk,dv,normT,wh,gwo,x,gm,vin,vec,gbu)
    return pl.pallas_call(functools.partial(finish_kernel,dp),
      in_specs=[pl.BlockSpec(memory_space=pl.ANY if 1<=i<=8 else pltpu.VMEM) for i in range(len(args))],
      out_specs=[pl.BlockSpec(memory_space=pl.ANY)]+[pl.BlockSpec(memory_space=pltpu.VMEM)]*3,
      out_shape=[jax.ShapeDtypeStruct((CH,2,R,128),BF),jax.ShapeDtypeStruct((HC,HR,128),BF),jax.ShapeDtypeStruct((V,128),F32),jax.ShapeDtypeStruct((2,T//2,D),BF)],
      scratch_shapes=[pltpu.VMEM((CH,2,R,128),BF),pltpu.SemaphoreType.DMA((CH,))]+[pltpu.VMEM(a.shape,a.dtype) for a in args[1:9]]+[pltpu.SemaphoreType.DMA((8,)),pltpu.VMEM((HC,2,HR,128),BF),pltpu.VMEM((HC,HR,128),BF),pltpu.VMEM((nv,V,128),F32),pltpu.VMEM((nv,V,128),F32),pltpu.VMEM((T,D),F32)]+[pltpu.VMEM((T,D),BF)]*3+[pltpu.VMEM((T//2,D),BF),pltpu.VMEM((8,D),F32)]+[pltpu.SemaphoreType.DMA((2,))]*2+hrecv
        +[pltpu.SemaphoreType.DMA((len(plan),n,CH))]*2+[pltpu.SemaphoreType.DMA((CH,))]*2+[pltpu.SemaphoreType.DMA((len(hplan),n,HC))]*4+[pltpu.SemaphoreType.DMA((nv,))]*2,
      compiler_params=pltpu.CompilerParams(vmem_limit_bytes=60*2**20,collective_id=1,has_side_effects=True),name="finish_gradients")(*args)

def widen_kernel(where,chunk,heads,mine,got,vec,wup,wdown,wqkv,wout,blk,*vectors):
    D=wup.shape[0]; q=wout.shape[0]; g=pl.program_id(0); HT=D//heads.shape[0]
    for i in range(FC//128):
        cols=slice(i*128,(i+1)*128)
        wup[:,cols]=chunk[0,i*D:(i+1)*D,:].astype(F32)
        wdown[cols,:]=chunk[1,i*D:(i+1)*D,:].T.astype(F32)
    @pl.when(g==0)
    def _():
        for t in range(heads.shape[0]):
            y=jnp.concatenate([heads[t,i*HT:(i+1)*HT,:] for i in range(heads.shape[1]//HT)],1).T.astype(F32)
            rr=slice(t*HT,(t+1)*HT)
            for c in range(3): wqkv[c,:,rr]=y[c*q:(c+1)*q,:]
            wout[:,rr]=y[3*q:,:]
        blk[where[0]]=mine[...]; blk[1-where[0]]=got[...]
        at=0
        for v in vectors:
            for i in range(v.shape[0]//128):
                v[i*128:(i+1)*128]=vec[at,:]; at+=1

def widen(tw,chunks,heads,mine,got,vec):
    CH,_,R,_=chunks.shape; D=R*128//FC; FF=CH*FC; q=heads.shape[0]*heads.shape[1]*128//(4*D); T2=mine.shape[0]
    outs=[(D,FF),(FF,D),(3,q,D),(q,D)]; sizes=[D]*6+[FF]
    res=pl.pallas_call(widen_kernel,grid=(CH,),
      in_specs=[pl.BlockSpec(memory_space=pltpu.SMEM),pl.BlockSpec((None,2,R,128),lambda g:(g,0,0,0))]+[pl.BlockSpec(memory_space=pltpu.VMEM)]*4,
      out_specs=[pl.BlockSpec((D,FC),lambda g:(0,g)),pl.BlockSpec((FC,D),lambda g:(g,0))]+[pl.BlockSpec(memory_space=pltpu.VMEM)]*(3+len(sizes)),
      out_shape=[jax.ShapeDtypeStruct(o,F32) for o in outs]+[jax.ShapeDtypeStruct((2,T2,D),BF)]+[jax.ShapeDtypeStruct((z,),F32) for z in sizes],
      compiler_params=pltpu.CompilerParams(vmem_limit_bytes=50*2**20),name="widen")(tw.reshape(1),chunks,heads,mine,got,vec)
    return res[:5],res[5:]

def front_kernel(tok,w,b,vin,seg,x_o,normT_o,q_o,k_o,v_o,wh_o,mq_o,mk_o,x,norm,normT,qkv,wh,wgot,bgot,mq,mk,tsem,bsem,csem,ysem,xsem,osem):
    p=Peers(); Q,D=tok.shape[1:]; T=2*Q; L=2*T; E=w.shape[1]; HALF=E//2
    barrier(p,["th","tw",0])
    def tcopy(): return send(tok.at[1-p.tw],x.at[rows_at(p.tw*Q,Q),:],tsem.at[0],tsem.at[1],p.peer("tw"))
    def bcopy(): return send(b,bgot,bsem.at[0],bsem.at[1],p.peer("tw"))
    def ycopy(c):
        r=rows_at(p.bit(0)*HALF,HALF)
        return send(w.at[c,r,:],wgot.at[c,r,:],ysem.at[0,c],ysem.at[1,c],p.peer("tw"))
    def xcopy(c,landed):
        ref=wgot.at[c,rows_at((1-p.bit(0) if landed else p.bit(0))*HALF,HALF),:]
        return send(ref,ref,xsem.at[0,c],xsem.at[1,c],p.peer(0))
    def ccopy(i,landed):
        core=1-p.th if landed else p.th
        quarter=p.tw if i==0 else 1-p.tw
        ref=norm.at[rows_at(core*T+quarter*Q,Q),:]
        return send(ref,ref,csem.at[0,i],csem.at[1,i],p.peer("th"))
    tcopy().start(); bcopy().start()
    for c in range(3): ycopy(c).start()
    def normalize(src,row):
        for t in range(Q//128):
            v=src(t)
            y=(norm_parts(v.astype(F32))[0]*vin[4:5,:]+vin[5:6,:]).astype(BF)
            norm[rows_at(row+t*128,128),:]=y
    def put(src,dst,i): return pltpu.make_async_copy(src,dst,osem.at[i])
    x[rows_at(p.tw*Q,Q),:]=tok[p.tw]
    normalize(lambda t: tok[p.tw,t*128:(t+1)*128,:],p.th*T+p.tw*Q)
    onehot=lax.broadcasted_iota(jnp.int32,(128,L),0)
    same=onehot==seg[...]
    mk[...]=jnp.where(same,1.0,0.0).T.astype(BF)
    ccopy(0,False).start()
    mq[...]=jnp.where(same|(onehot>=8),0.0,-float(2**40)).T.astype(BF)
    put(mk,mk_o,0).start(); put(mq,mq_o,1).start()
    tcopy().wait_recv()
    normalize(lambda t: x[rows_at((1-p.tw)*Q+t*128,128),:],p.th*T+(1-p.tw)*Q)
    put(x,x_o,2).start()
    bcopy().wait_recv()
    tiles=[slice(t*TT,(t+1)*TT) for t in range(L//TT)]
    def bias(c,ref): return ref[c//2:c//2+1,:] if c!=1 else None
    def project(c,wt,bs,r):
        y=dot(norm[r,:],wt,NT)
        if bs is not None: y=y+bs
        y=y.astype(BF)
        return y*BF(0.125) if c==0 else y
    ccopy(1,False).start()
    ccopy(0,True).wait_recv()
    ccopy(1,True).wait_recv()
    for c in range(3):
        for r in tiles: qkv[c,r,0:E]=project(c,w[c],bias(c,b),r)
    for r in tiles: normT[:,r]=norm[r,:].T
    put(normT,normT_o,3).start()
    for c in range(3):
        ycopy(c).wait_recv()
        xcopy(c,False).start()
    for c in range(3):
        xcopy(c,True).wait_recv()
        for r in tiles: qkv[c,r,E:2*E]=project(c,wgot[c],bias(c,bgot),r)
        put(qkv.at[c],(q_o,k_o,v_o)[c],4+c).start()
        wh[c,0:E,:]=w[c]; wh[c,E:2*E,:]=wgot[c]
    put(wh,wh_o,7).start()
    for src,dst,i in ((mk,mk_o,0),(mq,mq_o,1),(x,x_o,2),(normT,normT_o,3),(wh,wh_o,7)): put(src,dst,i).wait()
    for c in range(3):
        put(qkv.at[c],(q_o,k_o,v_o)[c],4+c).wait()
        ycopy(c).wait_send(); xcopy(c,False).wait_send()
    tcopy().wait_send(); bcopy().wait_send()
    for i in range(2): ccopy(i,False).wait_send()

def front(tok,w,b,vin,seg):
    _,Q,D=tok.shape; T=2*Q; L=2*T; E=w.shape[1]
    outs=[((T,D),BF),((D,L),BF)]+[((L,2*E),BF)]*3+[((3,2*E,D),BF)]+[((L,128),BF)]*2
    sem=pltpu.SemaphoreType.DMA
    return pl.pallas_call(front_kernel,
      in_specs=[pl.BlockSpec(memory_space=pltpu.VMEM)]*5,out_specs=[pl.BlockSpec(memory_space=pl.ANY)]*len(outs),
      out_shape=[jax.ShapeDtypeStruct(*o) for o in outs],
      scratch_shapes=[pltpu.VMEM((T,D),BF),pltpu.VMEM((L,D),BF),pltpu.VMEM((D,L),BF),pltpu.VMEM((3,L,2*E),BF),pltpu.VMEM((3,2*E,D),BF),pltpu.VMEM((3,E,D),BF),
        pltpu.VMEM(b.shape,F32),pltpu.VMEM((L,128),BF),pltpu.VMEM((L,128),BF),sem((2,)),sem((2,)),sem((2,2)),sem((2,3)),sem((2,3)),sem((8,))],
      compiler_params=pltpu.CompilerParams(vmem_limit_bytes=60*2**20,collective_id=2,has_side_effects=True),name="front")(tok,w,b,vin,seg)


SWAP = [(0, 1), (1, 0)]


def swap(value, axis):
    return lax.ppermute(value, axis, SWAP)


def in_order(mine, other, index, axis):
    return jnp.where(
        index == 0, jnp.concatenate([mine, other], axis), jnp.concatenate([other, mine], axis)
    )


def own_row(rows, tw):
    mine = lax.dynamic_index_in_dim(rows, tw, 0, keepdims=False)
    other = lax.dynamic_index_in_dim(rows, 1 - tw, 0, keepdims=False)
    return in_order(mine, swap(other, "tw"), tw, 0)


def body(
    dp_size,
    tokens,
    segment_ids,
    norm1_gain,
    norm1_shift,
    w_qkv,
    b_qv,
    w_out,
    b_out,
    norm2_gain,
    norm2_shift,
    w_up,
    b_up,
    w_down,
    b_down,
    cotangent,
):
    th, tw = lax.axis_index("th"), lax.axis_index("tw")
    d = tokens.shape[-1]
    mine = w_qkv.shape[2]
    vectors = jnp.stack([b_out, norm2_gain, norm2_shift, b_down, norm1_gain, norm1_shift, b_down, b_down])
    seg = lax.dynamic_index_in_dim(segment_ids, tw, 0)
    x, normed_t, query, key, value, w_heads, mq, mk = front(
        tokens, w_qkv.transpose(0, 2, 1), b_qv, vectors, seg
    )
    tables = (mq, mk, *block_ranges(seg[0]))
    later = lax.optimization_barrier((cotangent, w_out, query))
    cot = own_row(later[0], tw)
    w_out_heads = jnp.concatenate([w_out, swap(later[1], "tw")], 0)
    attended, totals = attn_fwd(query, key, value, *tables)
    out_mine, out_other, grad_middle, grad_b_up, sums, red, grad_heads, grad_w_out = ffn(
        dp_size, attended, w_out_heads, x, vectors, cot, w_up, w_down, b_up[None]
    )
    out_got = swap(out_other, "tw")
    dq, dk, dv = attn_bwd(query, key, value, grad_heads, attended, totals, *tables)
    chunks, heads, small, grad_tokens = finish(
        dp_size, red, dq, dk, dv, normed_t, w_heads, grad_w_out, x, grad_middle, vectors, sums, grad_b_up
    )
    (up, down, w_qkv_grad, w_out_grad, block_out), vecs = widen(tw, chunks, heads, out_mine, out_got, small)
    b_qv_grad = lax.dynamic_slice_in_dim(small[-16:].reshape(4, 2, 256), 2 * th + tw, 1, 0)[0, :, :mine]
    return (
        block_out,
        grad_tokens,
        vecs[0],
        vecs[1],
        w_qkv_grad.transpose(0, 2, 1),
        b_qv_grad,
        w_out_grad,
        vecs[2],
        vecs[3],
        vecs[4],
        up,
        vecs[6],
        down,
        vecs[5],
    )


def solution(mesh):
    return jax.shard_map(
        functools.partial(body, mesh.shape["dp"]),
        mesh=mesh,
        in_specs=(
            P("dp", ("th", "tw"), None),
            P("dp", None),
            P(),
            P(),
            P(None, None, ("th", "tw")),
            P(None, ("th", "tw")),
            P(("th", "tw"), None),
            P(),
            P(),
            P(),
            P(),
            P(),
            P(),
            P(),
            P("dp", ("th", "tw"), None),
        ),
        out_specs=(
            P("dp", ("th", "tw"), None),
            P("dp", ("th", "tw"), None),
            P(),
            P(),
            P(None, None, ("th", "tw")),
            P(None, ("th", "tw")),
            P(("th", "tw"), None),
            P(),
            P(),
            P(),
            P(),
            P(),
            P(),
            P(),
        ),
        check_vma=False,
    )
```

```python
import functools

import jax
import jax.numpy as jnp
from jax import lax
from jax.experimental import pallas as pl
from jax.experimental.pallas import tpu as pltpu
from jax.sharding import PartitionSpec as P

NT=(((1,),(1,)),((),())); NN=(((1,),(0,)),((),())); TN=(((0,),(0,)),((),()))
F32=jnp.float32; BF=jnp.bfloat16
BQ=256; BK=256; HD=64
def dot(a,b,d): return lax.dot_general(a,b,d,preferred_element_type=F32)

AL=128; VR=80
def key_rows(lo_ref,mk_ref,i,j):
    L=mk_ref.shape[0]
    want=lo_ref[i]+j*BK
    start=pl.multiple_of(jnp.minimum(want,L-BK),AL)
    row=lax.broadcasted_iota(jnp.int32,(BK,128),0); lane=lax.broadcasted_iota(jnp.int32,(BK,128),1)
    ks=pl.ds(start,BK)
    return ks,jnp.where((lane==8)&(row<want-start),jnp.ones((BK,128),BF),mk_ref[ks,:])

def fwd_kernel(lo_ref, n_ref, q_ref, k_ref, v_ref, mq_ref, mk_ref, o_ref, lse_ref, m_ref, acc_ref, vT_ref, *score_refs):
    i=pl.program_id(0); H=q_ref.shape[1]//HD
    lane=lax.broadcasted_iota(jnp.int32,(1,128),1)
    halves=(lane<HD, lane>=HD)
    @pl.when(i==0)
    def _():
        row=lax.broadcasted_iota(jnp.int32,(VR-HD,v_ref.shape[0]),0)
        for p in range(H//2):
            t=v_ref[:,p*128:(p+1)*128].T
            for e in range(2):
                vT_ref[2*p+e,0:HD,:]=t[e*HD:(e+1)*HD,:]
                vT_ref[2*p+e,HD:VR,:]=jnp.where(row==0,1.0,0.0).astype(BF)
    m_ref[...]=jnp.full(m_ref.shape,-1e30,F32)
    acc_ref[...]=jnp.zeros_like(acc_ref)
    def score(h,ks,mk):
        cols=slice(h//2*128,h//2*128+128)
        k2=k_ref[ks,cols]
        return dot(jnp.concatenate([jnp.where(halves[h%2],k2,jnp.zeros_like(k2)),mk],1),jnp.concatenate([q_ref[:,cols],mq_ref[...]],1),NT)
    def soft(h,s):
        m_old=m_ref[h:h+1,:]
        m_new=jnp.maximum(m_old,jnp.max(s,axis=0,keepdims=True))
        m_ref[h:h+1,:]=m_new
        return jnp.exp(s-m_new).astype(BF),jnp.exp(m_old-m_new)
    def weigh(h,ks,pe,alpha):
        acc_ref[h]=acc_ref[h]*alpha+dot(vT_ref[h,:,ks],pe,NN)
    n=n_ref[i]
    def half(j,now,then):
        ks,_=key_rows(lo_ref,mk_ref,i,j)
        kn,mk=key_rows(lo_ref,mk_ref,i,j+1)
        last=None
        for h in range(H):
            then[h]=score(h,kn,mk)
            probs=soft(h,now[h])
            if last is not None: weigh(h-1,ks,*last)
            last=probs
        weigh(H-1,ks,*last)
    ks,mk=key_rows(lo_ref,mk_ref,i,0)
    for h in range(H): score_refs[0][h]=score(h,ks,mk)
    def body(t,_):
        half(2*t,*score_refs)
        @pl.when(2*t+1<n)
        def _(): half(2*t+1,*score_refs[::-1])
        return 0
    lax.fori_loop(0,(n+1)//2,body,0)
    for p in range(H//2):
        parts=[acc_ref[h,0:HD,:]*(1.0/acc_ref[h,HD:HD+1,:]) for h in (2*p,2*p+1)]
        o_ref[:,p*128:(p+1)*128]=jnp.concatenate(parts,0).T.astype(BF)
    for h in range(H): lse_ref[h:h+1,:]=m_ref[h:h+1,:]+jnp.log(acc_ref[h,HD:HD+1,:])
    lse_ref[H:,:]=jnp.zeros((lse_ref.shape[0]-H,BQ),F32)

def attn_fwd(q,k,v,mq,mk,lo,n):
    L,C=q.shape
    return pl.pallas_call(fwd_kernel,
        grid_spec=pltpu.PrefetchScalarGridSpec(num_scalar_prefetch=2,grid=(L//BQ,),
          in_specs=[pl.BlockSpec((BQ,C),lambda i,*_:(i,0)),pl.BlockSpec((L,C),lambda i,*_:(0,0)),pl.BlockSpec((L,C),lambda i,*_:(0,0)),
                    pl.BlockSpec((BQ,128),lambda i,*_:(i,0)),pl.BlockSpec((L,128),lambda i,*_:(0,0))],
          out_specs=[pl.BlockSpec((BQ,C),lambda i,*_:(i,0)),pl.BlockSpec((8,BQ),lambda i,*_:(0,i))],
          scratch_shapes=[pltpu.VMEM((8,BQ),F32),pltpu.VMEM((C//HD,VR,BQ),F32),pltpu.VMEM((C//HD,VR,L),BF),pltpu.VMEM((C//HD,BK,BQ),F32),pltpu.VMEM((C//HD,BK,BQ),F32)]),
        out_shape=[jax.ShapeDtypeStruct((L,C),BF),jax.ShapeDtypeStruct((8,L),F32)],
        name="attention_forward",
    )(lo,n,q,k,v,mq,mk)

def bwd_kernel(lo_ref, n_ref, q_ref, k_ref, v_ref, do_ref, o_ref, lse_ref, mq_ref, mk_ref, dq_ref, dk_ref, dv_ref, dk_acc, dv_acc, dq_acc, qcat, docat):
    i=pl.program_id(0); n=pl.num_programs(0)
    C=q_ref.shape[1]; pairs=C//128
    lane=lax.broadcasted_iota(jnp.int32,(1,128),1)
    halves=(lane<HD, lane>=HD)
    @pl.when(i==0)
    def _():
        dk_acc[...]=jnp.zeros_like(dk_acc); dv_acc[...]=jnp.zeros_like(dv_acc)
    dq_acc[...]=jnp.zeros_like(dq_acc)
    sel=(lax.broadcasted_iota(jnp.int32,(8,C),1)//HD==lax.broadcasted_iota(jnp.int32,(8,C),0)).astype(BF)
    prod=do_ref[...].astype(F32)*o_ref[...].astype(F32)
    high=prod.astype(BF)
    delta=dot(sel,high,NT)+dot(sel,(prod-high.astype(F32)).astype(BF),NT)
    for p in range(pairs):
        cols=slice(p*128,(p+1)*128)
        for e in range(2):
            q2=q_ref[:,cols]; d2=do_ref[:,cols]
            qcat[p,e*BQ:(e+1)*BQ,:]=jnp.where(halves[e],q2,jnp.zeros_like(q2))
            docat[p,e*BQ:(e+1)*BQ,:]=jnp.where(halves[e],d2,jnp.zeros_like(d2))
    lse=lse_ref[...]
    def body(j,_):
        ks,mk=key_rows(lo_ref,mk_ref,i,j)
        for p in range(pairs):
            cols=slice(p*128,(p+1)*128)
            qx=jnp.concatenate([q_ref[:,cols],mq_ref[...]],1)
            k2=k_ref[ks,cols]; v2=v_ref[ks,cols]; d2=do_ref[:,cols]
            ps=[]; dss=[]; kms=[]
            for e in range(2):
                h=2*p+e
                km=jnp.where(halves[e],k2,jnp.zeros_like(k2)); vm=jnp.where(halves[e],v2,jnp.zeros_like(v2))
                s=dot(jnp.concatenate([km,mk],1),qx,NT)
                pr=jnp.exp(s-lse[h:h+1,:])
                dp=dot(vm,d2,NT)
                ds=pr*(dp-delta[h:h+1,:])
                ps.append(pr.astype(BF)); dss.append(ds.astype(BF)); kms.append(km)
            dv_acc[ks,cols]+=dot(jnp.concatenate(ps,1),docat[p],NN)
            dk_acc[ks,cols]+=dot(jnp.concatenate(dss,1),qcat[p],NN)
            dq_acc[cols,:]+=dot(jnp.concatenate(kms,0),jnp.concatenate(dss,0),TN)
        return 0
    lax.fori_loop(0,n_ref[i],body,0)
    dq_ref[...]=(dq_acc[...]*0.125).T.astype(BF)
    @pl.when(i==n-1)
    def _():
        dk_ref[...]=dk_acc[...].astype(BF); dv_ref[...]=dv_acc[...].astype(BF)

def attn_bwd(q,k,v,do,o,lse,mq,mk,lo,n):
    L,C=q.shape
    blk=pl.BlockSpec((BQ,C),lambda i,*_:(i,0)); full=pl.BlockSpec((L,C),lambda i,*_:(0,0))
    return pl.pallas_call(bwd_kernel,
        grid_spec=pltpu.PrefetchScalarGridSpec(num_scalar_prefetch=2,grid=(L//BQ,),
          in_specs=[blk,full,full,blk,blk,pl.BlockSpec((8,BQ),lambda i,*_:(0,i)),pl.BlockSpec((BQ,128),lambda i,*_:(i,0)),pl.BlockSpec((L,128),lambda i,*_:(0,0))],
          out_specs=[blk,full,full],
          scratch_shapes=[pltpu.VMEM((L,C),F32),pltpu.VMEM((L,C),F32),pltpu.VMEM((C,BQ),F32),pltpu.VMEM((C//128,2*BQ,128),BF),pltpu.VMEM((C//128,2*BQ,128),BF)]),
        out_shape=[jax.ShapeDtypeStruct((L,C),BF)]*3,
        name="attention_backward",
    )(lo,n,q,k,v,do,o,lse,mq,mk)

def block_ranges(seg):
    first=seg[::BQ]; last=seg[BQ-1::BQ]
    lo=jnp.sum(seg[None,:]<first[:,None],axis=1,dtype=jnp.int32)//AL*AL
    hi=jnp.sum(seg[None,:]<=last[:,None],axis=1,dtype=jnp.int32)
    return lo,(hi-lo+BK-1)//BK


TT=256; FC=512
LAG=2; GLAG=5; HLAG=4; HSP=2; GSP=4; VLAG=5; FL=3

def bits_of(dp): return dp.bit_length()-1

def big_plan(dp,rows):
    n=bits_of(dp)
    orders=(["tw"]+list(range(n)),[0,"tw"]+list(range(1,n)),[1,2,0,"tw"]+list(range(3,n)))
    unit=16<<(n+1)
    units=rows//unit
    third=max(1,units//4)
    shares=[units-units//3-third,units//3,third]
    return streams(orders,shares,unit)

def head_plan(dp,rows):
    n=bits_of(dp)
    orders=(["tw"]+list(range(n)),[0,"tw"]+list(range(1,n)),[1,2,0,"tw"]+list(range(3,n)))
    unit=16<<n
    units=rows//unit
    low=max(1,units//6)
    mid=max(1,units//3)
    return streams(orders,[units-mid-low,mid,low],unit)

def streams(orders,shares,unit):
    out=[]; start=0
    for order,share in zip(orders,shares):
        out.append((order,start,share*unit)); start+=share*unit
    return out

class Peers:
    def __init__(self):
        self.dp=lax.axis_index("dp"); self.th=lax.axis_index("th"); self.tw=lax.axis_index("tw")
    def bit(self,axis):
        return self.tw if axis=="tw" else (self.dp//(1<<axis))%2
    def peer(self,axis):
        if axis=="tw": return {"tw":1-self.tw}
        if axis=="th": return {"th":1-self.th}
        return {"dp":self.dp+(1-2*self.bit(axis))*(1<<axis)}

def send(src,dst,ssem,rsem,peer):
    return pltpu.make_async_remote_copy(src,dst,ssem,rsem,device_id=peer,device_id_type=pl.DeviceIdType.MESH)

def barrier(p,axes):
    sem=pltpu.get_barrier_semaphore()
    for a in axes:
        pl.semaphore_signal(sem,inc=1,device_id=p.peer(a),device_id_type=pl.DeviceIdType.MESH)
    pl.semaphore_wait(sem,len(axes))

def halves(p,order,row,rows,keep_tw=False):
    out=[]
    for axis in order:
        if keep_tw and axis=="tw": out.append((row,row,rows)); continue
        rows//=2; bit=p.bit(axis)
        out.append((row+(1-bit)*rows,row+bit*rows,rows)); row=row+bit*rows
    return out
def run_steps(steps):
    total=max(f+sp*(cnt-1) for f,sp,cnt,_ in steps)+1
    def body(i,_):
        for r in range(2):
            g=2*i+r
            for f,sp,cnt,what in steps:
                if sp==2:
                    if f%2!=r: continue
                    c=i-f//2
                else: c=g-f
                if cnt==1:
                    pl.when(c==0)(functools.partial(what,0))
                else: pl.when((c>=0)&(c<cnt))(functools.partial(what,c))
        return 0
    lax.fori_loop(0,(total+1)//2,body,0)
def al(x): return x if isinstance(x,int) else pl.multiple_of(x,16)
def rows_at(row,n): return pl.ds(al(row),n)

EPS=1e-06
def norm_parts(x):
    mean=jnp.mean(x,axis=-1,keepdims=True)
    cen=x-mean
    r=lax.rsqrt(jnp.mean(cen*cen,axis=-1,keepdims=True)+EPS)
    return cen*r,r
def norm_back(e,n,r,gain):
    t=e*gain
    return r*(t-jnp.mean(t,axis=-1,keepdims=True)-n*jnp.mean(t*n,axis=-1,keepdims=True))
def colsum(x): return jnp.sum(x,axis=0,keepdims=True)

def ffn_kernel(dp,att,wo,x,vb,vg,vs,vd,cot,wu_h,wd_h,bu,mine,other,gm,gb,vec,red,gheads,gwo,
               wu,wd,cotT,mid,n2,n2T,obuf,orecv,grow,act,gh,dw,chip_recv,wsem,osem,gsem,*rest):
    CH=dw.shape[0]; T,D=x.shape; SLOTS=chip_recv.shape[0]
    plan=big_plan(dp,dw.shape[2]); n=len(plan[0][0]); K=len(plan)
    recv=[rest[k*n:(k+1)*n] for k in range(K)]
    send_sem,recv_sem,chip_send,chip_got=rest[K*n:]
    p=Peers()
    b_row,g_row,s_row,d_row=[v[...].reshape(1,D) for v in (vb,vg,vs,vd)]
    tiles=[slice(t*TT,(t+1)*TT) for t in range(T//TT)]; NT_=len(tiles)
    regs=[halves(p,*s) for s in plan]
    def copy(k,s,c):
        out,_,nr=regs[k][s]
        return send(dw.at[c,p.th,rows_at(out,nr),:],recv[k][s].at[c],send_sem.at[k,s,c],recv_sem.at[k,s,c],p.peer(plan[k][0][s]))
    def chip_copy(c):
        return send(dw.at[c,1-p.th],chip_recv.at[c%SLOTS],chip_send.at[c],chip_got.at[c],p.peer("th"))
    def ocopy(): return send(obuf,orecv,osem.at[0],osem.at[1],p.peer("th"))
    def gcopy(landed):
        ref=grow.at[rows_at((1-p.th if landed else p.th)*T,T),:]
        return send(ref,ref,gsem.at[0],gsem.at[1],p.peer("th"))
    def wload(c):
        return (pltpu.make_async_copy(wu_h.at[:,pl.ds(pl.multiple_of(c*FC,FC),FC)],wu.at[c],wsem.at[0,c]),
                pltpu.make_async_copy(wd_h.at[pl.ds(pl.multiple_of(c*FC,FC),FC),:],wd.at[c],wsem.at[1,c]))
    def load(c,_):
        for w in wload(c): w.start()
        return 0
    lax.fori_loop(0,CH,load,0)
    barrier(p,["th"]+plan[0][0])
    for r in tiles:
        obuf[r,:]=dot(att[rows_at((1-p.th)*T+r.start,TT),:],wo[...],NN).astype(BF)
    for t,r in enumerate(tiles):
        mid[r,:]=x[r,:].astype(F32)+dot(att[rows_at(p.th*T+r.start,TT),:],wo[...],NN)+b_row
        if t==0: ocopy().start()
        cotT[:,r]=cot[r,:].T
    ocopy().wait_recv()
    for r in tiles:
        m=mid[r,:]+orecv[r,:].astype(F32)
        mid[r,:]=m
        nn,_=norm_parts(m)
        y=(nn*g_row+s_row).astype(BF)
        n2[r,:]=y; n2T[:,r]=y.T
    vec[...]=jnp.zeros_like(vec)
    def sum_step(s,c):
        news=[]
        for k in range(K):
            copy(k,s,c).wait_recv()
            _,kr,nr=regs[k][s]
            at=(c,p.th,rows_at(kr,nr),slice(None))
            new=(dw[at].astype(F32)+recv[k][s][c].astype(F32)).astype(BF)
            if s<n-1: dw[at]=new
            else: news.append((kr,nr,new))
        if s<n-1:
            for k in range(K): copy(k,s+1,c).start()
        else:
            out=0
            for kr,nr,new in news:
                red[c,out:out+nr,:]=new; out+=nr
    def chip_sum(c):
        chip_copy(c).wait_recv()
        def add(q,_):
            r=rows_at(q*TT,TT)
            dw[c,p.th,r,:]=(dw[c,p.th,r,:].astype(F32)+chip_recv[c%SLOTS,r,:].astype(F32)).astype(BF)
            return 0
        lax.fori_loop(0,dw.shape[2]//TT,add,0)
        for k in range(K): copy(k,0,c).start()
    def hidden(c):
        for w in wload(c): w.wait()
        cols=pl.ds(pl.multiple_of(c*FC,FC),FC)
        gsum=jnp.zeros((1,FC),F32)
        for r in tiles:
            h=dot(n2[r,:],wu[c],NN)+bu[:,cols]
            ga=dot(cot[r,:],wd[c],NT)
            cdf=0.5*(1.0+lax.erf(h*(0.5**0.5)))
            a=(h*cdf).astype(BF)
            gr=(ga*(cdf+h*(jnp.exp(h*h*-0.5)*0.3989422804014327))).astype(BF)
            act[c,r,:]=a; gh[c,r,:]=gr
            gsum+=colsum(gr.astype(F32))
        gb[:,cols]=gsum
    def weight_grads(c):
        for t in range(D//TT):
            r=slice(t*TT,(t+1)*TT)
            for m,(lhs,rhs) in enumerate(((n2T,gh),(cotT,act))):
                y=dot(lhs[r,:],rhs[c],NN).astype(BF)
                for q in range(FC//128): dw[c,m,q*D+t*TT:q*D+(t+1)*TT,:]=y[:,q*128:(q+1)*128]
    def norm_two_back(t):
        r=rows_at(t*TT,TT)
        e=dot(gh[0,r,:],wu[0],NT)
        for c in range(1,CH): e+=dot(gh[c,r,:],wu[c],NT)
        nn,rs=norm_parts(mid[r,:])
        ct=cot[r,:].astype(F32)
        gmid=ct+norm_back(e,nn,rs,g_row)
        gm[r,:]=gmid
        gbr=gmid.astype(BF)
        grow[rows_at(p.th*T+t*TT,TT),:]=gbr
        vec[0:1,:]+=colsum(gbr.astype(F32)); vec[1:2,:]+=colsum(e*nn); vec[2:3,:]+=colsum(e); vec[3:4,:]+=colsum(ct)
    def block_out(t):
        r=rows_at(t*TT,TT)
        y=mid[r,:]+d_row
        for c in range(CH): y+=dot(act[c,r,:],wd[c],NN)
        n2[r,:]=y.astype(BF)
    def split_out(_):
        gcopy(True).wait_recv()
        mine[...]=n2[rows_at(p.tw*(T//2),T//2),:]
        other[...]=n2[rows_at((1-p.tw)*(T//2),T//2),:]
    def grad_heads(u):
        for t in range(NT_):
            r=rows_at(u*T+t*TT,TT)
            gheads[r,:]=dot(grow[r,:],wo[...],NT).astype(BF)
    def grad_wo(_):
        for t in range(D//TT):
            r=slice(t*TT,(t+1)*TT)
            gwo[r,:]=dot(grow[:,r],att[...],TN).astype(BF)
    P2=2*CH; P3=P2+NT_; P4=P3+NT_
    part=functools.partial
    steps=[(3+FL*(s+1),2,CH,part(sum_step,s)) for s in reversed(range(n))]
    steps+=[(3,2,CH,chip_sum),(2,2,CH,lambda c: chip_copy(c).start())]
    steps+=[(0,2,CH,hidden),(1,2,CH,weight_grads),(P2,1,NT_,norm_two_back),(P3,1,1,lambda _: gcopy(False).start()),(P3,1,NT_,block_out),
            (P4,1,1,split_out),(P4,1,2,grad_heads),(P4+2,1,1,grad_wo)]
    run_steps(steps)
    ocopy().wait_send(); gcopy(False).wait_send()
    def drain(c,_):
        chip_copy(c).wait_send()
        for k in range(K):
            for s in range(n): copy(k,s,c).wait_send()
        return 0
    lax.fori_loop(0,CH,drain,0)

def whole(shape):
    return pl.BlockSpec(memory_space=pltpu.VMEM)

def ffn(dp,att,wo,x,vb,vg,vs,vd,cot,wu,wd,bu):
    T,D=x.shape; FF=wu.shape[1]; CH=FF//FC; R=FC//128*D; C=att.shape[1]
    plan=big_plan(dp,R); n=len(plan[0][0])
    fin=R>>n
    recv=[pltpu.VMEM((CH,rows>>(s+1),128),BF) for _,_,rows in plan for s in range(n)]
    outs=[((T//2,D),BF),((T//2,D),BF),((T,D),F32),((1,FF),F32),((8,D),F32),((CH,fin,128),BF),((2*T,C),BF),((D,C),BF)]
    specs=[whole(o[0]) for o in outs]
    hbm=pl.BlockSpec(memory_space=pl.ANY)
    V=pltpu.VMEM; sem=pltpu.SemaphoreType.DMA
    return pl.pallas_call(functools.partial(ffn_kernel,dp),
      in_specs=[whole(v.shape) for v in (att,wo,x,vb,vg,vs,vd,cot)]+[hbm,hbm,whole(bu.shape)],
      out_specs=specs,out_shape=[jax.ShapeDtypeStruct(*o) for o in outs],
      scratch_shapes=[V((CH,D,FC),BF),V((CH,FC,D),BF),V((D,T),BF),V((T,D),F32),V((T,D),BF),V((D,T),BF),V((T,D),BF),V((T,D),BF),V((2*T,D),BF),
          V((CH,T,FC),BF),V((CH,T,FC),BF),V((CH,2,R,128),BF),V((3,R,128),BF),sem((2,CH)),sem((2,)),sem((2,))]+recv
        +[sem((len(plan),n,CH))]*2+[sem((CH,))]*2,
      compiler_params=pltpu.CompilerParams(vmem_limit_bytes=63*2**20+2**19,collective_id=0,has_side_effects=True),name="feed_forward")(att,wo,x,vb,vg,vs,vd,cot,wu,wd,bu)

def finish_kernel(dp,red,dq_h,dk_h,dv_h,normT_h,wh_h,gwo_h,x_h,gm_h,gain,vec,gbu,gathered,heads_out,vec_out,tok,full,fsem,dq,dk,dv,normT,wh,gwo,x,gm,isem,hp,hg,vbuf,vrecv,own,obuf,orecv,tbuf,trecv,vrow,osem,tsem,*rest):
    CH=full.shape[0]; R=full.shape[2]; T,D=x.shape; C=dq.shape[1]; Q=T//2
    plan=big_plan(dp,R); n=len(plan[0][0]); K=len(plan)
    HR=hp.shape[2]; hplan=head_plan(dp,HR); HK=len(hplan); HC=hp.shape[0]
    hrecv=[rest[k*n:(k+1)*n] for k in range(HK)]
    send_sem,recv_sem,chip_send,chip_got,hs_sem,hr_sem,ha_send,ha_recv,vs_sem,vr_sem=rest[HK*n:]
    p=Peers()
    regs=[halves(p,*s) for s in plan]
    hregs=[halves(p,*s,keep_tw=True) for s in hplan]
    def gat(k,s,c,landed):
        other,mine,nr=regs[k][s]
        ref=full.at[c,p.th,rows_at(other if landed else mine,nr),:]
        return send(ref,ref,send_sem.at[k,s,c],recv_sem.at[k,s,c],p.peer(plan[k][0][s]))
    def chip(c,landed):
        ref=full.at[c,1-p.th if landed else p.th]
        return send(ref,ref,chip_send.at[c],chip_got.at[c],p.peer("th"))
    def fput(c): return pltpu.make_async_copy(full.at[c],gathered.at[c],fsem.at[c])
    def hsum(k,s,c):
        order=hplan[k][0]; other,_,nr=hregs[k][s]
        if order[s]=="tw": src=hp.at[c,pl.ds(1,1),rows_at(other,nr),:]
        elif order.index("tw")>s: src=hp.at[c,:,rows_at(other,nr),:]
        else: src=hp.at[c,pl.ds(0,1),rows_at(other,nr),:]
        return send(src,hrecv[k][s].at[c],hs_sem.at[k,s,c],hr_sem.at[k,s,c],p.peer(order[s]))
    def hgat(k,s,c,landed):
        order=hplan[k][0]; other,mine,nr=hregs[k][s]
        ref=hg.at[c,rows_at(other if landed else mine,nr),:]
        return send(ref,ref,ha_send.at[k,s,c],ha_recv.at[k,s,c],p.peer(order[s]))
    backs=[[s for s in reversed(range(n)) if o[s]!="tw"] for o,_,_ in hplan]
    vaxes=["th","tw"]+list(range(n-1))
    def vcopy(i): return send(vbuf.at[i],vrecv.at[i],vs_sem.at[i],vr_sem.at[i],p.peer(vaxes[i]))
    def ocopy(): return send(obuf,orecv,osem.at[0],osem.at[1],p.peer("th"))
    def tcopy(): return send(tbuf.at[rows_at((1-p.tw)*Q,Q),:],trecv,tsem.at[0],tsem.at[1],p.peer("tw"))
    loads=[pltpu.make_async_copy(a,b,isem.at[i]) for i,(a,b) in enumerate(((normT_h,normT),(dq_h,dq),(dk_h,dk),(dv_h,dv),(gwo_h,gwo),(wh_h,wh),(x_h,x),(gm_h,gm)))]
    for l in loads: l.start()
    def arrived(a,b):
        for l in loads[a:b]: l.wait()
    out=0
    for k in range(K):
        _,kr,nr=regs[k][n-1]
        for c in range(CH): full[c,p.th,rows_at(kr,nr),:]=red[c,out:out+nr,:]
        out+=nr
    vbuf[0]=jnp.zeros(vbuf.shape[1:],F32)
    vrow[...]=jnp.zeros(vrow.shape,F32)
    barrier(p,["th"]+plan[0][0])
    last=n+n-1
    def head_step(j,c):
        for k in range(HK):
            order=hplan[k][0]
            if 0<j<=n:
                s=j-1
                hsum(k,s,c).wait_recv()
                _,kr,nr=hregs[k][s]
                q=slice(0,2) if order.index("tw")>s else slice(0,1)
                at=(c,q,rows_at(kr,nr),slice(None))
                new=(hp[at].astype(F32)+hrecv[k][s][c].astype(F32)).astype(BF)
                if j<n: hp[at]=new
                else: hg[c,rows_at(kr,nr),:]=new[0]
            elif j>n: hgat(k,backs[k][j-n-1],c,True).wait_recv()
        for k in range(HK):
            if j<n: hsum(k,j,c).start()
            elif j<last: hgat(k,backs[k][j-n],c,False).start()
        if j==last: heads_out[c]=hg[c]
    def gather_step(j,c):
        if 0<j<=n:
            for k in range(K): gat(k,n-j,c,True).wait_recv()
        if j<n:
            for k in range(K): gat(k,n-1-j,c,False).start()
        elif j==n: chip(c,False).start()
        else:
            chip(c,True).wait_recv()
            fput(c).start()
    HT=D//HC
    def weight_grads(t):
        r=rows_at(t*HT,HT)
        parts=[dot(normT[r,:],d[...],NN).astype(BF) for d in (dq,dk,dv)]+[gwo[r,:]]
        for q in range(2):
            y=jnp.concatenate([z[:,q*(C//2):(q+1)*(C//2)] for z in parts],1)
            for i in range(y.shape[1]//128): hp[t,q,i*HT:(i+1)*HT,:]=y[:,i*128:(i+1)*128]
    def norm_grad(core,t):
        rr=rows_at(core*T+t*TT,TT)
        return dot(dq[rr,:],wh[0],NN)+dot(dk[rr,:],wh[1],NN)+dot(dv[rr,:],wh[2],NN)
    def other_half(t): obuf[rows_at(t*TT,TT),:]=norm_grad(1-p.th,t).astype(BF)
    def own_half(t): own[rows_at(t*TT,TT),:]=norm_grad(p.th,t)
    def norm_one_back(i):
        quarter=(1-i)*(1-p.tw)+i*p.tw
        for t in range(Q//128):
            r=rows_at(quarter*Q+t*128,128)
            e=own[r,:]+orecv[r,:].astype(F32)
            nn,rs=norm_parts(x[r,:].astype(F32))
            tbuf[r,:]=(gm[r,:]+norm_back(e,nn,rs,gain[...].reshape(1,D))).astype(BF)
            vrow[0:1,:]+=colsum(e*nn); vrow[1:2,:]+=colsum(e)
    def vectors(_):
        tok[p.tw]=tbuf[rows_at(p.tw*Q,Q),:]
        rows=[vrow[0:1,:],vrow[1:2,:]]+[vec[i:i+1,:] for i in range(4)]+[gbu[...]]
        at=0
        for v in rows:
            for i in range(v.shape[1]//128):
                vbuf[0,at:at+1,:]=v[:,i*128:(i+1)*128]; at+=1
        for i,d in enumerate((dq,dv)):
            bs=colsum(d[...].astype(F32))
            for q in range(2):
                quarter=2*p.th+(p.tw if q==0 else 1-p.tw)
                y=jnp.concatenate([bs[:,q*(C//2):(q+1)*(C//2)],jnp.zeros((1,256-C//2),F32)],1)
                for z in range(2):
                    vbuf[0,pl.ds(at+quarter*4+i*2+z,1),:]=y[:,z*128:(z+1)*128]
    def vector_step(i,_):
        if i>0:
            vcopy(i-1).wait_recv()
            y=vbuf[i-1]+vrecv[i-1]
            if i<len(vaxes): vbuf[i]=y
            else: vec_out[...]=y
        if i<len(vaxes): vcopy(i).start()
    part=functools.partial
    NT_=T//TT; G1=HC; G2=G1+2*NT_
    steps=[(1+HLAG*j,HSP,HC,part(head_step,j)) for j in reversed(range(last+1))]
    steps+=[(GLAG*j,2,CH,part(gather_step,j)) for j in reversed(range(n+2))]
    steps+=[(G2+3+VLAG*i,1,1,part(vector_step,i)) for i in range(len(vaxes)+1)]
    steps+=[(0,1,1,lambda _: arrived(0,5)),(0,1,HC,weight_grads),(G1,1,1,lambda _: arrived(5,6)),(G2,1,1,lambda _: arrived(6,8)),(G1,1,NT_,other_half),(G1+NT_,1,1,lambda _: ocopy().start()),(G1+NT_,1,NT_,own_half),
            (G2,1,1,lambda _: ocopy().wait_recv()),(G2+1,1,1,lambda _: tcopy().start()),(G2,1,2,norm_one_back),(G2+2,1,1,vectors)]
    run_steps(steps)
    def drain(c,_):
        chip(c,False).wait_send(); fput(c).wait()
        for k in range(K):
            for s in range(n): gat(k,s,c,False).wait_send()
        return 0
    lax.fori_loop(0,CH,drain,0)
    def hdrain(c,_):
        for k in range(HK):
            for s in range(n): hsum(k,s,c).wait_send()
            for s in backs[k]: hgat(k,s,c,False).wait_send()
        return 0
    lax.fori_loop(0,HC,hdrain,0)
    for i in range(len(vaxes)): vcopy(i).wait_send()
    ocopy().wait_send(); tcopy().wait()
    tok[1-p.tw]=trecv[...]

def finish(dp,red,dq,dk,dv,normT,wh,gwo,x,gm,gain,vec,gbu):
    T,D=x.shape; CH,fin,_=red.shape; R=FC//128*D
    plan=big_plan(dp,R); n=len(plan[0][0])
    HC=D//TT; HR=2*dq.shape[1]//128*TT; hplan=head_plan(dp,HR)
    hrecv=[]
    for order,_,rows in hplan:
        q=2
        for axis in order:
            if axis=="tw": q=1
            else: rows//=2
            hrecv.append(pltpu.VMEM((HC,q,rows,128),BF))
    V=(6*D+gbu.shape[1])//128+16; nv=n+1; args=(red,dq,dk,dv,normT,wh,gwo,x,gm,gain,vec,gbu)
    return pl.pallas_call(functools.partial(finish_kernel,dp),
      in_specs=[pl.BlockSpec(memory_space=pl.ANY if 1<=i<=8 else pltpu.VMEM) for i in range(len(args))],
      out_specs=[pl.BlockSpec(memory_space=pl.ANY)]+[pl.BlockSpec(memory_space=pltpu.VMEM)]*3,
      out_shape=[jax.ShapeDtypeStruct((CH,2,R,128),BF),jax.ShapeDtypeStruct((HC,HR,128),BF),jax.ShapeDtypeStruct((V,128),F32),jax.ShapeDtypeStruct((2,T//2,D),BF)],
      scratch_shapes=[pltpu.VMEM((CH,2,R,128),BF),pltpu.SemaphoreType.DMA((CH,))]+[pltpu.VMEM(a.shape,a.dtype) for a in args[1:9]]+[pltpu.SemaphoreType.DMA((8,)),pltpu.VMEM((HC,2,HR,128),BF),pltpu.VMEM((HC,HR,128),BF),pltpu.VMEM((nv,V,128),F32),pltpu.VMEM((nv,V,128),F32),pltpu.VMEM((T,D),F32)]+[pltpu.VMEM((T,D),BF)]*3+[pltpu.VMEM((T//2,D),BF),pltpu.VMEM((8,D),F32)]+[pltpu.SemaphoreType.DMA((2,))]*2+hrecv
        +[pltpu.SemaphoreType.DMA((len(plan),n,CH))]*2+[pltpu.SemaphoreType.DMA((CH,))]*2+[pltpu.SemaphoreType.DMA((len(hplan),n,HC))]*4+[pltpu.SemaphoreType.DMA((nv,))]*2,
      compiler_params=pltpu.CompilerParams(vmem_limit_bytes=60*2**20,collective_id=1,has_side_effects=True),name="finish_gradients")(*args)

def widen_kernel(where,chunk,heads,mine,got,vec,wup,wdown,wqkv,wout,blk,*vectors):
    D=wup.shape[0]; q=wout.shape[0]; g=pl.program_id(0); HT=D//heads.shape[0]
    for i in range(FC//128):
        cols=slice(i*128,(i+1)*128)
        wup[:,cols]=chunk[0,i*D:(i+1)*D,:].astype(F32)
        wdown[cols,:]=chunk[1,i*D:(i+1)*D,:].T.astype(F32)
    @pl.when(g==0)
    def _():
        for t in range(heads.shape[0]):
            y=jnp.concatenate([heads[t,i*HT:(i+1)*HT,:] for i in range(heads.shape[1]//HT)],1).T.astype(F32)
            rr=slice(t*HT,(t+1)*HT)
            for c in range(3): wqkv[c,:,rr]=y[c*q:(c+1)*q,:]
            wout[:,rr]=y[3*q:,:]
        blk[where[0]]=mine[...]; blk[1-where[0]]=got[...]
        at=0
        for v in vectors:
            for i in range(v.shape[0]//128):
                v[i*128:(i+1)*128]=vec[at,:]; at+=1

def widen(tw,chunks,heads,mine,got,vec):
    CH,_,R,_=chunks.shape; D=R*128//FC; FF=CH*FC; q=heads.shape[0]*heads.shape[1]*128//(4*D); T2=mine.shape[0]
    outs=[(D,FF),(FF,D),(3,q,D),(q,D)]; sizes=[D]*6+[FF]
    res=pl.pallas_call(widen_kernel,grid=(CH,),
      in_specs=[pl.BlockSpec(memory_space=pltpu.SMEM),pl.BlockSpec((None,2,R,128),lambda g:(g,0,0,0))]+[pl.BlockSpec(memory_space=pltpu.VMEM)]*4,
      out_specs=[pl.BlockSpec((D,FC),lambda g:(0,g)),pl.BlockSpec((FC,D),lambda g:(g,0))]+[pl.BlockSpec(memory_space=pltpu.VMEM)]*(3+len(sizes)),
      out_shape=[jax.ShapeDtypeStruct(o,F32) for o in outs]+[jax.ShapeDtypeStruct((2,T2,D),BF)]+[jax.ShapeDtypeStruct((z,),F32) for z in sizes],
      compiler_params=pltpu.CompilerParams(vmem_limit_bytes=50*2**20),name="widen")(tw.reshape(1),chunks,heads,mine,got,vec)
    return res[:5],res[5:]

def front_kernel(tok,w,b,gain,shift,seg,x_o,normT_o,q_o,k_o,v_o,wh_o,mq_o,mk_o,x,norm,normT,qkv,wh,wgot,bgot,bias,mq,mk,tsem,bsem,csem,ysem,xsem,zsem,osem):
    p=Peers(); Q,D=tok.shape[1:]; T=2*Q; L=2*T; E=w.shape[1]; PART=E//4
    b0,b1=p.bit(0),p.bit(1)
    barrier(p,["th","tw",0,1])
    def tcopy(): return send(tok.at[1-p.tw],x.at[rows_at(p.tw*Q,Q),:],tsem.at[0],tsem.at[1],p.peer("tw"))
    def bcopy(): return send(b,bgot,bsem.at[0],bsem.at[1],p.peer("tw"))
    def ycopy(c):
        r=rows_at((2*b1+b0)*PART,PART)
        return send(w.at[c,r,:],wgot.at[c,r,:],ysem.at[0,c],ysem.at[1,c],p.peer("tw"))
    def xcopy(c,landed):
        ref=wgot.at[c,rows_at((2*b1+(1-b0 if landed else b0))*PART,PART),:]
        return send(ref,ref,xsem.at[0,c],xsem.at[1,c],p.peer(0))
    def zcopy(c,landed):
        ref=wgot.at[c,rows_at((1-b1 if landed else b1)*2*PART,2*PART),:]
        return send(ref,ref,zsem.at[0,c],zsem.at[1,c],p.peer(1))
    def ccopy(i,landed):
        core=1-p.th if landed else p.th
        quarter=p.tw if i==0 else 1-p.tw
        ref=norm.at[rows_at(core*T+quarter*Q,Q),:]
        return send(ref,ref,csem.at[0,i],csem.at[1,i],p.peer("th"))
    for c in range(3): ycopy(c).start()
    bcopy().start()
    tcopy().start()
    g_row=gain[...].reshape(1,D); s_row=shift[...].reshape(1,D)
    def normalize(src,row):
        for t in range(Q//128):
            y=(norm_parts(src(t).astype(F32))[0]*g_row+s_row).astype(BF)
            norm[rows_at(row+t*128,128),:]=y
    def put(src,dst,i): return pltpu.make_async_copy(src,dst,osem.at[i])
    x[rows_at(p.tw*Q,Q),:]=tok[p.tw]
    normalize(lambda t: tok[p.tw,t*128:(t+1)*128,:],p.th*T+p.tw*Q)
    onehot=lax.broadcasted_iota(jnp.int32,(128,L),0)
    same=onehot==seg[...]
    mk[...]=jnp.where(same,1.0,0.0).T.astype(BF)
    ccopy(0,False).start()
    for c in range(3):
        ycopy(c).wait_recv()
        xcopy(c,False).start()
    mq[...]=jnp.where(same|(onehot>=9),0.0,-float(2**40)).T.astype(BF)
    put(mk,mk_o,0).start(); put(mq,mq_o,1).start()
    bcopy().wait_recv()
    bias[...]=jnp.zeros_like(bias)
    for m,src in enumerate((b,bgot)):
        for i,c in enumerate((0,2)): bias[m,c:c+1,:]=src[i:i+1,:]
    for c in range(3):
        xcopy(c,True).wait_recv()
        zcopy(c,False).start()
    def project(row,weights,m):
        r=rows_at(row,Q)
        def one(c,_):
            y=(dot(norm[r,:],weights[c],NT)+bias[m,pl.ds(c,1),:]).astype(BF)
            y=y*jnp.where(c==0,0.125,1.0).astype(BF)
            qkv[c,r,m*E:(m+1)*E]=y
            return 0
        lax.fori_loop(0,3,one,0)
    def transpose(quarter):
        for core in range(2):
            for t in range(Q//128):
                at=core*T+quarter*Q+t*128
                normT[:,pl.ds(pl.multiple_of(at,128),128)]=norm[rows_at(at,128),:].T
    ccopy(0,True).wait_recv()
    for core in range(2): project(core*T+p.tw*Q,w,0)
    transpose(p.tw)
    for c in range(3): zcopy(c,True).wait_recv()
    for core in range(2): project(core*T+p.tw*Q,wgot,1)
    for c in range(3): wh[c,0:E,:]=w[c]; wh[c,E:2*E,:]=wgot[c]
    put(wh,wh_o,7).start()
    tcopy().wait_recv()
    normalize(lambda t: x[rows_at((1-p.tw)*Q+t*128,128),:],p.th*T+(1-p.tw)*Q)
    put(x,x_o,2).start()
    for m,weights in enumerate((w,wgot)):
        project(p.th*T+(1-p.tw)*Q,weights,m)
        if m==0: ccopy(1,False).start()
    ccopy(1,True).wait_recv()
    for m,weights in enumerate((w,wgot)): project((1-p.th)*T+(1-p.tw)*Q,weights,m)
    for c in range(3): put(qkv.at[c],(q_o,k_o,v_o)[c],4+c).start()
    transpose(1-p.tw)
    put(normT,normT_o,3).start()
    for src,dst,i in ((mk,mk_o,0),(mq,mq_o,1),(x,x_o,2),(normT,normT_o,3),(wh,wh_o,7)): put(src,dst,i).wait()
    for c in range(3):
        put(qkv.at[c],(q_o,k_o,v_o)[c],4+c).wait()
        ycopy(c).wait_send(); xcopy(c,False).wait_send(); zcopy(c,False).wait_send()
    tcopy().wait_send(); bcopy().wait_send()
    for i in range(2): ccopy(i,False).wait_send()

def front(tok,w,b,gain,shift,seg):
    _,Q,D=tok.shape; T=2*Q; L=2*T; E=w.shape[1]
    outs=[((T,D),BF),((D,L),BF)]+[((L,2*E),BF)]*3+[((3,2*E,D),BF)]+[((L,128),BF)]*2
    sem=pltpu.SemaphoreType.DMA
    return pl.pallas_call(front_kernel,
      in_specs=[pl.BlockSpec(memory_space=pltpu.VMEM)]*6,out_specs=[pl.BlockSpec(memory_space=pl.ANY)]*len(outs),
      out_shape=[jax.ShapeDtypeStruct(*o) for o in outs],
      scratch_shapes=[pltpu.VMEM((T,D),BF),pltpu.VMEM((L,D),BF),pltpu.VMEM((D,L),BF),pltpu.VMEM((3,L,2*E),BF),pltpu.VMEM((3,2*E,D),BF),pltpu.VMEM((3,E,D),BF),
        pltpu.VMEM(b.shape,F32),pltpu.VMEM((2,8,E),F32),pltpu.VMEM((L,128),BF),pltpu.VMEM((L,128),BF),sem((2,)),sem((2,)),sem((2,2)),sem((2,3)),sem((2,3)),sem((2,3)),sem((8,))],
      compiler_params=pltpu.CompilerParams(vmem_limit_bytes=60*2**20,collective_id=2,has_side_effects=True),name="front")(tok,w,b,gain,shift,seg)


SWAP = [(0, 1), (1, 0)]


def swap(value, axis):
    return lax.ppermute(value, axis, SWAP)


def in_order(mine, other, index, axis):
    return jnp.where(
        index == 0, jnp.concatenate([mine, other], axis), jnp.concatenate([other, mine], axis)
    )


def own_row(rows, tw):
    mine = lax.dynamic_index_in_dim(rows, tw, 0, keepdims=False)
    other = lax.dynamic_index_in_dim(rows, 1 - tw, 0, keepdims=False)
    return in_order(mine, swap(other, "tw"), tw, 0)


def body(
    dp_size,
    tokens,
    segment_ids,
    norm1_gain,
    norm1_shift,
    w_qkv,
    b_qv,
    w_out,
    b_out,
    norm2_gain,
    norm2_shift,
    w_up,
    b_up,
    w_down,
    b_down,
    cotangent,
):
    th, tw = lax.axis_index("th"), lax.axis_index("tw")
    d = tokens.shape[-1]
    mine = w_qkv.shape[2]
    seg = lax.dynamic_index_in_dim(segment_ids, tw, 0)
    x, normed_t, query, key, value, w_heads, mq, mk = front(
        tokens, w_qkv.transpose(0, 2, 1), b_qv, norm1_gain, norm1_shift, seg
    )
    tables = (mq, mk, *block_ranges(seg[0]))
    later = lax.optimization_barrier((cotangent, w_out, query))
    cot = own_row(later[0], tw)
    w_out_heads = jnp.concatenate([w_out, swap(later[1], "tw")], 0)
    attended, totals = attn_fwd(query, key, value, *tables)
    out_mine, out_other, grad_middle, grad_b_up, sums, red, grad_heads, grad_w_out = ffn(
        dp_size, attended, w_out_heads, x, b_out, norm2_gain, norm2_shift, b_down, cot, w_up, w_down, b_up[None]
    )
    out_got = swap(out_other, "tw")
    dq, dk, dv = attn_bwd(query, key, value, grad_heads, attended, totals, *tables)
    chunks, heads, small, grad_tokens = finish(
        dp_size, red, dq, dk, dv, normed_t, w_heads, grad_w_out, x, grad_middle, norm1_gain, sums, grad_b_up
    )
    (up, down, w_qkv_grad, w_out_grad, block_out), vecs = widen(tw, chunks, heads, out_mine, out_got, small)
    b_qv_grad = lax.dynamic_slice_in_dim(small[-16:].reshape(4, 2, 256), 2 * th + tw, 1, 0)[0, :, :mine]
    return (
        block_out,
        grad_tokens,
        vecs[0],
        vecs[1],
        w_qkv_grad.transpose(0, 2, 1),
        b_qv_grad,
        w_out_grad,
        vecs[2],
        vecs[3],
        vecs[4],
        up,
        vecs[6],
        down,
        vecs[5],
    )


def solution(mesh):
    return jax.shard_map(
        functools.partial(body, mesh.shape["dp"]),
        mesh=mesh,
        in_specs=(
            P("dp", ("th", "tw"), None),
            P("dp", None),
            P(),
            P(),
            P(None, None, ("th", "tw")),
            P(None, ("th", "tw")),
            P(("th", "tw"), None),
            P(),
            P(),
            P(),
            P(),
            P(),
            P(),
            P(),
            P("dp", ("th", "tw"), None),
        ),
        out_specs=(
            P("dp", ("th", "tw"), None),
            P("dp", ("th", "tw"), None),
            P(),
            P(),
            P(None, None, ("th", "tw")),
            P(None, ("th", "tw")),
            P(("th", "tw"), None),
            P(),
            P(),
            P(),
            P(),
            P(),
            P(),
            P(),
        ),
        check_vma=False,
    )
```

```python
import functools

import jax
import jax.numpy as jnp
from jax import lax
from jax.experimental import pallas as pl
from jax.experimental.pallas import tpu as pltpu
from jax.sharding import PartitionSpec as P

NT=(((1,),(1,)),((),())); NN=(((1,),(0,)),((),())); TN=(((0,),(0,)),((),()))
F32=jnp.float32; BF=jnp.bfloat16
BQ=256; BK=256; HD=64
def dot(a,b,d): return lax.dot_general(a,b,d,preferred_element_type=F32)

AL=128; VR=80; GRP=3
def key_rows(lo_ref,mk_ref,i,j):
    L=mk_ref.shape[0]
    want=lo_ref[i]+j*BK
    start=pl.multiple_of(jnp.minimum(want,L-BK),AL)
    row=lax.broadcasted_iota(jnp.int32,(BK,128),0); lane=lax.broadcasted_iota(jnp.int32,(BK,128),1)
    ks=pl.ds(start,BK)
    return ks,jnp.where(((lane==8)|(lane==HD+8))&(row<want-start),jnp.ones((BK,128),BF),mk_ref[ks,:])

def fwd_kernel(lo_ref, n_ref, q_ref, k_ref, v_ref, mq_ref, mk_ref, o_ref, lse_ref, m_ref, acc_ref, vT_ref, qm_ref, *score_refs):
    i=pl.program_id(0); H=q_ref.shape[1]//HD
    lane=lax.broadcasted_iota(jnp.int32,(1,128),1)
    halves=(lane<HD, lane>=HD)
    @pl.when(i==0)
    def _():
        row=lax.broadcasted_iota(jnp.int32,(VR-HD,v_ref.shape[0]),0)
        for p in range(H//2):
            t=v_ref[:,p*128:(p+1)*128].T
            for e in range(2):
                vT_ref[2*p+e,0:HD,:]=t[e*HD:(e+1)*HD,:]
                vT_ref[2*p+e,HD:VR,:]=jnp.where(row==0,1.0,0.0).astype(BF)
    m_ref[...]=jnp.full(m_ref.shape,-1e30,F32)
    acc_ref[...]=jnp.zeros_like(acc_ref)
    for h in range(H): qm_ref[h]=jnp.where(halves[h%2],q_ref[:,h//2*128:h//2*128+128],mq_ref[...])
    def score(h,ks,mk):
        cols=slice(h//2*128,h//2*128+128)
        return dot(jnp.where(halves[h%2],k_ref[ks,cols],mk),qm_ref[h],NT)
    def soft(h,s):
        m_old=m_ref[h:h+1,:]
        m_new=jnp.maximum(m_old,jnp.max(s,axis=0,keepdims=True))
        m_ref[h:h+1,:]=m_new
        return jnp.exp(s-m_new).astype(BF),jnp.exp(m_old-m_new)
    def weigh(h,ks,pe,alpha):
        acc_ref[h]=acc_ref[h]*alpha+dot(vT_ref[h,:,ks],pe,NN)
    n=n_ref[i]
    def half(j,now,then):
        ks,_=key_rows(lo_ref,mk_ref,i,j)
        kn,mk=key_rows(lo_ref,mk_ref,i,j+1)
        last=None
        for h in range(H):
            then[h]=score(h,kn,mk)
            probs=soft(h,now[h])
            if last is not None: weigh(h-1,ks,*last)
            last=probs
        weigh(H-1,ks,*last)
    ks,mk=key_rows(lo_ref,mk_ref,i,0)
    for h in range(H): score_refs[0][h]=score(h,ks,mk)
    def body(t,_):
        half(2*t,*score_refs)
        @pl.when(2*t+1<n)
        def _(): half(2*t+1,*score_refs[::-1])
        return 0
    lax.fori_loop(0,(n+1)//2,body,0)
    for p in range(H//2):
        parts=[acc_ref[h,0:HD,:]*(1.0/acc_ref[h,HD:HD+1,:]) for h in (2*p,2*p+1)]
        o_ref[:,p*128:(p+1)*128]=jnp.concatenate(parts,0).T.astype(BF)
    for h in range(H): lse_ref[h:h+1,:]=m_ref[h:h+1,:]+jnp.log(acc_ref[h,HD:HD+1,:])
    lse_ref[H:,:]=jnp.zeros((lse_ref.shape[0]-H,BQ),F32)

def attn_fwd(q,k,v,mq,mk,lo,n):
    L,C=q.shape
    return pl.pallas_call(fwd_kernel,
        grid_spec=pltpu.PrefetchScalarGridSpec(num_scalar_prefetch=2,grid=(L//BQ,),
          in_specs=[pl.BlockSpec((BQ,C),lambda i,*_:(i,0)),pl.BlockSpec((L,C),lambda i,*_:(0,0)),pl.BlockSpec((L,C),lambda i,*_:(0,0)),
                    pl.BlockSpec((BQ,128),lambda i,*_:(i,0)),pl.BlockSpec((L,128),lambda i,*_:(0,0))],
          out_specs=[pl.BlockSpec((BQ,C),lambda i,*_:(i,0)),pl.BlockSpec((8,BQ),lambda i,*_:(0,i))],
          scratch_shapes=[pltpu.VMEM((8,BQ),F32),pltpu.VMEM((C//HD,VR,BQ),F32),pltpu.VMEM((C//HD,VR,L),BF),pltpu.VMEM((C//HD,BQ,128),BF),pltpu.VMEM((C//HD,BK,BQ),F32),pltpu.VMEM((C//HD,BK,BQ),F32)]),
        out_shape=[jax.ShapeDtypeStruct((L,C),BF),jax.ShapeDtypeStruct((8,L),F32)],
        name="attention_forward",
    )(lo,n,q,k,v,mq,mk)

def bwd_kernel(lo_ref, n_ref, q_ref, k_ref, v_ref, do_ref, o_ref, lse_ref, mq_ref, mk_ref, dq_ref, dk_ref, dv_ref, dk_acc, dv_acc, dq_acc, qcat, docat, qm, kT):
    i=pl.program_id(0); n=pl.num_programs(0)
    C=q_ref.shape[1]; pairs=C//128
    lane=lax.broadcasted_iota(jnp.int32,(1,128),1)
    halves=(lane<HD, lane>=HD)
    @pl.when(i==0)
    def _():
        dk_acc[...]=jnp.zeros_like(dk_acc); dv_acc[...]=jnp.zeros_like(dv_acc)
        kT[...]=k_ref[...].T
    dq_acc[...]=jnp.zeros_like(dq_acc)
    sel=(lax.broadcasted_iota(jnp.int32,(8,C),1)//HD==lax.broadcasted_iota(jnp.int32,(8,C),0)).astype(BF)
    prod=do_ref[...].astype(F32)*o_ref[...].astype(F32)
    high=prod.astype(BF)
    delta=dot(sel,high,NT)+dot(sel,(prod-high.astype(F32)).astype(BF),NT)
    for p in range(pairs):
        cols=slice(p*128,(p+1)*128)
        for e in range(2):
            q2=q_ref[:,cols]; d2=do_ref[:,cols]
            qcat[p,e*BQ:(e+1)*BQ,:]=jnp.where(halves[e],q2,jnp.zeros_like(q2))
            qm[p,e*BQ:(e+1)*BQ,:]=jnp.where(halves[e],q2,mq_ref[...])
            docat[p,e*BQ:(e+1)*BQ,:]=jnp.where(halves[e],d2,jnp.zeros_like(d2))
    lse=lse_ref[...]
    def body(j,_):
        ks,mk=key_rows(lo_ref,mk_ref,i,j)
        for g in range(0,pairs,GRP):
            work=[]
            for p in range(g,g+GRP):
                cols=slice(p*128,(p+1)*128)
                k2=k_ref[ks,cols]; v2=v_ref[ks,cols]; d2=do_ref[:,cols]
                for e in range(2):
                    s=dot(jnp.where(halves[e],k2,mk),qm[p,e*BQ:(e+1)*BQ,:],NT)
                    work.append((s,dot(jnp.where(halves[e],v2,jnp.zeros_like(v2)),d2,NT)))
            out=[]
            for t,(s,dp) in enumerate(work):
                h=2*g+t
                pr=jnp.exp(s-lse[h:h+1,:])
                out.append((pr.astype(BF),(pr*(dp-delta[h:h+1,:])).astype(BF)))
            for p in range(g,g+GRP):
                cols=slice(p*128,(p+1)*128); k2=k_ref[ks,cols]
                (p0,d0),(p1,d1)=out[2*(p-g):2*(p-g)+2]
                dv_acc[ks,cols]+=dot(jnp.concatenate([p0,p1],1),docat[p],NN)
                dk_acc[ks,cols]+=dot(jnp.concatenate([d0,d1],1),qcat[p],NN)
                for e,d in enumerate((d0,d1)):
                    r=slice((2*p+e)*HD,(2*p+e+1)*HD)
                    dq_acc[r,:]+=dot(kT[r,ks],d,NN)
        return 0
    lax.fori_loop(0,n_ref[i],body,0)
    dq_ref[...]=(dq_acc[...]*0.125).T.astype(BF)
    @pl.when(i==n-1)
    def _():
        dk_ref[...]=dk_acc[...].astype(BF); dv_ref[...]=dv_acc[...].astype(BF)

def attn_bwd(q,k,v,do,o,lse,mq,mk,lo,n):
    L,C=q.shape
    blk=pl.BlockSpec((BQ,C),lambda i,*_:(i,0)); full=pl.BlockSpec((L,C),lambda i,*_:(0,0))
    return pl.pallas_call(bwd_kernel,
        grid_spec=pltpu.PrefetchScalarGridSpec(num_scalar_prefetch=2,grid=(L//BQ,),
          in_specs=[blk,full,full,blk,blk,pl.BlockSpec((8,BQ),lambda i,*_:(0,i)),pl.BlockSpec((BQ,128),lambda i,*_:(i,0)),pl.BlockSpec((L,128),lambda i,*_:(0,0))],
          out_specs=[blk,full,full],
          scratch_shapes=[pltpu.VMEM((L,C),F32),pltpu.VMEM((L,C),F32),pltpu.VMEM((C,BQ),F32),pltpu.VMEM((C//128,2*BQ,128),BF),pltpu.VMEM((C//128,2*BQ,128),BF),pltpu.VMEM((C//128,2*BQ,128),BF),pltpu.VMEM((C,L),BF)]),
        out_shape=[jax.ShapeDtypeStruct((L,C),BF)]*3,
        name="attention_backward",
    )(lo,n,q,k,v,do,o,lse,mq,mk)

def block_ranges(seg):
    first=seg[::BQ]; last=seg[BQ-1::BQ]
    lo=jnp.sum(seg[None,:]<first[:,None],axis=1,dtype=jnp.int32)//AL*AL
    hi=jnp.sum(seg[None,:]<=last[:,None],axis=1,dtype=jnp.int32)
    return lo,(hi-lo+BK-1)//BK


TT=256; FC=512
LAG=2; GLAG=5; HLAG=4; HSP=2; GSP=4; VLAG=5; FL=3

def bits_of(dp): return dp.bit_length()-1

def big_plan(dp,rows):
    n=bits_of(dp)
    orders=(["tw"]+list(range(n)),[0,"tw"]+list(range(1,n)),[1,2,0,"tw"]+list(range(3,n)))
    unit=16<<(n+1)
    units=rows//unit
    third=max(1,units//4)
    shares=[units-units//3-third,units//3,third]
    return streams(orders,shares,unit)

def head_plan(dp,rows):
    n=bits_of(dp)
    orders=(["tw"]+list(range(n)),[0,"tw"]+list(range(1,n)),[1,2,0,"tw"]+list(range(3,n)))
    unit=16<<n
    units=rows//unit
    low=max(1,units//6)
    mid=max(1,units//3)
    return streams(orders,[units-mid-low,mid,low],unit)

def streams(orders,shares,unit):
    out=[]; start=0
    for order,share in zip(orders,shares):
        out.append((order,start,share*unit)); start+=share*unit
    return out

class Peers:
    def __init__(self):
        self.dp=lax.axis_index("dp"); self.th=lax.axis_index("th"); self.tw=lax.axis_index("tw")
    def bit(self,axis):
        return self.tw if axis=="tw" else (self.dp//(1<<axis))%2
    def peer(self,axis):
        if axis=="tw": return {"tw":1-self.tw}
        if axis=="th": return {"th":1-self.th}
        return {"dp":self.dp+(1-2*self.bit(axis))*(1<<axis)}

def send(src,dst,ssem,rsem,peer):
    return pltpu.make_async_remote_copy(src,dst,ssem,rsem,device_id=peer,device_id_type=pl.DeviceIdType.MESH)

def barrier(p,axes):
    sem=pltpu.get_barrier_semaphore()
    for a in axes:
        pl.semaphore_signal(sem,inc=1,device_id=p.peer(a),device_id_type=pl.DeviceIdType.MESH)
    pl.semaphore_wait(sem,len(axes))

def halves(p,order,row,rows,keep_tw=False):
    out=[]
    for axis in order:
        if keep_tw and axis=="tw": out.append((row,row,rows)); continue
        rows//=2; bit=p.bit(axis)
        out.append((row+(1-bit)*rows,row+bit*rows,rows)); row=row+bit*rows
    return out
def run_steps(steps):
    total=max(f+sp*(cnt-1) for f,sp,cnt,_ in steps)+1
    def body(i,_):
        for r in range(2):
            g=2*i+r
            for f,sp,cnt,what in steps:
                if sp==2:
                    if f%2!=r: continue
                    c=i-f//2
                else: c=g-f
                if cnt==1:
                    pl.when(c==0)(functools.partial(what,0))
                else: pl.when((c>=0)&(c<cnt))(functools.partial(what,c))
        return 0
    lax.fori_loop(0,(total+1)//2,body,0)
def al(x): return x if isinstance(x,int) else pl.multiple_of(x,16)
def rows_at(row,n): return pl.ds(al(row),n)

EPS=1e-06
def norm_parts(x):
    mean=jnp.mean(x,axis=-1,keepdims=True)
    cen=x-mean
    r=lax.rsqrt(jnp.mean(cen*cen,axis=-1,keepdims=True)+EPS)
    return cen*r,r
def norm_back(e,n,r,gain):
    t=e*gain
    return r*(t-jnp.mean(t,axis=-1,keepdims=True)-n*jnp.mean(t*n,axis=-1,keepdims=True))
def colsum(x): return jnp.sum(x,axis=0,keepdims=True)

def ffn_kernel(dp,att,x,vb,vg,vs,vd,wo_h,wo_got,cot_h,cot_got,wu_h,wd_h,bu,mine,other,gm,gb,vec,red,gheads,gwo,
               wo,cot,lsem,wu,wd,cotT,mid,n2,n2T,obuf,orecv,grow,act,gh,dw,chip_recv,wsem,osem,gsem,*rest):
    CH=dw.shape[0]; T,D=x.shape; SLOTS=chip_recv.shape[0]
    plan=big_plan(dp,dw.shape[2]); n=len(plan[0][0]); K=len(plan)
    recv=[rest[k*n:(k+1)*n] for k in range(K)]
    send_sem,recv_sem,chip_send,chip_got=rest[K*n:]
    p=Peers()
    b_row,g_row,s_row,d_row=[v[...].reshape(1,D) for v in (vb,vg,vs,vd)]
    tiles=[slice(t*TT,(t+1)*TT) for t in range(T//TT)]; NT_=len(tiles)
    regs=[halves(p,*s) for s in plan]
    def copy(k,s,c):
        out,_,nr=regs[k][s]
        return send(dw.at[c,p.th,rows_at(out,nr),:],recv[k][s].at[c],send_sem.at[k,s,c],recv_sem.at[k,s,c],p.peer(plan[k][0][s]))
    def chip_copy(c):
        return send(dw.at[c,1-p.th],chip_recv.at[c%SLOTS],chip_send.at[c],chip_got.at[c],p.peer("th"))
    def ocopy(): return send(obuf,orecv,osem.at[0],osem.at[1],p.peer("th"))
    def gcopy(landed):
        ref=grow.at[rows_at((1-p.th if landed else p.th)*T,T),:]
        return send(ref,ref,gsem.at[0],gsem.at[1],p.peer("th"))
    def wload(c):
        return (pltpu.make_async_copy(wu_h.at[:,pl.ds(pl.multiple_of(c*FC,FC),FC)],wu.at[c],wsem.at[0,c]),
                pltpu.make_async_copy(wd_h.at[pl.ds(pl.multiple_of(c*FC,FC),FC),:],wd.at[c],wsem.at[1,c]))
    E=wo_h.shape[0]; Q=T//2
    loads=[pltpu.make_async_copy(a,b,lsem.at[i]) for i,(a,b) in enumerate(((wo_h,wo.at[0:E,:]),(wo_got,wo.at[E:2*E,:]),
        (cot_h.at[p.tw],cot.at[rows_at(p.tw*Q,Q),:]),(cot_got,cot.at[rows_at((1-p.tw)*Q,Q),:])))]
    for l in loads: l.start()
    def load(c,_):
        for w in wload(c): w.start()
        return 0
    lax.fori_loop(0,CH,load,0)
    barrier(p,["th"]+plan[0][0])
    for l in loads[:2]: l.wait()
    for r in tiles:
        obuf[r,:]=dot(att[rows_at((1-p.th)*T+r.start,TT),:],wo[...],NN).astype(BF)
    for l in loads[2:]: l.wait()
    for t,r in enumerate(tiles):
        mid[r,:]=x[r,:].astype(F32)+dot(att[rows_at(p.th*T+r.start,TT),:],wo[...],NN)+b_row
        if t==0: ocopy().start()
        cotT[:,r]=cot[r,:].T
    ocopy().wait_recv()
    for r in tiles:
        m=mid[r,:]+orecv[r,:].astype(F32)
        mid[r,:]=m
        nn,_=norm_parts(m)
        y=(nn*g_row+s_row).astype(BF)
        n2[r,:]=y; n2T[:,r]=y.T
    vec[...]=jnp.zeros_like(vec)
    def sum_step(s,c):
        news=[]
        for k in range(K):
            copy(k,s,c).wait_recv()
            _,kr,nr=regs[k][s]
            at=(c,p.th,rows_at(kr,nr),slice(None))
            new=(dw[at].astype(F32)+recv[k][s][c].astype(F32)).astype(BF)
            if s<n-1: dw[at]=new
            else: news.append((kr,nr,new))
        if s<n-1:
            for k in range(K): copy(k,s+1,c).start()
        else:
            out=0
            for kr,nr,new in news:
                red[c,out:out+nr,:]=new; out+=nr
    def chip_sum(c):
        chip_copy(c).wait_recv()
        def add(q,_):
            r=rows_at(q*TT,TT)
            dw[c,p.th,r,:]=(dw[c,p.th,r,:].astype(F32)+chip_recv[c%SLOTS,r,:].astype(F32)).astype(BF)
            return 0
        lax.fori_loop(0,dw.shape[2]//TT,add,0)
        for k in range(K): copy(k,0,c).start()
    def hidden(c):
        for w in wload(c): w.wait()
        cols=pl.ds(pl.multiple_of(c*FC,FC),FC)
        gsum=jnp.zeros((1,FC),F32)
        for r in tiles:
            h=dot(n2[r,:],wu[c],NN)+bu[:,cols]
            ga=dot(cot[r,:],wd[c],NT)
            cdf=0.5*(1.0+lax.erf(h*(0.5**0.5)))
            a=(h*cdf).astype(BF)
            gr=(ga*(cdf+h*(jnp.exp(h*h*-0.5)*0.3989422804014327))).astype(BF)
            act[c,r,:]=a; gh[c,r,:]=gr
            gsum+=colsum(gr.astype(F32))
        gb[:,cols]=gsum
    def weight_grads(c):
        for t in range(D//TT):
            r=slice(t*TT,(t+1)*TT)
            for m,(lhs,rhs) in enumerate(((n2T,gh),(cotT,act))):
                y=dot(lhs[r,:],rhs[c],NN).astype(BF)
                for q in range(FC//128): dw[c,m,q*D+t*TT:q*D+(t+1)*TT,:]=y[:,q*128:(q+1)*128]
    def norm_two_back(t):
        r=rows_at(t*TT,TT)
        e=dot(gh[0,r,:],wu[0],NT)
        for c in range(1,CH): e+=dot(gh[c,r,:],wu[c],NT)
        nn,rs=norm_parts(mid[r,:])
        ct=cot[r,:].astype(F32)
        gmid=ct+norm_back(e,nn,rs,g_row)
        gm[r,:]=gmid
        gbr=gmid.astype(BF)
        grow[rows_at(p.th*T+t*TT,TT),:]=gbr
        vec[0:1,:]+=colsum(gbr.astype(F32)); vec[1:2,:]+=colsum(e*nn); vec[2:3,:]+=colsum(e); vec[3:4,:]+=colsum(ct)
    def block_out(t):
        r=rows_at(t*TT,TT)
        y=mid[r,:]+d_row
        for c in range(CH): y+=dot(act[c,r,:],wd[c],NN)
        n2[r,:]=y.astype(BF)
    def split_out(_):
        gcopy(True).wait_recv()
        mine[...]=n2[rows_at(p.tw*(T//2),T//2),:]
        other[...]=n2[rows_at((1-p.tw)*(T//2),T//2),:]
    def grad_heads(u):
        for t in range(NT_):
            r=rows_at(u*T+t*TT,TT)
            gheads[r,:]=dot(grow[r,:],wo[...],NT).astype(BF)
    def grad_wo(_):
        for t in range(D//TT):
            r=slice(t*TT,(t+1)*TT)
            gwo[r,:]=dot(grow[:,r],att[...],TN).astype(BF)
    P2=2*CH; P3=P2+NT_; P4=P3+NT_
    part=functools.partial
    steps=[(3+FL*(s+1),2,CH,part(sum_step,s)) for s in reversed(range(n))]
    steps+=[(3,2,CH,chip_sum),(2,2,CH,lambda c: chip_copy(c).start())]
    steps+=[(0,2,CH,hidden),(1,2,CH,weight_grads),(P2,1,NT_,norm_two_back),(P3,1,1,lambda _: gcopy(False).start()),(P3,1,NT_,block_out),
            (P4,1,1,split_out),(P4,1,2,grad_heads),(P4+2,1,1,grad_wo)]
    run_steps(steps)
    ocopy().wait_send(); gcopy(False).wait_send()
    def drain(c,_):
        chip_copy(c).wait_send()
        for k in range(K):
            for s in range(n): copy(k,s,c).wait_send()
        return 0
    lax.fori_loop(0,CH,drain,0)

def whole(shape):
    return pl.BlockSpec(memory_space=pltpu.VMEM)

def ffn(dp,att,x,vb,vg,vs,vd,wo,wo_got,cot,cot_got,wu,wd,bu):
    T,D=x.shape; FF=wu.shape[1]; CH=FF//FC; R=FC//128*D; C=att.shape[1]
    plan=big_plan(dp,R); n=len(plan[0][0])
    fin=R>>n
    recv=[pltpu.VMEM((CH,rows>>(s+1),128),BF) for _,_,rows in plan for s in range(n)]
    outs=[((T//2,D),BF),((T//2,D),BF),((T,D),F32),((1,FF),F32),((8,D),F32),((CH,fin,128),BF),((2*T,C),BF),((D,C),BF)]
    specs=[whole(o[0]) for o in outs]
    hbm=pl.BlockSpec(memory_space=pl.ANY)
    V=pltpu.VMEM; sem=pltpu.SemaphoreType.DMA
    return pl.pallas_call(functools.partial(ffn_kernel,dp),
      in_specs=[whole(v.shape) for v in (att,x,vb,vg,vs,vd)]+[hbm]*6+[whole(bu.shape)],
      out_specs=specs,out_shape=[jax.ShapeDtypeStruct(*o) for o in outs],
      scratch_shapes=[V((C,D),BF),V((T,D),BF),sem((4,)),V((CH,D,FC),BF),V((CH,FC,D),BF),V((D,T),BF),V((T,D),F32),V((T,D),BF),V((D,T),BF),V((T,D),BF),V((T,D),BF),V((2*T,D),BF),
          V((CH,T,FC),BF),V((CH,T,FC),BF),V((CH,2,R,128),BF),V((3,R,128),BF),sem((2,CH)),sem((2,)),sem((2,))]+recv
        +[sem((len(plan),n,CH))]*2+[sem((CH,))]*2,
      compiler_params=pltpu.CompilerParams(vmem_limit_bytes=63*2**20+2**19,collective_id=0,has_side_effects=True),name="feed_forward")(att,x,vb,vg,vs,vd,wo,wo_got,cot,cot_got,wu,wd,bu)

def finish_kernel(dp,red,dq_h,dk_h,dv_h,normT_h,wh_h,gwo_h,x_h,gm_h,gain,vec,gbu,gathered,heads_out,vec_out,tok,full,fsem,dq,dk,dv,normT,wh,gwo,x,gm,isem,hp,hg,vbuf,vrecv,own,obuf,orecv,tbuf,trecv,vrow,osem,tsem,*rest):
    CH=full.shape[0]; R=full.shape[2]; T,D=x.shape; C=dq.shape[1]; Q=T//2
    plan=big_plan(dp,R); n=len(plan[0][0]); K=len(plan)
    HR=hp.shape[2]; hplan=head_plan(dp,HR); HK=len(hplan); HC=hp.shape[0]
    hrecv=[rest[k*n:(k+1)*n] for k in range(HK)]
    send_sem,recv_sem,chip_send,chip_got,hs_sem,hr_sem,ha_send,ha_recv,vs_sem,vr_sem=rest[HK*n:]
    p=Peers()
    regs=[halves(p,*s) for s in plan]
    hregs=[halves(p,*s,keep_tw=True) for s in hplan]
    def gat(k,s,c,landed):
        other,mine,nr=regs[k][s]
        ref=full.at[c,p.th,rows_at(other if landed else mine,nr),:]
        return send(ref,ref,send_sem.at[k,s,c],recv_sem.at[k,s,c],p.peer(plan[k][0][s]))
    def chip(c,landed):
        ref=full.at[c,1-p.th if landed else p.th]
        return send(ref,ref,chip_send.at[c],chip_got.at[c],p.peer("th"))
    def fput(c): return pltpu.make_async_copy(full.at[c],gathered.at[c],fsem.at[c])
    def hsum(k,s,c):
        order=hplan[k][0]; other,_,nr=hregs[k][s]
        if order[s]=="tw": src=hp.at[c,pl.ds(1,1),rows_at(other,nr),:]
        elif order.index("tw")>s: src=hp.at[c,:,rows_at(other,nr),:]
        else: src=hp.at[c,pl.ds(0,1),rows_at(other,nr),:]
        return send(src,hrecv[k][s].at[c],hs_sem.at[k,s,c],hr_sem.at[k,s,c],p.peer(order[s]))
    def hgat(k,s,c,landed):
        order=hplan[k][0]; other,mine,nr=hregs[k][s]
        ref=hg.at[c,rows_at(other if landed else mine,nr),:]
        return send(ref,ref,ha_send.at[k,s,c],ha_recv.at[k,s,c],p.peer(order[s]))
    backs=[[s for s in reversed(range(n)) if o[s]!="tw"] for o,_,_ in hplan]
    vaxes=["th","tw"]+list(range(n-1))
    def vcopy(i): return send(vbuf.at[i],vrecv.at[i],vs_sem.at[i],vr_sem.at[i],p.peer(vaxes[i]))
    def ocopy(): return send(obuf,orecv,osem.at[0],osem.at[1],p.peer("th"))
    def tcopy(): return send(tbuf.at[rows_at((1-p.tw)*Q,Q),:],trecv,tsem.at[0],tsem.at[1],p.peer("tw"))
    loads=[pltpu.make_async_copy(a,b,isem.at[i]) for i,(a,b) in enumerate(((normT_h,normT),(dq_h,dq),(dk_h,dk),(dv_h,dv),(gwo_h,gwo),(wh_h,wh),(x_h,x),(gm_h,gm)))]
    for l in loads: l.start()
    def arrived(a,b):
        for l in loads[a:b]: l.wait()
    out=0
    for k in range(K):
        _,kr,nr=regs[k][n-1]
        for c in range(CH): full[c,p.th,rows_at(kr,nr),:]=red[c,out:out+nr,:]
        out+=nr
    vbuf[0]=jnp.zeros(vbuf.shape[1:],F32)
    vrow[...]=jnp.zeros(vrow.shape,F32)
    barrier(p,["th"]+plan[0][0])
    last=n+n-1
    def head_step(j,c):
        for k in range(HK):
            order=hplan[k][0]
            if 0<j<=n:
                s=j-1
                hsum(k,s,c).wait_recv()
                _,kr,nr=hregs[k][s]
                q=slice(0,2) if order.index("tw")>s else slice(0,1)
                at=(c,q,rows_at(kr,nr),slice(None))
                new=(hp[at].astype(F32)+hrecv[k][s][c].astype(F32)).astype(BF)
                if j<n: hp[at]=new
                else: hg[c,rows_at(kr,nr),:]=new[0]
            elif j>n: hgat(k,backs[k][j-n-1],c,True).wait_recv()
        for k in range(HK):
            if j<n: hsum(k,j,c).start()
            elif j<last: hgat(k,backs[k][j-n],c,False).start()
        if j==last: heads_out[c]=hg[c]
    def gather_step(j,c):
        if 0<j<=n:
            for k in range(K): gat(k,n-j,c,True).wait_recv()
        if j<n:
            for k in range(K): gat(k,n-1-j,c,False).start()
        elif j==n: chip(c,False).start()
        else:
            chip(c,True).wait_recv()
            fput(c).start()
    HT=D//HC
    def weight_grads(t):
        r=rows_at(t*HT,HT)
        parts=[dot(normT[r,:],d[...],NN).astype(BF) for d in (dq,dk,dv)]+[gwo[r,:]]
        for q in range(2):
            y=jnp.concatenate([z[:,q*(C//2):(q+1)*(C//2)] for z in parts],1)
            for i in range(y.shape[1]//128): hp[t,q,i*HT:(i+1)*HT,:]=y[:,i*128:(i+1)*128]
    def norm_grad(core,t):
        rr=rows_at(core*T+t*TT,TT)
        return dot(dq[rr,:],wh[0],NN)+dot(dk[rr,:],wh[1],NN)+dot(dv[rr,:],wh[2],NN)
    def other_half(t): obuf[rows_at(t*TT,TT),:]=norm_grad(1-p.th,t).astype(BF)
    def own_half(t): own[rows_at(t*TT,TT),:]=norm_grad(p.th,t)
    def norm_one_back(i):
        quarter=(1-i)*(1-p.tw)+i*p.tw
        for t in range(Q//128):
            r=rows_at(quarter*Q+t*128,128)
            e=own[r,:]+orecv[r,:].astype(F32)
            nn,rs=norm_parts(x[r,:].astype(F32))
            tbuf[r,:]=(gm[r,:]+norm_back(e,nn,rs,gain[...].reshape(1,D))).astype(BF)
            vrow[0:1,:]+=colsum(e*nn); vrow[1:2,:]+=colsum(e)
    def vectors(_):
        tok[p.tw]=tbuf[rows_at(p.tw*Q,Q),:]
        rows=[vrow[0:1,:],vrow[1:2,:]]+[vec[i:i+1,:] for i in range(4)]+[gbu[...]]
        at=0
        for v in rows:
            for i in range(v.shape[1]//128):
                vbuf[0,at:at+1,:]=v[:,i*128:(i+1)*128]; at+=1
        for i,d in enumerate((dq,dv)):
            bs=colsum(d[...].astype(F32))
            for q in range(2):
                quarter=2*p.th+(p.tw if q==0 else 1-p.tw)
                y=jnp.concatenate([bs[:,q*(C//2):(q+1)*(C//2)],jnp.zeros((1,256-C//2),F32)],1)
                for z in range(2):
                    vbuf[0,pl.ds(at+quarter*4+i*2+z,1),:]=y[:,z*128:(z+1)*128]
    def vector_step(i,_):
        if i>0:
            vcopy(i-1).wait_recv()
            y=vbuf[i-1]+vrecv[i-1]
            if i<len(vaxes): vbuf[i]=y
            else: vec_out[...]=y
        if i<len(vaxes): vcopy(i).start()
    part=functools.partial
    NT_=T//TT; G1=HC; G2=G1+2*NT_
    steps=[(1+HLAG*j,HSP,HC,part(head_step,j)) for j in reversed(range(last+1))]
    steps+=[(GLAG*j,2,CH,part(gather_step,j)) for j in reversed(range(n+2))]
    steps+=[(G2+3+VLAG*i,1,1,part(vector_step,i)) for i in range(len(vaxes)+1)]
    steps+=[(0,1,1,lambda _: arrived(0,5)),(0,1,HC,weight_grads),(G1,1,1,lambda _: arrived(5,6)),(G2,1,1,lambda _: arrived(6,8)),(G1,1,NT_,other_half),(G1+NT_,1,1,lambda _: ocopy().start()),(G1+NT_,1,NT_,own_half),
            (G2,1,1,lambda _: ocopy().wait_recv()),(G2+1,1,1,lambda _: tcopy().start()),(G2,1,2,norm_one_back),(G2+2,1,1,vectors)]
    run_steps(steps)
    def drain(c,_):
        chip(c,False).wait_send(); fput(c).wait()
        for k in range(K):
            for s in range(n): gat(k,s,c,False).wait_send()
        return 0
    lax.fori_loop(0,CH,drain,0)
    def hdrain(c,_):
        for k in range(HK):
            for s in range(n): hsum(k,s,c).wait_send()
            for s in backs[k]: hgat(k,s,c,False).wait_send()
        return 0
    lax.fori_loop(0,HC,hdrain,0)
    for i in range(len(vaxes)): vcopy(i).wait_send()
    ocopy().wait_send(); tcopy().wait()
    tok[1-p.tw]=trecv[...]

def finish(dp,red,dq,dk,dv,normT,wh,gwo,x,gm,gain,vec,gbu):
    T,D=x.shape; CH,fin,_=red.shape; R=FC//128*D
    plan=big_plan(dp,R); n=len(plan[0][0])
    HC=D//TT; HR=2*dq.shape[1]//128*TT; hplan=head_plan(dp,HR)
    hrecv=[]
    for order,_,rows in hplan:
        q=2
        for axis in order:
            if axis=="tw": q=1
            else: rows//=2
            hrecv.append(pltpu.VMEM((HC,q,rows,128),BF))
    V=(6*D+gbu.shape[1])//128+16; nv=n+1; args=(red,dq,dk,dv,normT,wh,gwo,x,gm,gain,vec,gbu)
    return pl.pallas_call(functools.partial(finish_kernel,dp),
      in_specs=[pl.BlockSpec(memory_space=pl.ANY if 1<=i<=8 else pltpu.VMEM) for i in range(len(args))],
      out_specs=[pl.BlockSpec(memory_space=pl.ANY)]+[pl.BlockSpec(memory_space=pltpu.VMEM)]*3,
      out_shape=[jax.ShapeDtypeStruct((CH,2,R,128),BF),jax.ShapeDtypeStruct((HC,HR,128),BF),jax.ShapeDtypeStruct((V,128),F32),jax.ShapeDtypeStruct((2,T//2,D),BF)],
      scratch_shapes=[pltpu.VMEM((CH,2,R,128),BF),pltpu.SemaphoreType.DMA((CH,))]+[pltpu.VMEM(a.shape,a.dtype) for a in args[1:9]]+[pltpu.SemaphoreType.DMA((8,)),pltpu.VMEM((HC,2,HR,128),BF),pltpu.VMEM((HC,HR,128),BF),pltpu.VMEM((nv,V,128),F32),pltpu.VMEM((nv,V,128),F32),pltpu.VMEM((T,D),F32)]+[pltpu.VMEM((T,D),BF)]*3+[pltpu.VMEM((T//2,D),BF),pltpu.VMEM((8,D),F32)]+[pltpu.SemaphoreType.DMA((2,))]*2+hrecv
        +[pltpu.SemaphoreType.DMA((len(plan),n,CH))]*2+[pltpu.SemaphoreType.DMA((CH,))]*2+[pltpu.SemaphoreType.DMA((len(hplan),n,HC))]*4+[pltpu.SemaphoreType.DMA((nv,))]*2,
      compiler_params=pltpu.CompilerParams(vmem_limit_bytes=60*2**20,collective_id=1,has_side_effects=True),name="finish_gradients")(*args)

def widen_kernel(where,chunk,heads,mine,got,vec,tok,wup,wdown,wqkv,wout,blk,tok_o,bqv,*vectors):
    D=wup.shape[0]; q=wout.shape[0]; g=pl.program_id(0); HT=D//heads.shape[0]
    for i in range(FC//128):
        cols=slice(i*128,(i+1)*128)
        wup[:,cols]=chunk[0,i*D:(i+1)*D,:].astype(F32)
        wdown[cols,:]=chunk[1,i*D:(i+1)*D,:].T.astype(F32)
    @pl.when(g==0)
    def _():
        for t in range(heads.shape[0]):
            y=jnp.concatenate([heads[t,i*HT:(i+1)*HT,:] for i in range(heads.shape[1]//HT)],1).T.astype(F32)
            rr=slice(t*HT,(t+1)*HT)
            for c in range(3): wqkv[c,:,rr]=y[c*q:(c+1)*q,:]
            wout[:,rr]=y[3*q:,:]
        blk[where[0]]=mine[...]; blk[1-where[0]]=got[...]
        tok_o[...]=tok[...]
        at=sum(v.shape[0] for v in vectors)//128
        for i in range(2):
            for z,w in ((0,128),(1,q-128)): bqv[i:i+1,z*128:z*128+w]=vec[pl.ds(at+4*where[1]+2*i+z,1),0:w]
        at=0
        for v in vectors:
            for i in range(v.shape[0]//128):
                v[i*128:(i+1)*128]=vec[at,:]; at+=1

def widen(where,chunks,heads,mine,got,vec,tok):
    CH,_,R,_=chunks.shape; D=R*128//FC; FF=CH*FC; q=heads.shape[0]*heads.shape[1]*128//(4*D); T2=mine.shape[0]
    outs=[(D,FF),(FF,D),(3,q,D),(q,D)]; sizes=[D]*6+[FF]
    res=pl.pallas_call(widen_kernel,grid=(CH,),
      in_specs=[pl.BlockSpec(memory_space=pltpu.SMEM),pl.BlockSpec((None,2,R,128),lambda g:(g,0,0,0))]+[pl.BlockSpec(memory_space=pltpu.VMEM)]*5,
      out_specs=[pl.BlockSpec((D,FC),lambda g:(0,g)),pl.BlockSpec((FC,D),lambda g:(g,0))]+[pl.BlockSpec(memory_space=pltpu.VMEM)]*(5+len(sizes)),
      out_shape=[jax.ShapeDtypeStruct(o,F32) for o in outs]+[jax.ShapeDtypeStruct((2,T2,D),BF)]*2+[jax.ShapeDtypeStruct((2,q),F32)]+[jax.ShapeDtypeStruct((z,),F32) for z in sizes],
      compiler_params=pltpu.CompilerParams(vmem_limit_bytes=50*2**20),name="widen")(where,chunks,heads,mine,got,vec,tok)
    return res[:7],res[7:]

def front_kernel(tok,w,b,gain,shift,seg,x_o,normT_o,q_o,k_o,v_o,wh_o,mq_o,mk_o,x,norm,normT,qkv,wh,wgot,bgot,bias,mq,mk,tsem,bsem,csem,ysem,xsem,zsem,osem):
    p=Peers(); Q,D=tok.shape[1:]; T=2*Q; L=2*T; E=w.shape[1]; PART=E//4
    b0,b1=p.bit(0),p.bit(1)
    barrier(p,["th","tw",0,1])
    def tcopy(): return send(tok.at[1-p.tw],x.at[rows_at(p.tw*Q,Q),:],tsem.at[0],tsem.at[1],p.peer("tw"))
    def bcopy(): return send(b,bgot,bsem.at[0],bsem.at[1],p.peer("tw"))
    def ycopy(c):
        r=rows_at((2*b1+b0)*PART,PART)
        return send(w.at[c,r,:],wgot.at[c,r,:],ysem.at[0,c],ysem.at[1,c],p.peer("tw"))
    def xcopy(c,landed):
        ref=wgot.at[c,rows_at((2*b1+(1-b0 if landed else b0))*PART,PART),:]
        return send(ref,ref,xsem.at[0,c],xsem.at[1,c],p.peer(0))
    def zcopy(c,landed):
        ref=wgot.at[c,rows_at((1-b1 if landed else b1)*2*PART,2*PART),:]
        return send(ref,ref,zsem.at[0,c],zsem.at[1,c],p.peer(1))
    def ccopy(i,landed):
        core=1-p.th if landed else p.th
        quarter=p.tw if i==0 else 1-p.tw
        ref=norm.at[rows_at(core*T+quarter*Q,Q),:]
        return send(ref,ref,csem.at[0,i],csem.at[1,i],p.peer("th"))
    for c in range(3): ycopy(c).start()
    bcopy().start()
    tcopy().start()
    g_row=gain[...].reshape(1,D); s_row=shift[...].reshape(1,D)
    def normalize(src,row):
        for t in range(Q//128):
            y=(norm_parts(src(t).astype(F32))[0]*g_row+s_row).astype(BF)
            norm[rows_at(row+t*128,128),:]=y
    def put(src,dst,i): return pltpu.make_async_copy(src,dst,osem.at[i])
    x[rows_at(p.tw*Q,Q),:]=tok[p.tw]
    normalize(lambda t: tok[p.tw,t*128:(t+1)*128,:],p.th*T+p.tw*Q)
    onehot=lax.broadcasted_iota(jnp.int32,(128,L),0)
    onehot=jnp.where(onehot<HD,onehot,onehot-HD)
    same=onehot==seg[pl.ds(p.tw,1),:]
    mk[...]=jnp.where(same,1.0,0.0).T.astype(BF)
    ccopy(0,False).start()
    for c in range(3):
        ycopy(c).wait_recv()
        xcopy(c,False).start()
    mq[...]=jnp.where(same|(onehot>=9),0.0,-float(2**40)).T.astype(BF)
    put(mk,mk_o,0).start(); put(mq,mq_o,1).start()
    bcopy().wait_recv()
    bias[...]=jnp.zeros_like(bias)
    for m,src in enumerate((b,bgot)):
        for i,c in enumerate((0,2)): bias[m,c:c+1,:]=src[i:i+1,:]
    for c in range(3):
        xcopy(c,True).wait_recv()
        zcopy(c,False).start()
    def project(row,weights,m):
        r=rows_at(row,Q)
        def one(c,_):
            y=(dot(norm[r,:],weights[c],NT)+bias[m,pl.ds(c,1),:]).astype(BF)
            y=y*jnp.where(c==0,0.125,1.0).astype(BF)
            qkv[c,r,m*E:(m+1)*E]=y
            return 0
        lax.fori_loop(0,3,one,0)
    def transpose(quarter):
        for core in range(2):
            for t in range(Q//128):
                at=core*T+quarter*Q+t*128
                normT[:,pl.ds(pl.multiple_of(at,128),128)]=norm[rows_at(at,128),:].T
    ccopy(0,True).wait_recv()
    for core in range(2): project(core*T+p.tw*Q,w,0)
    transpose(p.tw)
    for c in range(3): zcopy(c,True).wait_recv()
    for core in range(2): project(core*T+p.tw*Q,wgot,1)
    for c in range(3): wh[c,0:E,:]=w[c]; wh[c,E:2*E,:]=wgot[c]
    put(wh,wh_o,7).start()
    tcopy().wait_recv()
    normalize(lambda t: x[rows_at((1-p.tw)*Q+t*128,128),:],p.th*T+(1-p.tw)*Q)
    put(x,x_o,2).start()
    for m,weights in enumerate((w,wgot)):
        project(p.th*T+(1-p.tw)*Q,weights,m)
        if m==0: ccopy(1,False).start()
    ccopy(1,True).wait_recv()
    for m,weights in enumerate((w,wgot)): project((1-p.th)*T+(1-p.tw)*Q,weights,m)
    for c in range(3): put(qkv.at[c],(q_o,k_o,v_o)[c],4+c).start()
    transpose(1-p.tw)
    put(normT,normT_o,3).start()
    for src,dst,i in ((mk,mk_o,0),(mq,mq_o,1),(x,x_o,2),(normT,normT_o,3),(wh,wh_o,7)): put(src,dst,i).wait()
    for c in range(3):
        put(qkv.at[c],(q_o,k_o,v_o)[c],4+c).wait()
        ycopy(c).wait_send(); xcopy(c,False).wait_send(); zcopy(c,False).wait_send()
    tcopy().wait_send(); bcopy().wait_send()
    for i in range(2): ccopy(i,False).wait_send()

def front(tok,w,b,gain,shift,seg):
    _,Q,D=tok.shape; T=2*Q; L=2*T; E=w.shape[1]
    outs=[((T,D),BF),((D,L),BF)]+[((L,2*E),BF)]*3+[((3,2*E,D),BF)]+[((L,128),BF)]*2
    sem=pltpu.SemaphoreType.DMA
    return pl.pallas_call(front_kernel,
      in_specs=[pl.BlockSpec(memory_space=pltpu.VMEM)]*6,out_specs=[pl.BlockSpec(memory_space=pl.ANY)]*len(outs),
      out_shape=[jax.ShapeDtypeStruct(*o) for o in outs],
      scratch_shapes=[pltpu.VMEM((T,D),BF),pltpu.VMEM((L,D),BF),pltpu.VMEM((D,L),BF),pltpu.VMEM((3,L,2*E),BF),pltpu.VMEM((3,2*E,D),BF),pltpu.VMEM((3,E,D),BF),
        pltpu.VMEM(b.shape,F32),pltpu.VMEM((2,8,E),F32),pltpu.VMEM((L,128),BF),pltpu.VMEM((L,128),BF),sem((2,)),sem((2,)),sem((2,2)),sem((2,3)),sem((2,3)),sem((2,3)),sem((8,))],
      compiler_params=pltpu.CompilerParams(vmem_limit_bytes=60*2**20,collective_id=2,has_side_effects=True),name="front")(tok,w,b,gain,shift,seg)


SWAP = [(0, 1), (1, 0)]


def swap(value, axis):
    return lax.ppermute(value, axis, SWAP)


def body(
    dp_size,
    tokens,
    segment_ids,
    norm1_gain,
    norm1_shift,
    w_qkv,
    b_qv,
    w_out,
    b_out,
    norm2_gain,
    norm2_shift,
    w_up,
    b_up,
    w_down,
    b_down,
    cotangent,
):
    th, tw = lax.axis_index("th"), lax.axis_index("tw")
    x, normed_t, query, key, value, w_heads, mq, mk = front(
        tokens, w_qkv.transpose(0, 2, 1), b_qv, norm1_gain, norm1_shift, segment_ids
    )
    tables = (mq, mk, *block_ranges(lax.dynamic_index_in_dim(segment_ids, tw, 0, False)))
    later = lax.optimization_barrier((cotangent, w_out, query))
    cot_got = swap(lax.dynamic_index_in_dim(later[0], 1 - tw, 0, False), "tw")
    w_out_got = swap(later[1], "tw")
    attended, totals = attn_fwd(query, key, value, *tables)
    out_mine, out_other, grad_middle, grad_b_up, sums, red, grad_heads, grad_w_out = ffn(
        dp_size, attended, x, b_out, norm2_gain, norm2_shift, b_down, w_out, w_out_got, cotangent, cot_got, w_up, w_down, b_up[None]
    )
    out_got = swap(out_other, "tw")
    dq, dk, dv = attn_bwd(query, key, value, grad_heads, attended, totals, *tables)
    chunks, heads, small, grad_tokens = finish(
        dp_size, red, dq, dk, dv, normed_t, w_heads, grad_w_out, x, grad_middle, norm1_gain, sums, grad_b_up
    )
    where = jnp.stack([tw, 2 * th + tw]).astype(jnp.int32)
    (up, down, w_qkv_grad, w_out_grad, block_out, grad_tokens, b_qv_grad), vecs = widen(
        where, chunks, heads, out_mine, out_got, small, grad_tokens
    )
    return (
        block_out,
        grad_tokens,
        vecs[0],
        vecs[1],
        w_qkv_grad.transpose(0, 2, 1),
        b_qv_grad,
        w_out_grad,
        vecs[2],
        vecs[3],
        vecs[4],
        up,
        vecs[6],
        down,
        vecs[5],
    )


def solution(mesh):
    return jax.shard_map(
        functools.partial(body, mesh.shape["dp"]),
        mesh=mesh,
        in_specs=(
            P("dp", ("th", "tw"), None),
            P("dp", None),
            P(),
            P(),
            P(None, None, ("th", "tw")),
            P(None, ("th", "tw")),
            P(("th", "tw"), None),
            P(),
            P(),
            P(),
            P(),
            P(),
            P(),
            P(),
            P("dp", ("th", "tw"), None),
        ),
        out_specs=(
            P("dp", ("th", "tw"), None),
            P("dp", ("th", "tw"), None),
            P(),
            P(),
            P(None, None, ("th", "tw")),
            P(None, ("th", "tw")),
            P(("th", "tw"), None),
            P(),
            P(),
            P(),
            P(),
            P(),
            P(),
            P(),
        ),
        check_vma=False,
    )
```

```python
import functools

import jax
import jax.numpy as jnp
from jax import lax
from jax.experimental import pallas as pl
from jax.experimental.pallas import tpu as pltpu
from jax.sharding import PartitionSpec as P

NT=(((1,),(1,)),((),())); NN=(((1,),(0,)),((),())); TN=(((0,),(0,)),((),()))
F32=jnp.float32; BF=jnp.bfloat16
BQ=256; BK=256; HD=64
def dot(a,b,d): return lax.dot_general(a,b,d,preferred_element_type=F32)

AL=128; VR=80; GRP=3
def each_chunk(lo_ref,n_ref,i,body):
    lo=lo_ref[i]; n=n_ref[i]
    def full(j,_):
        body(pl.ds(pl.multiple_of(lo+j*BK,AL),BK))
        return 0
    lax.fori_loop(0,n//2,full,0)
    @pl.when(n%2==1)
    def _(): body(pl.ds(pl.multiple_of(lo+n//2*BK,AL),AL))

def fwd_kernel(lo_ref, n_ref, q_ref, k_ref, v_ref, mq_ref, mk_ref, o_ref, lse_ref, m_ref, acc_ref, vT_ref, qm_ref):
    i=pl.program_id(0); H=q_ref.shape[1]//HD
    lane=lax.broadcasted_iota(jnp.int32,(1,128),1)
    halves=(lane<HD, lane>=HD)
    @pl.when(i==0)
    def _():
        row=lax.broadcasted_iota(jnp.int32,(VR-HD,v_ref.shape[0]),0)
        for p in range(H//2):
            t=v_ref[:,p*128:(p+1)*128].T
            for e in range(2):
                vT_ref[2*p+e,0:HD,:]=t[e*HD:(e+1)*HD,:]
                vT_ref[2*p+e,HD:VR,:]=jnp.where(row==0,1.0,0.0).astype(BF)
    m_ref[...]=jnp.full(m_ref.shape,-1e30,F32)
    acc_ref[...]=jnp.zeros_like(acc_ref)
    for h in range(H): qm_ref[h]=jnp.where(halves[h%2],q_ref[:,h//2*128:h//2*128+128],mq_ref[...])
    def score(h,ks,mk):
        cols=slice(h//2*128,h//2*128+128)
        return dot(jnp.where(halves[h%2],k_ref[ks,cols],mk),qm_ref[h],NT)
    def soft(h,s):
        m_old=m_ref[h:h+1,:]
        m_new=jnp.maximum(m_old,jnp.max(s,axis=0,keepdims=True))
        m_ref[h:h+1,:]=m_new
        return jnp.exp(s-m_new).astype(BF),jnp.exp(m_old-m_new)
    def weigh(h,ks,pe,alpha):
        acc_ref[h]=acc_ref[h]*alpha+dot(vT_ref[h,:,ks],pe,NN)
    def body(ks):
        mk=mk_ref[ks,:]
        scores=[score(h,ks,mk) for h in range(H)]
        probs=[soft(h,scores[h]) for h in range(H)]
        for h in range(H): weigh(h,ks,*probs[h])
    each_chunk(lo_ref,n_ref,i,body)
    for p in range(H//2):
        parts=[acc_ref[h,0:HD,:]*(1.0/acc_ref[h,HD:HD+1,:]) for h in (2*p,2*p+1)]
        o_ref[:,p*128:(p+1)*128]=jnp.concatenate(parts,0).T.astype(BF)
    for h in range(H): lse_ref[h:h+1,:]=m_ref[h:h+1,:]+jnp.log(acc_ref[h,HD:HD+1,:])
    lse_ref[H:,:]=jnp.zeros((lse_ref.shape[0]-H,BQ),F32)

def attn_fwd(q,k,v,mq,mk,lo,n):
    L,C=q.shape
    return pl.pallas_call(fwd_kernel,
        grid_spec=pltpu.PrefetchScalarGridSpec(num_scalar_prefetch=2,grid=(L//BQ,),
          in_specs=[pl.BlockSpec((BQ,C),lambda i,*_:(i,0)),pl.BlockSpec((L,C),lambda i,*_:(0,0)),pl.BlockSpec((L,C),lambda i,*_:(0,0)),
                    pl.BlockSpec((BQ,128),lambda i,*_:(i,0)),pl.BlockSpec((L,128),lambda i,*_:(0,0))],
          out_specs=[pl.BlockSpec((BQ,C),lambda i,*_:(i,0)),pl.BlockSpec((8,BQ),lambda i,*_:(0,i))],
          scratch_shapes=[pltpu.VMEM((8,BQ),F32),pltpu.VMEM((C//HD,VR,BQ),F32),pltpu.VMEM((C//HD,VR,L),BF),pltpu.VMEM((C//HD,BQ,128),BF)]),
        out_shape=[jax.ShapeDtypeStruct((L,C),BF),jax.ShapeDtypeStruct((8,L),F32)],
        name="attention_forward",
    )(lo,n,q,k,v,mq,mk)

def bwd_kernel(lo_ref, n_ref, q_ref, k_ref, v_ref, do_ref, o_ref, lse_ref, mq_ref, mk_ref, dq_ref, dk_ref, dv_ref, dk_acc, dv_acc, dq_acc, qcat, docat, qm, kT):
    i=pl.program_id(0); n=pl.num_programs(0)
    C=q_ref.shape[1]; pairs=C//128
    lane=lax.broadcasted_iota(jnp.int32,(1,128),1)
    halves=(lane<HD, lane>=HD)
    @pl.when(i==0)
    def _():
        dk_acc[...]=jnp.zeros_like(dk_acc); dv_acc[...]=jnp.zeros_like(dv_acc)
        kT[...]=k_ref[...].T
    dq_acc[...]=jnp.zeros_like(dq_acc)
    sel=(lax.broadcasted_iota(jnp.int32,(8,C),1)//HD==lax.broadcasted_iota(jnp.int32,(8,C),0)).astype(BF)
    prod=do_ref[...].astype(F32)*o_ref[...].astype(F32)
    high=prod.astype(BF)
    delta=dot(sel,high,NT)+dot(sel,(prod-high.astype(F32)).astype(BF),NT)
    for p in range(pairs):
        cols=slice(p*128,(p+1)*128)
        for e in range(2):
            q2=q_ref[:,cols]; d2=do_ref[:,cols]
            qcat[p,e*BQ:(e+1)*BQ,:]=jnp.where(halves[e],q2,jnp.zeros_like(q2))
            qm[p,e*BQ:(e+1)*BQ,:]=jnp.where(halves[e],q2,mq_ref[...])
            docat[p,e*BQ:(e+1)*BQ,:]=jnp.where(halves[e],d2,jnp.zeros_like(d2))
    lse=lse_ref[...]
    def body(ks):
        mk=mk_ref[ks,:]
        for g in range(0,pairs,GRP):
            work=[]
            for p in range(g,g+GRP):
                cols=slice(p*128,(p+1)*128)
                k2=k_ref[ks,cols]; v2=v_ref[ks,cols]; d2=do_ref[:,cols]
                for e in range(2):
                    s=dot(jnp.where(halves[e],k2,mk),qm[p,e*BQ:(e+1)*BQ,:],NT)
                    work.append((s,dot(jnp.where(halves[e],v2,jnp.zeros_like(v2)),d2,NT)))
            out=[]
            for t,(s,dp) in enumerate(work):
                h=2*g+t
                pr=jnp.exp(s-lse[h:h+1,:])
                out.append((pr.astype(BF),(pr*(dp-delta[h:h+1,:])).astype(BF)))
            for p in range(g,g+GRP):
                cols=slice(p*128,(p+1)*128); k2=k_ref[ks,cols]
                (p0,d0),(p1,d1)=out[2*(p-g):2*(p-g)+2]
                dv_acc[ks,cols]+=dot(jnp.concatenate([p0,p1],1),docat[p],NN)
                dk_acc[ks,cols]+=dot(jnp.concatenate([d0,d1],1),qcat[p],NN)
                for e,d in enumerate((d0,d1)):
                    r=slice((2*p+e)*HD,(2*p+e+1)*HD)
                    dq_acc[r,:]+=dot(kT[r,ks],d,NN)
    each_chunk(lo_ref,n_ref,i,body)
    dq_ref[...]=(dq_acc[...]*0.125).T.astype(BF)
    @pl.when(i==n-1)
    def _():
        dk_ref[...]=dk_acc[...].astype(BF); dv_ref[...]=dv_acc[...].astype(BF)

def attn_bwd(q,k,v,do,o,lse,mq,mk,lo,n):
    L,C=q.shape
    blk=pl.BlockSpec((BQ,C),lambda i,*_:(i,0)); full=pl.BlockSpec((L,C),lambda i,*_:(0,0))
    return pl.pallas_call(bwd_kernel,
        grid_spec=pltpu.PrefetchScalarGridSpec(num_scalar_prefetch=2,grid=(L//BQ,),
          in_specs=[blk,full,full,blk,blk,pl.BlockSpec((8,BQ),lambda i,*_:(0,i)),pl.BlockSpec((BQ,128),lambda i,*_:(i,0)),pl.BlockSpec((L,128),lambda i,*_:(0,0))],
          out_specs=[blk,full,full],
          scratch_shapes=[pltpu.VMEM((L,C),F32),pltpu.VMEM((L,C),F32),pltpu.VMEM((C,BQ),F32),pltpu.VMEM((C//128,2*BQ,128),BF),pltpu.VMEM((C//128,2*BQ,128),BF),pltpu.VMEM((C//128,2*BQ,128),BF),pltpu.VMEM((C,L),BF)]),
        out_shape=[jax.ShapeDtypeStruct((L,C),BF)]*3,
        name="attention_backward",
    )(lo,n,q,k,v,do,o,lse,mq,mk)

def block_ranges(seg):
    first=seg[::BQ]; last=seg[BQ-1::BQ]
    lo=jnp.sum(seg[None,:]<first[:,None],axis=1,dtype=jnp.int32)//AL*AL
    hi=jnp.sum(seg[None,:]<=last[:,None],axis=1,dtype=jnp.int32)
    return lo,(hi-lo+AL-1)//AL


TT=256; FC=512
LAG=2; GLAG=5; HLAG=4; HSP=2; GSP=4; VLAG=5; FL=3

def bits_of(dp): return dp.bit_length()-1

def big_plan(dp,rows):
    n=bits_of(dp)
    orders=(["tw"]+list(range(n)),[0,"tw"]+list(range(1,n)),[1,2,0,"tw"]+list(range(3,n)))
    unit=16<<(n+1)
    units=rows//unit
    third=max(1,units//4)
    shares=[units-units//3-third,units//3,third]
    return streams(orders,shares,unit)

def head_plan(dp,rows):
    n=bits_of(dp)
    orders=(["tw"]+list(range(n)),[0,"tw"]+list(range(1,n)),[1,2,0,"tw"]+list(range(3,n)))
    unit=16<<n
    units=rows//unit
    low=max(1,units//6)
    mid=max(1,units//3)
    return streams(orders,[units-mid-low,mid,low],unit)

def streams(orders,shares,unit):
    out=[]; start=0
    for order,share in zip(orders,shares):
        out.append((order,start,share*unit)); start+=share*unit
    return out

class Peers:
    def __init__(self):
        self.dp=lax.axis_index("dp"); self.th=lax.axis_index("th"); self.tw=lax.axis_index("tw")
    def bit(self,axis):
        return self.tw if axis=="tw" else (self.dp//(1<<axis))%2
    def peer(self,axis):
        if axis=="tw": return {"tw":1-self.tw}
        if axis=="th": return {"th":1-self.th}
        return {"dp":self.dp+(1-2*self.bit(axis))*(1<<axis)}

def send(src,dst,ssem,rsem,peer):
    return pltpu.make_async_remote_copy(src,dst,ssem,rsem,device_id=peer,device_id_type=pl.DeviceIdType.MESH)

def barrier(p,axes):
    sem=pltpu.get_barrier_semaphore()
    for a in axes:
        pl.semaphore_signal(sem,inc=1,device_id=p.peer(a),device_id_type=pl.DeviceIdType.MESH)
    pl.semaphore_wait(sem,len(axes))

def halves(p,order,row,rows,keep_tw=False):
    out=[]
    for axis in order:
        if keep_tw and axis=="tw": out.append((row,row,rows)); continue
        rows//=2; bit=p.bit(axis)
        out.append((row+(1-bit)*rows,row+bit*rows,rows)); row=row+bit*rows
    return out
def run_steps(steps):
    total=max(f+sp*(cnt-1) for f,sp,cnt,_ in steps)+1
    def body(i,_):
        for r in range(2):
            g=2*i+r
            for f,sp,cnt,what in steps:
                if sp==2:
                    if f%2!=r: continue
                    c=i-f//2
                else: c=g-f
                if cnt==1:
                    pl.when(c==0)(functools.partial(what,0))
                else: pl.when((c>=0)&(c<cnt))(functools.partial(what,c))
        return 0
    lax.fori_loop(0,(total+1)//2,body,0)
def al(x): return x if isinstance(x,int) else pl.multiple_of(x,16)
def rows_at(row,n): return pl.ds(al(row),n)

EPS=1e-06
def norm_parts(x):
    mean=jnp.mean(x,axis=-1,keepdims=True)
    cen=x-mean
    r=lax.rsqrt(jnp.mean(cen*cen,axis=-1,keepdims=True)+EPS)
    return cen*r,r
def norm_back(e,n,r,gain):
    t=e*gain
    return r*(t-jnp.mean(t,axis=-1,keepdims=True)-n*jnp.mean(t*n,axis=-1,keepdims=True))
def colsum(x): return jnp.sum(x,axis=0,keepdims=True)

def ffn_kernel(dp,att,x,vb,vg,vs,vd,wo_h,wo_got,cot_h,cot_got,wu_h,wd_h,bu,mine,other,gm,gb,vec,red,gheads,gwo,
               wo,cot,lsem,wu,wd,cotT,mid,n2,n2T,obuf,orecv,grow,act,gh,dw,chip_recv,wsem,osem,gsem,*rest):
    CH=dw.shape[0]; T,D=x.shape; SLOTS=chip_recv.shape[0]
    plan=big_plan(dp,dw.shape[2]); n=len(plan[0][0]); K=len(plan)
    recv=[rest[k*n:(k+1)*n] for k in range(K)]
    send_sem,recv_sem,chip_send,chip_got=rest[K*n:]
    p=Peers()
    b_row,g_row,s_row,d_row=[v[...].reshape(1,D) for v in (vb,vg,vs,vd)]
    tiles=[slice(t*TT,(t+1)*TT) for t in range(T//TT)]; NT_=len(tiles)
    regs=[halves(p,*s) for s in plan]
    def copy(k,s,c):
        out,_,nr=regs[k][s]
        return send(dw.at[c,p.th,rows_at(out,nr),:],recv[k][s].at[c],send_sem.at[k,s,c],recv_sem.at[k,s,c],p.peer(plan[k][0][s]))
    def chip_copy(c):
        return send(dw.at[c,1-p.th],chip_recv.at[c%SLOTS],chip_send.at[c],chip_got.at[c],p.peer("th"))
    def ocopy(): return send(obuf,orecv,osem.at[0],osem.at[1],p.peer("th"))
    def gcopy(landed):
        ref=grow.at[rows_at((1-p.th if landed else p.th)*T,T),:]
        return send(ref,ref,gsem.at[0],gsem.at[1],p.peer("th"))
    def wload(c):
        return (pltpu.make_async_copy(wu_h.at[:,pl.ds(pl.multiple_of(c*FC,FC),FC)],wu.at[c],wsem.at[0,c]),
                pltpu.make_async_copy(wd_h.at[pl.ds(pl.multiple_of(c*FC,FC),FC),:],wd.at[c],wsem.at[1,c]))
    E=wo_h.shape[0]; Q=T//2
    loads=[pltpu.make_async_copy(a,b,lsem.at[i]) for i,(a,b) in enumerate(((wo_h,wo.at[0:E,:]),(wo_got,wo.at[E:2*E,:]),
        (cot_h.at[p.tw],cot.at[rows_at(p.tw*Q,Q),:]),(cot_got,cot.at[rows_at((1-p.tw)*Q,Q),:])))]
    for l in loads: l.start()
    def load(c,_):
        for w in wload(c): w.start()
        return 0
    lax.fori_loop(0,CH,load,0)
    barrier(p,["th"]+plan[0][0])
    for l in loads[:2]: l.wait()
    for r in tiles:
        obuf[r,:]=dot(att[rows_at((1-p.th)*T+r.start,TT),:],wo[...],NN).astype(BF)
    for l in loads[2:]: l.wait()
    for t,r in enumerate(tiles):
        mid[r,:]=x[r,:].astype(F32)+dot(att[rows_at(p.th*T+r.start,TT),:],wo[...],NN)+b_row
        if t==0: ocopy().start()
        cotT[:,r]=cot[r,:].T
    ocopy().wait_recv()
    for r in tiles:
        m=mid[r,:]+orecv[r,:].astype(F32)
        mid[r,:]=m
        nn,_=norm_parts(m)
        y=(nn*g_row+s_row).astype(BF)
        n2[r,:]=y; n2T[:,r]=y.T
    vec[...]=jnp.zeros_like(vec)
    def sum_step(s,c):
        news=[]
        for k in range(K):
            copy(k,s,c).wait_recv()
            _,kr,nr=regs[k][s]
            at=(c,p.th,rows_at(kr,nr),slice(None))
            new=(dw[at].astype(F32)+recv[k][s][c].astype(F32)).astype(BF)
            if s<n-1: dw[at]=new
            else: news.append((kr,nr,new))
        if s<n-1:
            for k in range(K): copy(k,s+1,c).start()
        else:
            out=0
            for kr,nr,new in news:
                red[c,out:out+nr,:]=new; out+=nr
    def chip_sum(c):
        chip_copy(c).wait_recv()
        def add(q,_):
            r=rows_at(q*TT,TT)
            dw[c,p.th,r,:]=(dw[c,p.th,r,:].astype(F32)+chip_recv[c%SLOTS,r,:].astype(F32)).astype(BF)
            return 0
        lax.fori_loop(0,dw.shape[2]//TT,add,0)
        for k in range(K): copy(k,0,c).start()
    def hidden(c):
        for w in wload(c): w.wait()
        cols=pl.ds(pl.multiple_of(c*FC,FC),FC)
        gsum=jnp.zeros((1,FC),F32)
        for r in tiles:
            h=dot(n2[r,:],wu[c],NN)+bu[:,cols]
            ga=dot(cot[r,:],wd[c],NT)
            cdf=0.5*(1.0+lax.erf(h*(0.5**0.5)))
            a=(h*cdf).astype(BF)
            gr=(ga*(cdf+h*(jnp.exp(h*h*-0.5)*0.3989422804014327))).astype(BF)
            act[c,r,:]=a; gh[c,r,:]=gr
            gsum+=colsum(gr.astype(F32))
        gb[:,cols]=gsum
    def weight_grads(c):
        for t in range(D//TT):
            r=slice(t*TT,(t+1)*TT)
            for m,(lhs,rhs) in enumerate(((n2T,gh),(cotT,act))):
                y=dot(lhs[r,:],rhs[c],NN).astype(BF)
                for q in range(FC//128): dw[c,m,q*D+t*TT:q*D+(t+1)*TT,:]=y[:,q*128:(q+1)*128]
    def norm_two_back(t):
        r=rows_at(t*TT,TT)
        e=dot(gh[0,r,:],wu[0],NT)
        for c in range(1,CH): e+=dot(gh[c,r,:],wu[c],NT)
        nn,rs=norm_parts(mid[r,:])
        ct=cot[r,:].astype(F32)
        gmid=ct+norm_back(e,nn,rs,g_row)
        gm[r,:]=gmid
        gbr=gmid.astype(BF)
        grow[rows_at(p.th*T+t*TT,TT),:]=gbr
        vec[0:1,:]+=colsum(gbr.astype(F32)); vec[1:2,:]+=colsum(e*nn); vec[2:3,:]+=colsum(e); vec[3:4,:]+=colsum(ct)
    def block_out(t):
        r=rows_at(t*TT,TT)
        y=mid[r,:]+d_row
        for c in range(CH): y+=dot(act[c,r,:],wd[c],NN)
        n2[r,:]=y.astype(BF)
    def split_out(_):
        gcopy(True).wait_recv()
        mine[...]=n2[rows_at(p.tw*(T//2),T//2),:]
        other[...]=n2[rows_at((1-p.tw)*(T//2),T//2),:]
    def grad_heads(u):
        for t in range(NT_):
            r=rows_at(u*T+t*TT,TT)
            gheads[r,:]=dot(grow[r,:],wo[...],NT).astype(BF)
    def grad_wo(_):
        for t in range(D//TT):
            r=slice(t*TT,(t+1)*TT)
            gwo[r,:]=dot(grow[:,r],att[...],TN).astype(BF)
    P2=2*CH; P3=P2+NT_; P4=P3+NT_
    part=functools.partial
    steps=[(3+FL*(s+1),2,CH,part(sum_step,s)) for s in reversed(range(n))]
    steps+=[(3,2,CH,chip_sum),(2,2,CH,lambda c: chip_copy(c).start())]
    steps+=[(0,2,CH,hidden),(1,2,CH,weight_grads),(P2,1,NT_,norm_two_back),(P3,1,1,lambda _: gcopy(False).start()),(P3,1,NT_,block_out),
            (P4,1,1,split_out),(P4,1,2,grad_heads),(P4+2,1,1,grad_wo)]
    run_steps(steps)
    ocopy().wait_send(); gcopy(False).wait_send()
    def drain(c,_):
        chip_copy(c).wait_send()
        for k in range(K):
            for s in range(n): copy(k,s,c).wait_send()
        return 0
    lax.fori_loop(0,CH,drain,0)

def whole(shape):
    return pl.BlockSpec(memory_space=pltpu.VMEM)

def ffn(dp,att,x,vb,vg,vs,vd,wo,wo_got,cot,cot_got,wu,wd,bu):
    T,D=x.shape; FF=wu.shape[1]; CH=FF//FC; R=FC//128*D; C=att.shape[1]
    plan=big_plan(dp,R); n=len(plan[0][0])
    fin=R>>n
    recv=[pltpu.VMEM((CH,rows>>(s+1),128),BF) for _,_,rows in plan for s in range(n)]
    outs=[((T//2,D),BF),((T//2,D),BF),((T,D),F32),((1,FF),F32),((8,D),F32),((CH,fin,128),BF),((2*T,C),BF),((D,C),BF)]
    specs=[whole(o[0]) for o in outs]
    hbm=pl.BlockSpec(memory_space=pl.ANY)
    V=pltpu.VMEM; sem=pltpu.SemaphoreType.DMA
    return pl.pallas_call(functools.partial(ffn_kernel,dp),
      in_specs=[whole(v.shape) for v in (att,x,vb,vg,vs,vd)]+[hbm]*6+[whole(bu.shape)],
      out_specs=specs,out_shape=[jax.ShapeDtypeStruct(*o) for o in outs],
      scratch_shapes=[V((C,D),BF),V((T,D),BF),sem((4,)),V((CH,D,FC),BF),V((CH,FC,D),BF),V((D,T),BF),V((T,D),F32),V((T,D),BF),V((D,T),BF),V((T,D),BF),V((T,D),BF),V((2*T,D),BF),
          V((CH,T,FC),BF),V((CH,T,FC),BF),V((CH,2,R,128),BF),V((3,R,128),BF),sem((2,CH)),sem((2,)),sem((2,))]+recv
        +[sem((len(plan),n,CH))]*2+[sem((CH,))]*2,
      compiler_params=pltpu.CompilerParams(vmem_limit_bytes=63*2**20+2**19,collective_id=0,has_side_effects=True),name="feed_forward")(att,x,vb,vg,vs,vd,wo,wo_got,cot,cot_got,wu,wd,bu)

def finish_kernel(dp,red,dq_h,dk_h,dv_h,normT_h,wh_h,gwo_h,x_h,gm_h,gain,vec,gbu,gathered,heads_out,vec_out,tok,full,fsem,dq,dk,dv,normT,wh,gwo,x,gm,isem,hp,hg,vbuf,vrecv,own,obuf,orecv,tbuf,trecv,vrow,osem,tsem,*rest):
    CH=full.shape[0]; R=full.shape[2]; T,D=x.shape; C=dq.shape[1]; Q=T//2
    plan=big_plan(dp,R); n=len(plan[0][0]); K=len(plan)
    HR=hp.shape[2]; hplan=head_plan(dp,HR); HK=len(hplan); HC=hp.shape[0]
    hrecv=[rest[k*n:(k+1)*n] for k in range(HK)]
    send_sem,recv_sem,chip_send,chip_got,hs_sem,hr_sem,ha_send,ha_recv,vs_sem,vr_sem=rest[HK*n:]
    p=Peers()
    regs=[halves(p,*s) for s in plan]
    hregs=[halves(p,*s,keep_tw=True) for s in hplan]
    def gat(k,s,c,landed):
        other,mine,nr=regs[k][s]
        ref=full.at[c,p.th,rows_at(other if landed else mine,nr),:]
        return send(ref,ref,send_sem.at[k,s,c],recv_sem.at[k,s,c],p.peer(plan[k][0][s]))
    def chip(c,landed):
        ref=full.at[c,1-p.th if landed else p.th]
        return send(ref,ref,chip_send.at[c],chip_got.at[c],p.peer("th"))
    def fput(c): return pltpu.make_async_copy(full.at[c],gathered.at[c],fsem.at[c])
    def hsum(k,s,c):
        order=hplan[k][0]; other,_,nr=hregs[k][s]
        if order[s]=="tw": src=hp.at[c,pl.ds(1,1),rows_at(other,nr),:]
        elif order.index("tw")>s: src=hp.at[c,:,rows_at(other,nr),:]
        else: src=hp.at[c,pl.ds(0,1),rows_at(other,nr),:]
        return send(src,hrecv[k][s].at[c],hs_sem.at[k,s,c],hr_sem.at[k,s,c],p.peer(order[s]))
    def hgat(k,s,c,landed):
        order=hplan[k][0]; other,mine,nr=hregs[k][s]
        ref=hg.at[c,rows_at(other if landed else mine,nr),:]
        return send(ref,ref,ha_send.at[k,s,c],ha_recv.at[k,s,c],p.peer(order[s]))
    backs=[[s for s in reversed(range(n)) if o[s]!="tw"] for o,_,_ in hplan]
    vaxes=["th","tw"]+list(range(n-1))
    def vcopy(i): return send(vbuf.at[i],vrecv.at[i],vs_sem.at[i],vr_sem.at[i],p.peer(vaxes[i]))
    def ocopy(): return send(obuf,orecv,osem.at[0],osem.at[1],p.peer("th"))
    def tcopy(): return send(tbuf.at[rows_at((1-p.tw)*Q,Q),:],trecv,tsem.at[0],tsem.at[1],p.peer("tw"))
    loads=[pltpu.make_async_copy(a,b,isem.at[i]) for i,(a,b) in enumerate(((normT_h,normT),(dq_h,dq),(dk_h,dk),(dv_h,dv),(gwo_h,gwo),(wh_h,wh),(x_h,x),(gm_h,gm)))]
    for l in loads: l.start()
    def arrived(a,b):
        for l in loads[a:b]: l.wait()
    out=0
    for k in range(K):
        _,kr,nr=regs[k][n-1]
        for c in range(CH): full[c,p.th,rows_at(kr,nr),:]=red[c,out:out+nr,:]
        out+=nr
    vbuf[0]=jnp.zeros(vbuf.shape[1:],F32)
    vrow[...]=jnp.zeros(vrow.shape,F32)
    barrier(p,["th"]+plan[0][0])
    last=n+n-1
    def head_step(j,c):
        for k in range(HK):
            order=hplan[k][0]
            if 0<j<=n:
                s=j-1
                hsum(k,s,c).wait_recv()
                _,kr,nr=hregs[k][s]
                q=slice(0,2) if order.index("tw")>s else slice(0,1)
                at=(c,q,rows_at(kr,nr),slice(None))
                new=(hp[at].astype(F32)+hrecv[k][s][c].astype(F32)).astype(BF)
                if j<n: hp[at]=new
                else: hg[c,rows_at(kr,nr),:]=new[0]
            elif j>n: hgat(k,backs[k][j-n-1],c,True).wait_recv()
        for k in range(HK):
            if j<n: hsum(k,j,c).start()
            elif j<last: hgat(k,backs[k][j-n],c,False).start()
        if j==last: heads_out[c]=hg[c]
    def gather_step(j,c):
        if 0<j<=n:
            for k in range(K): gat(k,n-j,c,True).wait_recv()
        if j<n:
            for k in range(K): gat(k,n-1-j,c,False).start()
        elif j==n: chip(c,False).start()
        else:
            chip(c,True).wait_recv()
            fput(c).start()
    HT=D//HC
    def weight_grads(t):
        r=rows_at(t*HT,HT)
        parts=[dot(normT[r,:],d[...],NN).astype(BF) for d in (dq,dk,dv)]+[gwo[r,:]]
        for q in range(2):
            y=jnp.concatenate([z[:,q*(C//2):(q+1)*(C//2)] for z in parts],1)
            for i in range(y.shape[1]//128): hp[t,q,i*HT:(i+1)*HT,:]=y[:,i*128:(i+1)*128]
    def norm_grad(core,t):
        rr=rows_at(core*T+t*TT,TT)
        return dot(dq[rr,:],wh[0],NN)+dot(dk[rr,:],wh[1],NN)+dot(dv[rr,:],wh[2],NN)
    def other_half(t): obuf[rows_at(t*TT,TT),:]=norm_grad(1-p.th,t).astype(BF)
    def own_half(t): own[rows_at(t*TT,TT),:]=norm_grad(p.th,t)
    def norm_one_back(i):
        quarter=(1-i)*(1-p.tw)+i*p.tw
        for t in range(Q//128):
            r=rows_at(quarter*Q+t*128,128)
            e=own[r,:]+orecv[r,:].astype(F32)
            nn,rs=norm_parts(x[r,:].astype(F32))
            tbuf[r,:]=(gm[r,:]+norm_back(e,nn,rs,gain[...].reshape(1,D))).astype(BF)
            vrow[0:1,:]+=colsum(e*nn); vrow[1:2,:]+=colsum(e)
    def vectors(_):
        tok[p.tw]=tbuf[rows_at(p.tw*Q,Q),:]
        rows=[vrow[0:1,:],vrow[1:2,:]]+[vec[i:i+1,:] for i in range(4)]+[gbu[...]]
        at=0
        for v in rows:
            for i in range(v.shape[1]//128):
                vbuf[0,at:at+1,:]=v[:,i*128:(i+1)*128]; at+=1
        for i,d in enumerate((dq,dv)):
            bs=colsum(d[...].astype(F32))
            for q in range(2):
                quarter=2*p.th+(p.tw if q==0 else 1-p.tw)
                y=jnp.concatenate([bs[:,q*(C//2):(q+1)*(C//2)],jnp.zeros((1,256-C//2),F32)],1)
                for z in range(2):
                    vbuf[0,pl.ds(at+quarter*4+i*2+z,1),:]=y[:,z*128:(z+1)*128]
    def vector_step(i,_):
        if i>0:
            vcopy(i-1).wait_recv()
            y=vbuf[i-1]+vrecv[i-1]
            if i<len(vaxes): vbuf[i]=y
            else: vec_out[...]=y
        if i<len(vaxes): vcopy(i).start()
    part=functools.partial
    NT_=T//TT; G1=HC; G2=G1+2*NT_
    steps=[(1+HLAG*j,HSP,HC,part(head_step,j)) for j in reversed(range(last+1))]
    steps+=[(GLAG*j,2,CH,part(gather_step,j)) for j in reversed(range(n+2))]
    steps+=[(G2+3+VLAG*i,1,1,part(vector_step,i)) for i in range(len(vaxes)+1)]
    steps+=[(0,1,1,lambda _: arrived(0,5)),(0,1,HC,weight_grads),(G1,1,1,lambda _: arrived(5,6)),(G2,1,1,lambda _: arrived(6,8)),(G1,1,NT_,other_half),(G1+NT_,1,1,lambda _: ocopy().start()),(G1+NT_,1,NT_,own_half),
            (G2,1,1,lambda _: ocopy().wait_recv()),(G2+1,1,1,lambda _: tcopy().start()),(G2,1,2,norm_one_back),(G2+2,1,1,vectors)]
    run_steps(steps)
    def drain(c,_):
        chip(c,False).wait_send(); fput(c).wait()
        for k in range(K):
            for s in range(n): gat(k,s,c,False).wait_send()
        return 0
    lax.fori_loop(0,CH,drain,0)
    def hdrain(c,_):
        for k in range(HK):
            for s in range(n): hsum(k,s,c).wait_send()
            for s in backs[k]: hgat(k,s,c,False).wait_send()
        return 0
    lax.fori_loop(0,HC,hdrain,0)
    for i in range(len(vaxes)): vcopy(i).wait_send()
    ocopy().wait_send(); tcopy().wait()
    tok[1-p.tw]=trecv[...]

def finish(dp,red,dq,dk,dv,normT,wh,gwo,x,gm,gain,vec,gbu):
    T,D=x.shape; CH,fin,_=red.shape; R=FC//128*D
    plan=big_plan(dp,R); n=len(plan[0][0])
    HC=D//TT; HR=2*dq.shape[1]//128*TT; hplan=head_plan(dp,HR)
    hrecv=[]
    for order,_,rows in hplan:
        q=2
        for axis in order:
            if axis=="tw": q=1
            else: rows//=2
            hrecv.append(pltpu.VMEM((HC,q,rows,128),BF))
    V=(6*D+gbu.shape[1])//128+16; nv=n+1; args=(red,dq,dk,dv,normT,wh,gwo,x,gm,gain,vec,gbu)
    return pl.pallas_call(functools.partial(finish_kernel,dp),
      in_specs=[pl.BlockSpec(memory_space=pl.ANY if 1<=i<=8 else pltpu.VMEM) for i in range(len(args))],
      out_specs=[pl.BlockSpec(memory_space=pl.ANY)]+[pl.BlockSpec(memory_space=pltpu.VMEM)]*3,
      out_shape=[jax.ShapeDtypeStruct((CH,2,R,128),BF),jax.ShapeDtypeStruct((HC,HR,128),BF),jax.ShapeDtypeStruct((V,128),F32),jax.ShapeDtypeStruct((2,T//2,D),BF)],
      scratch_shapes=[pltpu.VMEM((CH,2,R,128),BF),pltpu.SemaphoreType.DMA((CH,))]+[pltpu.VMEM(a.shape,a.dtype) for a in args[1:9]]+[pltpu.SemaphoreType.DMA((8,)),pltpu.VMEM((HC,2,HR,128),BF),pltpu.VMEM((HC,HR,128),BF),pltpu.VMEM((nv,V,128),F32),pltpu.VMEM((nv,V,128),F32),pltpu.VMEM((T,D),F32)]+[pltpu.VMEM((T,D),BF)]*3+[pltpu.VMEM((T//2,D),BF),pltpu.VMEM((8,D),F32)]+[pltpu.SemaphoreType.DMA((2,))]*2+hrecv
        +[pltpu.SemaphoreType.DMA((len(plan),n,CH))]*2+[pltpu.SemaphoreType.DMA((CH,))]*2+[pltpu.SemaphoreType.DMA((len(hplan),n,HC))]*4+[pltpu.SemaphoreType.DMA((nv,))]*2,
      compiler_params=pltpu.CompilerParams(vmem_limit_bytes=60*2**20,collective_id=1,has_side_effects=True),name="finish_gradients")(*args)

def widen_kernel(where,chunk,heads,mine,got,vec,tok,wup,wdown,wqkv,wout,blk,tok_o,bqv,*vectors):
    D=wup.shape[0]; q=wout.shape[0]; g=pl.program_id(0); HT=D//heads.shape[0]
    for i in range(FC//128):
        cols=slice(i*128,(i+1)*128)
        wup[:,cols]=chunk[0,i*D:(i+1)*D,:].astype(F32)
        wdown[cols,:]=chunk[1,i*D:(i+1)*D,:].T.astype(F32)
    @pl.when(g==0)
    def _():
        for t in range(heads.shape[0]):
            y=jnp.concatenate([heads[t,i*HT:(i+1)*HT,:] for i in range(heads.shape[1]//HT)],1).T.astype(F32)
            rr=slice(t*HT,(t+1)*HT)
            for c in range(3): wqkv[c,:,rr]=y[c*q:(c+1)*q,:]
            wout[:,rr]=y[3*q:,:]
        blk[where[0]]=mine[...]; blk[1-where[0]]=got[...]
        tok_o[...]=tok[...]
        at=sum(v.shape[0] for v in vectors)//128
        for i in range(2):
            for z,w in ((0,128),(1,q-128)): bqv[i:i+1,z*128:z*128+w]=vec[pl.ds(at+4*where[1]+2*i+z,1),0:w]
        at=0
        for v in vectors:
            for i in range(v.shape[0]//128):
                v[i*128:(i+1)*128]=vec[at,:]; at+=1

def widen(where,chunks,heads,mine,got,vec,tok):
    CH,_,R,_=chunks.shape; D=R*128//FC; FF=CH*FC; q=heads.shape[0]*heads.shape[1]*128//(4*D); T2=mine.shape[0]
    outs=[(D,FF),(FF,D),(3,q,D),(q,D)]; sizes=[D]*6+[FF]
    res=pl.pallas_call(widen_kernel,grid=(CH,),
      in_specs=[pl.BlockSpec(memory_space=pltpu.SMEM),pl.BlockSpec((None,2,R,128),lambda g:(g,0,0,0))]+[pl.BlockSpec(a.shape,lambda g,n=a.ndim:(0,)*n) for a in (heads,mine,got,vec,tok)],
      out_specs=[pl.BlockSpec((D,FC),lambda g:(0,g)),pl.BlockSpec((FC,D),lambda g:(g,0))]+[pl.BlockSpec(memory_space=pltpu.VMEM)]*(5+len(sizes)),
      out_shape=[jax.ShapeDtypeStruct(o,F32) for o in outs]+[jax.ShapeDtypeStruct((2,T2,D),BF)]*2+[jax.ShapeDtypeStruct((2,q),F32)]+[jax.ShapeDtypeStruct((z,),F32) for z in sizes],
      compiler_params=pltpu.CompilerParams(vmem_limit_bytes=63*2**20),name="widen")(where,chunks,heads,mine,got,vec,tok)
    return res[:7],res[7:]

def front_kernel(tok,w,b,gain,shift,seg,x_o,normT_o,q_o,k_o,v_o,wh_o,mq_o,mk_o,x,norm,normT,qkv,wh,wgot,bgot,bias,mq,mk,tsem,bsem,csem,ysem,xsem,zsem,osem):
    p=Peers(); Q,D=tok.shape[1:]; T=2*Q; L=2*T; E=w.shape[1]; PART=E//4
    b0,b1=p.bit(0),p.bit(1)
    barrier(p,["th","tw",0,1])
    def tcopy(): return send(tok.at[1-p.tw],x.at[rows_at(p.tw*Q,Q),:],tsem.at[0],tsem.at[1],p.peer("tw"))
    def bcopy(): return send(b,bgot,bsem.at[0],bsem.at[1],p.peer("tw"))
    def ycopy(c):
        r=rows_at((2*b1+b0)*PART,PART)
        return send(w.at[c,r,:],wgot.at[c,r,:],ysem.at[0,c],ysem.at[1,c],p.peer("tw"))
    def xcopy(c,landed):
        ref=wgot.at[c,rows_at((2*b1+(1-b0 if landed else b0))*PART,PART),:]
        return send(ref,ref,xsem.at[0,c],xsem.at[1,c],p.peer(0))
    def zcopy(c,landed):
        ref=wgot.at[c,rows_at((1-b1 if landed else b1)*2*PART,2*PART),:]
        return send(ref,ref,zsem.at[0,c],zsem.at[1,c],p.peer(1))
    def ccopy(i,landed):
        core=1-p.th if landed else p.th
        quarter=p.tw if i==0 else 1-p.tw
        ref=norm.at[rows_at(core*T+quarter*Q,Q),:]
        return send(ref,ref,csem.at[0,i],csem.at[1,i],p.peer("th"))
    for c in range(3): ycopy(c).start()
    bcopy().start()
    tcopy().start()
    g_row=gain[...].reshape(1,D); s_row=shift[...].reshape(1,D)
    def normalize(src,row):
        for t in range(Q//128):
            y=(norm_parts(src(t).astype(F32))[0]*g_row+s_row).astype(BF)
            norm[rows_at(row+t*128,128),:]=y
    def put(src,dst,i): return pltpu.make_async_copy(src,dst,osem.at[i])
    x[rows_at(p.tw*Q,Q),:]=tok[p.tw]
    normalize(lambda t: tok[p.tw,t*128:(t+1)*128,:],p.th*T+p.tw*Q)
    onehot=lax.broadcasted_iota(jnp.int32,(128,L),0)
    onehot=jnp.where(onehot<HD,onehot,onehot-HD)
    same=onehot==seg[pl.ds(p.tw,1),:]
    mk[...]=jnp.where(same,1.0,0.0).T.astype(BF)
    ccopy(0,False).start()
    for c in range(3):
        ycopy(c).wait_recv()
        xcopy(c,False).start()
    mq[...]=jnp.where(same|(onehot>=9),0.0,-float(2**40)).T.astype(BF)
    put(mk,mk_o,0).start(); put(mq,mq_o,1).start()
    bcopy().wait_recv()
    bias[...]=jnp.zeros_like(bias)
    for m,src in enumerate((b,bgot)):
        for i,c in enumerate((0,2)): bias[m,c:c+1,:]=src[i:i+1,:]
    for c in range(3):
        xcopy(c,True).wait_recv()
        zcopy(c,False).start()
    def project(row,weights,m):
        r=rows_at(row,Q)
        def one(c,_):
            y=(dot(norm[r,:],weights[c],NT)+bias[m,pl.ds(c,1),:]).astype(BF)
            y=y*jnp.where(c==0,0.125,1.0).astype(BF)
            qkv[c,r,m*E:(m+1)*E]=y
            return 0
        lax.fori_loop(0,3,one,0)
    def transpose(quarter):
        for core in range(2):
            for t in range(Q//128):
                at=core*T+quarter*Q+t*128
                normT[:,pl.ds(pl.multiple_of(at,128),128)]=norm[rows_at(at,128),:].T
    ccopy(0,True).wait_recv()
    for core in range(2): project(core*T+p.tw*Q,w,0)
    transpose(p.tw)
    for c in range(3): zcopy(c,True).wait_recv()
    for core in range(2): project(core*T+p.tw*Q,wgot,1)
    for c in range(3): wh[c,0:E,:]=w[c]; wh[c,E:2*E,:]=wgot[c]
    put(wh,wh_o,7).start()
    tcopy().wait_recv()
    normalize(lambda t: x[rows_at((1-p.tw)*Q+t*128,128),:],p.th*T+(1-p.tw)*Q)
    put(x,x_o,2).start()
    for m,weights in enumerate((w,wgot)):
        project(p.th*T+(1-p.tw)*Q,weights,m)
        if m==0: ccopy(1,False).start()
    ccopy(1,True).wait_recv()
    for m,weights in enumerate((w,wgot)): project((1-p.th)*T+(1-p.tw)*Q,weights,m)
    for c in range(3): put(qkv.at[c],(q_o,k_o,v_o)[c],4+c).start()
    transpose(1-p.tw)
    put(normT,normT_o,3).start()
    for src,dst,i in ((mk,mk_o,0),(mq,mq_o,1),(x,x_o,2),(normT,normT_o,3),(wh,wh_o,7)): put(src,dst,i).wait()
    for c in range(3):
        put(qkv.at[c],(q_o,k_o,v_o)[c],4+c).wait()
        ycopy(c).wait_send(); xcopy(c,False).wait_send(); zcopy(c,False).wait_send()
    tcopy().wait_send(); bcopy().wait_send()
    for i in range(2): ccopy(i,False).wait_send()

def front(tok,w,b,gain,shift,seg):
    _,Q,D=tok.shape; T=2*Q; L=2*T; E=w.shape[1]
    outs=[((T,D),BF),((D,L),BF)]+[((L,2*E),BF)]*3+[((3,2*E,D),BF)]+[((L,128),BF)]*2
    sem=pltpu.SemaphoreType.DMA
    return pl.pallas_call(front_kernel,
      in_specs=[pl.BlockSpec(memory_space=pltpu.VMEM)]*6,out_specs=[pl.BlockSpec(memory_space=pl.ANY)]*len(outs),
      out_shape=[jax.ShapeDtypeStruct(*o) for o in outs],
      scratch_shapes=[pltpu.VMEM((T,D),BF),pltpu.VMEM((L,D),BF),pltpu.VMEM((D,L),BF),pltpu.VMEM((3,L,2*E),BF),pltpu.VMEM((3,2*E,D),BF),pltpu.VMEM((3,E,D),BF),
        pltpu.VMEM(b.shape,F32),pltpu.VMEM((2,8,E),F32),pltpu.VMEM((L,128),BF),pltpu.VMEM((L,128),BF),sem((2,)),sem((2,)),sem((2,2)),sem((2,3)),sem((2,3)),sem((2,3)),sem((8,))],
      compiler_params=pltpu.CompilerParams(vmem_limit_bytes=60*2**20,collective_id=2,has_side_effects=True),name="front")(tok,w,b,gain,shift,seg)


SWAP = [(0, 1), (1, 0)]


def swap(value, axis):
    return lax.ppermute(value, axis, SWAP)


def body(
    dp_size,
    tokens,
    segment_ids,
    norm1_gain,
    norm1_shift,
    w_qkv,
    b_qv,
    w_out,
    b_out,
    norm2_gain,
    norm2_shift,
    w_up,
    b_up,
    w_down,
    b_down,
    cotangent,
):
    th, tw = lax.axis_index("th"), lax.axis_index("tw")
    x, normed_t, query, key, value, w_heads, mq, mk = front(
        tokens, w_qkv.transpose(0, 2, 1), b_qv, norm1_gain, norm1_shift, segment_ids
    )
    tables = (mq, mk, *block_ranges(lax.dynamic_index_in_dim(segment_ids, tw, 0, False)))
    later = lax.optimization_barrier((cotangent, w_out, query))
    cot_got = swap(lax.dynamic_index_in_dim(later[0], 1 - tw, 0, False), "tw")
    w_out_got = swap(later[1], "tw")
    attended, totals = attn_fwd(query, key, value, *tables)
    out_mine, out_other, grad_middle, grad_b_up, sums, red, grad_heads, grad_w_out = ffn(
        dp_size, attended, x, b_out, norm2_gain, norm2_shift, b_down, w_out, w_out_got, cotangent, cot_got, w_up, w_down, b_up[None]
    )
    out_got = swap(out_other, "tw")
    dq, dk, dv = attn_bwd(query, key, value, grad_heads, attended, totals, *tables)
    chunks, heads, small, grad_tokens = finish(
        dp_size, red, dq, dk, dv, normed_t, w_heads, grad_w_out, x, grad_middle, norm1_gain, sums, grad_b_up
    )
    where = jnp.stack([tw, 2 * th + tw]).astype(jnp.int32)
    (up, down, w_qkv_grad, w_out_grad, block_out, grad_tokens, b_qv_grad), vecs = widen(
        where, chunks, heads, out_mine, out_got, small, grad_tokens
    )
    return (
        block_out,
        grad_tokens,
        vecs[0],
        vecs[1],
        w_qkv_grad.transpose(0, 2, 1),
        b_qv_grad,
        w_out_grad,
        vecs[2],
        vecs[3],
        vecs[4],
        up,
        vecs[6],
        down,
        vecs[5],
    )


def solution(mesh):
    return jax.shard_map(
        functools.partial(body, mesh.shape["dp"]),
        mesh=mesh,
        in_specs=(
            P("dp", ("th", "tw"), None),
            P("dp", None),
            P(),
            P(),
            P(None, None, ("th", "tw")),
            P(None, ("th", "tw")),
            P(("th", "tw"), None),
            P(),
            P(),
            P(),
            P(),
            P(),
            P(),
            P(),
            P("dp", ("th", "tw"), None),
        ),
        out_specs=(
            P("dp", ("th", "tw"), None),
            P("dp", ("th", "tw"), None),
            P(),
            P(),
            P(None, None, ("th", "tw")),
            P(None, ("th", "tw")),
            P(("th", "tw"), None),
            P(),
            P(),
            P(),
            P(),
            P(),
            P(),
            P(),
        ),
        check_vma=False,
    )
```

```python
import functools

import jax
import jax.numpy as jnp
from jax import lax
from jax.experimental import pallas as pl
from jax.experimental.pallas import tpu as pltpu
from jax.sharding import PartitionSpec as P

NT=(((1,),(1,)),((),())); NN=(((1,),(0,)),((),())); TN=(((0,),(0,)),((),()))
F32=jnp.float32; BF=jnp.bfloat16
BQ=256; BK=256; HD=64
def dot(a,b,d): return lax.dot_general(a,b,d,preferred_element_type=F32)

AL=128; VR=80; GRP=3
def each_chunk(lo_ref,n_ref,i,body):
    lo=lo_ref[i]; n=n_ref[i]
    def full(j,_):
        body(pl.ds(pl.multiple_of(lo+j*BK,AL),BK))
        return 0
    lax.fori_loop(0,n//2,full,0)
    @pl.when(n%2==1)
    def _(): body(pl.ds(pl.multiple_of(lo+n//2*BK,AL),AL))

def fwd_kernel(lo_ref, n_ref, q_ref, k_ref, v_ref, mq_ref, mk_ref, o_ref, lse_ref, m_ref, acc_ref, vT_ref, qm_ref):
    i=pl.program_id(0); H=q_ref.shape[1]//HD
    lane=lax.broadcasted_iota(jnp.int32,(1,128),1)
    halves=(lane<HD, lane>=HD)
    @pl.when(i==0)
    def _():
        row=lax.broadcasted_iota(jnp.int32,(VR-HD,v_ref.shape[0]),0)
        for p in range(H//2):
            t=v_ref[:,p*128:(p+1)*128].T
            for e in range(2):
                vT_ref[2*p+e,0:HD,:]=t[e*HD:(e+1)*HD,:]
                vT_ref[2*p+e,HD:VR,:]=jnp.where(row==0,1.0,0.0).astype(BF)
    m_ref[...]=jnp.full(m_ref.shape,-1e30,F32)
    acc_ref[...]=jnp.zeros_like(acc_ref)
    for h in range(H): qm_ref[h]=jnp.where(halves[h%2],q_ref[:,h//2*128:h//2*128+128],mq_ref[...])
    def score(h,ks,mk):
        cols=slice(h//2*128,h//2*128+128)
        return dot(jnp.where(halves[h%2],k_ref[ks,cols],mk),qm_ref[h],NT)
    def soft(h,s):
        m_old=m_ref[h:h+1,:]
        m_new=jnp.maximum(m_old,jnp.max(s,axis=0,keepdims=True))
        m_ref[h:h+1,:]=m_new
        return jnp.exp(s-m_new).astype(BF),jnp.exp(m_old-m_new)
    def weigh(h,ks,pe,alpha):
        acc_ref[h]=acc_ref[h]*alpha+dot(vT_ref[h,:,ks],pe,NN)
    def body(ks):
        mk=mk_ref[ks,:]
        scores=[score(h,ks,mk) for h in range(H)]
        probs=[soft(h,scores[h]) for h in range(H)]
        for h in range(H): weigh(h,ks,*probs[h])
    each_chunk(lo_ref,n_ref,i,body)
    for p in range(H//2):
        parts=[acc_ref[h,0:HD,:]*(1.0/acc_ref[h,HD:HD+1,:]) for h in (2*p,2*p+1)]
        o_ref[:,p*128:(p+1)*128]=jnp.concatenate(parts,0).T.astype(BF)
    for h in range(H): lse_ref[h:h+1,:]=m_ref[h:h+1,:]+jnp.log(acc_ref[h,HD:HD+1,:])
    lse_ref[H:,:]=jnp.zeros((lse_ref.shape[0]-H,BQ),F32)

def attn_fwd(q,k,v,mq,mk,lo,n):
    L,C=q.shape
    return pl.pallas_call(fwd_kernel,
        grid_spec=pltpu.PrefetchScalarGridSpec(num_scalar_prefetch=2,grid=(L//BQ,),
          in_specs=[pl.BlockSpec((BQ,C),lambda i,*_:(i,0)),pl.BlockSpec((L,C),lambda i,*_:(0,0)),pl.BlockSpec((L,C),lambda i,*_:(0,0)),
                    pl.BlockSpec((BQ,128),lambda i,*_:(i,0)),pl.BlockSpec((L,128),lambda i,*_:(0,0))],
          out_specs=[pl.BlockSpec((BQ,C),lambda i,*_:(i,0)),pl.BlockSpec((8,BQ),lambda i,*_:(0,i))],
          scratch_shapes=[pltpu.VMEM((8,BQ),F32),pltpu.VMEM((C//HD,VR,BQ),F32),pltpu.VMEM((C//HD,VR,L),BF),pltpu.VMEM((C//HD,BQ,128),BF)]),
        out_shape=[jax.ShapeDtypeStruct((L,C),BF),jax.ShapeDtypeStruct((8,L),F32)],
        name="attention_forward",
    )(lo,n,q,k,v,mq,mk)

def bwd_kernel(lo_ref, n_ref, q_ref, k_ref, v_ref, do_ref, o_ref, lse_ref, mq_ref, mk_ref, dq_ref, dk_ref, dv_ref, dk_acc, dv_acc, dq_acc, qcat, docat, qm, kT):
    i=pl.program_id(0); n=pl.num_programs(0)
    C=q_ref.shape[1]; pairs=C//128
    lane=lax.broadcasted_iota(jnp.int32,(1,128),1)
    halves=(lane<HD, lane>=HD)
    @pl.when(i==0)
    def _():
        dk_acc[...]=jnp.zeros_like(dk_acc); dv_acc[...]=jnp.zeros_like(dv_acc)
        kT[...]=k_ref[...].T
    dq_acc[...]=jnp.zeros_like(dq_acc)
    sel=(lax.broadcasted_iota(jnp.int32,(8,C),1)//HD==lax.broadcasted_iota(jnp.int32,(8,C),0)).astype(BF)
    prod=do_ref[...].astype(F32)*o_ref[...].astype(F32)
    high=prod.astype(BF)
    delta=dot(sel,high,NT)+dot(sel,(prod-high.astype(F32)).astype(BF),NT)
    for p in range(pairs):
        cols=slice(p*128,(p+1)*128)
        for e in range(2):
            q2=q_ref[:,cols]; d2=do_ref[:,cols]
            qcat[p,e*BQ:(e+1)*BQ,:]=jnp.where(halves[e],q2,jnp.zeros_like(q2))
            qm[p,e*BQ:(e+1)*BQ,:]=jnp.where(halves[e],q2,mq_ref[...])
            docat[p,e*BQ:(e+1)*BQ,:]=jnp.where(halves[e],d2,jnp.zeros_like(d2))
    lse=lse_ref[...]
    def body(ks):
        mk=mk_ref[ks,:]
        for g in range(0,pairs,GRP):
            work=[]
            for p in range(g,g+GRP):
                cols=slice(p*128,(p+1)*128)
                k2=k_ref[ks,cols]; v2=v_ref[ks,cols]; d2=do_ref[:,cols]
                for e in range(2):
                    s=dot(jnp.where(halves[e],k2,mk),qm[p,e*BQ:(e+1)*BQ,:],NT)
                    work.append((s,dot(jnp.where(halves[e],v2,jnp.zeros_like(v2)),d2,NT)))
            out=[]
            for t,(s,dp) in enumerate(work):
                h=2*g+t
                pr=jnp.exp(s-lse[h:h+1,:])
                out.append((pr.astype(BF),(pr*(dp-delta[h:h+1,:])).astype(BF)))
            for p in range(g,g+GRP):
                cols=slice(p*128,(p+1)*128); k2=k_ref[ks,cols]
                (p0,d0),(p1,d1)=out[2*(p-g):2*(p-g)+2]
                dv_acc[ks,cols]+=dot(jnp.concatenate([p0,p1],1),docat[p],NN)
                dk_acc[ks,cols]+=dot(jnp.concatenate([d0,d1],1),qcat[p],NN)
                for e,d in enumerate((d0,d1)):
                    r=slice((2*p+e)*HD,(2*p+e+1)*HD)
                    dq_acc[r,:]+=dot(kT[r,ks],d,NN)
    each_chunk(lo_ref,n_ref,i,body)
    dq_ref[...]=(dq_acc[...]*0.125).T.astype(BF)
    @pl.when(i==n-1)
    def _():
        dk_ref[...]=dk_acc[...].astype(BF); dv_ref[...]=dv_acc[...].astype(BF)

def attn_bwd(q,k,v,do,o,lse,mq,mk,lo,n):
    L,C=q.shape
    blk=pl.BlockSpec((BQ,C),lambda i,*_:(i,0)); full=pl.BlockSpec((L,C),lambda i,*_:(0,0))
    return pl.pallas_call(bwd_kernel,
        grid_spec=pltpu.PrefetchScalarGridSpec(num_scalar_prefetch=2,grid=(L//BQ,),
          in_specs=[blk,full,full,blk,blk,pl.BlockSpec((8,BQ),lambda i,*_:(0,i)),pl.BlockSpec((BQ,128),lambda i,*_:(i,0)),pl.BlockSpec((L,128),lambda i,*_:(0,0))],
          out_specs=[blk,full,full],
          scratch_shapes=[pltpu.VMEM((L,C),F32),pltpu.VMEM((L,C),F32),pltpu.VMEM((C,BQ),F32),pltpu.VMEM((C//128,2*BQ,128),BF),pltpu.VMEM((C//128,2*BQ,128),BF),pltpu.VMEM((C//128,2*BQ,128),BF),pltpu.VMEM((C,L),BF)]),
        out_shape=[jax.ShapeDtypeStruct((L,C),BF)]*3,
        name="attention_backward",
    )(lo,n,q,k,v,do,o,lse,mq,mk)

def block_ranges(seg):
    first=seg[::BQ]; last=seg[BQ-1::BQ]
    lo=jnp.sum(seg[None,:]<first[:,None],axis=1,dtype=jnp.int32)//AL*AL
    hi=jnp.sum(seg[None,:]<=last[:,None],axis=1,dtype=jnp.int32)
    return lo,(hi-lo+AL-1)//AL


TT=256; FC=512
LAG=2; GLAG=5; HLAG=4; HSP=2; GSP=4; VLAG=5; FL=3

def bits_of(dp): return dp.bit_length()-1

def big_plan(dp,rows):
    n=bits_of(dp)
    orders=(["tw"]+list(range(n)),[0,"tw"]+list(range(1,n)),[1,2,0,"tw"]+list(range(3,n)))
    unit=16<<(n+1)
    units=rows//unit
    third=max(1,units//4)
    shares=[units-units//3-third,units//3,third]
    return streams(orders,shares,unit)

def head_plan(dp,rows):
    n=bits_of(dp)
    orders=(["tw"]+list(range(n)),[0,"tw"]+list(range(1,n)),[1,2,0,"tw"]+list(range(3,n)))
    unit=16<<n
    units=rows//unit
    low=max(1,units//4)
    mid=max(1,units//3)
    return streams(orders,[units-mid-low,mid,low],unit)

def streams(orders,shares,unit):
    out=[]; start=0
    for order,share in zip(orders,shares):
        out.append((order,start,share*unit)); start+=share*unit
    return out

class Peers:
    def __init__(self):
        self.dp=lax.axis_index("dp"); self.th=lax.axis_index("th"); self.tw=lax.axis_index("tw")
    def bit(self,axis):
        return self.tw if axis=="tw" else (self.dp//(1<<axis))%2
    def peer(self,axis):
        if axis=="tw": return {"tw":1-self.tw}
        if axis=="th": return {"th":1-self.th}
        return {"dp":self.dp+(1-2*self.bit(axis))*(1<<axis)}

def send(src,dst,ssem,rsem,peer):
    return pltpu.make_async_remote_copy(src,dst,ssem,rsem,device_id=peer,device_id_type=pl.DeviceIdType.MESH)

def barrier(p,axes):
    sem=pltpu.get_barrier_semaphore()
    for a in axes:
        pl.semaphore_signal(sem,inc=1,device_id=p.peer(a),device_id_type=pl.DeviceIdType.MESH)
    pl.semaphore_wait(sem,len(axes))

def halves(p,order,row,rows,keep_tw=False):
    out=[]
    for axis in order:
        if keep_tw and axis=="tw": out.append((row,row,rows)); continue
        rows//=2; bit=p.bit(axis)
        out.append((row+(1-bit)*rows,row+bit*rows,rows)); row=row+bit*rows
    return out
def run_steps(steps):
    total=max(f+sp*(cnt-1) for f,sp,cnt,_ in steps)+1
    def body(i,_):
        for r in range(2):
            g=2*i+r
            for f,sp,cnt,what in steps:
                if sp==2:
                    if f%2!=r: continue
                    c=i-f//2
                else: c=g-f
                if cnt==1:
                    pl.when(c==0)(functools.partial(what,0))
                else: pl.when((c>=0)&(c<cnt))(functools.partial(what,c))
        return 0
    lax.fori_loop(0,(total+1)//2,body,0)
def al(x): return x if isinstance(x,int) else pl.multiple_of(x,16)
def rows_at(row,n): return pl.ds(al(row),n)

EPS=1e-06
def norm_parts(x):
    mean=jnp.mean(x,axis=-1,keepdims=True)
    cen=x-mean
    r=lax.rsqrt(jnp.mean(cen*cen,axis=-1,keepdims=True)+EPS)
    return cen*r,r
def norm_back(e,n,r,gain):
    t=e*gain
    return r*(t-jnp.mean(t,axis=-1,keepdims=True)-n*jnp.mean(t*n,axis=-1,keepdims=True))
def colsum(x): return jnp.sum(x,axis=0,keepdims=True)

def ffn_kernel(dp,att,x,vb,vg,vs,vd,wo_h,wo_got,cot_h,cot_got,wu_h,wd_h,bu,mine,other,gm,gb,vec,red,gheads,gwo,
               wo,cot,lsem,wu,wd,cotT,mid,n2,n2T,obuf,orecv,grow,act,gh,dw,chip_recv,wsem,osem,gsem,*rest):
    CH=dw.shape[0]; T,D=x.shape; SLOTS=chip_recv.shape[0]
    plan=big_plan(dp,dw.shape[2]); n=len(plan[0][0]); K=len(plan)
    recv=[rest[k*n:(k+1)*n] for k in range(K)]
    send_sem,recv_sem,chip_send,chip_got=rest[K*n:]
    p=Peers()
    b_row,g_row,s_row,d_row=[v[...].reshape(1,D) for v in (vb,vg,vs,vd)]
    tiles=[slice(t*TT,(t+1)*TT) for t in range(T//TT)]; NT_=len(tiles)
    regs=[halves(p,*s) for s in plan]
    def copy(k,s,c):
        out,_,nr=regs[k][s]
        return send(dw.at[c,p.th,rows_at(out,nr),:],recv[k][s].at[c],send_sem.at[k,s,c],recv_sem.at[k,s,c],p.peer(plan[k][0][s]))
    def chip_copy(c):
        return send(dw.at[c,1-p.th],chip_recv.at[c%SLOTS],chip_send.at[c],chip_got.at[c],p.peer("th"))
    def ocopy(): return send(obuf,orecv,osem.at[0],osem.at[1],p.peer("th"))
    def gcopy(landed):
        ref=grow.at[rows_at((1-p.th if landed else p.th)*T,T),:]
        return send(ref,ref,gsem.at[0],gsem.at[1],p.peer("th"))
    def wload(c):
        return (pltpu.make_async_copy(wu_h.at[:,pl.ds(pl.multiple_of(c*FC,FC),FC)],wu.at[c],wsem.at[0,c]),
                pltpu.make_async_copy(wd_h.at[pl.ds(pl.multiple_of(c*FC,FC),FC),:],wd.at[c],wsem.at[1,c]))
    E=wo_h.shape[0]; Q=T//2
    loads=[pltpu.make_async_copy(a,b,lsem.at[i]) for i,(a,b) in enumerate(((wo_h,wo.at[0:E,:]),(wo_got,wo.at[E:2*E,:]),
        (cot_h.at[p.tw],cot.at[rows_at(p.tw*Q,Q),:]),(cot_got,cot.at[rows_at((1-p.tw)*Q,Q),:])))]
    for l in loads: l.start()
    def load(c,_):
        for w in wload(c): w.start()
        return 0
    lax.fori_loop(0,CH,load,0)
    barrier(p,["th"]+plan[0][0])
    for l in loads[:2]: l.wait()
    for r in tiles:
        obuf[r,:]=dot(att[rows_at((1-p.th)*T+r.start,TT),:],wo[...],NN).astype(BF)
    for l in loads[2:]: l.wait()
    for t,r in enumerate(tiles):
        mid[r,:]=x[r,:].astype(F32)+dot(att[rows_at(p.th*T+r.start,TT),:],wo[...],NN)+b_row
        if t==0: ocopy().start()
        cotT[:,r]=cot[r,:].T
    ocopy().wait_recv()
    for r in tiles:
        m=mid[r,:]+orecv[r,:].astype(F32)
        mid[r,:]=m
        nn,_=norm_parts(m)
        y=(nn*g_row+s_row).astype(BF)
        n2[r,:]=y; n2T[:,r]=y.T
    vec[...]=jnp.zeros_like(vec)
    def sum_step(s,c):
        news=[]
        for k in range(K):
            copy(k,s,c).wait_recv()
            _,kr,nr=regs[k][s]
            at=(c,p.th,rows_at(kr,nr),slice(None))
            new=(dw[at].astype(F32)+recv[k][s][c].astype(F32)).astype(BF)
            if s<n-1: dw[at]=new
            else: news.append((kr,nr,new))
        if s<n-1:
            for k in range(K): copy(k,s+1,c).start()
        else:
            out=0
            for kr,nr,new in news:
                red[c,out:out+nr,:]=new; out+=nr
    def chip_sum(c):
        chip_copy(c).wait_recv()
        def add(q,_):
            r=rows_at(q*TT,TT)
            dw[c,p.th,r,:]=(dw[c,p.th,r,:].astype(F32)+chip_recv[c%SLOTS,r,:].astype(F32)).astype(BF)
            return 0
        lax.fori_loop(0,dw.shape[2]//TT,add,0)
        for k in range(K): copy(k,0,c).start()
    def hidden(c):
        for w in wload(c): w.wait()
        cols=pl.ds(pl.multiple_of(c*FC,FC),FC)
        gsum=jnp.zeros((1,FC),F32)
        for r in tiles:
            h=dot(n2[r,:],wu[c],NN)+bu[:,cols]
            ga=dot(cot[r,:],wd[c],NT)
            cdf=0.5*(1.0+lax.erf(h*(0.5**0.5)))
            a=(h*cdf).astype(BF)
            gr=(ga*(cdf+h*(jnp.exp(h*h*-0.5)*0.3989422804014327))).astype(BF)
            act[c,r,:]=a; gh[c,r,:]=gr
            gsum+=colsum(gr.astype(F32))
        gb[:,cols]=gsum
    def weight_grads(c):
        for t in range(D//TT):
            r=slice(t*TT,(t+1)*TT)
            for m,(lhs,rhs) in enumerate(((n2T,gh),(cotT,act))):
                y=dot(lhs[r,:],rhs[c],NN).astype(BF)
                for q in range(FC//128): dw[c,m,q*D+t*TT:q*D+(t+1)*TT,:]=y[:,q*128:(q+1)*128]
    def norm_two_back(t):
        r=rows_at(t*TT,TT)
        e=dot(gh[0,r,:],wu[0],NT)
        for c in range(1,CH): e+=dot(gh[c,r,:],wu[c],NT)
        nn,rs=norm_parts(mid[r,:])
        ct=cot[r,:].astype(F32)
        gmid=ct+norm_back(e,nn,rs,g_row)
        gm[r,:]=gmid
        gbr=gmid.astype(BF)
        grow[rows_at(p.th*T+t*TT,TT),:]=gbr
        vec[0:1,:]+=colsum(gbr.astype(F32)); vec[1:2,:]+=colsum(e*nn); vec[2:3,:]+=colsum(e); vec[3:4,:]+=colsum(ct)
    def block_out(t):
        r=rows_at(t*TT,TT)
        y=mid[r,:]+d_row
        for c in range(CH): y+=dot(act[c,r,:],wd[c],NN)
        n2[r,:]=y.astype(BF)
    def split_out(_):
        gcopy(True).wait_recv()
        mine[...]=n2[rows_at(p.tw*(T//2),T//2),:]
        other[...]=n2[rows_at((1-p.tw)*(T//2),T//2),:]
    def grad_heads(u):
        for t in range(NT_):
            r=rows_at(u*T+t*TT,TT)
            gheads[r,:]=dot(grow[r,:],wo[...],NT).astype(BF)
    def grad_wo(_):
        for t in range(D//TT):
            r=slice(t*TT,(t+1)*TT)
            gwo[r,:]=dot(grow[:,r],att[...],TN).astype(BF)
    P2=2*CH; P3=P2+NT_; P4=P3+NT_
    part=functools.partial
    steps=[(3+FL*(s+1),2,CH,part(sum_step,s)) for s in reversed(range(n))]
    steps+=[(3,2,CH,chip_sum),(2,2,CH,lambda c: chip_copy(c).start())]
    steps+=[(0,2,CH,hidden),(1,2,CH,weight_grads),(P2,1,NT_,norm_two_back),(P3,1,1,lambda _: gcopy(False).start()),(P3,1,NT_,block_out),
            (P4,1,1,split_out),(P4,1,2,grad_heads),(P4+2,1,1,grad_wo)]
    run_steps(steps)
    ocopy().wait_send(); gcopy(False).wait_send()
    def drain(c,_):
        chip_copy(c).wait_send()
        for k in range(K):
            for s in range(n): copy(k,s,c).wait_send()
        return 0
    lax.fori_loop(0,CH,drain,0)

def whole(shape):
    return pl.BlockSpec(memory_space=pltpu.VMEM)

def ffn(dp,att,x,vb,vg,vs,vd,wo,wo_got,cot,cot_got,wu,wd,bu):
    T,D=x.shape; FF=wu.shape[1]; CH=FF//FC; R=FC//128*D; C=att.shape[1]
    plan=big_plan(dp,R); n=len(plan[0][0])
    fin=R>>n
    recv=[pltpu.VMEM((CH,rows>>(s+1),128),BF) for _,_,rows in plan for s in range(n)]
    outs=[((T//2,D),BF),((T//2,D),BF),((T,D),F32),((1,FF),F32),((8,D),F32),((CH,fin,128),BF),((2*T,C),BF),((D,C),BF)]
    specs=[whole(o[0]) for o in outs]
    hbm=pl.BlockSpec(memory_space=pl.ANY)
    V=pltpu.VMEM; sem=pltpu.SemaphoreType.DMA
    return pl.pallas_call(functools.partial(ffn_kernel,dp),
      in_specs=[whole(v.shape) for v in (att,x,vb,vg,vs,vd)]+[hbm]*6+[whole(bu.shape)],
      out_specs=specs,out_shape=[jax.ShapeDtypeStruct(*o) for o in outs],
      scratch_shapes=[V((C,D),BF),V((T,D),BF),sem((4,)),V((CH,D,FC),BF),V((CH,FC,D),BF),V((D,T),BF),V((T,D),F32),V((T,D),BF),V((D,T),BF),V((T,D),BF),V((T,D),BF),V((2*T,D),BF),
          V((CH,T,FC),BF),V((CH,T,FC),BF),V((CH,2,R,128),BF),V((3,R,128),BF),sem((2,CH)),sem((2,)),sem((2,))]+recv
        +[sem((len(plan),n,CH))]*2+[sem((CH,))]*2,
      compiler_params=pltpu.CompilerParams(vmem_limit_bytes=63*2**20+2**19,collective_id=0,has_side_effects=True),name="feed_forward")(att,x,vb,vg,vs,vd,wo,wo_got,cot,cot_got,wu,wd,bu)

def finish_kernel(dp,red,dq_h,dk_h,dv_h,normT_h,wh_h,gwo_h,x_h,gm_h,gain,vec,gbu,gathered,heads_out,vec_out,tok,full,fsem,dq,dk,dv,normT,wh,gwo,x,gm,isem,hp,hg,vbuf,vrecv,own,obuf,orecv,tbuf,trecv,vrow,osem,tsem,*rest):
    CH=full.shape[0]; R=full.shape[2]; T,D=x.shape; C=dq.shape[1]; Q=T//2
    plan=big_plan(dp,R); n=len(plan[0][0]); K=len(plan)
    HR=hp.shape[2]; hplan=head_plan(dp,HR); HK=len(hplan); HC=hp.shape[0]
    hrecv=[rest[k*n:(k+1)*n] for k in range(HK)]
    send_sem,recv_sem,chip_send,chip_got,hs_sem,hr_sem,ha_send,ha_recv,vs_sem,vr_sem=rest[HK*n:]
    p=Peers()
    regs=[halves(p,*s) for s in plan]
    hregs=[halves(p,*s,keep_tw=True) for s in hplan]
    def gat(k,s,c,landed):
        other,mine,nr=regs[k][s]
        ref=full.at[c,p.th,rows_at(other if landed else mine,nr),:]
        return send(ref,ref,send_sem.at[k,s,c],recv_sem.at[k,s,c],p.peer(plan[k][0][s]))
    def chip(c,landed):
        ref=full.at[c,1-p.th if landed else p.th]
        return send(ref,ref,chip_send.at[c],chip_got.at[c],p.peer("th"))
    def fput(c): return pltpu.make_async_copy(full.at[c],gathered.at[c],fsem.at[c])
    def hsum(k,s,c):
        order=hplan[k][0]; other,_,nr=hregs[k][s]
        if order[s]=="tw": src=hp.at[c,pl.ds(1,1),rows_at(other,nr),:]
        elif order.index("tw")>s: src=hp.at[c,:,rows_at(other,nr),:]
        else: src=hp.at[c,pl.ds(0,1),rows_at(other,nr),:]
        return send(src,hrecv[k][s].at[c],hs_sem.at[k,s,c],hr_sem.at[k,s,c],p.peer(order[s]))
    def hgat(k,s,c,landed):
        order=hplan[k][0]; other,mine,nr=hregs[k][s]
        ref=hg.at[c,rows_at(other if landed else mine,nr),:]
        return send(ref,ref,ha_send.at[k,s,c],ha_recv.at[k,s,c],p.peer(order[s]))
    backs=[[s for s in reversed(range(n)) if o[s]!="tw"] for o,_,_ in hplan]
    vaxes=["th","tw"]+list(range(n-1))
    def vcopy(i): return send(vbuf.at[i],vrecv.at[i],vs_sem.at[i],vr_sem.at[i],p.peer(vaxes[i]))
    def ocopy(): return send(obuf,orecv,osem.at[0],osem.at[1],p.peer("th"))
    def tcopy(): return send(tbuf.at[rows_at((1-p.tw)*Q,Q),:],trecv,tsem.at[0],tsem.at[1],p.peer("tw"))
    loads=[pltpu.make_async_copy(a,b,isem.at[i]) for i,(a,b) in enumerate(((normT_h,normT),(dq_h,dq),(dk_h,dk),(dv_h,dv),(gwo_h,gwo),(wh_h,wh),(x_h,x),(gm_h,gm)))]
    for l in loads: l.start()
    def arrived(a,b):
        for l in loads[a:b]: l.wait()
    out=0
    for k in range(K):
        _,kr,nr=regs[k][n-1]
        for c in range(CH): full[c,p.th,rows_at(kr,nr),:]=red[c,out:out+nr,:]
        out+=nr
    vbuf[0]=jnp.zeros(vbuf.shape[1:],F32)
    vrow[...]=jnp.zeros(vrow.shape,F32)
    barrier(p,["th"]+plan[0][0])
    last=n+n-1
    def head_step(j,c):
        for k in range(HK):
            order=hplan[k][0]
            if 0<j<=n:
                s=j-1
                hsum(k,s,c).wait_recv()
                _,kr,nr=hregs[k][s]
                q=slice(0,2) if order.index("tw")>s else slice(0,1)
                at=(c,q,rows_at(kr,nr),slice(None))
                new=(hp[at].astype(F32)+hrecv[k][s][c].astype(F32)).astype(BF)
                if j<n: hp[at]=new
                else: hg[c,rows_at(kr,nr),:]=new[0]
            elif j>n: hgat(k,backs[k][j-n-1],c,True).wait_recv()
        for k in range(HK):
            if j<n: hsum(k,j,c).start()
            elif j<last: hgat(k,backs[k][j-n],c,False).start()
        if j==last: heads_out[c]=hg[c]
    def gather_step(j,c):
        if 0<j<=n:
            for k in range(K): gat(k,n-j,c,True).wait_recv()
        if j<n:
            for k in range(K): gat(k,n-1-j,c,False).start()
        elif j==n: chip(c,False).start()
        else:
            chip(c,True).wait_recv()
            fput(c).start()
    HT=D//HC
    def weight_grads(t):
        r=rows_at(t*HT,HT)
        parts=[dot(normT[r,:],d[...],NN).astype(BF) for d in (dq,dk,dv)]+[gwo[r,:]]
        for q in range(2):
            y=jnp.concatenate([z[:,q*(C//2):(q+1)*(C//2)] for z in parts],1)
            for i in range(y.shape[1]//128): hp[t,q,i*HT:(i+1)*HT,:]=y[:,i*128:(i+1)*128]
    def norm_grad(core,t):
        rr=rows_at(core*T+t*TT,TT)
        return dot(dq[rr,:],wh[0],NN)+dot(dk[rr,:],wh[1],NN)+dot(dv[rr,:],wh[2],NN)
    def other_half(t): obuf[rows_at(t*TT,TT),:]=norm_grad(1-p.th,t).astype(BF)
    def own_half(t): own[rows_at(t*TT,TT),:]=norm_grad(p.th,t)
    def norm_one_back(i):
        quarter=(1-i)*(1-p.tw)+i*p.tw
        for t in range(Q//128):
            r=rows_at(quarter*Q+t*128,128)
            e=own[r,:]+orecv[r,:].astype(F32)
            nn,rs=norm_parts(x[r,:].astype(F32))
            tbuf[r,:]=(gm[r,:]+norm_back(e,nn,rs,gain[...].reshape(1,D))).astype(BF)
            vrow[0:1,:]+=colsum(e*nn); vrow[1:2,:]+=colsum(e)
    def vectors(_):
        tok[p.tw]=tbuf[rows_at(p.tw*Q,Q),:]
        rows=[vrow[0:1,:],vrow[1:2,:]]+[vec[i:i+1,:] for i in range(4)]+[gbu[...]]
        at=0
        for v in rows:
            for i in range(v.shape[1]//128):
                vbuf[0,at:at+1,:]=v[:,i*128:(i+1)*128]; at+=1
        for i,d in enumerate((dq,dv)):
            bs=colsum(d[...].astype(F32))
            for q in range(2):
                quarter=2*p.th+(p.tw if q==0 else 1-p.tw)
                y=jnp.concatenate([bs[:,q*(C//2):(q+1)*(C//2)],jnp.zeros((1,256-C//2),F32)],1)
                for z in range(2):
                    vbuf[0,pl.ds(at+quarter*4+i*2+z,1),:]=y[:,z*128:(z+1)*128]
    def vector_step(i,_):
        if i>0:
            vcopy(i-1).wait_recv()
            y=vbuf[i-1]+vrecv[i-1]
            if i<len(vaxes): vbuf[i]=y
            else: vec_out[...]=y
        if i<len(vaxes): vcopy(i).start()
    part=functools.partial
    NT_=T//TT; G1=HC; G2=G1+2*NT_
    steps=[(1+HLAG*j,HSP,HC,part(head_step,j)) for j in reversed(range(last+1))]
    steps+=[(GLAG*j,2,CH,part(gather_step,j)) for j in reversed(range(n+2))]
    steps+=[(G2+3+VLAG*i,1,1,part(vector_step,i)) for i in range(len(vaxes)+1)]
    steps+=[(0,1,1,lambda _: arrived(0,5)),(0,1,HC,weight_grads),(G1,1,1,lambda _: arrived(5,6)),(G2,1,1,lambda _: arrived(6,8)),(G1,1,NT_,other_half),(G1+NT_,1,1,lambda _: ocopy().start()),(G1+NT_,1,NT_,own_half),
            (G2,1,1,lambda _: ocopy().wait_recv()),(G2+1,1,1,lambda _: tcopy().start()),(G2,1,2,norm_one_back),(G2+2,1,1,vectors)]
    run_steps(steps)
    def drain(c,_):
        chip(c,False).wait_send(); fput(c).wait()
        for k in range(K):
            for s in range(n): gat(k,s,c,False).wait_send()
        return 0
    lax.fori_loop(0,CH,drain,0)
    def hdrain(c,_):
        for k in range(HK):
            for s in range(n): hsum(k,s,c).wait_send()
            for s in backs[k]: hgat(k,s,c,False).wait_send()
        return 0
    lax.fori_loop(0,HC,hdrain,0)
    for i in range(len(vaxes)): vcopy(i).wait_send()
    ocopy().wait_send(); tcopy().wait()
    tok[1-p.tw]=trecv[...]

def finish(dp,red,dq,dk,dv,normT,wh,gwo,x,gm,gain,vec,gbu):
    T,D=x.shape; CH,fin,_=red.shape; R=FC//128*D
    plan=big_plan(dp,R); n=len(plan[0][0])
    HC=D//TT; HR=2*dq.shape[1]//128*TT; hplan=head_plan(dp,HR)
    hrecv=[]
    for order,_,rows in hplan:
        q=2
        for axis in order:
            if axis=="tw": q=1
            else: rows//=2
            hrecv.append(pltpu.VMEM((HC,q,rows,128),BF))
    V=(6*D+gbu.shape[1])//128+16; nv=n+1; args=(red,dq,dk,dv,normT,wh,gwo,x,gm,gain,vec,gbu)
    return pl.pallas_call(functools.partial(finish_kernel,dp),
      in_specs=[pl.BlockSpec(memory_space=pl.ANY if 1<=i<=8 else pltpu.VMEM) for i in range(len(args))],
      out_specs=[pl.BlockSpec(memory_space=pl.ANY)]+[pl.BlockSpec(memory_space=pltpu.VMEM)]*3,
      out_shape=[jax.ShapeDtypeStruct((CH,2,R,128),BF),jax.ShapeDtypeStruct((HC,HR,128),BF),jax.ShapeDtypeStruct((V,128),F32),jax.ShapeDtypeStruct((2,T//2,D),BF)],
      scratch_shapes=[pltpu.VMEM((CH,2,R,128),BF),pltpu.SemaphoreType.DMA((CH,))]+[pltpu.VMEM(a.shape,a.dtype) for a in args[1:9]]+[pltpu.SemaphoreType.DMA((8,)),pltpu.VMEM((HC,2,HR,128),BF),pltpu.VMEM((HC,HR,128),BF),pltpu.VMEM((nv,V,128),F32),pltpu.VMEM((nv,V,128),F32),pltpu.VMEM((T,D),F32)]+[pltpu.VMEM((T,D),BF)]*3+[pltpu.VMEM((T//2,D),BF),pltpu.VMEM((8,D),F32)]+[pltpu.SemaphoreType.DMA((2,))]*2+hrecv
        +[pltpu.SemaphoreType.DMA((len(plan),n,CH))]*2+[pltpu.SemaphoreType.DMA((CH,))]*2+[pltpu.SemaphoreType.DMA((len(hplan),n,HC))]*4+[pltpu.SemaphoreType.DMA((nv,))]*2,
      compiler_params=pltpu.CompilerParams(vmem_limit_bytes=60*2**20,collective_id=1,has_side_effects=True),name="finish_gradients")(*args)

def widen_kernel(where,chunk,heads,mine,got,vec,tok,wup,wdown,wqkv,wout,blk,tok_o,bqv,*vectors):
    D=wup.shape[0]; q=wout.shape[0]; g=pl.program_id(0); HT=D//heads.shape[0]
    for i in range(FC//128):
        cols=slice(i*128,(i+1)*128)
        wup[:,cols]=chunk[0,i*D:(i+1)*D,:].astype(F32)
        wdown[cols,:]=chunk[1,i*D:(i+1)*D,:].T.astype(F32)
    @pl.when(g==0)
    def _():
        for t in range(heads.shape[0]):
            y=jnp.concatenate([heads[t,i*HT:(i+1)*HT,:] for i in range(heads.shape[1]//HT)],1).T.astype(F32)
            rr=slice(t*HT,(t+1)*HT)
            for c in range(3): wqkv[c,:,rr]=y[c*q:(c+1)*q,:]
            wout[:,rr]=y[3*q:,:]
        blk[where[0]]=mine[...]; blk[1-where[0]]=got[...]
        tok_o[...]=tok[...]
        at=sum(v.shape[0] for v in vectors)//128
        for i in range(2):
            for z,w in ((0,128),(1,q-128)): bqv[i:i+1,z*128:z*128+w]=vec[pl.ds(at+4*where[1]+2*i+z,1),0:w]
        at=0
        for v in vectors:
            for i in range(v.shape[0]//128):
                v[i*128:(i+1)*128]=vec[at,:]; at+=1

def widen(where,chunks,heads,mine,got,vec,tok):
    CH,_,R,_=chunks.shape; D=R*128//FC; FF=CH*FC; q=heads.shape[0]*heads.shape[1]*128//(4*D); T2=mine.shape[0]
    outs=[(D,FF),(FF,D),(3,q,D),(q,D)]; sizes=[D]*6+[FF]
    res=pl.pallas_call(widen_kernel,grid=(CH,),
      in_specs=[pl.BlockSpec(memory_space=pltpu.SMEM),pl.BlockSpec((None,2,R,128),lambda g:(g,0,0,0))]+[pl.BlockSpec(a.shape,lambda g,n=a.ndim:(0,)*n) for a in (heads,mine,got,vec,tok)],
      out_specs=[pl.BlockSpec((D,FC),lambda g:(0,g)),pl.BlockSpec((FC,D),lambda g:(g,0))]+[pl.BlockSpec(memory_space=pltpu.VMEM)]*(5+len(sizes)),
      out_shape=[jax.ShapeDtypeStruct(o,F32) for o in outs]+[jax.ShapeDtypeStruct((2,T2,D),BF)]*2+[jax.ShapeDtypeStruct((2,q),F32)]+[jax.ShapeDtypeStruct((z,),F32) for z in sizes],
      compiler_params=pltpu.CompilerParams(vmem_limit_bytes=63*2**20),name="widen")(where,chunks,heads,mine,got,vec,tok)
    return res[:7],res[7:]

def front_kernel(tok,w,b,gain,shift,seg,x_o,normT_o,q_o,k_o,v_o,wh_o,mq_o,mk_o,x,norm,normT,qkv,wh,wgot,bgot,bias,mq,mk,tsem,bsem,csem,ysem,xsem,zsem,osem):
    p=Peers(); Q,D=tok.shape[1:]; T=2*Q; L=2*T; E=w.shape[1]; PART=E//4; HQ=Q//2
    b0,b1=p.bit(0),p.bit(1)
    barrier(p,["th","tw",0,1])
    def tcopy(i): return send(tok.at[1-p.tw,i*HQ:(i+1)*HQ,:],x.at[rows_at(p.tw*Q+i*HQ,HQ),:],tsem.at[0,i],tsem.at[1,i],p.peer("tw"))
    def bcopy(): return send(b,bgot,bsem.at[0],bsem.at[1],p.peer("tw"))
    def ycopy(c):
        r=rows_at((2*b1+b0)*PART,PART)
        return send(w.at[c,r,:],wgot.at[c,r,:],ysem.at[0,c],ysem.at[1,c],p.peer("tw"))
    def xcopy(c,landed):
        ref=wgot.at[c,rows_at((2*b1+(1-b0 if landed else b0))*PART,PART),:]
        return send(ref,ref,xsem.at[0,c],xsem.at[1,c],p.peer(0))
    def zcopy(c,landed):
        ref=wgot.at[c,rows_at((1-b1 if landed else b1)*2*PART,2*PART),:]
        return send(ref,ref,zsem.at[0,c],zsem.at[1,c],p.peer(1))
    def ccopy(i,landed):
        core=1-p.th if landed else p.th
        row=core*T+(p.tw*Q if i==0 else (1-p.tw)*Q+(i-1)*HQ)
        ref=norm.at[rows_at(row,Q if i==0 else HQ),:]
        return send(ref,ref,csem.at[0,i],csem.at[1,i],p.peer("th"))
    for c in range(3): ycopy(c).start()
    bcopy().start()
    for i in range(2): tcopy(i).start()
    g_row=gain[...].reshape(1,D); s_row=shift[...].reshape(1,D)
    def normalize(src,row,rows):
        for t in range(rows//HQ):
            y=(norm_parts(src(t).astype(F32))[0]*g_row+s_row).astype(BF)
            norm[rows_at(row+t*HQ,HQ),:]=y
    def put(src,dst,i): return pltpu.make_async_copy(src,dst,osem.at[i])
    x[rows_at(p.tw*Q,Q),:]=tok[p.tw]
    normalize(lambda t: tok[p.tw,t*HQ:(t+1)*HQ,:],p.th*T+p.tw*Q,Q)
    onehot=lax.broadcasted_iota(jnp.int32,(128,L),0)
    onehot=jnp.where(onehot<HD,onehot,onehot-HD)
    same=onehot==seg[pl.ds(p.tw,1),:]
    mk[...]=jnp.where(same,1.0,0.0).T.astype(BF)
    ccopy(0,False).start()
    for c in range(3):
        ycopy(c).wait_recv()
        xcopy(c,False).start()
    mq[...]=jnp.where(same|(onehot>=9),0.0,-float(2**40)).T.astype(BF)
    put(mk,mk_o,0).start(); put(mq,mq_o,1).start()
    bcopy().wait_recv()
    bias[...]=jnp.zeros_like(bias)
    for m,src in enumerate((b,bgot)):
        for i,c in enumerate((0,2)): bias[m,c:c+1,:]=src[i:i+1,:]
    for c in range(3):
        xcopy(c,True).wait_recv()
        zcopy(c,False).start()
    def project(row,weights,m,rows=Q):
        r=rows_at(row,rows)
        def one(c,_):
            y=(dot(norm[r,:],weights[c],NT)+bias[m,pl.ds(c,1),:]).astype(BF)
            y=y*jnp.where(c==0,0.125,1.0).astype(BF)
            qkv[c,r,m*E:(m+1)*E]=y
            return 0
        lax.fori_loop(0,3,one,0)
    def transpose(quarter):
        for core in range(2):
            for t in range(Q//128):
                at=core*T+quarter*Q+t*128
                normT[:,pl.ds(pl.multiple_of(at,128),128)]=norm[rows_at(at,128),:].T
    ccopy(0,True).wait_recv()
    for core in range(2): project(core*T+p.tw*Q,w,0)
    transpose(p.tw)
    for c in range(3): zcopy(c,True).wait_recv()
    for core in range(2): project(core*T+p.tw*Q,wgot,1)
    for c in range(3): wh[c,0:E,:]=w[c]; wh[c,E:2*E,:]=wgot[c]
    put(wh,wh_o,7).start()
    for i in range(2):
        row=(1-p.tw)*Q+i*HQ
        tcopy(i).wait_recv()
        normalize(lambda t: x[rows_at(row,HQ),:],p.th*T+row,HQ)
        if i==1: put(x,x_o,2).start()
        for m,weights in enumerate((w,wgot)):
            project(p.th*T+row,weights,m,HQ)
            if m==0: ccopy(1+i,False).start()
        ccopy(1+i,True).wait_recv()
        for m,weights in enumerate((w,wgot)): project((1-p.th)*T+row,weights,m,HQ)
    for c in range(3): put(qkv.at[c],(q_o,k_o,v_o)[c],4+c).start()
    transpose(1-p.tw)
    put(normT,normT_o,3).start()
    for src,dst,i in ((mk,mk_o,0),(mq,mq_o,1),(x,x_o,2),(normT,normT_o,3),(wh,wh_o,7)): put(src,dst,i).wait()
    for c in range(3):
        put(qkv.at[c],(q_o,k_o,v_o)[c],4+c).wait()
        ycopy(c).wait_send(); xcopy(c,False).wait_send(); zcopy(c,False).wait_send()
    bcopy().wait_send()
    for i in range(2): tcopy(i).wait_send()
    for i in range(3): ccopy(i,False).wait_send()

def front(tok,w,b,gain,shift,seg):
    _,Q,D=tok.shape; T=2*Q; L=2*T; E=w.shape[1]
    outs=[((T,D),BF),((D,L),BF)]+[((L,2*E),BF)]*3+[((3,2*E,D),BF)]+[((L,128),BF)]*2
    sem=pltpu.SemaphoreType.DMA
    return pl.pallas_call(front_kernel,
      in_specs=[pl.BlockSpec(memory_space=pltpu.VMEM)]*6,out_specs=[pl.BlockSpec(memory_space=pl.ANY)]*len(outs),
      out_shape=[jax.ShapeDtypeStruct(*o) for o in outs],
      scratch_shapes=[pltpu.VMEM((T,D),BF),pltpu.VMEM((L,D),BF),pltpu.VMEM((D,L),BF),pltpu.VMEM((3,L,2*E),BF),pltpu.VMEM((3,2*E,D),BF),pltpu.VMEM((3,E,D),BF),
        pltpu.VMEM(b.shape,F32),pltpu.VMEM((2,8,E),F32),pltpu.VMEM((L,128),BF),pltpu.VMEM((L,128),BF),sem((2,2)),sem((2,)),sem((2,3)),sem((2,3)),sem((2,3)),sem((2,3)),sem((8,))],
      compiler_params=pltpu.CompilerParams(vmem_limit_bytes=60*2**20,collective_id=2,has_side_effects=True),name="front")(tok,w,b,gain,shift,seg)


SWAP = [(0, 1), (1, 0)]


def swap(value, axis):
    return lax.ppermute(value, axis, SWAP)


def body(
    dp_size,
    tokens,
    segment_ids,
    norm1_gain,
    norm1_shift,
    w_qkv,
    b_qv,
    w_out,
    b_out,
    norm2_gain,
    norm2_shift,
    w_up,
    b_up,
    w_down,
    b_down,
    cotangent,
):
    th, tw = lax.axis_index("th"), lax.axis_index("tw")
    x, normed_t, query, key, value, w_heads, mq, mk = front(
        tokens, w_qkv.transpose(0, 2, 1), b_qv, norm1_gain, norm1_shift, segment_ids
    )
    tables = (mq, mk, *block_ranges(lax.dynamic_index_in_dim(segment_ids, tw, 0, False)))
    later = lax.optimization_barrier((cotangent, w_out, query))
    cot_got = swap(lax.dynamic_index_in_dim(later[0], 1 - tw, 0, False), "tw")
    w_out_got = swap(later[1], "tw")
    attended, totals = attn_fwd(query, key, value, *tables)
    out_mine, out_other, grad_middle, grad_b_up, sums, red, grad_heads, grad_w_out = ffn(
        dp_size, attended, x, b_out, norm2_gain, norm2_shift, b_down, w_out, w_out_got, cotangent, cot_got, w_up, w_down, b_up[None]
    )
    out_got = swap(out_other, "tw")
    dq, dk, dv = attn_bwd(query, key, value, grad_heads, attended, totals, *tables)
    chunks, heads, small, grad_tokens = finish(
        dp_size, red, dq, dk, dv, normed_t, w_heads, grad_w_out, x, grad_middle, norm1_gain, sums, grad_b_up
    )
    where = jnp.stack([tw, 2 * th + tw]).astype(jnp.int32)
    (up, down, w_qkv_grad, w_out_grad, block_out, grad_tokens, b_qv_grad), vecs = widen(
        where, chunks, heads, out_mine, out_got, small, grad_tokens
    )
    return (
        block_out,
        grad_tokens,
        vecs[0],
        vecs[1],
        w_qkv_grad.transpose(0, 2, 1),
        b_qv_grad,
        w_out_grad,
        vecs[2],
        vecs[3],
        vecs[4],
        up,
        vecs[6],
        down,
        vecs[5],
    )


def solution(mesh):
    return jax.shard_map(
        functools.partial(body, mesh.shape["dp"]),
        mesh=mesh,
        in_specs=(
            P("dp", ("th", "tw"), None),
            P("dp", None),
            P(),
            P(),
            P(None, None, ("th", "tw")),
            P(None, ("th", "tw")),
            P(("th", "tw"), None),
            P(),
            P(),
            P(),
            P(),
            P(),
            P(),
            P(),
            P("dp", ("th", "tw"), None),
        ),
        out_specs=(
            P("dp", ("th", "tw"), None),
            P("dp", ("th", "tw"), None),
            P(),
            P(),
            P(None, None, ("th", "tw")),
            P(None, ("th", "tw")),
            P(("th", "tw"), None),
            P(),
            P(),
            P(),
            P(),
            P(),
            P(),
            P(),
        ),
        check_vma=False,
    )
```

```python
import functools

import jax
import jax.numpy as jnp
from jax import lax
from jax.experimental import pallas as pl
from jax.experimental.pallas import tpu as pltpu
from jax.sharding import PartitionSpec as P

NT=(((1,),(1,)),((),())); NN=(((1,),(0,)),((),())); TN=(((0,),(0,)),((),()))
F32=jnp.float32; BF=jnp.bfloat16
BQ=256; BK=256; HD=64
def dot(a,b,d): return lax.dot_general(a,b,d,preferred_element_type=F32)

AL=128; VR=80; GRP=3
def each_chunk(lo_ref,n_ref,i,body):
    lo=lo_ref[i]; n=n_ref[i]
    def full(j,_):
        body(pl.ds(pl.multiple_of(lo+j*BK,AL),BK))
        return 0
    lax.fori_loop(0,n//2,full,0)
    @pl.when(n%2==1)
    def _(): body(pl.ds(pl.multiple_of(lo+n//2*BK,AL),AL))

def fwd_kernel(lo_ref, n_ref, q_ref, k_ref, v_ref, mq_ref, mk_ref, o_ref, lse_ref, m_ref, acc_ref, vT_ref, qm_ref):
    i=pl.program_id(0); H=q_ref.shape[1]//HD
    lane=lax.broadcasted_iota(jnp.int32,(1,128),1)
    halves=(lane<HD, lane>=HD)
    @pl.when(i==0)
    def _():
        row=lax.broadcasted_iota(jnp.int32,(VR-HD,v_ref.shape[0]),0)
        for p in range(H//2):
            t=v_ref[:,p*128:(p+1)*128].T
            for e in range(2):
                vT_ref[2*p+e,0:HD,:]=t[e*HD:(e+1)*HD,:]
                vT_ref[2*p+e,HD:VR,:]=jnp.where(row==0,1.0,0.0).astype(BF)
    m_ref[...]=jnp.full(m_ref.shape,-1e30,F32)
    acc_ref[...]=jnp.zeros_like(acc_ref)
    for h in range(H): qm_ref[h]=jnp.where(halves[h%2],q_ref[:,h//2*128:h//2*128+128],mq_ref[...])
    def score(h,ks,mk):
        cols=slice(h//2*128,h//2*128+128)
        return dot(jnp.where(halves[h%2],k_ref[ks,cols],mk),qm_ref[h],NT)
    def soft(h,s):
        m_old=m_ref[h:h+1,:]
        m_new=jnp.maximum(m_old,jnp.max(s,axis=0,keepdims=True))
        m_ref[h:h+1,:]=m_new
        return jnp.exp(s-m_new).astype(BF),jnp.exp(m_old-m_new)
    def weigh(h,ks,pe,alpha):
        acc_ref[h]=acc_ref[h]*alpha+dot(vT_ref[h,:,ks],pe,NN)
    def body(ks):
        mk=mk_ref[ks,:]
        scores=[score(h,ks,mk) for h in range(H)]
        probs=[soft(h,scores[h]) for h in range(H)]
        for h in range(H): weigh(h,ks,*probs[h])
    each_chunk(lo_ref,n_ref,i,body)
    for p in range(H//2):
        parts=[acc_ref[h,0:HD,:]*(1.0/acc_ref[h,HD:HD+1,:]) for h in (2*p,2*p+1)]
        o_ref[:,p*128:(p+1)*128]=jnp.concatenate(parts,0).T.astype(BF)
    for h in range(H): lse_ref[h:h+1,:]=m_ref[h:h+1,:]+jnp.log(acc_ref[h,HD:HD+1,:])
    lse_ref[H:,:]=jnp.zeros((lse_ref.shape[0]-H,BQ),F32)

def attn_fwd(q,k,v,mq,mk,lo,n):
    L,C=q.shape
    return pl.pallas_call(fwd_kernel,
        grid_spec=pltpu.PrefetchScalarGridSpec(num_scalar_prefetch=2,grid=(L//BQ,),
          in_specs=[pl.BlockSpec((BQ,C),lambda i,*_:(i,0)),pl.BlockSpec((L,C),lambda i,*_:(0,0)),pl.BlockSpec((L,C),lambda i,*_:(0,0)),
                    pl.BlockSpec((BQ,128),lambda i,*_:(i,0)),pl.BlockSpec((L,128),lambda i,*_:(0,0))],
          out_specs=[pl.BlockSpec((BQ,C),lambda i,*_:(i,0)),pl.BlockSpec((8,BQ),lambda i,*_:(0,i))],
          scratch_shapes=[pltpu.VMEM((8,BQ),F32),pltpu.VMEM((C//HD,VR,BQ),F32),pltpu.VMEM((C//HD,VR,L),BF),pltpu.VMEM((C//HD,BQ,128),BF)]),
        out_shape=[jax.ShapeDtypeStruct((L,C),BF),jax.ShapeDtypeStruct((8,L),F32)],
        name="attention_forward",
    )(lo,n,q,k,v,mq,mk)

def bwd_kernel(lo_ref, n_ref, q_ref, k_ref, v_ref, do_ref, o_ref, lse_ref, mq_ref, mk_ref, dq_ref, dk_ref, dv_ref, dk_acc, dv_acc, dq_acc, qcat, docat, qm, kT):
    i=pl.program_id(0); n=pl.num_programs(0)
    C=q_ref.shape[1]; pairs=C//128
    lane=lax.broadcasted_iota(jnp.int32,(1,128),1)
    halves=(lane<HD, lane>=HD)
    @pl.when(i==0)
    def _():
        dk_acc[...]=jnp.zeros_like(dk_acc); dv_acc[...]=jnp.zeros_like(dv_acc)
        kT[...]=k_ref[...].T
    dq_acc[...]=jnp.zeros_like(dq_acc)
    sel=(lax.broadcasted_iota(jnp.int32,(8,C),1)//HD==lax.broadcasted_iota(jnp.int32,(8,C),0)).astype(BF)
    prod=do_ref[...].astype(F32)*o_ref[...].astype(F32)
    high=prod.astype(BF)
    delta=dot(sel,high,NT)+dot(sel,(prod-high.astype(F32)).astype(BF),NT)
    for p in range(pairs):
        cols=slice(p*128,(p+1)*128)
        for e in range(2):
            q2=q_ref[:,cols]; d2=do_ref[:,cols]
            qcat[p,e*BQ:(e+1)*BQ,:]=jnp.where(halves[e],q2,jnp.zeros_like(q2))
            qm[p,e*BQ:(e+1)*BQ,:]=jnp.where(halves[e],q2,mq_ref[...])
            docat[p,e*BQ:(e+1)*BQ,:]=jnp.where(halves[e],d2,jnp.zeros_like(d2))
    lse=lse_ref[...]
    def body(ks):
        mk=mk_ref[ks,:]
        for g in range(0,pairs,GRP):
            work=[]
            for p in range(g,g+GRP):
                cols=slice(p*128,(p+1)*128)
                k2=k_ref[ks,cols]; v2=v_ref[ks,cols]; d2=do_ref[:,cols]
                for e in range(2):
                    s=dot(jnp.where(halves[e],k2,mk),qm[p,e*BQ:(e+1)*BQ,:],NT)
                    work.append((s,dot(jnp.where(halves[e],v2,jnp.zeros_like(v2)),d2,NT)))
            out=[]
            for t,(s,dp) in enumerate(work):
                h=2*g+t
                pr=jnp.exp(s-lse[h:h+1,:])
                out.append((pr.astype(BF),(pr*(dp-delta[h:h+1,:])).astype(BF)))
            for p in range(g,g+GRP):
                cols=slice(p*128,(p+1)*128); k2=k_ref[ks,cols]
                (p0,d0),(p1,d1)=out[2*(p-g):2*(p-g)+2]
                dv_acc[ks,cols]+=dot(jnp.concatenate([p0,p1],1),docat[p],NN)
                dk_acc[ks,cols]+=dot(jnp.concatenate([d0,d1],1),qcat[p],NN)
                for e,d in enumerate((d0,d1)):
                    r=slice((2*p+e)*HD,(2*p+e+1)*HD)
                    dq_acc[r,:]+=dot(kT[r,ks],d,NN)
    each_chunk(lo_ref,n_ref,i,body)
    dq_ref[...]=(dq_acc[...]*0.125).T.astype(BF)
    @pl.when(i==n-1)
    def _():
        dk_ref[...]=dk_acc[...].astype(BF); dv_ref[...]=dv_acc[...].astype(BF)

def attn_bwd(q,k,v,do,o,lse,mq,mk,lo,n):
    L,C=q.shape
    blk=pl.BlockSpec((BQ,C),lambda i,*_:(i,0)); full=pl.BlockSpec((L,C),lambda i,*_:(0,0))
    return pl.pallas_call(bwd_kernel,
        grid_spec=pltpu.PrefetchScalarGridSpec(num_scalar_prefetch=2,grid=(L//BQ,),
          in_specs=[blk,full,full,blk,blk,pl.BlockSpec((8,BQ),lambda i,*_:(0,i)),pl.BlockSpec((BQ,128),lambda i,*_:(i,0)),pl.BlockSpec((L,128),lambda i,*_:(0,0))],
          out_specs=[blk,full,full],
          scratch_shapes=[pltpu.VMEM((L,C),F32),pltpu.VMEM((L,C),F32),pltpu.VMEM((C,BQ),F32),pltpu.VMEM((C//128,2*BQ,128),BF),pltpu.VMEM((C//128,2*BQ,128),BF),pltpu.VMEM((C//128,2*BQ,128),BF),pltpu.VMEM((C,L),BF)]),
        out_shape=[jax.ShapeDtypeStruct((L,C),BF)]*3,
        name="attention_backward",
    )(lo,n,q,k,v,do,o,lse,mq,mk)

def block_ranges(seg):
    first=seg[::BQ]; last=seg[BQ-1::BQ]
    lo=jnp.sum(seg[None,:]<first[:,None],axis=1,dtype=jnp.int32)//AL*AL
    hi=jnp.sum(seg[None,:]<=last[:,None],axis=1,dtype=jnp.int32)
    return lo,(hi-lo+AL-1)//AL


TT=256; FC=512
LAG=2; GLAG=5; HLAG=4; HSP=2; GSP=4; VLAG=5; FL=3

def bits_of(dp): return dp.bit_length()-1

def big_plan(dp,rows):
    n=bits_of(dp)
    orders=(["tw"]+list(range(n)),[0,"tw"]+list(range(1,n)),[1,2,0,"tw"]+list(range(3,n)))
    unit=16<<(n+1)
    units=rows//unit
    third=max(1,units//4)
    shares=[units-units//3-third,units//3,third]
    return streams(orders,shares,unit)

def head_plan(dp,rows):
    n=bits_of(dp)
    orders=(["tw"]+list(range(n)),[0,"tw"]+list(range(1,n)),[1,2,0,"tw"]+list(range(3,n)))
    unit=16<<n
    units=rows//unit
    low=max(1,units//4)
    mid=max(1,units//3)
    return streams(orders,[units-mid-low,mid,low],unit)

def streams(orders,shares,unit):
    out=[]; start=0
    for order,share in zip(orders,shares):
        out.append((order,start,share*unit)); start+=share*unit
    return out

class Peers:
    def __init__(self):
        self.dp=lax.axis_index("dp"); self.th=lax.axis_index("th"); self.tw=lax.axis_index("tw")
    def bit(self,axis):
        return self.tw if axis=="tw" else (self.dp//(1<<axis))%2
    def peer(self,axis):
        if axis=="tw": return {"tw":1-self.tw}
        if axis=="th": return {"th":1-self.th}
        return {"dp":self.dp+(1-2*self.bit(axis))*(1<<axis)}

def send(src,dst,ssem,rsem,peer):
    return pltpu.make_async_remote_copy(src,dst,ssem,rsem,device_id=peer,device_id_type=pl.DeviceIdType.MESH)

def barrier(p,axes):
    sem=pltpu.get_barrier_semaphore()
    for a in axes:
        pl.semaphore_signal(sem,inc=1,device_id=p.peer(a),device_id_type=pl.DeviceIdType.MESH)
    pl.semaphore_wait(sem,len(axes))

def halves(p,order,row,rows,keep_tw=False):
    out=[]
    for axis in order:
        if keep_tw and axis=="tw": out.append((row,row,rows)); continue
        rows//=2; bit=p.bit(axis)
        out.append((row+(1-bit)*rows,row+bit*rows,rows)); row=row+bit*rows
    return out
def run_steps(steps):
    total=max(f+sp*(cnt-1) for f,sp,cnt,_ in steps)+1
    def body(i,_):
        for r in range(2):
            g=2*i+r
            for f,sp,cnt,what in steps:
                if sp==2:
                    if f%2!=r: continue
                    c=i-f//2
                else: c=g-f
                if cnt==1:
                    pl.when(c==0)(functools.partial(what,0))
                else: pl.when((c>=0)&(c<cnt))(functools.partial(what,c))
        return 0
    lax.fori_loop(0,(total+1)//2,body,0)
def al(x): return x if isinstance(x,int) else pl.multiple_of(x,16)
def rows_at(row,n): return pl.ds(al(row),n)

EPS=1e-06
def norm_parts(x):
    mean=jnp.mean(x,axis=-1,keepdims=True)
    cen=x-mean
    r=lax.rsqrt(jnp.mean(cen*cen,axis=-1,keepdims=True)+EPS)
    return cen*r,r
def norm_back(e,n,r,gain):
    t=e*gain
    return r*(t-jnp.mean(t,axis=-1,keepdims=True)-n*jnp.mean(t*n,axis=-1,keepdims=True))
def colsum(x): return jnp.sum(x,axis=0,keepdims=True)

def ffn_kernel(dp,att,x,vb,vg,vs,vd,wo_h,wo_got,cot_h,cot_got,wu_h,wd_h,bu,mine,other,gm,gb,vec,red,gheads,gwo,
               wo,cot,lsem,wu,wd,cotT,mid,n2,n2T,obuf,orecv,grow,act,gh,dw,chip_recv,wsem,osem,gsem,*rest):
    CH=dw.shape[0]; T,D=x.shape; SLOTS=chip_recv.shape[0]
    plan=big_plan(dp,dw.shape[2]); n=len(plan[0][0]); K=len(plan)
    recv=[rest[k*n:(k+1)*n] for k in range(K)]
    send_sem,recv_sem,chip_send,chip_got=rest[K*n:]
    p=Peers()
    b_row,g_row,s_row,d_row=[v[...].reshape(1,D) for v in (vb,vg,vs,vd)]
    tiles=[slice(t*TT,(t+1)*TT) for t in range(T//TT)]; NT_=len(tiles)
    regs=[halves(p,*s) for s in plan]
    def copy(k,s,c):
        out,_,nr=regs[k][s]
        return send(dw.at[c,p.th,rows_at(out,nr),:],recv[k][s].at[c],send_sem.at[k,s,c],recv_sem.at[k,s,c],p.peer(plan[k][0][s]))
    def chip_copy(c):
        return send(dw.at[c,1-p.th],chip_recv.at[c%SLOTS],chip_send.at[c],chip_got.at[c],p.peer("th"))
    def ocopy(): return send(obuf,orecv,osem.at[0],osem.at[1],p.peer("th"))
    def gcopy(landed):
        ref=grow.at[rows_at((1-p.th if landed else p.th)*T,T),:]
        return send(ref,ref,gsem.at[0],gsem.at[1],p.peer("th"))
    def wload(c):
        return (pltpu.make_async_copy(wu_h.at[:,pl.ds(pl.multiple_of(c*FC,FC),FC)],wu.at[c],wsem.at[0,c]),
                pltpu.make_async_copy(wd_h.at[pl.ds(pl.multiple_of(c*FC,FC),FC),:],wd.at[c],wsem.at[1,c]))
    E=wo_h.shape[0]; Q=T//2
    loads=[pltpu.make_async_copy(a,b,lsem.at[i]) for i,(a,b) in enumerate(((wo_h,wo.at[0:E,:]),(wo_got,wo.at[E:2*E,:]),
        (cot_h.at[p.tw],cot.at[rows_at(p.tw*Q,Q),:]),(cot_got,cot.at[rows_at((1-p.tw)*Q,Q),:])))]
    for l in loads: l.start()
    def load(c,_):
        for w in wload(c): w.start()
        return 0
    lax.fori_loop(0,CH,load,0)
    barrier(p,["th"]+plan[0][0])
    for l in loads[:2]: l.wait()
    for r in tiles:
        obuf[r,:]=dot(att[rows_at((1-p.th)*T+r.start,TT),:],wo[...],NN).astype(BF)
    for l in loads[2:]: l.wait()
    for t,r in enumerate(tiles):
        mid[r,:]=x[r,:].astype(F32)+dot(att[rows_at(p.th*T+r.start,TT),:],wo[...],NN)+b_row
        if t==0: ocopy().start()
        cotT[:,r]=cot[r,:].T
    ocopy().wait_recv()
    for r in tiles:
        m=mid[r,:]+orecv[r,:].astype(F32)
        mid[r,:]=m
        nn,_=norm_parts(m)
        y=(nn*g_row+s_row).astype(BF)
        n2[r,:]=y; n2T[:,r]=y.T
    vec[...]=jnp.zeros_like(vec)
    def sum_step(s,c):
        news=[]
        for k in range(K):
            copy(k,s,c).wait_recv()
            _,kr,nr=regs[k][s]
            at=(c,p.th,rows_at(kr,nr),slice(None))
            new=(dw[at].astype(F32)+recv[k][s][c].astype(F32)).astype(BF)
            if s<n-1: dw[at]=new
            else: news.append((kr,nr,new))
        if s<n-1:
            for k in range(K): copy(k,s+1,c).start()
        else:
            out=0
            for kr,nr,new in news:
                red[c,out:out+nr,:]=new; out+=nr
    def chip_sum(c):
        chip_copy(c).wait_recv()
        def add(q,_):
            r=rows_at(q*TT,TT)
            dw[c,p.th,r,:]=(dw[c,p.th,r,:].astype(F32)+chip_recv[c%SLOTS,r,:].astype(F32)).astype(BF)
            return 0
        lax.fori_loop(0,dw.shape[2]//TT,add,0)
        for k in range(K): copy(k,0,c).start()
    def hidden(c):
        for w in wload(c): w.wait()
        cols=pl.ds(pl.multiple_of(c*FC,FC),FC)
        gsum=jnp.zeros((1,FC),F32)
        for r in tiles:
            h=dot(n2[r,:],wu[c],NN)+bu[:,cols]
            ga=dot(cot[r,:],wd[c],NT)
            cdf=0.5*(1.0+lax.erf(h*(0.5**0.5)))
            a=(h*cdf).astype(BF)
            gr=(ga*(cdf+h*(jnp.exp(h*h*-0.5)*0.3989422804014327))).astype(BF)
            act[c,r,:]=a; gh[c,r,:]=gr
            gsum+=colsum(gr.astype(F32))
        gb[:,cols]=gsum
    def weight_grads(c):
        for t in range(D//TT):
            r=slice(t*TT,(t+1)*TT)
            for m,(lhs,rhs) in enumerate(((n2T,gh),(cotT,act))):
                y=dot(lhs[r,:],rhs[c],NN).astype(BF)
                for q in range(FC//128): dw[c,m,q*D+t*TT:q*D+(t+1)*TT,:]=y[:,q*128:(q+1)*128]
    def norm_two_back(t):
        r=rows_at(t*TT,TT)
        e=dot(gh[0,r,:],wu[0],NT)
        for c in range(1,CH): e+=dot(gh[c,r,:],wu[c],NT)
        nn,rs=norm_parts(mid[r,:])
        ct=cot[r,:].astype(F32)
        gmid=ct+norm_back(e,nn,rs,g_row)
        gm[r,:]=gmid
        gbr=gmid.astype(BF)
        grow[rows_at(p.th*T+t*TT,TT),:]=gbr
        vec[0:1,:]+=colsum(gbr.astype(F32)); vec[1:2,:]+=colsum(e*nn); vec[2:3,:]+=colsum(e); vec[3:4,:]+=colsum(ct)
    def block_out(t):
        r=rows_at(t*TT,TT)
        y=mid[r,:]+d_row
        for c in range(CH): y+=dot(act[c,r,:],wd[c],NN)
        n2[r,:]=y.astype(BF)
    def split_out(_):
        gcopy(True).wait_recv()
        mine[...]=n2[rows_at(p.tw*(T//2),T//2),:]
        other[...]=n2[rows_at((1-p.tw)*(T//2),T//2),:]
    def grad_heads(u):
        for t in range(NT_):
            r=rows_at(u*T+t*TT,TT)
            gheads[r,:]=dot(grow[r,:],wo[...],NT).astype(BF)
    def grad_wo(_):
        for t in range(D//TT):
            r=slice(t*TT,(t+1)*TT)
            gwo[r,:]=dot(grow[:,r],att[...],TN).astype(BF)
    P2=2*CH; P3=P2+NT_; P4=P3+NT_
    part=functools.partial
    steps=[(3+FL*(s+1),2,CH,part(sum_step,s)) for s in reversed(range(n))]
    steps+=[(3,2,CH,chip_sum),(2,2,CH,lambda c: chip_copy(c).start())]
    steps+=[(0,2,CH,hidden),(1,2,CH,weight_grads),(P2,1,NT_,norm_two_back),(P3,1,1,lambda _: gcopy(False).start()),(P3,1,NT_,block_out),
            (P4,1,1,split_out),(P4,1,2,grad_heads),(P4+2,1,1,grad_wo)]
    run_steps(steps)
    ocopy().wait_send(); gcopy(False).wait_send()
    def drain(c,_):
        chip_copy(c).wait_send()
        for k in range(K):
            for s in range(n): copy(k,s,c).wait_send()
        return 0
    lax.fori_loop(0,CH,drain,0)

def whole(shape):
    return pl.BlockSpec(memory_space=pltpu.VMEM)

def ffn(dp,att,x,vb,vg,vs,vd,wo,wo_got,cot,cot_got,wu,wd,bu):
    T,D=x.shape; FF=wu.shape[1]; CH=FF//FC; R=FC//128*D; C=att.shape[1]
    plan=big_plan(dp,R); n=len(plan[0][0])
    fin=R>>n
    recv=[pltpu.VMEM((CH,rows>>(s+1),128),BF) for _,_,rows in plan for s in range(n)]
    outs=[((T//2,D),BF),((T//2,D),BF),((T,D),F32),((1,FF),F32),((8,D),F32),((CH,fin,128),BF),((2*T,C),BF),((D,C),BF)]
    specs=[whole(o[0]) for o in outs]
    hbm=pl.BlockSpec(memory_space=pl.ANY)
    V=pltpu.VMEM; sem=pltpu.SemaphoreType.DMA
    return pl.pallas_call(functools.partial(ffn_kernel,dp),
      in_specs=[whole(v.shape) for v in (att,x,vb,vg,vs,vd)]+[hbm]*6+[whole(bu.shape)],
      out_specs=specs,out_shape=[jax.ShapeDtypeStruct(*o) for o in outs],
      scratch_shapes=[V((C,D),BF),V((T,D),BF),sem((4,)),V((CH,D,FC),BF),V((CH,FC,D),BF),V((D,T),BF),V((T,D),F32),V((T,D),BF),V((D,T),BF),V((T,D),BF),V((T,D),BF),V((2*T,D),BF),
          V((CH,T,FC),BF),V((CH,T,FC),BF),V((CH,2,R,128),BF),V((3,R,128),BF),sem((2,CH)),sem((2,)),sem((2,))]+recv
        +[sem((len(plan),n,CH))]*2+[sem((CH,))]*2,
      compiler_params=pltpu.CompilerParams(vmem_limit_bytes=63*2**20+2**19,collective_id=0,has_side_effects=True),name="feed_forward")(att,x,vb,vg,vs,vd,wo,wo_got,cot,cot_got,wu,wd,bu)

def finish_kernel(dp,red,dq_h,dk_h,dv_h,normT_h,wh_h,gwo_h,x_h,gm_h,gain,vec,gbu,gathered,heads_out,vec_out,tok,full,fsem,dq,dk,dv,normT,wh,gwo,x,gm,isem,hp,hg,vbuf,vrecv,own,obuf,orecv,tbuf,trecv,vrow,osem,tsem,*rest):
    CH=full.shape[0]; R=full.shape[2]; T,D=x.shape; C=dq.shape[1]; Q=T//2
    plan=big_plan(dp,R); n=len(plan[0][0]); K=len(plan)
    HR=hp.shape[2]; hplan=head_plan(dp,HR); HK=len(hplan); HC=hp.shape[0]
    hrecv=[rest[k*n:(k+1)*n] for k in range(HK)]
    send_sem,recv_sem,chip_send,chip_got,hs_sem,hr_sem,ha_send,ha_recv,vs_sem,vr_sem=rest[HK*n:]
    p=Peers()
    regs=[halves(p,*s) for s in plan]
    hregs=[halves(p,*s,keep_tw=True) for s in hplan]
    def gat(k,s,c,landed):
        other,mine,nr=regs[k][s]
        ref=full.at[c,p.th,rows_at(other if landed else mine,nr),:]
        return send(ref,ref,send_sem.at[k,s,c],recv_sem.at[k,s,c],p.peer(plan[k][0][s]))
    def chip(c,landed):
        ref=full.at[c,1-p.th if landed else p.th]
        return send(ref,ref,chip_send.at[c],chip_got.at[c],p.peer("th"))
    def fput(c): return pltpu.make_async_copy(full.at[c],gathered.at[c],fsem.at[c])
    def hsum(k,s,c):
        order=hplan[k][0]; other,_,nr=hregs[k][s]
        if order[s]=="tw": src=hp.at[c,pl.ds(1,1),rows_at(other,nr),:]
        elif order.index("tw")>s: src=hp.at[c,:,rows_at(other,nr),:]
        else: src=hp.at[c,pl.ds(0,1),rows_at(other,nr),:]
        return send(src,hrecv[k][s].at[c],hs_sem.at[k,s,c],hr_sem.at[k,s,c],p.peer(order[s]))
    def hgat(k,s,c,landed):
        order=hplan[k][0]; other,mine,nr=hregs[k][s]
        ref=hg.at[c,rows_at(other if landed else mine,nr),:]
        return send(ref,ref,ha_send.at[k,s,c],ha_recv.at[k,s,c],p.peer(order[s]))
    backs=[[s for s in reversed(range(n)) if o[s]!="tw"] for o,_,_ in hplan]
    vaxes=["th","tw"]+list(range(n-1))
    def vcopy(i): return send(vbuf.at[i],vrecv.at[i],vs_sem.at[i],vr_sem.at[i],p.peer(vaxes[i]))
    def ocopy(): return send(obuf,orecv,osem.at[0],osem.at[1],p.peer("th"))
    def tcopy(): return send(tbuf.at[rows_at((1-p.tw)*Q,Q),:],trecv,tsem.at[0],tsem.at[1],p.peer("tw"))
    loads=[pltpu.make_async_copy(a,b,isem.at[i]) for i,(a,b) in enumerate(((normT_h,normT),(dq_h,dq),(dk_h,dk),(dv_h,dv),(gwo_h,gwo),(wh_h,wh),(x_h,x),(gm_h,gm)))]
    for l in loads: l.start()
    def arrived(a,b):
        for l in loads[a:b]: l.wait()
    out=0
    for k in range(K):
        _,kr,nr=regs[k][n-1]
        for c in range(CH): full[c,p.th,rows_at(kr,nr),:]=red[c,out:out+nr,:]
        out+=nr
    vbuf[0]=jnp.zeros(vbuf.shape[1:],F32)
    vrow[...]=jnp.zeros(vrow.shape,F32)
    barrier(p,["th"]+plan[0][0])
    last=n+n-1
    def head_step(j,c):
        for k in range(HK):
            order=hplan[k][0]
            if 0<j<=n:
                s=j-1
                hsum(k,s,c).wait_recv()
                _,kr,nr=hregs[k][s]
                q=slice(0,2) if order.index("tw")>s else slice(0,1)
                at=(c,q,rows_at(kr,nr),slice(None))
                new=(hp[at].astype(F32)+hrecv[k][s][c].astype(F32)).astype(BF)
                if j<n: hp[at]=new
                else: hg[c,rows_at(kr,nr),:]=new[0]
            elif j>n: hgat(k,backs[k][j-n-1],c,True).wait_recv()
        for k in range(HK):
            if j<n: hsum(k,j,c).start()
            elif j<last: hgat(k,backs[k][j-n],c,False).start()
        if j==last: heads_out[c]=hg[c]
    def gather_step(j,c):
        if 0<j<=n:
            for k in range(K): gat(k,n-j,c,True).wait_recv()
        if j<n:
            for k in range(K): gat(k,n-1-j,c,False).start()
        elif j==n: chip(c,False).start()
        else:
            chip(c,True).wait_recv()
            fput(c).start()
    HT=D//HC
    def weight_grads(t):
        r=rows_at(t*HT,HT)
        parts=[dot(normT[r,:],d[...],NN).astype(BF) for d in (dq,dk,dv)]+[gwo[r,:]]
        for q in range(2):
            y=jnp.concatenate([z[:,q*(C//2):(q+1)*(C//2)] for z in parts],1)
            for i in range(y.shape[1]//128): hp[t,q,i*HT:(i+1)*HT,:]=y[:,i*128:(i+1)*128]
    def norm_grad(core,t):
        rr=rows_at(core*T+t*TT,TT)
        return dot(dq[rr,:],wh[0],NN)+dot(dk[rr,:],wh[1],NN)+dot(dv[rr,:],wh[2],NN)
    def other_half(t): obuf[rows_at(t*TT,TT),:]=norm_grad(1-p.th,t).astype(BF)
    def own_half(t): own[rows_at(t*TT,TT),:]=norm_grad(p.th,t)
    def norm_one_back(i):
        quarter=(1-i)*(1-p.tw)+i*p.tw
        for t in range(Q//128):
            r=rows_at(quarter*Q+t*128,128)
            e=own[r,:]+orecv[r,:].astype(F32)
            nn,rs=norm_parts(x[r,:].astype(F32))
            tbuf[r,:]=(gm[r,:]+norm_back(e,nn,rs,gain[...].reshape(1,D))).astype(BF)
            vrow[0:1,:]+=colsum(e*nn); vrow[1:2,:]+=colsum(e)
    def vectors(_):
        tok[p.tw]=tbuf[rows_at(p.tw*Q,Q),:]
        rows=[vrow[0:1,:],vrow[1:2,:]]+[vec[i:i+1,:] for i in range(4)]+[gbu[...]]
        at=0
        for v in rows:
            for i in range(v.shape[1]//128):
                vbuf[0,at:at+1,:]=v[:,i*128:(i+1)*128]; at+=1
        for i,d in enumerate((dq,dv)):
            bs=colsum(d[...].astype(F32))
            for q in range(2):
                quarter=2*p.th+(p.tw if q==0 else 1-p.tw)
                y=jnp.concatenate([bs[:,q*(C//2):(q+1)*(C//2)],jnp.zeros((1,256-C//2),F32)],1)
                for z in range(2):
                    vbuf[0,pl.ds(at+quarter*4+i*2+z,1),:]=y[:,z*128:(z+1)*128]
    def vector_step(i,_):
        if i>0:
            vcopy(i-1).wait_recv()
            y=vbuf[i-1]+vrecv[i-1]
            if i<len(vaxes): vbuf[i]=y
            else: vec_out[...]=y
        if i<len(vaxes): vcopy(i).start()
    part=functools.partial
    NT_=T//TT; G1=HC; G2=G1+2*NT_
    steps=[(1+HLAG*j,HSP,HC,part(head_step,j)) for j in reversed(range(last+1))]
    steps+=[(GLAG*j,2,CH,part(gather_step,j)) for j in reversed(range(n+2))]
    steps+=[(G2+3+VLAG*i,1,1,part(vector_step,i)) for i in range(len(vaxes)+1)]
    steps+=[(0,1,1,lambda _: arrived(0,5)),(0,1,HC,weight_grads),(G1,1,1,lambda _: arrived(5,6)),(G2,1,1,lambda _: arrived(6,8)),(G1,1,NT_,other_half),(G1+NT_,1,1,lambda _: ocopy().start()),(G1+NT_,1,NT_,own_half),
            (G2,1,1,lambda _: ocopy().wait_recv()),(G2+1,1,1,lambda _: tcopy().start()),(G2,1,2,norm_one_back),(G2+2,1,1,vectors)]
    run_steps(steps)
    def drain(c,_):
        chip(c,False).wait_send(); fput(c).wait()
        for k in range(K):
            for s in range(n): gat(k,s,c,False).wait_send()
        return 0
    lax.fori_loop(0,CH,drain,0)
    def hdrain(c,_):
        for k in range(HK):
            for s in range(n): hsum(k,s,c).wait_send()
            for s in backs[k]: hgat(k,s,c,False).wait_send()
        return 0
    lax.fori_loop(0,HC,hdrain,0)
    for i in range(len(vaxes)): vcopy(i).wait_send()
    ocopy().wait_send(); tcopy().wait()
    tok[1-p.tw]=trecv[...]

def finish(dp,red,dq,dk,dv,normT,wh,gwo,x,gm,gain,vec,gbu):
    T,D=x.shape; CH,fin,_=red.shape; R=FC//128*D
    plan=big_plan(dp,R); n=len(plan[0][0])
    HC=D//TT; HR=2*dq.shape[1]//128*TT; hplan=head_plan(dp,HR)
    hrecv=[]
    for order,_,rows in hplan:
        q=2
        for axis in order:
            if axis=="tw": q=1
            else: rows//=2
            hrecv.append(pltpu.VMEM((HC,q,rows,128),BF))
    V=(6*D+gbu.shape[1])//128+16; nv=n+1; args=(red,dq,dk,dv,normT,wh,gwo,x,gm,gain,vec,gbu)
    return pl.pallas_call(functools.partial(finish_kernel,dp),
      in_specs=[pl.BlockSpec(memory_space=pl.ANY if 1<=i<=8 else pltpu.VMEM) for i in range(len(args))],
      out_specs=[pl.BlockSpec(memory_space=pl.ANY)]+[pl.BlockSpec(memory_space=pltpu.VMEM)]*3,
      out_shape=[jax.ShapeDtypeStruct((CH,2,R,128),BF),jax.ShapeDtypeStruct((HC,HR,128),BF),jax.ShapeDtypeStruct((V,128),F32),jax.ShapeDtypeStruct((2,T//2,D),BF)],
      scratch_shapes=[pltpu.VMEM((CH,2,R,128),BF),pltpu.SemaphoreType.DMA((CH,))]+[pltpu.VMEM(a.shape,a.dtype) for a in args[1:9]]+[pltpu.SemaphoreType.DMA((8,)),pltpu.VMEM((HC,2,HR,128),BF),pltpu.VMEM((HC,HR,128),BF),pltpu.VMEM((nv,V,128),F32),pltpu.VMEM((nv,V,128),F32),pltpu.VMEM((T,D),F32)]+[pltpu.VMEM((T,D),BF)]*3+[pltpu.VMEM((T//2,D),BF),pltpu.VMEM((8,D),F32)]+[pltpu.SemaphoreType.DMA((2,))]*2+hrecv
        +[pltpu.SemaphoreType.DMA((len(plan),n,CH))]*2+[pltpu.SemaphoreType.DMA((CH,))]*2+[pltpu.SemaphoreType.DMA((len(hplan),n,HC))]*4+[pltpu.SemaphoreType.DMA((nv,))]*2,
      compiler_params=pltpu.CompilerParams(vmem_limit_bytes=60*2**20,collective_id=1,has_side_effects=True),name="finish_gradients")(*args)

def widen_kernel(chunk,heads,mine,got,vec,tok,wup,wdown,wqkv,wout,blk,tok_o,bqv,*vectors):
    D=wup.shape[0]; q=wout.shape[0]; g=pl.program_id(0); HT=D//heads.shape[0]
    for i in range(FC//128):
        cols=slice(i*128,(i+1)*128)
        wup[:,cols]=chunk[0,i*D:(i+1)*D,:].astype(F32)
        wdown[cols,:]=chunk[1,i*D:(i+1)*D,:].T.astype(F32)
    @pl.when(g==0)
    def _():
        for t in range(heads.shape[0]):
            y=jnp.concatenate([heads[t,i*HT:(i+1)*HT,:] for i in range(heads.shape[1]//HT)],1).T.astype(F32)
            rr=slice(t*HT,(t+1)*HT)
            for c in range(3): wqkv[c,:,rr]=y[c*q:(c+1)*q,:]
            wout[:,rr]=y[3*q:,:]
        th,tw=lax.axis_index("th"),lax.axis_index("tw")
        blk[tw]=mine[...]; blk[1-tw]=got[...]
        tok_o[...]=tok[...]
        at=sum(v.shape[0] for v in vectors)//128
        for i in range(2):
            for z,w in ((0,128),(1,q-128)): bqv[i:i+1,z*128:z*128+w]=vec[pl.ds(at+4*(2*th+tw)+2*i+z,1),0:w]
        at=0
        for v in vectors:
            for i in range(v.shape[0]//128):
                v[i*128:(i+1)*128]=vec[at,:]; at+=1

def widen(chunks,heads,mine,got,vec,tok):
    CH,_,R,_=chunks.shape; D=R*128//FC; FF=CH*FC; q=heads.shape[0]*heads.shape[1]*128//(4*D); T2=mine.shape[0]
    outs=[(D,FF),(FF,D),(3,q,D),(q,D)]; sizes=[D]*6+[FF]
    res=pl.pallas_call(widen_kernel,grid=(CH,),
      in_specs=[pl.BlockSpec((None,2,R,128),lambda g:(g,0,0,0))]+[pl.BlockSpec(a.shape,lambda g,n=a.ndim:(0,)*n) for a in (heads,mine,got,vec,tok)],
      out_specs=[pl.BlockSpec((D,FC),lambda g:(0,g)),pl.BlockSpec((FC,D),lambda g:(g,0))]+[pl.BlockSpec(memory_space=pltpu.VMEM)]*(5+len(sizes)),
      out_shape=[jax.ShapeDtypeStruct(o,F32) for o in outs]+[jax.ShapeDtypeStruct((2,T2,D),BF)]*2+[jax.ShapeDtypeStruct((2,q),F32)]+[jax.ShapeDtypeStruct((z,),F32) for z in sizes],
      compiler_params=pltpu.CompilerParams(vmem_limit_bytes=63*2**20),name="widen")(chunks,heads,mine,got,vec,tok)
    return res[:7],res[7:]

def front_kernel(tok,w,b,gain,shift,seg,x_o,normT_o,q_o,k_o,v_o,wh_o,mq_o,mk_o,x,norm,normT,qkv,wh,wgot,bgot,bias,mq,mk,tsem,bsem,csem,ysem,xsem,zsem,osem):
    p=Peers(); Q,D=tok.shape[1:]; T=2*Q; L=2*T; E=w.shape[1]; PART=E//4
    b0,b1=p.bit(0),p.bit(1)
    barrier(p,["th","tw",0,1])
    def tcopy(): return send(tok.at[1-p.tw],x.at[rows_at(p.tw*Q,Q),:],tsem.at[0],tsem.at[1],p.peer("tw"))
    def bcopy(): return send(b,bgot,bsem.at[0],bsem.at[1],p.peer("tw"))
    def ycopy(c):
        r=rows_at((2*b1+b0)*PART,PART)
        return send(w.at[c,r,:],wgot.at[c,r,:],ysem.at[0,c],ysem.at[1,c],p.peer("tw"))
    def xcopy(c,landed):
        ref=wgot.at[c,rows_at((2*b1+(1-b0 if landed else b0))*PART,PART),:]
        return send(ref,ref,xsem.at[0,c],xsem.at[1,c],p.peer(0))
    def zcopy(c,landed):
        ref=wgot.at[c,rows_at((1-b1 if landed else b1)*2*PART,2*PART),:]
        return send(ref,ref,zsem.at[0,c],zsem.at[1,c],p.peer(1))
    def ccopy(i,landed):
        core=1-p.th if landed else p.th
        quarter=p.tw if i==0 else 1-p.tw
        ref=norm.at[rows_at(core*T+quarter*Q,Q),:]
        return send(ref,ref,csem.at[0,i],csem.at[1,i],p.peer("th"))
    for c in range(3): ycopy(c).start()
    bcopy().start()
    tcopy().start()
    g_row=gain[...].reshape(1,D); s_row=shift[...].reshape(1,D)
    def normalize(src,row):
        for t in range(Q//128):
            y=(norm_parts(src(t).astype(F32))[0]*g_row+s_row).astype(BF)
            norm[rows_at(row+t*128,128),:]=y
    def put(src,dst,i): return pltpu.make_async_copy(src,dst,osem.at[i])
    x[rows_at(p.tw*Q,Q),:]=tok[p.tw]
    normalize(lambda t: tok[p.tw,t*128:(t+1)*128,:],p.th*T+p.tw*Q)
    onehot=lax.broadcasted_iota(jnp.int32,(128,L),0)
    onehot=jnp.where(onehot<HD,onehot,onehot-HD)
    same=onehot==seg[pl.ds(p.tw,1),:]
    mk[...]=jnp.where(same,1.0,0.0).T.astype(BF)
    ccopy(0,False).start()
    for c in range(3):
        ycopy(c).wait_recv()
        xcopy(c,False).start()
    mq[...]=jnp.where(same|(onehot>=9),0.0,-float(2**40)).T.astype(BF)
    put(mk,mk_o,0).start(); put(mq,mq_o,1).start()
    bcopy().wait_recv()
    bias[...]=jnp.zeros_like(bias)
    for m,src in enumerate((b,bgot)):
        for i,c in enumerate((0,2)): bias[m,c:c+1,:]=src[i:i+1,:]
    for c in range(3):
        xcopy(c,True).wait_recv()
        zcopy(c,False).start()
    def project(row,weights,m):
        r=rows_at(row,Q)
        def one(c,_):
            y=(dot(norm[r,:],weights[c],NT)+bias[m,pl.ds(c,1),:]).astype(BF)
            y=y*jnp.where(c==0,0.125,1.0).astype(BF)
            qkv[c,r,m*E:(m+1)*E]=y
            return 0
        lax.fori_loop(0,3,one,0)
    def transpose(quarter):
        for core in range(2):
            for t in range(Q//128):
                at=core*T+quarter*Q+t*128
                normT[:,pl.ds(pl.multiple_of(at,128),128)]=norm[rows_at(at,128),:].T
    ccopy(0,True).wait_recv()
    for core in range(2): project(core*T+p.tw*Q,w,0)
    transpose(p.tw)
    for c in range(3): zcopy(c,True).wait_recv()
    for core in range(2): project(core*T+p.tw*Q,wgot,1)
    for c in range(3): wh[c,0:E,:]=w[c]; wh[c,E:2*E,:]=wgot[c]
    put(wh,wh_o,7).start()
    tcopy().wait_recv()
    normalize(lambda t: x[rows_at((1-p.tw)*Q+t*128,128),:],p.th*T+(1-p.tw)*Q)
    put(x,x_o,2).start()
    for m,weights in enumerate((w,wgot)):
        project(p.th*T+(1-p.tw)*Q,weights,m)
        if m==0: ccopy(1,False).start()
    ccopy(1,True).wait_recv()
    for m,weights in enumerate((w,wgot)): project((1-p.th)*T+(1-p.tw)*Q,weights,m)
    for c in range(3): put(qkv.at[c],(q_o,k_o,v_o)[c],4+c).start()
    transpose(1-p.tw)
    put(normT,normT_o,3).start()
    for src,dst,i in ((mk,mk_o,0),(mq,mq_o,1),(x,x_o,2),(normT,normT_o,3),(wh,wh_o,7)): put(src,dst,i).wait()
    for c in range(3):
        put(qkv.at[c],(q_o,k_o,v_o)[c],4+c).wait()
        ycopy(c).wait_send(); xcopy(c,False).wait_send(); zcopy(c,False).wait_send()
    tcopy().wait_send(); bcopy().wait_send()
    for i in range(2): ccopy(i,False).wait_send()

def front(tok,w,b,gain,shift,seg):
    _,Q,D=tok.shape; T=2*Q; L=2*T; E=w.shape[1]
    outs=[((T,D),BF),((D,L),BF)]+[((L,2*E),BF)]*3+[((3,2*E,D),BF)]+[((L,128),BF)]*2
    sem=pltpu.SemaphoreType.DMA
    return pl.pallas_call(front_kernel,
      in_specs=[pl.BlockSpec(memory_space=pltpu.VMEM)]*6,out_specs=[pl.BlockSpec(memory_space=pl.ANY)]*len(outs),
      out_shape=[jax.ShapeDtypeStruct(*o) for o in outs],
      scratch_shapes=[pltpu.VMEM((T,D),BF),pltpu.VMEM((L,D),BF),pltpu.VMEM((D,L),BF),pltpu.VMEM((3,L,2*E),BF),pltpu.VMEM((3,2*E,D),BF),pltpu.VMEM((3,E,D),BF),
        pltpu.VMEM(b.shape,F32),pltpu.VMEM((2,8,E),F32),pltpu.VMEM((L,128),BF),pltpu.VMEM((L,128),BF),sem((2,)),sem((2,)),sem((2,2)),sem((2,3)),sem((2,3)),sem((2,3)),sem((8,))],
      compiler_params=pltpu.CompilerParams(vmem_limit_bytes=60*2**20,collective_id=2,has_side_effects=True),name="front")(tok,w,b,gain,shift,seg)


SWAP = [(0, 1), (1, 0)]


def swap(value, axis):
    return lax.ppermute(value, axis, SWAP)


def body(
    dp_size,
    tokens,
    segment_ids,
    norm1_gain,
    norm1_shift,
    w_qkv,
    b_qv,
    w_out,
    b_out,
    norm2_gain,
    norm2_shift,
    w_up,
    b_up,
    w_down,
    b_down,
    cotangent,
):
    tw = lax.axis_index("tw")
    x, normed_t, query, key, value, w_heads, mq, mk = front(
        tokens, w_qkv.transpose(0, 2, 1), b_qv, norm1_gain, norm1_shift, segment_ids
    )
    tables = (mq, mk, *block_ranges(lax.dynamic_index_in_dim(segment_ids, tw, 0, False)))
    later = lax.optimization_barrier((cotangent, w_out, query))
    cot_got = swap(lax.dynamic_index_in_dim(later[0], 1 - tw, 0, False), "tw")
    w_out_got = swap(later[1], "tw")
    attended, totals = attn_fwd(query, key, value, *tables)
    out_mine, out_other, grad_middle, grad_b_up, sums, red, grad_heads, grad_w_out = ffn(
        dp_size, attended, x, b_out, norm2_gain, norm2_shift, b_down, w_out, w_out_got, cotangent, cot_got, w_up, w_down, b_up[None]
    )
    out_got = swap(out_other, "tw")
    dq, dk, dv = attn_bwd(query, key, value, grad_heads, attended, totals, *tables)
    chunks, heads, small, grad_tokens = finish(
        dp_size, red, dq, dk, dv, normed_t, w_heads, grad_w_out, x, grad_middle, norm1_gain, sums, grad_b_up
    )
    (up, down, w_qkv_grad, w_out_grad, block_out, grad_tokens, b_qv_grad), vecs = widen(
        chunks, heads, out_mine, out_got, small, grad_tokens
    )
    return (
        block_out,
        grad_tokens,
        vecs[0],
        vecs[1],
        w_qkv_grad.transpose(0, 2, 1),
        b_qv_grad,
        w_out_grad,
        vecs[2],
        vecs[3],
        vecs[4],
        up,
        vecs[6],
        down,
        vecs[5],
    )


def solution(mesh):
    return jax.shard_map(
        functools.partial(body, mesh.shape["dp"]),
        mesh=mesh,
        in_specs=(
            P("dp", ("th", "tw"), None),
            P("dp", None),
            P(),
            P(),
            P(None, None, ("th", "tw")),
            P(None, ("th", "tw")),
            P(("th", "tw"), None),
            P(),
            P(),
            P(),
            P(),
            P(),
            P(),
            P(),
            P("dp", ("th", "tw"), None),
        ),
        out_specs=(
            P("dp", ("th", "tw"), None),
            P("dp", ("th", "tw"), None),
            P(),
            P(),
            P(None, None, ("th", "tw")),
            P(None, ("th", "tw")),
            P(("th", "tw"), None),
            P(),
            P(),
            P(),
            P(),
            P(),
            P(),
            P(),
        ),
        check_vma=False,
    )
```

```python
import functools

import jax
import jax.numpy as jnp
from jax import lax
from jax.experimental import pallas as pl
from jax.experimental.pallas import tpu as pltpu
from jax.sharding import PartitionSpec as P

NT=(((1,),(1,)),((),())); NN=(((1,),(0,)),((),())); TN=(((0,),(0,)),((),()))
F32=jnp.float32; BF=jnp.bfloat16
BQ=256; BK=256; HD=64
def dot(a,b,d): return lax.dot_general(a,b,d,preferred_element_type=F32)

AL=128; VR=80; GRP=3
def each_chunk(lo_ref,n_ref,i,body):
    lo=lo_ref[i]; n=n_ref[i]
    def full(j,_):
        body(pl.ds(pl.multiple_of(lo+j*BK,AL),BK))
        return 0
    lax.fori_loop(0,n//2,full,0)
    @pl.when(n%2==1)
    def _(): body(pl.ds(pl.multiple_of(lo+n//2*BK,AL),AL))

def fwd_kernel(lo_ref, n_ref, q_ref, k_ref, v_ref, mq_ref, mk_ref, o_ref, lse_ref, m_ref, acc_ref, vT_ref, qm_ref):
    i=pl.program_id(0); H=q_ref.shape[1]//HD
    lane=lax.broadcasted_iota(jnp.int32,(1,128),1)
    halves=(lane<HD, lane>=HD)
    @pl.when(i==0)
    def _():
        row=lax.broadcasted_iota(jnp.int32,(VR-HD,v_ref.shape[0]),0)
        for p in range(H//2):
            t=v_ref[:,p*128:(p+1)*128].T
            for e in range(2):
                vT_ref[2*p+e,0:HD,:]=t[e*HD:(e+1)*HD,:]
                vT_ref[2*p+e,HD:VR,:]=jnp.where(row==0,1.0,0.0).astype(BF)
    m_ref[...]=jnp.full(m_ref.shape,-1e30,F32)
    acc_ref[...]=jnp.zeros_like(acc_ref)
    for h in range(H): qm_ref[h]=jnp.where(halves[h%2],q_ref[:,h//2*128:h//2*128+128],mq_ref[...])
    def score(h,ks,mk):
        cols=slice(h//2*128,h//2*128+128)
        return dot(jnp.where(halves[h%2],k_ref[ks,cols],mk),qm_ref[h],NT)
    def soft(h,s):
        m_old=m_ref[h:h+1,:]
        m_new=jnp.maximum(m_old,jnp.max(s,axis=0,keepdims=True))
        m_ref[h:h+1,:]=m_new
        return jnp.exp(s-m_new).astype(BF),jnp.exp(m_old-m_new)
    def weigh(h,ks,pe,alpha):
        acc_ref[h]=acc_ref[h]*alpha+dot(vT_ref[h,:,ks],pe,NN)
    def body(ks):
        mk=mk_ref[ks,:]
        scores=[score(h,ks,mk) for h in range(H)]
        probs=[soft(h,scores[h]) for h in range(H)]
        for h in range(H): weigh(h,ks,*probs[h])
    each_chunk(lo_ref,n_ref,i,body)
    for p in range(H//2):
        parts=[acc_ref[h,0:HD,:]*(1.0/acc_ref[h,HD:HD+1,:]) for h in (2*p,2*p+1)]
        o_ref[:,p*128:(p+1)*128]=jnp.concatenate(parts,0).T.astype(BF)
    for h in range(H): lse_ref[h:h+1,:]=m_ref[h:h+1,:]+jnp.log(acc_ref[h,HD:HD+1,:])
    lse_ref[H:,:]=jnp.zeros((lse_ref.shape[0]-H,BQ),F32)

def attn_fwd(q,k,v,mq,mk,lo,n):
    L,C=q.shape
    return pl.pallas_call(fwd_kernel,
        grid_spec=pltpu.PrefetchScalarGridSpec(num_scalar_prefetch=2,grid=(L//BQ,),
          in_specs=[pl.BlockSpec((BQ,C),lambda i,*_:(i,0)),pl.BlockSpec((L,C),lambda i,*_:(0,0)),pl.BlockSpec((L,C),lambda i,*_:(0,0)),
                    pl.BlockSpec((BQ,128),lambda i,*_:(i,0)),pl.BlockSpec((L,128),lambda i,*_:(0,0))],
          out_specs=[pl.BlockSpec((BQ,C),lambda i,*_:(i,0)),pl.BlockSpec((8,BQ),lambda i,*_:(0,i))],
          scratch_shapes=[pltpu.VMEM((8,BQ),F32),pltpu.VMEM((C//HD,VR,BQ),F32),pltpu.VMEM((C//HD,VR,L),BF),pltpu.VMEM((C//HD,BQ,128),BF)]),
        out_shape=[jax.ShapeDtypeStruct((L,C),BF),jax.ShapeDtypeStruct((8,L),F32)],
        name="attention_forward",
    )(lo,n,q,k,v,mq,mk)

def bwd_kernel(lo_ref, n_ref, q_ref, k_ref, v_ref, do_ref, o_ref, lse_ref, mq_ref, mk_ref, dq_ref, dk_ref, dv_ref, dk_acc, dv_acc, dq_acc, qcat, docat, qm, kT):
    i=pl.program_id(0); n=pl.num_programs(0)
    C=q_ref.shape[1]; pairs=C//128
    lane=lax.broadcasted_iota(jnp.int32,(1,128),1)
    halves=(lane<HD, lane>=HD)
    @pl.when(i==0)
    def _():
        dk_acc[...]=jnp.zeros_like(dk_acc); dv_acc[...]=jnp.zeros_like(dv_acc)
        kT[...]=k_ref[...].T
    dq_acc[...]=jnp.zeros_like(dq_acc)
    sel=(lax.broadcasted_iota(jnp.int32,(8,C),1)//HD==lax.broadcasted_iota(jnp.int32,(8,C),0)).astype(BF)
    prod=do_ref[...].astype(F32)*o_ref[...].astype(F32)
    high=prod.astype(BF)
    delta=dot(sel,high,NT)+dot(sel,(prod-high.astype(F32)).astype(BF),NT)
    for p in range(pairs):
        cols=slice(p*128,(p+1)*128)
        for e in range(2):
            q2=q_ref[:,cols]; d2=do_ref[:,cols]
            qcat[p,e*BQ:(e+1)*BQ,:]=jnp.where(halves[e],q2,jnp.zeros_like(q2))
            qm[p,e*BQ:(e+1)*BQ,:]=jnp.where(halves[e],q2,mq_ref[...])
            docat[p,e*BQ:(e+1)*BQ,:]=jnp.where(halves[e],d2,jnp.zeros_like(d2))
    lse=lse_ref[...]
    def body(ks):
        mk=mk_ref[ks,:]
        for g in range(0,pairs,GRP):
            work=[]
            for p in range(g,g+GRP):
                cols=slice(p*128,(p+1)*128)
                k2=k_ref[ks,cols]; v2=v_ref[ks,cols]; d2=do_ref[:,cols]
                for e in range(2):
                    s=dot(jnp.where(halves[e],k2,mk),qm[p,e*BQ:(e+1)*BQ,:],NT)
                    work.append((s,dot(jnp.where(halves[e],v2,jnp.zeros_like(v2)),d2,NT)))
            out=[]
            for t,(s,dp) in enumerate(work):
                h=2*g+t
                pr=jnp.exp(s-lse[h:h+1,:])
                out.append((pr.astype(BF),(pr*(dp-delta[h:h+1,:])).astype(BF)))
            for p in range(g,g+GRP):
                cols=slice(p*128,(p+1)*128); k2=k_ref[ks,cols]
                (p0,d0),(p1,d1)=out[2*(p-g):2*(p-g)+2]
                dv_acc[ks,cols]+=dot(jnp.concatenate([p0,p1],1),docat[p],NN)
                dk_acc[ks,cols]+=dot(jnp.concatenate([d0,d1],1),qcat[p],NN)
                for e,d in enumerate((d0,d1)):
                    r=slice((2*p+e)*HD,(2*p+e+1)*HD)
                    dq_acc[r,:]+=dot(kT[r,ks],d,NN)
    each_chunk(lo_ref,n_ref,i,body)
    dq_ref[...]=(dq_acc[...]*0.125).T.astype(BF)
    @pl.when(i==n-1)
    def _():
        dk_ref[...]=dk_acc[...].astype(BF); dv_ref[...]=dv_acc[...].astype(BF)

def attn_bwd(q,k,v,do,o,lse,mq,mk,lo,n):
    L,C=q.shape
    blk=pl.BlockSpec((BQ,C),lambda i,*_:(i,0)); full=pl.BlockSpec((L,C),lambda i,*_:(0,0))
    return pl.pallas_call(bwd_kernel,
        grid_spec=pltpu.PrefetchScalarGridSpec(num_scalar_prefetch=2,grid=(L//BQ,),
          in_specs=[blk,full,full,blk,blk,pl.BlockSpec((8,BQ),lambda i,*_:(0,i)),pl.BlockSpec((BQ,128),lambda i,*_:(i,0)),pl.BlockSpec((L,128),lambda i,*_:(0,0))],
          out_specs=[blk,full,full],
          scratch_shapes=[pltpu.VMEM((L,C),F32),pltpu.VMEM((L,C),F32),pltpu.VMEM((C,BQ),F32),pltpu.VMEM((C//128,2*BQ,128),BF),pltpu.VMEM((C//128,2*BQ,128),BF),pltpu.VMEM((C//128,2*BQ,128),BF),pltpu.VMEM((C,L),BF)]),
        out_shape=[jax.ShapeDtypeStruct((L,C),BF)]*3,
        name="attention_backward",
    )(lo,n,q,k,v,do,o,lse,mq,mk)

def block_ranges(seg):
    first=seg[::BQ]; last=seg[BQ-1::BQ]
    lo=jnp.sum(seg[None,:]<first[:,None],axis=1,dtype=jnp.int32)//AL*AL
    hi=jnp.sum(seg[None,:]<=last[:,None],axis=1,dtype=jnp.int32)
    return lo,(hi-lo+AL-1)//AL


TT=256; FC=512
LAG=2; GLAG=5; HLAG=4; HSP=2; GSP=4; VLAG=5; FL=3

def bits_of(dp): return dp.bit_length()-1

def big_plan(dp,rows):
    n=bits_of(dp)
    orders=(["tw"]+list(range(n)),[0,"tw"]+list(range(1,n)),[1,2,0,"tw"]+list(range(3,n)))
    unit=16<<(n+1)
    units=rows//unit
    third=max(1,units//4)
    shares=[units-units//3-third,units//3,third]
    return streams(orders,shares,unit)

def head_plan(dp,rows):
    n=bits_of(dp)
    orders=(["tw"]+list(range(n)),[0,"tw"]+list(range(1,n)),[1,2,0,"tw"]+list(range(3,n)))
    unit=16<<n
    units=rows//unit
    low=max(1,units//4)
    mid=max(1,units//3)
    return streams(orders,[units-mid-low,mid,low],unit)

def streams(orders,shares,unit):
    out=[]; start=0
    for order,share in zip(orders,shares):
        out.append((order,start,share*unit)); start+=share*unit
    return out

class Peers:
    def __init__(self):
        self.dp=lax.axis_index("dp"); self.th=lax.axis_index("th"); self.tw=lax.axis_index("tw")
    def bit(self,axis):
        return self.tw if axis=="tw" else (self.dp//(1<<axis))%2
    def peer(self,axis):
        if axis=="tw": return {"tw":1-self.tw}
        if axis=="th": return {"th":1-self.th}
        return {"dp":self.dp+(1-2*self.bit(axis))*(1<<axis)}

def send(src,dst,ssem,rsem,peer):
    return pltpu.make_async_remote_copy(src,dst,ssem,rsem,device_id=peer,device_id_type=pl.DeviceIdType.MESH)

def barrier(p,axes):
    sem=pltpu.get_barrier_semaphore()
    for a in axes:
        pl.semaphore_signal(sem,inc=1,device_id=p.peer(a),device_id_type=pl.DeviceIdType.MESH)
    pl.semaphore_wait(sem,len(axes))

def halves(p,order,row,rows,keep_tw=False):
    out=[]
    for axis in order:
        if keep_tw and axis=="tw": out.append((row,row,rows)); continue
        rows//=2; bit=p.bit(axis)
        out.append((row+(1-bit)*rows,row+bit*rows,rows)); row=row+bit*rows
    return out
def run_steps(steps):
    total=max(f+sp*(cnt-1) for f,sp,cnt,_ in steps)+1
    def body(i,_):
        for r in range(2):
            g=2*i+r
            for f,sp,cnt,what in steps:
                if sp==2:
                    if f%2!=r: continue
                    c=i-f//2
                else: c=g-f
                if cnt==1:
                    pl.when(c==0)(functools.partial(what,0))
                else: pl.when((c>=0)&(c<cnt))(functools.partial(what,c))
        return 0
    lax.fori_loop(0,(total+1)//2,body,0)
def al(x): return x if isinstance(x,int) else pl.multiple_of(x,16)
def rows_at(row,n): return pl.ds(al(row),n)

EPS=1e-06
def norm_parts(x):
    mean=jnp.mean(x,axis=-1,keepdims=True)
    cen=x-mean
    r=lax.rsqrt(jnp.mean(cen*cen,axis=-1,keepdims=True)+EPS)
    return cen*r,r
def norm_back(e,n,r,gain):
    t=e*gain
    return r*(t-jnp.mean(t,axis=-1,keepdims=True)-n*jnp.mean(t*n,axis=-1,keepdims=True))
def colsum(x): return jnp.sum(x,axis=0,keepdims=True)

def ffn_kernel(dp,att,x,vb,vg,vs,vd,wo_h,wo_got,cot_h,cot_got,wu_h,wd_h,bu,mine,other,gm,gb,vec,red,gheads,gwo,
               wo,cot,lsem,wu,wd,cotT,mid,n2,n2T,obuf,orecv,grow,act,gh,dw,chip_recv,wsem,osem,gsem,*rest):
    CH=dw.shape[0]; T,D=x.shape; SLOTS=chip_recv.shape[0]
    plan=big_plan(dp,dw.shape[2]); n=len(plan[0][0]); K=len(plan)
    recv=[rest[k*n:(k+1)*n] for k in range(K)]
    send_sem,recv_sem,chip_send,chip_got=rest[K*n:]
    p=Peers()
    b_row,g_row,s_row,d_row=[v[...].reshape(1,D) for v in (vb,vg,vs,vd)]
    tiles=[slice(t*TT,(t+1)*TT) for t in range(T//TT)]; NT_=len(tiles)
    regs=[halves(p,*s) for s in plan]
    def copy(k,s,c):
        out,_,nr=regs[k][s]
        return send(dw.at[c,p.th,rows_at(out,nr),:],recv[k][s].at[c],send_sem.at[k,s,c],recv_sem.at[k,s,c],p.peer(plan[k][0][s]))
    def chip_copy(c):
        return send(dw.at[c,1-p.th],chip_recv.at[c%SLOTS],chip_send.at[c],chip_got.at[c],p.peer("th"))
    def ocopy(): return send(obuf,orecv,osem.at[0],osem.at[1],p.peer("th"))
    def gcopy(landed):
        ref=grow.at[rows_at((1-p.th if landed else p.th)*T,T),:]
        return send(ref,ref,gsem.at[0],gsem.at[1],p.peer("th"))
    def wload(c):
        return (pltpu.make_async_copy(wu_h.at[:,pl.ds(pl.multiple_of(c*FC,FC),FC)],wu.at[c],wsem.at[0,c]),
                pltpu.make_async_copy(wd_h.at[pl.ds(pl.multiple_of(c*FC,FC),FC),:],wd.at[c],wsem.at[1,c]))
    E=wo_h.shape[0]; Q=T//2
    loads=[pltpu.make_async_copy(a,b,lsem.at[i]) for i,(a,b) in enumerate(((wo_h,wo.at[0:E,:]),(wo_got,wo.at[E:2*E,:]),
        (cot_h.at[p.tw],cot.at[rows_at(p.tw*Q,Q),:]),(cot_got,cot.at[rows_at((1-p.tw)*Q,Q),:])))]
    for l in loads: l.start()
    def load(c,_):
        for w in wload(c): w.start()
        return 0
    lax.fori_loop(0,CH,load,0)
    barrier(p,["th"]+plan[0][0])
    for l in loads[:2]: l.wait()
    for r in tiles:
        obuf[r,:]=dot(att[rows_at((1-p.th)*T+r.start,TT),:],wo[...],NN).astype(BF)
    for l in loads[2:]: l.wait()
    for t,r in enumerate(tiles):
        mid[r,:]=x[r,:].astype(F32)+dot(att[rows_at(p.th*T+r.start,TT),:],wo[...],NN)+b_row
        if t==0: ocopy().start()
        cotT[:,r]=cot[r,:].T
    ocopy().wait_recv()
    for r in tiles:
        m=mid[r,:]+orecv[r,:].astype(F32)
        mid[r,:]=m
        nn,_=norm_parts(m)
        y=(nn*g_row+s_row).astype(BF)
        n2[r,:]=y; n2T[:,r]=y.T
    vec[...]=jnp.zeros_like(vec)
    def sum_step(s,c):
        news=[]
        for k in range(K):
            copy(k,s,c).wait_recv()
            _,kr,nr=regs[k][s]
            at=(c,p.th,rows_at(kr,nr),slice(None))
            new=(dw[at].astype(F32)+recv[k][s][c].astype(F32)).astype(BF)
            if s<n-1: dw[at]=new
            else: news.append((kr,nr,new))
        if s<n-1:
            for k in range(K): copy(k,s+1,c).start()
        else:
            out=0
            for kr,nr,new in news:
                red[c,out:out+nr,:]=new; out+=nr
    def chip_sum(c):
        chip_copy(c).wait_recv()
        def add(q,_):
            r=rows_at(q*TT,TT)
            dw[c,p.th,r,:]=(dw[c,p.th,r,:].astype(F32)+chip_recv[c%SLOTS,r,:].astype(F32)).astype(BF)
            return 0
        lax.fori_loop(0,dw.shape[2]//TT,add,0)
        for k in range(K): copy(k,0,c).start()
    def hidden(c):
        for w in wload(c): w.wait()
        cols=pl.ds(pl.multiple_of(c*FC,FC),FC)
        gsum=jnp.zeros((1,FC),F32)
        for r in tiles:
            h=dot(n2[r,:],wu[c],NN)+bu[:,cols]
            ga=dot(cot[r,:],wd[c],NT)
            cdf=0.5*(1.0+lax.erf(h*(0.5**0.5)))
            a=(h*cdf).astype(BF)
            gr=(ga*(cdf+h*(jnp.exp(h*h*-0.5)*0.3989422804014327))).astype(BF)
            act[c,r,:]=a; gh[c,r,:]=gr
            gsum+=colsum(gr.astype(F32))
        gb[:,cols]=gsum
    def weight_grads(c):
        for t in range(D//TT):
            r=slice(t*TT,(t+1)*TT)
            for m,(lhs,rhs) in enumerate(((n2T,gh),(cotT,act))):
                y=dot(lhs[r,:],rhs[c],NN).astype(BF)
                for q in range(FC//128): dw[c,m,q*D+t*TT:q*D+(t+1)*TT,:]=y[:,q*128:(q+1)*128]
    def norm_two_back(t):
        r=rows_at(t*TT,TT)
        e=dot(gh[0,r,:],wu[0],NT)
        for c in range(1,CH): e+=dot(gh[c,r,:],wu[c],NT)
        nn,rs=norm_parts(mid[r,:])
        ct=cot[r,:].astype(F32)
        gmid=ct+norm_back(e,nn,rs,g_row)
        gm[r,:]=gmid
        gbr=gmid.astype(BF)
        grow[rows_at(p.th*T+t*TT,TT),:]=gbr
        vec[0:1,:]+=colsum(gbr.astype(F32)); vec[1:2,:]+=colsum(e*nn); vec[2:3,:]+=colsum(e); vec[3:4,:]+=colsum(ct)
    def block_out(t):
        r=rows_at(t*TT,TT)
        y=mid[r,:]+d_row
        for c in range(CH): y+=dot(act[c,r,:],wd[c],NN)
        n2[r,:]=y.astype(BF)
    def split_out(_):
        gcopy(True).wait_recv()
        mine[...]=n2[rows_at(p.tw*(T//2),T//2),:]
        other[...]=n2[rows_at((1-p.tw)*(T//2),T//2),:]
    def grad_heads(u):
        for t in range(NT_):
            r=rows_at(u*T+t*TT,TT)
            gheads[r,:]=dot(grow[r,:],wo[...],NT).astype(BF)
    def grad_wo(_):
        for t in range(D//TT):
            r=slice(t*TT,(t+1)*TT)
            gwo[r,:]=dot(grow[:,r],att[...],TN).astype(BF)
    P2=2*CH; P3=P2+NT_; P4=P3+NT_
    part=functools.partial
    steps=[(3+FL*(s+1),2,CH,part(sum_step,s)) for s in reversed(range(n))]
    steps+=[(3,2,CH,chip_sum),(2,2,CH,lambda c: chip_copy(c).start())]
    steps+=[(0,2,CH,hidden),(1,2,CH,weight_grads),(P2,1,NT_,norm_two_back),(P3,1,1,lambda _: gcopy(False).start()),(P3,1,NT_,block_out),
            (P4,1,1,split_out),(P4,1,2,grad_heads),(P4+2,1,1,grad_wo)]
    run_steps(steps)
    ocopy().wait_send(); gcopy(False).wait_send()
    def drain(c,_):
        chip_copy(c).wait_send()
        for k in range(K):
            for s in range(n): copy(k,s,c).wait_send()
        return 0
    lax.fori_loop(0,CH,drain,0)

def whole(shape):
    return pl.BlockSpec(memory_space=pltpu.VMEM)

def ffn(dp,att,x,vb,vg,vs,vd,wo,wo_got,cot,cot_got,wu,wd,bu):
    T,D=x.shape; FF=wu.shape[1]; CH=FF//FC; R=FC//128*D; C=att.shape[1]
    plan=big_plan(dp,R); n=len(plan[0][0])
    fin=R>>n
    recv=[pltpu.VMEM((CH,rows>>(s+1),128),BF) for _,_,rows in plan for s in range(n)]
    outs=[((T//2,D),BF),((T//2,D),BF),((T,D),F32),((1,FF),F32),((8,D),F32),((CH,fin,128),BF),((2*T,C),BF),((D,C),BF)]
    specs=[whole(o[0]) for o in outs]
    hbm=pl.BlockSpec(memory_space=pl.ANY)
    V=pltpu.VMEM; sem=pltpu.SemaphoreType.DMA
    return pl.pallas_call(functools.partial(ffn_kernel,dp),
      in_specs=[whole(v.shape) for v in (att,x,vb,vg,vs,vd)]+[hbm]*6+[whole(bu.shape)],
      out_specs=specs,out_shape=[jax.ShapeDtypeStruct(*o) for o in outs],
      scratch_shapes=[V((C,D),BF),V((T,D),BF),sem((4,)),V((CH,D,FC),BF),V((CH,FC,D),BF),V((D,T),BF),V((T,D),F32),V((T,D),BF),V((D,T),BF),V((T,D),BF),V((T,D),BF),V((2*T,D),BF),
          V((CH,T,FC),BF),V((CH,T,FC),BF),V((CH,2,R,128),BF),V((3,R,128),BF),sem((2,CH)),sem((2,)),sem((2,))]+recv
        +[sem((len(plan),n,CH))]*2+[sem((CH,))]*2,
      compiler_params=pltpu.CompilerParams(vmem_limit_bytes=63*2**20+2**19,collective_id=0,has_side_effects=True),name="feed_forward")(att,x,vb,vg,vs,vd,wo,wo_got,cot,cot_got,wu,wd,bu)

def finish_kernel(dp,red,dq_h,dk_h,dv_h,normT_h,wh_h,gwo_h,x_h,gm_h,gain,vec,gbu,gathered,heads_out,vec_out,tok,full,fsem,dq,dk,dv,normT,wh,gwo,x,gm,isem,hp,hg,vbuf,vrecv,own,obuf,orecv,tbuf,trecv,vrow,osem,tsem,*rest):
    CH=full.shape[0]; R=full.shape[2]; T,D=x.shape; C=dq.shape[1]; Q=T//2
    plan=big_plan(dp,R); n=len(plan[0][0]); K=len(plan)
    HR=hp.shape[2]; hplan=head_plan(dp,HR); HK=len(hplan); HC=hp.shape[0]
    hrecv=[rest[k*n:(k+1)*n] for k in range(HK)]
    send_sem,recv_sem,chip_send,chip_got,hs_sem,hr_sem,ha_send,ha_recv,vs_sem,vr_sem=rest[HK*n:]
    p=Peers()
    regs=[halves(p,*s) for s in plan]
    hregs=[halves(p,*s,keep_tw=True) for s in hplan]
    def gat(k,s,c,landed):
        other,mine,nr=regs[k][s]
        ref=full.at[c,p.th,rows_at(other if landed else mine,nr),:]
        return send(ref,ref,send_sem.at[k,s,c],recv_sem.at[k,s,c],p.peer(plan[k][0][s]))
    def chip(c,landed):
        ref=full.at[c,1-p.th if landed else p.th]
        return send(ref,ref,chip_send.at[c],chip_got.at[c],p.peer("th"))
    def fput(c): return pltpu.make_async_copy(full.at[c],gathered.at[c],fsem.at[c])
    def hsum(k,s,c):
        order=hplan[k][0]; other,_,nr=hregs[k][s]
        if order[s]=="tw": src=hp.at[c,pl.ds(1,1),rows_at(other,nr),:]
        elif order.index("tw")>s: src=hp.at[c,:,rows_at(other,nr),:]
        else: src=hp.at[c,pl.ds(0,1),rows_at(other,nr),:]
        return send(src,hrecv[k][s].at[c],hs_sem.at[k,s,c],hr_sem.at[k,s,c],p.peer(order[s]))
    def hgat(k,s,c,landed):
        order=hplan[k][0]; other,mine,nr=hregs[k][s]
        ref=hg.at[c,rows_at(other if landed else mine,nr),:]
        return send(ref,ref,ha_send.at[k,s,c],ha_recv.at[k,s,c],p.peer(order[s]))
    backs=[[s for s in reversed(range(n)) if o[s]!="tw"] for o,_,_ in hplan]
    vaxes=["th","tw"]+list(range(n-1))
    def vcopy(i): return send(vbuf.at[i],vrecv.at[i],vs_sem.at[i],vr_sem.at[i],p.peer(vaxes[i]))
    def ocopy(): return send(obuf,orecv,osem.at[0],osem.at[1],p.peer("th"))
    def tcopy(): return send(tbuf.at[rows_at((1-p.tw)*Q,Q),:],trecv,tsem.at[0],tsem.at[1],p.peer("tw"))
    loads=[pltpu.make_async_copy(a,b,isem.at[i]) for i,(a,b) in enumerate(((normT_h,normT),(dq_h,dq),(dk_h,dk),(dv_h,dv),(gwo_h,gwo),(wh_h,wh),(x_h,x),(gm_h,gm)))]
    for l in loads: l.start()
    def arrived(a,b):
        for l in loads[a:b]: l.wait()
    out=0
    for k in range(K):
        _,kr,nr=regs[k][n-1]
        for c in range(CH): full[c,p.th,rows_at(kr,nr),:]=red[c,out:out+nr,:]
        out+=nr
    vbuf[0]=jnp.zeros(vbuf.shape[1:],F32)
    vrow[...]=jnp.zeros(vrow.shape,F32)
    barrier(p,["th"]+plan[0][0])
    last=n+n-1
    def head_step(j,c):
        for k in range(HK):
            order=hplan[k][0]
            if 0<j<=n:
                s=j-1
                hsum(k,s,c).wait_recv()
                _,kr,nr=hregs[k][s]
                q=slice(0,2) if order.index("tw")>s else slice(0,1)
                at=(c,q,rows_at(kr,nr),slice(None))
                new=(hp[at].astype(F32)+hrecv[k][s][c].astype(F32)).astype(BF)
                if j<n: hp[at]=new
                else: hg[c,rows_at(kr,nr),:]=new[0]
            elif j>n: hgat(k,backs[k][j-n-1],c,True).wait_recv()
        for k in range(HK):
            if j<n: hsum(k,j,c).start()
            elif j<last: hgat(k,backs[k][j-n],c,False).start()
        if j==last: heads_out[c]=hg[c]
    def gather_step(j,c):
        if 0<j<=n:
            for k in range(K): gat(k,n-j,c,True).wait_recv()
        if j<n:
            for k in range(K): gat(k,n-1-j,c,False).start()
        elif j==n: chip(c,False).start()
        else:
            chip(c,True).wait_recv()
            fput(c).start()
    HT=D//HC
    def weight_grads(t):
        r=rows_at(t*HT,HT)
        parts=[dot(normT[r,:],d[...],NN).astype(BF) for d in (dq,dk,dv)]+[gwo[r,:]]
        for q in range(2):
            y=jnp.concatenate([z[:,q*(C//2):(q+1)*(C//2)] for z in parts],1)
            for i in range(y.shape[1]//128): hp[t,q,i*HT:(i+1)*HT,:]=y[:,i*128:(i+1)*128]
    def norm_grad(core,t):
        rr=rows_at(core*T+t*TT,TT)
        return dot(dq[rr,:],wh[0],NN)+dot(dk[rr,:],wh[1],NN)+dot(dv[rr,:],wh[2],NN)
    def other_half(t): obuf[rows_at(t*TT,TT),:]=norm_grad(1-p.th,t).astype(BF)
    def own_half(t): own[rows_at(t*TT,TT),:]=norm_grad(p.th,t)
    def norm_one_back(i):
        quarter=(1-i)*(1-p.tw)+i*p.tw
        for t in range(Q//128):
            r=rows_at(quarter*Q+t*128,128)
            e=own[r,:]+orecv[r,:].astype(F32)
            nn,rs=norm_parts(x[r,:].astype(F32))
            tbuf[r,:]=(gm[r,:]+norm_back(e,nn,rs,gain[...].reshape(1,D))).astype(BF)
            vrow[0:1,:]+=colsum(e*nn); vrow[1:2,:]+=colsum(e)
    def vectors(_):
        tok[p.tw]=tbuf[rows_at(p.tw*Q,Q),:]
        rows=[vrow[0:1,:],vrow[1:2,:]]+[vec[i:i+1,:] for i in range(4)]+[gbu[...]]
        at=0
        for v in rows:
            for i in range(v.shape[1]//128):
                vbuf[0,at:at+1,:]=v[:,i*128:(i+1)*128]; at+=1
        for i,d in enumerate((dq,dv)):
            bs=colsum(d[...].astype(F32))
            for q in range(2):
                quarter=2*p.th+(p.tw if q==0 else 1-p.tw)
                y=jnp.concatenate([bs[:,q*(C//2):(q+1)*(C//2)],jnp.zeros((1,256-C//2),F32)],1)
                for z in range(2):
                    vbuf[0,pl.ds(at+quarter*4+i*2+z,1),:]=y[:,z*128:(z+1)*128]
    def vector_step(i,_):
        if i>0:
            vcopy(i-1).wait_recv()
            y=vbuf[i-1]+vrecv[i-1]
            if i<len(vaxes): vbuf[i]=y
            else: vec_out[...]=y
        if i<len(vaxes): vcopy(i).start()
    part=functools.partial
    NT_=T//TT; G1=HC; G2=G1+2*NT_
    steps=[(1+HLAG*j,HSP,HC,part(head_step,j)) for j in reversed(range(last+1))]
    steps+=[(GLAG*j,2,CH,part(gather_step,j)) for j in reversed(range(n+2))]
    steps+=[(G2+3+VLAG*i,1,1,part(vector_step,i)) for i in range(len(vaxes)+1)]
    steps+=[(0,1,1,lambda _: arrived(0,5)),(0,1,HC,weight_grads),(G1,1,1,lambda _: arrived(5,6)),(G2,1,1,lambda _: arrived(6,8)),(G1,1,NT_,other_half),(G1+NT_,1,1,lambda _: ocopy().start()),(G1+NT_,1,NT_,own_half),
            (G2,1,1,lambda _: ocopy().wait_recv()),(G2+1,1,1,lambda _: tcopy().start()),(G2,1,2,norm_one_back),(G2+2,1,1,vectors)]
    run_steps(steps)
    def drain(c,_):
        chip(c,False).wait_send(); fput(c).wait()
        for k in range(K):
            for s in range(n): gat(k,s,c,False).wait_send()
        return 0
    lax.fori_loop(0,CH,drain,0)
    def hdrain(c,_):
        for k in range(HK):
            for s in range(n): hsum(k,s,c).wait_send()
            for s in backs[k]: hgat(k,s,c,False).wait_send()
        return 0
    lax.fori_loop(0,HC,hdrain,0)
    for i in range(len(vaxes)): vcopy(i).wait_send()
    ocopy().wait_send(); tcopy().wait()
    tok[1-p.tw]=trecv[...]

def finish(dp,red,dq,dk,dv,normT,wh,gwo,x,gm,gain,vec,gbu):
    T,D=x.shape; CH,fin,_=red.shape; R=FC//128*D
    plan=big_plan(dp,R); n=len(plan[0][0])
    HC=D//TT; HR=2*dq.shape[1]//128*TT; hplan=head_plan(dp,HR)
    hrecv=[]
    for order,_,rows in hplan:
        q=2
        for axis in order:
            if axis=="tw": q=1
            else: rows//=2
            hrecv.append(pltpu.VMEM((HC,q,rows,128),BF))
    V=(6*D+gbu.shape[1])//128+16; nv=n+1; args=(red,dq,dk,dv,normT,wh,gwo,x,gm,gain,vec,gbu)
    return pl.pallas_call(functools.partial(finish_kernel,dp),
      in_specs=[pl.BlockSpec(memory_space=pl.ANY if 1<=i<=8 else pltpu.VMEM) for i in range(len(args))],
      out_specs=[pl.BlockSpec(memory_space=pl.ANY)]+[pl.BlockSpec(memory_space=pltpu.VMEM)]*3,
      out_shape=[jax.ShapeDtypeStruct((CH,2,R,128),BF),jax.ShapeDtypeStruct((HC,HR,128),BF),jax.ShapeDtypeStruct((V,128),F32),jax.ShapeDtypeStruct((2,T//2,D),BF)],
      scratch_shapes=[pltpu.VMEM((CH,2,R,128),BF),pltpu.SemaphoreType.DMA((CH,))]+[pltpu.VMEM(a.shape,a.dtype) for a in args[1:9]]+[pltpu.SemaphoreType.DMA((8,)),pltpu.VMEM((HC,2,HR,128),BF),pltpu.VMEM((HC,HR,128),BF),pltpu.VMEM((nv,V,128),F32),pltpu.VMEM((nv,V,128),F32),pltpu.VMEM((T,D),F32)]+[pltpu.VMEM((T,D),BF)]*3+[pltpu.VMEM((T//2,D),BF),pltpu.VMEM((8,D),F32)]+[pltpu.SemaphoreType.DMA((2,))]*2+hrecv
        +[pltpu.SemaphoreType.DMA((len(plan),n,CH))]*2+[pltpu.SemaphoreType.DMA((CH,))]*2+[pltpu.SemaphoreType.DMA((len(hplan),n,HC))]*4+[pltpu.SemaphoreType.DMA((nv,))]*2,
      compiler_params=pltpu.CompilerParams(vmem_limit_bytes=60*2**20,collective_id=1,has_side_effects=True),name="finish_gradients")(*args)

def widen_kernel(chunk,heads,mine,got,vec,tok,wup,wdown,wqkv,wout,blk,tok_o,bqv,*vectors):
    D=wup.shape[0]; q=wout.shape[0]; g=pl.program_id(0); HT=wout.shape[1]
    for i in range(FC//128):
        cols=slice(i*128,(i+1)*128)
        wup[:,cols]=chunk[0,i*D:(i+1)*D,:].astype(F32)
        wdown[cols,:]=chunk[1,i*D:(i+1)*D,:].T.astype(F32)
    @pl.when(g<D//HT)
    def _():
        y=jnp.concatenate([heads[i*HT:(i+1)*HT,:] for i in range(heads.shape[0]//HT)],1).T.astype(F32)
        for c in range(3): wqkv[c]=y[c*q:(c+1)*q,:]
        wout[...]=y[3*q:,:]
    th,tw=lax.axis_index("th"),lax.axis_index("tw")
    blk[tw]=mine[...]; blk[1-tw]=got[...]
    tok_o[...]=tok[...]
    @pl.when(g==0)
    def _():
        at=sum(v.shape[0] for v in vectors)//128
        for i in range(2):
            for z,w in ((0,128),(1,q-128)): bqv[i:i+1,z*128:z*128+w]=vec[pl.ds(at+4*(2*th+tw)+2*i+z,1),0:w]
        at=0
        for v in vectors:
            for i in range(v.shape[0]//128):
                v[i*128:(i+1)*128]=vec[at,:]; at+=1

def widen(chunks,heads,mine,got,vec,tok):
    CH,_,R,_=chunks.shape; D=R*128//FC; FF=CH*FC; q=heads.shape[0]*heads.shape[1]*128//(4*D); T2=mine.shape[0]
    outs=[(D,FF),(FF,D),(3,q,D),(q,D)]; sizes=[D]*6+[FF]
    NH=heads.shape[0]; tile=lambda g: jnp.minimum(g,NH-1)
    res=pl.pallas_call(widen_kernel,grid=(CH,),
      in_specs=[pl.BlockSpec((None,2,R,128),lambda g:(g,0,0,0))]+[pl.BlockSpec((None,)+heads.shape[1:],lambda g:(tile(g),0,0)),pl.BlockSpec((T2//CH,D),lambda g:(g,0)),pl.BlockSpec((T2//CH,D),lambda g:(g,0)),
        pl.BlockSpec(vec.shape,lambda g:(0,0)),pl.BlockSpec((2,T2//CH,D),lambda g:(0,g,0))],
      out_specs=[pl.BlockSpec((D,FC),lambda g:(0,g)),pl.BlockSpec((FC,D),lambda g:(g,0))]+[pl.BlockSpec((3,q,D//NH),lambda g:(0,0,tile(g))),pl.BlockSpec((q,D//NH),lambda g:(0,tile(g)))]
        +[pl.BlockSpec((2,T2//CH,D),lambda g:(0,g,0))]*2+[pl.BlockSpec(memory_space=pltpu.VMEM)]*(1+len(sizes)),
      out_shape=[jax.ShapeDtypeStruct(o,F32) for o in outs]+[jax.ShapeDtypeStruct((2,T2,D),BF)]*2+[jax.ShapeDtypeStruct((2,q),F32)]+[jax.ShapeDtypeStruct((z,),F32) for z in sizes],
      compiler_params=pltpu.CompilerParams(vmem_limit_bytes=63*2**20),name="widen")(chunks,heads,mine,got,vec,tok)
    return res[:7],res[7:]

def front_kernel(tok,w,b,gain,shift,seg,x_o,normT_o,q_o,k_o,v_o,wh_o,mq_o,mk_o,x,norm,normT,qkv,wh,wgot,bgot,bias,mq,mk,tsem,bsem,csem,ysem,xsem,zsem,osem):
    p=Peers(); Q,D=tok.shape[1:]; T=2*Q; L=2*T; E=w.shape[1]; PART=E//4
    b0,b1=p.bit(0),p.bit(1)
    barrier(p,["th","tw",0,1])
    def tcopy(): return send(tok.at[1-p.tw],x.at[rows_at(p.tw*Q,Q),:],tsem.at[0],tsem.at[1],p.peer("tw"))
    def bcopy(): return send(b,bgot,bsem.at[0],bsem.at[1],p.peer("tw"))
    def ycopy(c):
        r=rows_at((2*b1+b0)*PART,PART)
        return send(w.at[c,r,:],wgot.at[c,r,:],ysem.at[0,c],ysem.at[1,c],p.peer("tw"))
    def xcopy(c,landed):
        ref=wgot.at[c,rows_at((2*b1+(1-b0 if landed else b0))*PART,PART),:]
        return send(ref,ref,xsem.at[0,c],xsem.at[1,c],p.peer(0))
    def zcopy(c,landed):
        ref=wgot.at[c,rows_at((1-b1 if landed else b1)*2*PART,2*PART),:]
        return send(ref,ref,zsem.at[0,c],zsem.at[1,c],p.peer(1))
    def ccopy(i,landed):
        core=1-p.th if landed else p.th
        quarter=p.tw if i==0 else 1-p.tw
        ref=norm.at[rows_at(core*T+quarter*Q,Q),:]
        return send(ref,ref,csem.at[0,i],csem.at[1,i],p.peer("th"))
    for c in range(3): ycopy(c).start()
    bcopy().start()
    tcopy().start()
    g_row=gain[...].reshape(1,D); s_row=shift[...].reshape(1,D)
    def normalize(src,row):
        for t in range(Q//128):
            y=(norm_parts(src(t).astype(F32))[0]*g_row+s_row).astype(BF)
            norm[rows_at(row+t*128,128),:]=y
    def put(src,dst,i): return pltpu.make_async_copy(src,dst,osem.at[i])
    x[rows_at(p.tw*Q,Q),:]=tok[p.tw]
    normalize(lambda t: tok[p.tw,t*128:(t+1)*128,:],p.th*T+p.tw*Q)
    onehot=lax.broadcasted_iota(jnp.int32,(128,L),0)
    onehot=jnp.where(onehot<HD,onehot,onehot-HD)
    same=onehot==seg[pl.ds(p.tw,1),:]
    mk[...]=jnp.where(same,1.0,0.0).T.astype(BF)
    ccopy(0,False).start()
    for c in range(3):
        ycopy(c).wait_recv()
        xcopy(c,False).start()
    mq[...]=jnp.where(same|(onehot>=9),0.0,-float(2**40)).T.astype(BF)
    put(mk,mk_o,0).start(); put(mq,mq_o,1).start()
    bcopy().wait_recv()
    bias[...]=jnp.zeros_like(bias)
    for m,src in enumerate((b,bgot)):
        for i,c in enumerate((0,2)): bias[m,c:c+1,:]=src[i:i+1,:]
    for c in range(3):
        xcopy(c,True).wait_recv()
        zcopy(c,False).start()
    def project(row,weights,m):
        r=rows_at(row,Q)
        def one(c,_):
            y=(dot(norm[r,:],weights[c],NT)+bias[m,pl.ds(c,1),:]).astype(BF)
            y=y*jnp.where(c==0,0.125,1.0).astype(BF)
            qkv[c,r,m*E:(m+1)*E]=y
            return 0
        lax.fori_loop(0,3,one,0)
    def transpose(quarter):
        for core in range(2):
            for t in range(Q//128):
                at=core*T+quarter*Q+t*128
                normT[:,pl.ds(pl.multiple_of(at,128),128)]=norm[rows_at(at,128),:].T
    ccopy(0,True).wait_recv()
    for core in range(2): project(core*T+p.tw*Q,w,0)
    transpose(p.tw)
    for c in range(3): zcopy(c,True).wait_recv()
    for core in range(2): project(core*T+p.tw*Q,wgot,1)
    for c in range(3): wh[c,0:E,:]=w[c]; wh[c,E:2*E,:]=wgot[c]
    put(wh,wh_o,7).start()
    tcopy().wait_recv()
    normalize(lambda t: x[rows_at((1-p.tw)*Q+t*128,128),:],p.th*T+(1-p.tw)*Q)
    put(x,x_o,2).start()
    for m,weights in enumerate((w,wgot)):
        project(p.th*T+(1-p.tw)*Q,weights,m)
        if m==0: ccopy(1,False).start()
    ccopy(1,True).wait_recv()
    for m,weights in enumerate((w,wgot)): project((1-p.th)*T+(1-p.tw)*Q,weights,m)
    for c in range(3): put(qkv.at[c],(q_o,k_o,v_o)[c],4+c).start()
    transpose(1-p.tw)
    put(normT,normT_o,3).start()
    for src,dst,i in ((mk,mk_o,0),(mq,mq_o,1),(x,x_o,2),(normT,normT_o,3),(wh,wh_o,7)): put(src,dst,i).wait()
    for c in range(3):
        put(qkv.at[c],(q_o,k_o,v_o)[c],4+c).wait()
        ycopy(c).wait_send(); xcopy(c,False).wait_send(); zcopy(c,False).wait_send()
    tcopy().wait_send(); bcopy().wait_send()
    for i in range(2): ccopy(i,False).wait_send()

def front(tok,w,b,gain,shift,seg):
    _,Q,D=tok.shape; T=2*Q; L=2*T; E=w.shape[1]
    outs=[((T,D),BF),((D,L),BF)]+[((L,2*E),BF)]*3+[((3,2*E,D),BF)]+[((L,128),BF)]*2
    sem=pltpu.SemaphoreType.DMA
    return pl.pallas_call(front_kernel,
      in_specs=[pl.BlockSpec(memory_space=pltpu.VMEM)]*6,out_specs=[pl.BlockSpec(memory_space=pl.ANY)]*len(outs),
      out_shape=[jax.ShapeDtypeStruct(*o) for o in outs],
      scratch_shapes=[pltpu.VMEM((T,D),BF),pltpu.VMEM((L,D),BF),pltpu.VMEM((D,L),BF),pltpu.VMEM((3,L,2*E),BF),pltpu.VMEM((3,2*E,D),BF),pltpu.VMEM((3,E,D),BF),
        pltpu.VMEM(b.shape,F32),pltpu.VMEM((2,8,E),F32),pltpu.VMEM((L,128),BF),pltpu.VMEM((L,128),BF),sem((2,)),sem((2,)),sem((2,2)),sem((2,3)),sem((2,3)),sem((2,3)),sem((8,))],
      compiler_params=pltpu.CompilerParams(vmem_limit_bytes=60*2**20,collective_id=2,has_side_effects=True),name="front")(tok,w,b,gain,shift,seg)


SWAP = [(0, 1), (1, 0)]


def swap(value, axis):
    return lax.ppermute(value, axis, SWAP)


def body(
    dp_size,
    tokens,
    segment_ids,
    norm1_gain,
    norm1_shift,
    w_qkv,
    b_qv,
    w_out,
    b_out,
    norm2_gain,
    norm2_shift,
    w_up,
    b_up,
    w_down,
    b_down,
    cotangent,
):
    tw = lax.axis_index("tw")
    x, normed_t, query, key, value, w_heads, mq, mk = front(
        tokens, w_qkv.transpose(0, 2, 1), b_qv, norm1_gain, norm1_shift, segment_ids
    )
    tables = (mq, mk, *block_ranges(lax.dynamic_index_in_dim(segment_ids, tw, 0, False)))
    later = lax.optimization_barrier((cotangent, w_out, query))
    cot_got = swap(lax.dynamic_index_in_dim(later[0], 1 - tw, 0, False), "tw")
    w_out_got = swap(later[1], "tw")
    attended, totals = attn_fwd(query, key, value, *tables)
    out_mine, out_other, grad_middle, grad_b_up, sums, red, grad_heads, grad_w_out = ffn(
        dp_size, attended, x, b_out, norm2_gain, norm2_shift, b_down, w_out, w_out_got, cotangent, cot_got, w_up, w_down, b_up[None]
    )
    out_got = swap(out_other, "tw")
    dq, dk, dv = attn_bwd(query, key, value, grad_heads, attended, totals, *tables)
    chunks, heads, small, grad_tokens = finish(
        dp_size, red, dq, dk, dv, normed_t, w_heads, grad_w_out, x, grad_middle, norm1_gain, sums, grad_b_up
    )
    (up, down, w_qkv_grad, w_out_grad, block_out, grad_tokens, b_qv_grad), vecs = widen(
        chunks, heads, out_mine, out_got, small, grad_tokens
    )
    return (
        block_out,
        grad_tokens,
        vecs[0],
        vecs[1],
        w_qkv_grad.transpose(0, 2, 1),
        b_qv_grad,
        w_out_grad,
        vecs[2],
        vecs[3],
        vecs[4],
        up,
        vecs[6],
        down,
        vecs[5],
    )


def solution(mesh):
    return jax.shard_map(
        functools.partial(body, mesh.shape["dp"]),
        mesh=mesh,
        in_specs=(
            P("dp", ("th", "tw"), None),
            P("dp", None),
            P(),
            P(),
            P(None, None, ("th", "tw")),
            P(None, ("th", "tw")),
            P(("th", "tw"), None),
            P(),
            P(),
            P(),
            P(),
            P(),
            P(),
            P(),
            P("dp", ("th", "tw"), None),
        ),
        out_specs=(
            P("dp", ("th", "tw"), None),
            P("dp", ("th", "tw"), None),
            P(),
            P(),
            P(None, None, ("th", "tw")),
            P(None, ("th", "tw")),
            P(("th", "tw"), None),
            P(),
            P(),
            P(),
            P(),
            P(),
            P(),
            P(),
        ),
        check_vma=False,
    )
```
